32 devices in a mesh: fsdp: 8 (over y, x, core), tp: 4 (over z).
Axes of the slice: x: 2, y: 2, z: 4, core: 2. Of those that a mesh axis runs over, the one named last changes fastest.
Arguments:
- content: bfloat16 [12288, 768], P(('fsdp', 'tp')), may hold values from -6 to 6
- query: bfloat16 [12288, 768], P(('fsdp', 'tp')), may hold values from -6 to 6
- w_query: bfloat16 [768, 768], P('fsdp', 'tp'), may hold values from -0.21875 to 0.21875
- w_key: bfloat16 [768, 768], P('fsdp', 'tp'), may hold values from -0.21875 to 0.21875
- w_value: bfloat16 [768, 768], P('fsdp', 'tp'), may hold values from -0.21875 to 0.21875
- w_out: bfloat16 [768, 768], P('tp', 'fsdp'), may hold values from -4 to 4
- w_in: bfloat16 [768, 3072], P('fsdp', 'tp'), may hold values from -0.21875 to 0.21875
- w_down: bfloat16 [3072, 768], P('tp', 'fsdp'), may hold values from -0.21875 to 0.21875
- gain_first: float32 [768], replicated, may hold values from 0.5 to 1.5
- shift_first: float32 [768], replicated, may hold values from -3 to 3
- gain_second: float32 [768], replicated, may hold values from 0.5 to 1.5
- shift_second: float32 [768], replicated, may hold values from -3 to 3
- bias_table: float32 [12, 32], replicated, may hold values from -4 to 4
- ranks: int32 [8, 1536], P('fsdp'), may hold values from 0 to 1535, each once within a row
- span_starts: int32 [8, 2], P('fsdp'), may hold values from 0 to 1280, as said below
- upstream_content: bfloat16 [12288, 768], P(('fsdp', 'tp')), may hold values from -6 to 6
- upstream_query: bfloat16 [12288, 768], P(('fsdp', 'tp')), may hold values from -6 to 6
Outputs:
- content_out: bfloat16 [12288, 768], P(('fsdp', 'tp'))
- query_out: bfloat16 [12288, 768], P(('fsdp', 'tp'))
- grad_content: float32 [12288, 768], P(('fsdp', 'tp'))
- grad_query: float32 [12288, 768], P(('fsdp', 'tp'))
- grad_w_query: float32 [768, 768], P('fsdp', 'tp')
- grad_w_key: float32 [768, 768], P('fsdp', 'tp')
- grad_w_value: float32 [768, 768], P('fsdp', 'tp')
- grad_w_out: float32 [768, 768], P('tp', 'fsdp')
- grad_w_in: float32 [768, 3072], P('fsdp', 'tp')
- grad_w_down: float32 [3072, 768], P('tp', 'fsdp')
- grad_gain_first: float32 [768], replicated
- grad_shift_first: float32 [768], replicated
- grad_gain_second: float32 [768], replicated
- grad_shift_second: float32 [768], replicated
- grad_bias_table: float32 [12, 32], replicated
The draws below stay inside these ranges and needn't reach their ends.
Inputs may be any that keep to these rules, and one draw needn't show every extreme that they name: `ranks`: each row is a permutation of 0 to 1535. `span_starts`: the k-th start of a sequence lies in [k * 768, (k + 1) * 768 - 256], so spans never intersect.
All inputs are finite; a program needn't handle non-finite values.
Results may differ from the reference program's by a relative error of at most 0.025.
Values may be sent and summed in bfloat16 or wider, within the bound.
A program may use at most 192 MiB of HBM per device.

```python
import jax
import jax.numpy as jnp
from jax import lax

D = 768
HEADS = 12
HEAD = 64
FF = 3072
NB = 32
PIC = 256
SPANS = 2
SEQ = 1536
SEQS = 8
TOKENS = 12288
PRED = 230


def draw_span_starts(key, part):
    slot_len = SEQ // SPANS
    offsets = jax.random.randint(key, (SEQS, SPANS), 0, slot_len - PIC + 1)
    first_row = jnp.arange(SEQS)[:, None] == 0
    columns = jnp.arange(SPANS)[None, :]
    offsets = jnp.where(first_row & (columns == 0), 0, offsets)
    offsets = jnp.where(first_row & (columns == SPANS - 1), slot_len - PIC, offsets)
    return (columns * slot_len + offsets).astype(jnp.int32)


def shard_levels(stream_key, extent, pieces, least, high):
    def one(position, parts):
        steps = jax.random.uniform(jax.random.fold_in(jax.random.fold_in(stream_key, 6), position), (parts,), jnp.float32, least / len(pieces), high / len(pieces))
        return jnp.repeat(jnp.exp(steps), extent[position] // parts).reshape((-1,) + (1,) * (len(extent) - position - 1))

    level = one(*pieces[0])
    for cut in pieces[1:]:
        level = level * one(*cut)
    return level


def centred(stream_key, extent, spread, reach, pieces=(), kind=jnp.bfloat16):
    loudness = shard_levels(stream_key, extent, pieces, -0.22, 0.18) if pieces else 1.0
    entries = jax.random.normal(stream_key, extent, jnp.float32) * spread * loudness
    return jnp.minimum(jnp.maximum(entries, -reach), reach).astype(kind)


def setup_inputs(seed: int = 0) -> dict:
    seeds = jax.random.split(jax.random.key(seed), 18)
    return {
        "content": centred(seeds[0], (TOKENS, D), 1.0, 6.0, ((0, 32),)),
        "query": centred(seeds[1], (TOKENS, D), 1.0, 6.0, ((0, 32),)),
        "w_query": centred(seeds[2], (D, D), D ** -0.5, 0.21875, ((0, 8), (1, 4))),
        "w_key": centred(seeds[3], (D, D), D ** -0.5, 0.21875, ((0, 8), (1, 4))),
        "w_value": centred(seeds[4], (D, D), D ** -0.5, 0.21875, ((0, 8), (1, 4))),
        "w_out": centred(seeds[5], (D, D), (max(1, 4 * D // SEQ)) ** -0.5, 4.0, ((0, 4), (1, 8))),
        "w_in": centred(seeds[6], (D, FF), D ** -0.5, 0.21875, ((0, 8), (1, 4))),
        "w_down": centred(seeds[7], (FF, D), (FF // 4) ** -0.5, 0.21875, ((0, 4), (1, 8))),
        "gain_first": jnp.clip(1.0 + 0.1 * jax.random.normal(seeds[8], (D,), jnp.float32), 0.5, 1.5),
        "shift_first": centred(seeds[9], (D,), 0.5, 3.0, (), jnp.float32),
        "gain_second": jnp.clip(1.0 + 0.1 * jax.random.normal(seeds[10], (D,), jnp.float32), 0.5, 1.5),
        "shift_second": centred(seeds[11], (D,), 0.5, 3.0, (), jnp.float32),
        "bias_table": centred(seeds[12], (HEADS, NB), 1.0, 4.0, (), jnp.float32),
        "ranks": jax.vmap(lambda own: jax.random.permutation(own, SEQ))(jax.random.split(seeds[13], SEQS)).reshape((SEQS, SEQ)).astype(jnp.int32),
        "span_starts": draw_span_starts(jax.random.fold_in(seeds[17], 71), 0),
        "upstream_content": centred(seeds[15], (TOKENS, D), 1.0, 6.0, ((0, 32),)),
        "upstream_query": centred(seeds[16], (TOKENS, D), 1.0, 6.0, ((0, 32),)),
    }


@jax.custom_vjp
def low(v):
    return lax.optimization_barrier(v.astype(jnp.bfloat16)).astype(jnp.float32)

@jax.custom_vjp
def low_back(v):
    return v

def low_keep(v):
    return (low(v), None)

def low_pass(kept, grad):
    return (grad,)

def back_keep(v):
    return (v, None)

def back_low(kept, grad):
    return (low(grad),)
low.defvjp(low_keep, low_pass)
low_back.defvjp(back_keep, back_low)
THRESHOLDS = (12, 16, 23, 32, 46, 64, 91)
EPSILON = 1e-05
HIGHEST = lax.Precision.HIGHEST

def both_ways(values):
    return low_back(low(values))

def matmul(first_op, second_op):
    return jnp.dot(first_op, second_op, precision=HIGHEST, preferred_element_type=jnp.float32)

def bucket_of(offsets):
    magnitude = jnp.abs(offsets)
    far_bucket = 8 + sum(((magnitude >= threshold).astype(jnp.int32) for threshold in THRESHOLDS))
    near_or_far = jnp.where(magnitude < 8, magnitude, far_bucket)
    return (near_or_far + 16 * (offsets > 0).astype(jnp.int32)).astype(jnp.int32)

def span_labels(starts, length):
    places = jnp.arange(length, dtype=jnp.int32)
    inside = (places[None, :] >= starts[:, None]) & (places[None, :] < starts[:, None] + PIC)
    labels = jnp.arange(starts.shape[0], dtype=jnp.int32)[:, None] + 1
    return lax.optimization_barrier(jnp.sum(jnp.where(inside, labels, 0), axis=0)).astype(jnp.int32) - 1

def allowed_keys(row_start, block_rows, rank_all, span_all, strict):
    length = rank_all.shape[0]
    places = jnp.arange(length, dtype=jnp.int32)
    row_places = row_start + jnp.arange(block_rows, dtype=jnp.int32)
    rank_rows = lax.dynamic_slice_in_dim(rank_all, row_start, block_rows)
    span_rows = lax.dynamic_slice_in_dim(span_all, row_start, block_rows)
    same_span = (span_rows[:, None] == span_all[None, :]) & (span_rows[:, None] >= 0)
    if strict:
        earlier = rank_all[None, :] < jnp.maximum(rank_rows, 1)[:, None]
        same_span = same_span & (row_places[:, None] != places[None, :])
    else:
        earlier = rank_all[None, :] <= rank_rows[:, None]
    return earlier | same_span

def layer_norm(residual, gain, shift):
    mean_row = lax.optimization_barrier(jnp.mean(residual, axis=-1, keepdims=True))
    centered = residual - mean_row
    variance = lax.optimization_barrier(jnp.mean(centered * centered, axis=-1, keepdims=True))
    return centered * lax.rsqrt(variance + EPSILON) * gain + shift

def attend_sequence(queries, key_proj, value_proj, rank_all, span_all, bias_table, strict):
    block_rows = min(512, SEQ)
    score_scale = HEAD ** (-0.5)
    places = jnp.arange(SEQ, dtype=jnp.int32)

    def one_block(row_start):
        query_rows = lax.dynamic_slice_in_dim(queries, row_start, block_rows, 0)
        raw_scores = jnp.einsum('qhd,khd->hqk', query_rows, key_proj, precision=HIGHEST) * score_scale
        offsets = places[None, :] - (row_start + jnp.arange(block_rows, dtype=jnp.int32))[:, None]
        scores = low_back(raw_scores + bias_table[:, bucket_of(offsets)])
        allowed = allowed_keys(row_start, block_rows, rank_all, span_all, strict)
        masked = jnp.where(allowed[None], scores, -1e+30)
        shifted = masked - lax.optimization_barrier(jnp.max(masked, axis=-1, keepdims=True))
        exponent = jnp.exp(shifted)
        attn_probs = exponent / lax.optimization_barrier(jnp.sum(exponent, axis=-1, keepdims=True))
        return jnp.einsum('hqk,khd->qhd', low(attn_probs), value_proj, precision=HIGHEST)
    starts_all = jnp.arange(SEQ // block_rows, dtype=jnp.int32) * block_rows
    mixed_heads = lax.map(jax.checkpoint(one_block), starts_all)
    return mixed_heads.reshape(SEQ, HEADS * HEAD)

def forward(content, query, w_query, w_key, w_value, w_out, w_in, w_down, gain_first, shift_first, gain_second, shift_second, bias_table, ranks, span_starts):
    query_content = both_ways(matmul(content, w_query))
    key_proj = both_ways(matmul(content, w_key))
    value_proj = both_ways(matmul(content, w_value))
    query_query = both_ways(matmul(query, w_query))
    head_shape = (SEQS, SEQ, HEADS, HEAD)
    span_all = jax.vmap(lambda starts: span_labels(starts, SEQ))(span_starts)

    def attend_all(queries, strict):

        def per_sequence(inputs):
            return attend_sequence(inputs[0], inputs[1], inputs[2], inputs[3], inputs[4], bias_table, strict)
        mixed_all = lax.map(per_sequence, (queries.reshape(head_shape), key_proj.reshape(head_shape), value_proj.reshape(head_shape), ranks, span_all))
        return mixed_all.reshape(TOKENS, D)
    mixed_content = both_ways(attend_all(query_content, False))
    mixed_query = both_ways(attend_all(query_query, True))
    normed_content = layer_norm(content + low_back(matmul(mixed_content, w_out)), gain_first, shift_first)
    normed_query = layer_norm(query + low_back(matmul(mixed_query, w_out)), gain_first, shift_first)

    def feed_forward(normed):
        lifted = low_back(matmul(low(normed), w_in))
        hidden = low(jax.nn.gelu(lifted, approximate=False))
        return low_back(matmul(hidden, w_down))
    second_content = layer_norm(normed_content + feed_forward(normed_content), gain_second, shift_second)
    second_query = layer_norm(normed_query + feed_forward(normed_query), gain_second, shift_second)
    return (second_content, second_query)

def reference(content, query, w_query, w_key, w_value, w_out, w_in, w_down, gain_first, shift_first, gain_second, shift_second, bias_table, ranks, span_starts, upstream_content, upstream_query):
    floats = tuple((argument.astype(jnp.float32) for argument in (content, query, w_query, w_key, w_value, w_out, w_in, w_down, gain_first, shift_first, gain_second, shift_second, bias_table)))

    def closed(*params):
        return forward(*params, ranks, span_starts)
    outputs, pullback = jax.vjp(closed, *floats)
    predicted = (ranks.reshape(TOKENS) >= SEQ - PRED).astype(jnp.float32)
    gradients = pullback((upstream_content.astype(jnp.float32), upstream_query.astype(jnp.float32) * predicted[:, None]))
    return (outputs[0].astype(jnp.bfloat16), outputs[1].astype(jnp.bfloat16), gradients[0], gradients[1], gradients[2], gradients[3], gradients[4], gradients[5], gradients[6], gradients[7], gradients[8], gradients[9], gradients[10], gradients[11], gradients[12])
```

```python
import functools
import jax, jax.numpy as jnp
from jax import lax
from jax.sharding import PartitionSpec as P
from jax.experimental import pallas as pl
from jax.experimental.pallas import tpu as pltpu

NEG = -1e30
LOG2E = 1.4426950408889634
LN2 = 0.6931471805599453
VLIM = 60 * 2**20

def nn(a, b):
    return lax.dot_general(a, b, (((1,), (0,)), ((), ())), preferred_element_type=jnp.float32)
def nt(a, b):
    return lax.dot_general(a, b, (((1,), (1,)), ((), ())), preferred_element_type=jnp.float32)

def band_kind(i, b, nrow, nkey):
    rel = (b - i) % nkey
    if rel == 0: return 2
    if rel == nkey - 1: return 0 if i == 0 else 1
    if rel == 1: return 4 if i == nrow - 1 else 3
    return None

def build_mask(mask, kcol, rrow, nkey, nrow):
    def one(b, _):
        keys = pl.ds(pl.multiple_of(b * 128, 128), 128)
        rank_k = kcol[0, keys, :]
        span_k = kcol[1, keys, :]
        kpos = b * 128 + lax.broadcasted_iota(jnp.int32, (128, 128), 0)
        for i in range(nrow):
            rank_r = rrow[0:1, i * 128:(i + 1) * 128]
            span_r = rrow[1:2, i * 128:(i + 1) * 128]
            rpos = i * 128 + lax.broadcasted_iota(jnp.int32, (128, 128), 1)
            same = (span_k == span_r) & (span_k >= 0)
            content = (rank_k <= rank_r) | same
            strict = (rank_k < jnp.maximum(rank_r, 1)) | (same & (kpos != rpos))
            mask[keys, i * 128:(i + 1) * 128] = jnp.where(content, 0.0, NEG)
            mask[keys, (nrow + i) * 128:(nrow + i + 1) * 128] = jnp.where(strict, 0.0, NEG)
        return 0
    lax.fori_loop(0, nkey, one, 0)

def band_tiles(band, vec, h):
    lane = lax.broadcasted_iota(jnp.int32, (128, 128), 1)
    sub = lax.broadcasted_iota(jnp.int32, (128, 128), 0)
    for k in range(5):
        direct, wrapped = (
            pltpu.roll(jnp.broadcast_to(vec[h, 2 * k + w:2 * k + w + 1, :], (128, 128)), 0, 1, stride=1, stride_axis=0)
            for w in range(2)
        )
        band[k] = jnp.where(lane >= sub, direct, wrapped)

def diagonal_sums(tile):
    lane = lax.broadcasted_iota(jnp.int32, (8, 128), 1)
    sub = lax.broadcasted_iota(jnp.int32, (8, 128), 0)
    direct = wrapped = jnp.zeros((8, 128), jnp.float32)
    for a in range(16):
        rows = tile[8 * a:8 * a + 8, :]
        kept = jnp.where(lane >= sub + 8 * a, rows, 0.0)
        left = rows - kept
        if a:
            kept, left = pltpu.roll(kept, 128 - 8 * a, 1), pltpu.roll(left, 128 - 8 * a, 1)
        direct, wrapped = direct + kept, wrapped + left
    for bit in (1, 2, 4):
        moved = (sub & bit) != 0
        direct = jnp.where(moved, pltpu.roll(direct, 128 - bit, 1), direct)
        wrapped = jnp.where(moved, pltpu.roll(wrapped, 128 - bit, 1), wrapped)
    return jnp.sum(direct, axis=0, keepdims=True), jnp.sum(wrapped, axis=0, keepdims=True)

def head_rows(ref, p, hh, cols):
    z = jnp.zeros((64, cols.stop - cols.start), jnp.bfloat16)
    rows = ref[pl.ds(pl.multiple_of((2 * p + hh) * 64, 64), 64), cols]
    return jnp.concatenate([rows, z] if hh == 0 else [z, rows], axis=0)

def fwd_kernel(nrow, nkey, kcol, rrow, cf, vec, kp, vt, qt, ot, lse, mask, t, band):
    build_mask(mask, kcol, rrow, nkey, nrow)
    ones = jnp.ones((16, 256), jnp.bfloat16)
    nchunk = 2 * nrow * 128 // 256
    def pair(p, _):
        for hh in range(2):
            h = 2 * p + hh
            hrows = pl.ds(pl.multiple_of(h * 64, 64), 64)
            band_tiles(band, vec, h)
            for c in range(nchunk):
                cols = slice(c * 256, (c + 1) * 256)
                qh = head_rows(qt, p, hh, cols)
                m8 = jnp.full((8, 256), -jnp.inf, jnp.float32)
                for b in range(nkey):
                    s = nn(kp[p, b * 128:(b + 1) * 128, :], qh)
                    s = s + mask[b * 128:(b + 1) * 128, cols]
                    kinds = [band_kind((2 * c + k) % nrow, b, nrow, nkey) for k in range(2)]
                    if any(k is not None for k in kinds):
                        s = jnp.concatenate([s[:, k * 128:(k + 1) * 128] + (band[kinds[k]] if kinds[k] is not None else 0.0) for k in range(2)], axis=1)
                    t[c, b * 128:(b + 1) * 128, :] = s
                    m8 = jnp.maximum(m8, jnp.max(s.reshape(16, 8, 256), axis=0) + cf[h, b:b + 1, cols])
                m = jnp.max(m8, axis=0, keepdims=True)
                acc = jnp.zeros((80, 256), jnp.float32)
                for g in range(nkey // 2):
                    ps = []
                    for b in (2 * g, 2 * g + 1):
                        ps.append(jnp.exp2(t[c, b * 128:(b + 1) * 128, :] - (m - cf[h, b:b + 1, cols])).astype(jnp.bfloat16))
                    lhs = jnp.concatenate([vt[hrows, g * 256:(g + 1) * 256], ones], axis=0)
                    acc = acc + nn(lhs, jnp.concatenate(ps, axis=0))
                l = acc[64:65, :]
                ot[hrows, cols] = (acc[:64, :] / l).astype(jnp.bfloat16)
                lse[h, 0:1, cols] = m + jnp.log2(l)
        return 0
    lax.fori_loop(0, kp.shape[0], pair, 0)

def attend_fwd(kcol, rrow, cf, vec, kp, vt, qt):
    pairs, seq, _ = kp.shape
    rows = qt.shape[1]
    nrow, nkey = rows // 256, seq // 128
    V = pl.BlockSpec(memory_space=pltpu.MemorySpace.VMEM)
    return pl.pallas_call(
        functools.partial(fwd_kernel, nrow, nkey),
        out_shape=(jax.ShapeDtypeStruct(qt.shape, jnp.bfloat16), jax.ShapeDtypeStruct((2 * pairs, 1, rows), jnp.float32)),
        in_specs=[V] * 7, out_specs=(V, V),
        scratch_shapes=[pltpu.VMEM((seq, rows), jnp.float32), pltpu.VMEM((rows // 256, seq, 256), jnp.float32), pltpu.VMEM((5, 128, 128), jnp.float32)],
        compiler_params=pltpu.CompilerParams(vmem_limit_bytes=VLIM),
        name="attend_fwd",
    )(kcol, rrow, cf, vec, kp, vt, qt)

def bwd_kernel(nrow, nkey, kcol, rrow, cf, vec, kp, vp, kt, qt, ot, got, lse, gqt, gkt, gvt, far, diag, mask, gq, bacc, band):
    build_mask(mask, kcol, rrow, nkey, nrow)
    rows = 2 * nrow * 128
    nchunk = rows // 256
    full = slice(0, rows)
    block_of = lax.broadcasted_iota(jnp.int32, (16, 256), 0)
    half_of = lax.broadcasted_iota(jnp.int32, (16, 256), 1) // 128
    def pair(p, _):
        for hh in range(2):
            h = 2 * p + hh
            hrows = pl.ds(pl.multiple_of(h * 64, 64), 64)
            band_tiles(band, vec, h)
            q_h = qt[hrows, :]
            go_h = got[hrows, :]
            delta = jnp.sum(ot[hrows, :].astype(jnp.float32) * go_h.astype(jnp.float32), axis=0, keepdims=True)
            for k in range(5):
                bacc[k] = jnp.zeros((128, 128), jnp.float32)
            gq[...] = jnp.zeros_like(gq)
            qm = head_rows(qt, p, hh, full)
            gm = head_rows(got, p, hh, full)
            for g in range(nkey // 2):
                pp, gg = [], []
                for c in range(nchunk):
                    cols = slice(c * 256, (c + 1) * 256)
                    pc, gc = [], []
                    for b in (2 * g, 2 * g + 1):
                        keys = slice(b * 128, (b + 1) * 128)
                        s = nn(kp[p, keys, :], qm[:, cols])
                        dp = nn(vp[p, keys, :], gm[:, cols])
                        s = s + mask[keys, cols]
                        kinds = [band_kind((2 * c + k) % nrow, b, nrow, nkey) for k in range(2)]
                        if any(k is not None for k in kinds):
                            s = jnp.concatenate([s[:, k * 128:(k + 1) * 128] + (band[kinds[k]] if kinds[k] is not None else 0.0) for k in range(2)], axis=1)
                        pr = jnp.exp2(s - (lse[h, 0:1, cols] - cf[h, b:b + 1, cols]))
                        gs = pr * (dp - delta[:, cols])
                        for k in range(2):
                            if kinds[k] is not None:
                                bacc[kinds[k]] += gs[:, k * 128:(k + 1) * 128]
                        pc.append(pr.astype(jnp.bfloat16))
                        gc.append(gs.astype(jnp.bfloat16))
                    pp.append(jnp.concatenate(pc, axis=0))
                    gg.append(jnp.concatenate(gc, axis=0))
                pall = jnp.concatenate(pp, axis=1)
                gall = jnp.concatenate(gg, axis=1)
                keys = slice(g * 256, (g + 1) * 256)
                onehot = (block_of == 2 * g + half_of).astype(jnp.bfloat16)
                gq[...] += nn(jnp.concatenate([kt[hrows, keys], onehot], axis=0), gall)
                gkt[hrows, keys] = (nt(q_h, gall) * LN2).astype(jnp.bfloat16)
                gvt[hrows, keys] = nt(go_h, pall).astype(jnp.bfloat16)
            gqt[hrows, :] = (gq[:64, :] * 0.125).astype(jnp.bfloat16)
            far[h] = gq[64:80, :]
            for k in range(5):
                direct, wrapped = diagonal_sums(bacc[k])
                diag[h, 2 * k:2 * k + 1, :] = direct
                diag[h, 2 * k + 1:2 * k + 2, :] = wrapped
        return 0
    lax.fori_loop(0, kp.shape[0], pair, 0)

def attend_bwd(kcol, rrow, cf, vec, kp, vp, kt, qt, ot, got, lse):
    pairs, seq, _ = kp.shape
    rows = qt.shape[1]
    nrow, nkey = rows // 256, seq // 128
    V = pl.BlockSpec(memory_space=pltpu.MemorySpace.VMEM)
    S = jax.ShapeDtypeStruct
    return pl.pallas_call(
        functools.partial(bwd_kernel, nrow, nkey),
        out_shape=(S(qt.shape, jnp.bfloat16), S(kt.shape, jnp.bfloat16), S(kt.shape, jnp.bfloat16), S((2 * pairs, 16, rows), jnp.float32), S((2 * pairs, 16, 128), jnp.float32)),
        in_specs=[V] * 11, out_specs=(V,) * 5,
        scratch_shapes=[pltpu.VMEM((seq, rows), jnp.float32), pltpu.VMEM((80, rows), jnp.float32), pltpu.VMEM((5, 128, 128), jnp.float32), pltpu.VMEM((5, 128, 128), jnp.float32)],
        compiler_params=pltpu.CompilerParams(vmem_limit_bytes=VLIM),
        name="attend_bwd",
    )(kcol, rrow, cf, vec, kp, vp, kt, qt, ot, got, lse)


HEAD = 64
NB = 32
PIC = 256
THRESHOLDS = (12, 16, 23, 32, 46, 64, 91)
EPSILON = 1e-05


def bucket_of(offsets):
    magnitude = jnp.abs(offsets)
    far_bucket = 8 + sum((magnitude >= threshold).astype(jnp.int32) for threshold in THRESHOLDS)
    return jnp.where(magnitude < 8, magnitude, far_bucket) + 16 * (offsets > 0).astype(jnp.int32)


def span_labels(starts, length):
    places = jnp.arange(length, dtype=jnp.int32)
    inside = (places[None, :] >= starts[:, None]) & (places[None, :] < starts[:, None] + PIC)
    labels = jnp.arange(starts.shape[0], dtype=jnp.int32)[:, None] + 1
    return jnp.sum(jnp.where(inside, labels, 0), axis=0) - 1


def dot(spec, a, b):
    return jnp.einsum(spec, a, b, preferred_element_type=jnp.float32)


def norm_stats(residual):
    centered = residual - jnp.mean(residual, axis=-1, keepdims=True)
    scale = lax.rsqrt(jnp.mean(centered * centered, axis=-1, keepdims=True) + EPSILON)
    return centered * scale, scale


def norm_back(cotangent, normal, scale, gain):
    inner = cotangent * gain
    mean_inner = jnp.mean(inner, axis=-1, keepdims=True)
    mean_cross = jnp.mean(inner * normal, axis=-1, keepdims=True)
    back = scale * (inner - mean_inner - normal * mean_cross)
    return back, jnp.sum(cotangent * normal, axis=0), jnp.sum(cotangent, axis=0)


def bucket_tables(nrow, nkey, tp_index, tp_size):
    lanes = jnp.arange(128, dtype=jnp.int32)
    rel = jnp.array([-1, -1, 0, 1, 1], jnp.int32)
    offsets = 128 * rel[:, None, None] + 128 * jnp.arange(2, dtype=jnp.int32)[None, :, None] - lanes
    buckets = bucket_of(offsets)
    far_right, far_left = bucket_of(jnp.int32(128)), bucket_of(jnp.int32(-128))
    buckets = buckets.at[0].set(jnp.where(tp_index == 0, far_right, buckets[0]))
    buckets = buckets.at[4].set(jnp.where(tp_index == tp_size - 1, far_left, buckets[4]))
    key_block = jnp.arange(16, dtype=jnp.int32)[:, None]
    row_block = jnp.arange(nrow, dtype=jnp.int32)[None, :]
    gap = (key_block - row_block) % nkey
    far = (gap != 0) & (gap != 1) & (gap != nkey - 1) & (key_block < nkey)
    key_place = (key_block + nrow * tp_index) % nkey
    left = far & (key_place < row_block + nrow * tp_index)
    right = far & (key_place > row_block + nrow * tp_index)
    return buckets.reshape(10, 128), left, right


def local(
    tp_size, content, query, w_query, w_key, w_value, w_out, w_in, w_down, gain_first, shift_first,
    gain_second, shift_second, bias_table, ranks, span_starts, upstream_content, upstream_query,
):
    rows, width = content.shape
    seq = ranks.shape[1]
    nrow, nkey = rows // 128, seq // 128
    heads = bias_table.shape[0]
    pairs = heads // 2
    tp_index = lax.axis_index("tp")
    both_axes = ("tp", "fsdp")
    narrow = w_query.shape[1]

    def gather(parts):
        shard = jnp.concatenate(parts, axis=1)
        return lax.all_gather(shard, both_axes, axis=0, tiled=True).reshape(tp_size, width, shard.shape[1])

    seq_content = lax.all_gather(content, "tp", axis=0, tiled=True)
    first = gather([w_query, w_key, w_value])
    second = gather([w_out.T, w_in, w_down.T])
    wq, wk, wv = (first[:, :, i * narrow:(i + 1) * narrow] for i in range(3))
    wide = w_in.shape[1]
    wo, wi, wd = second[:, :, :narrow], second[:, :, narrow:narrow + wide], second[:, :, narrow + wide:]

    shift = -rows * tp_index
    seq_rot = jnp.roll(seq_content, shift, axis=0)
    rank_all = ranks[0]
    span_all = span_labels(span_starts[0], seq)
    marks = jnp.roll(jnp.stack([rank_all, span_all]), shift, axis=1)
    kcol = jnp.broadcast_to(marks[:, :, None], (2, seq, 128))
    rrow = jnp.concatenate([marks[:, :rows], jnp.zeros((6, rows), jnp.int32)], axis=0)
    buckets, left, right = bucket_tables(nrow, nkey, tp_index, tp_size)
    one_hot = (buckets.reshape(-1)[None, :] == jnp.arange(NB, dtype=jnp.int32)[:, None]).astype(jnp.float32)
    table = bias_table * LOG2E
    vec = jnp.dot(table, one_hot, precision=lax.Precision.HIGHEST).reshape(heads, 10, 128)
    cf = jnp.where(left[None], table[:, 15, None, None], 0.0) + jnp.where(right[None], table[:, 31, None, None], 0.0)
    cf = jnp.broadcast_to(cf[:, :, None, :, None], (heads, 16, 2, nrow, 128)).reshape(heads, 16, 2 * rows)

    both = jnp.concatenate([content, query], axis=0)
    qt = (dot("tdc,rd->tcr", wq, both) * (HEAD ** -0.5 * LOG2E)).astype(jnp.bfloat16).reshape(width, 2 * rows)
    kt = dot("tdc,rd->tcr", wk, seq_rot).astype(jnp.bfloat16).reshape(width, seq)
    vt = dot("tdc,rd->tcr", wv, seq_rot).astype(jnp.bfloat16).reshape(width, seq)
    kp = jnp.swapaxes(kt.reshape(pairs, 128, seq), 1, 2)
    vp = jnp.swapaxes(vt.reshape(pairs, 128, seq), 1, 2)
    ot, lse = attend_fwd(kcol, rrow, cf, vec, kp, vt, qt)

    ot_blocks = ot.reshape(tp_size, narrow, 2 * rows)
    residual_first = both.astype(jnp.float32) + dot("tcr,tmc->rm", ot_blocks, wo)
    normal_first, scale_first = norm_stats(residual_first)
    normed_first = normal_first * gain_first + shift_first
    low_first = normed_first.astype(jnp.bfloat16)
    lifted = dot("rd,tdf->trf", low_first, wi)
    phi = 0.5 * (1.0 + lax.erf(lifted * (0.5 ** 0.5)))
    hidden = (lifted * phi).astype(jnp.bfloat16)
    slope = phi + lifted * jnp.exp(-0.5 * lifted * lifted) * 0.3989422804014327
    residual_second = normed_first + dot("trf,tmf->rm", hidden, wd)
    normal_second, scale_second = norm_stats(residual_second)
    normed_second = normal_second * gain_second + shift_second
    predicted = (marks[0, :rows] >= seq - seq * 15 // 100).astype(jnp.float32)
    upstream = jnp.concatenate(
        [upstream_content.astype(jnp.float32), upstream_query.astype(jnp.float32) * predicted[:, None]], axis=0
    )
    back_second, grad_gain_second, grad_shift_second = norm_back(upstream, normal_second, scale_second, gain_second)
    gf = back_second.astype(jnp.bfloat16)
    gu = (slope * dot("rm,tmf->trf", gf, wd)).astype(jnp.bfloat16)
    grad_down = dot("rm,trf->tmf", gf, hidden)
    grad_in = dot("rd,trf->tdf", low_first, gu)
    back_normed = back_second + dot("trf,tdf->rd", gu, wi)
    back_first, grad_gain_first, grad_shift_first = norm_back(back_normed, normal_first, scale_first, gain_first)
    ga = back_first.astype(jnp.bfloat16)
    grad_out = dot("rm,tcr->tmc", ga, ot_blocks)
    got = dot("rm,tmc->tcr", ga, wo).astype(jnp.bfloat16).reshape(width, 2 * rows)

    def scatter(blocks):
        flat = blocks.astype(jnp.bfloat16).reshape(tp_size * width, blocks.shape[2])
        return lax.psum_scatter(flat, both_axes, scatter_dimension=0, tiled=True).astype(jnp.float32)

    sum_down, sum_in, sum_out = scatter(grad_down), scatter(grad_in), scatter(grad_out)
    gqt, gkt, gvt, far, diag = attend_bwd(kcol, rrow, cf, vec, kp, vp, kt, qt, ot, got, lse)
    gq_blocks, gk_blocks, gv_blocks = (g.reshape(tp_size, narrow, g.shape[1]) for g in (gqt, gkt, gvt))
    sum_query = scatter(dot("rd,tcr->tdc", both, gq_blocks))
    sum_key = scatter(dot("rd,tcr->tdc", seq_rot, gk_blocks))
    sum_value = scatter(dot("rd,tcr->tdc", seq_rot, gv_blocks))
    back_seq = dot("tcr,tdc->rd", gk_blocks, wk) + dot("tcr,tdc->rd", gv_blocks, wv)
    back_seq = jnp.roll(back_seq.astype(jnp.bfloat16), -shift, axis=0)
    back_content = lax.psum_scatter(back_seq, "tp", scatter_dimension=0, tiled=True).astype(jnp.float32)
    back_inputs = back_first + dot("tcr,tdc->rd", gq_blocks, wq)

    far_sums = jnp.sum(far.reshape(heads, 16, 2, nrow, 128), axis=(2, 4))
    columns = jnp.arange(NB, dtype=jnp.int32)[None, :]
    grad_table = jnp.dot(diag[:, :10].reshape(heads, 1280), one_hot.T, precision=lax.Precision.HIGHEST)
    for side, column in ((left, 15), (right, 31)):
        grad_table = grad_table + jnp.sum(jnp.where(side[None], far_sums, 0.0), axis=(1, 2))[:, None] * (columns == column)
    norm_stack = jnp.stack([grad_gain_first, grad_shift_first, grad_gain_second, grad_shift_second])
    summed_norms, summed_table = lax.psum((norm_stack, grad_table), ("fsdp", "tp"))
    return (
        normed_second[:rows].astype(jnp.bfloat16), normed_second[rows:].astype(jnp.bfloat16),
        back_inputs[:rows] + back_content, back_inputs[rows:],
        sum_query, sum_key, sum_value, sum_out.T, sum_in, sum_down.T,
        summed_norms[0], summed_norms[1], summed_norms[2], summed_norms[3], summed_table,
    )


def solution(mesh):
    in_specs = (
        P(("fsdp", "tp"), None),
        P(("fsdp", "tp"), None),
        P("fsdp", "tp"),
        P("fsdp", "tp"),
        P("fsdp", "tp"),
        P("tp", "fsdp"),
        P("fsdp", "tp"),
        P("tp", "fsdp"),
        P(),
        P(),
        P(),
        P(),
        P(),
        P("fsdp", None),
        P("fsdp", None),
        P(("fsdp", "tp"), None),
        P(("fsdp", "tp"), None),
    )
    out_specs = (
        P(("fsdp", "tp"), None),
        P(("fsdp", "tp"), None),
        P(("fsdp", "tp"), None),
        P(("fsdp", "tp"), None),
        P("fsdp", "tp"),
        P("fsdp", "tp"),
        P("fsdp", "tp"),
        P("tp", "fsdp"),
        P("fsdp", "tp"),
        P("tp", "fsdp"),
        P(),
        P(),
        P(),
        P(),
        P(),
    )
    return jax.shard_map(functools.partial(local, mesh.shape["tp"]), mesh=mesh, in_specs=in_specs, out_specs=out_specs, check_vma=False)
```

```python
import functools
import jax, jax.numpy as jnp
from jax import lax
from jax.sharding import PartitionSpec as P
from jax.experimental import pallas as pl
from jax.experimental.pallas import tpu as pltpu

NEG = -1e30
LOG2E = 1.4426950408889634
LN2 = 0.6931471805599453
VLIM = 60 * 2**20
MESH = pl.DeviceIdType.MESH

def pick(index, values):
    result = jnp.int32(values[-1])
    for place in range(len(values) - 2, -1, -1):
        result = jnp.where(index == place, jnp.int32(values[place]), result)
    return result


class Place:
    def __init__(self):
        f, t = lax.axis_index("fsdp"), lax.axis_index("tp")
        self.f, self.t = f, t
        self.y, self.x, self.c = f // 4, (f // 2) % 2, f % 2
        self.core = (f + 1 - 2 * self.c, t)
        self.xn = (f + 2 - 4 * self.x, t)
        self.yn = (f + 4 - 8 * self.y, t)
        self.up, self.down = (f, t + 1), (f, t - 1)
        self.order = [pick(t, row) for row in ((3, 3, 0, 0), (2, 0, 3, 1), (1, 2, 1, 2), (0, 1, 2, 3))]

    def greet(self):
        barrier = pltpu.get_barrier_semaphore()
        for there in (self.core, self.xn, self.yn):
            pl.semaphore_signal(barrier, inc=1, device_id=there, device_id_type=MESH)
        for there in ((self.f, jnp.where(self.t > 0, self.t - 1, 3)), (self.f, jnp.where(self.t < 3, self.t + 1, 0))):
            pl.semaphore_signal(barrier, inc=1, device_id=there, device_id_type=MESH)
        pl.semaphore_wait(barrier, 5)


def rdma(src, dst, ss, rs, there):
    return pltpu.make_async_remote_copy(src_ref=src, dst_ref=dst, send_sem=ss, recv_sem=rs, device_id=there, device_id_type=MESH)


class Scatter:
    def __init__(self, at, g, own, r0, r1a, r1b, r2a, r2b, zs, zr, sems, keep_sems):
        self.at, self.g, self.own, self.keep_sems = at, g, own, keep_sems
        self.r0, self.r1a, self.r1b, self.r2a, self.r2b, self.zs, self.zr = r0, r1a, r1b, r2a, r2b, zs, zr
        self.sems = sems
        self.wa = r1a.shape[-1]

    def sem(self, i):
        return self.sems.at[0, i], self.sems.at[1, i]

    def copy0(self, k):
        a = self.at; d = a.order[k]
        return rdma(self.g.at[d, :, :, 1 - a.c], self.r0.at[d], *self.sem(k), a.core)

    def copy1(self, k):
        a = self.at; d = a.order[k]; wa = self.wa
        return (rdma(self.r0.at[d, :, 1 - a.x, :, :wa], self.r1a.at[d], *self.sem(4 + k), a.xn),
                rdma(self.r0.at[d, 1 - a.y, :, :, wa:], self.r1b.at[d], *self.sem(8 + k), a.yn))

    def copy2(self, k):
        a = self.at; d = a.order[k]
        return (rdma(self.r1a.at[d, 1 - a.y], self.r2a.at[d], *self.sem(12 + k), a.yn),
                rdma(self.r1b.at[d, 1 - a.x], self.r2b.at[d], *self.sem(16 + k), a.xn))

    def hop(self, side, h):
        a = self.at
        return rdma(self.zs.at[side, h - 1], self.zr.at[side, h - 1], *self.sem(20 + 3 * side + h - 1), a.down if side else a.up)

    def keep(self, k):
        a = self.at; d = a.order[k]
        return pltpu.make_async_copy(self.g.at[d, :, :, a.c], self.own.at[d], self.keep_sems.at[k])

    def start(self):
        for k in range(4):
            self.copy0(k).start()
            self.keep(k).start()

    def stage0(self, k):
        a = self.at; d = a.order[k]
        self.keep(k).wait()
        self.copy0(k).wait()
        self.r0[d] = self.r0[d] + self.own[d]
        for c in self.copy1(k): c.start()

    def stage1(self, k):
        a = self.at; d = a.order[k]; wa = self.wa
        for c in self.copy1(k): c.wait()
        self.r1a[d] = self.r1a[d] + self.r0[d, :, a.x, :, :wa]
        self.r1b[d] = self.r1b[d] + self.r0[d, a.y, :, :, wa:]
        for c in self.copy2(k): c.start()

    def stage2(self, k):
        a = self.at; d = a.order[k]
        for c in self.copy2(k): c.wait()
        self.r2a[d] = self.r2a[d] + self.r1a[d, a.y]
        self.r2b[d] = self.r2b[d] + self.r1b[d, a.x]

    def stage3(self, h):
        wa = self.wa
        for side in range(2):
            u = 3 - self.at.t if side else self.at.t
            d = (self.at.t + h - 4) if side else (self.at.t + 4 - h)
            if h > 1:
                @pl.when((u > 0) & (u < 3) & (u <= h - 1))
                def _():
                    self.hop(side, h - 1).wait_recv()
                    self.zs[side, h - 1, :, :wa] = self.r2a[d] + self.zr[side, h - 2, :, :wa]
                    self.zs[side, h - 1, :, wa:] = self.r2b[d] + self.zr[side, h - 2, :, wa:]
                    self.hop(side, h).start()
            @pl.when(u == 0)
            def _():
                self.zs[side, h - 1, :, :wa] = self.r2a[d]
                self.zs[side, h - 1, :, wa:] = self.r2b[d]
                self.hop(side, h).start()

    def finish(self, out):
        a = self.at; wa = self.wa
        for side in range(2):
            u = 3 - a.t if side else a.t
            @pl.when(u > 0)
            def _():
                self.hop(side, 3).wait_recv()
        mine = jnp.concatenate([self.r2a[a.t], self.r2b[a.t]], axis=1).astype(jnp.float32)
        below = jnp.where(a.t > 0, self.zr[0, 2].astype(jnp.float32), 0.0)
        above = jnp.where(a.t < 3, self.zr[1, 2].astype(jnp.float32), 0.0)
        out[...] = mine + below + above
        for side in range(2):
            u = 3 - a.t if side else a.t
            for h in range(1, 4):
                @pl.when(u < h)
                def _():
                    self.hop(side, h).wait_send()

def scatter_scratch(T, R, W):
    wa = (W // 256) * 128
    B = jnp.bfloat16
    return [pltpu.VMEM((T, 2, 2, R, W), B), pltpu.VMEM((T, 2, 2, R, W), B), pltpu.VMEM((T, 2, R, wa), B), pltpu.VMEM((T, 2, R, W - wa), B),
            pltpu.VMEM((T, R, wa), B), pltpu.VMEM((T, R, W - wa), B), pltpu.VMEM((2, 3, R, W), B), pltpu.VMEM((2, 3, R, W), B),
            pltpu.SemaphoreType.DMA((2, 26)), pltpu.SemaphoreType.DMA((4,))]

class Total:
    def __init__(self, at, source, acc, got, sems):
        self.at, self.source, self.acc, self.got, self.sems = at, source, acc, got, sems
        t = at.t
        self.partners = [at.core, at.xn, at.yn, (at.f, t + 1 - 2 * (t % 2)), (at.f, 3 - t)]

    def copy(self, i):
        return rdma(self.acc.at[i], self.got.at[i], self.sems.at[0, i], self.sems.at[1, i], self.partners[i])

    def start(self):
        self.acc[0] = self.source[...]
        self.copy(0).start()

    def step(self, i):
        self.copy(i).wait_recv()
        self.acc[i + 1] = self.acc[i] + self.got[i]
        if i < 4:
            self.copy(i + 1).start()

    def finish(self, out):
        for i in range(5):
            self.copy(i).wait_send()
        out[...] = self.acc[5]


def total_scratch(rows, width):
    F = jnp.float32
    return [pltpu.VMEM((6, rows, width), F), pltpu.VMEM((5, rows, width), F), pltpu.SemaphoreType.DMA((2, 5))]


def tail_kernel(g, small, out, small_out, *scratch):
    at = Place()
    at.greet()
    s, total = Scatter(at, g, *scratch[:10]), Total(at, small, *scratch[10:])
    s.start()
    total.start()
    for k in range(4):
        s.stage0(k)
        total.step(k)
    for k in range(4):
        s.stage1(k)
        if k == 0:
            total.step(4)
        if k:
            s.stage2(k - 1)
            s.stage3(k)
    s.stage2(3)
    s.finish(out)
    total.finish(small_out)


def reduce_scatter(g, small):
    T, _, _, _, R, W = g.shape
    V = pl.BlockSpec(memory_space=pltpu.MemorySpace.VMEM)
    return pl.pallas_call(
        tail_kernel,
        out_shape=(jax.ShapeDtypeStruct((R, W), jnp.float32), jax.ShapeDtypeStruct(small.shape, jnp.float32)),
        in_specs=[pl.BlockSpec(memory_space=pl.ANY), V], out_specs=(V, V),
        scratch_shapes=scatter_scratch(T, R, W) + total_scratch(*small.shape),
        compiler_params=pltpu.CompilerParams(vmem_limit_bytes=VLIM, collective_id=1, has_side_effects=True),
        name="reduce_scatter",
    )(g, small)


def nn(a, b):
    return lax.dot_general(a, b, (((1,), (0,)), ((), ())), preferred_element_type=jnp.float32)
def nt(a, b):
    return lax.dot_general(a, b, (((1,), (1,)), ((), ())), preferred_element_type=jnp.float32)

def band_kind(i, b, nrow, nkey):
    rel = (b - i) % nkey
    if rel == 0: return 2
    if rel == nkey - 1: return 0 if i == 0 else 1
    if rel == 1: return 4 if i == nrow - 1 else 3
    return None

def build_mask(mask, kcol, rrow, nkey, nrow):
    def one(b, _):
        keys = pl.ds(pl.multiple_of(b * 128, 128), 128)
        rank_k = kcol[0, keys, :]
        span_k = kcol[1, keys, :]
        kpos = b * 128 + lax.broadcasted_iota(jnp.int32, (128, 128), 0)
        for i in range(nrow):
            rank_r = rrow[0:1, i * 128:(i + 1) * 128]
            span_r = rrow[1:2, i * 128:(i + 1) * 128]
            rpos = i * 128 + lax.broadcasted_iota(jnp.int32, (128, 128), 1)
            same = (span_k == span_r) & (span_k >= 0)
            content = (rank_k <= rank_r) | same
            strict = (rank_k < jnp.maximum(rank_r, 1)) | (same & (kpos != rpos))
            mask[keys, i * 128:(i + 1) * 128] = jnp.where(content, 0.0, NEG)
            mask[keys, (nrow + i) * 128:(nrow + i + 1) * 128] = jnp.where(strict, 0.0, NEG)
        return 0
    lax.fori_loop(0, nkey, one, 0)

def band_tiles(band, vec, h):
    lane = lax.broadcasted_iota(jnp.int32, (128, 128), 1)
    sub = lax.broadcasted_iota(jnp.int32, (128, 128), 0)
    for k in range(5):
        direct, wrapped = (
            pltpu.roll(jnp.broadcast_to(vec[h, 2 * k + w:2 * k + w + 1, :], (128, 128)), 0, 1, stride=1, stride_axis=0)
            for w in range(2)
        )
        band[k] = jnp.where(lane >= sub, direct, wrapped)

def diagonal_sums(tile):
    lane = lax.broadcasted_iota(jnp.int32, (8, 128), 1)
    sub = lax.broadcasted_iota(jnp.int32, (8, 128), 0)
    direct = wrapped = jnp.zeros((8, 128), jnp.float32)
    for a in range(16):
        rows = tile[8 * a:8 * a + 8, :]
        kept = jnp.where(lane >= sub + 8 * a, rows, 0.0)
        left = rows - kept
        if a:
            kept, left = pltpu.roll(kept, 128 - 8 * a, 1), pltpu.roll(left, 128 - 8 * a, 1)
        direct, wrapped = direct + kept, wrapped + left
    for bit in (1, 2, 4):
        moved = (sub & bit) != 0
        direct = jnp.where(moved, pltpu.roll(direct, 128 - bit, 1), direct)
        wrapped = jnp.where(moved, pltpu.roll(wrapped, 128 - bit, 1), wrapped)
    return jnp.sum(direct, axis=0, keepdims=True), jnp.sum(wrapped, axis=0, keepdims=True)

def head_rows(ref, p, hh, cols):
    z = jnp.zeros((64, cols.stop - cols.start), jnp.bfloat16)
    rows = ref[pl.ds(pl.multiple_of((2 * p + hh) * 64, 64), 64), cols]
    return jnp.concatenate([rows, z] if hh == 0 else [z, rows], axis=0)

def fwd_kernel(nrow, nkey, kcol, rrow, cf, vec, kp, vt, qt, ot, lse, mask, t, band):
    build_mask(mask, kcol, rrow, nkey, nrow)
    ones = jnp.ones((16, 256), jnp.bfloat16)
    nchunk = 2 * nrow * 128 // 256
    def pair(p, _):
        for hh in range(2):
            h = 2 * p + hh
            hrows = pl.ds(pl.multiple_of(h * 64, 64), 64)
            band_tiles(band, vec, h)
            for c in range(nchunk):
                cols = slice(c * 256, (c + 1) * 256)
                qh = head_rows(qt, p, hh, cols)
                m8 = jnp.full((8, 256), -jnp.inf, jnp.float32)
                for b in range(nkey):
                    s = nn(kp[p, b * 128:(b + 1) * 128, :], qh)
                    s = s + mask[b * 128:(b + 1) * 128, cols]
                    kinds = [band_kind((2 * c + k) % nrow, b, nrow, nkey) for k in range(2)]
                    if any(k is not None for k in kinds):
                        s = jnp.concatenate([s[:, k * 128:(k + 1) * 128] + (band[kinds[k]] if kinds[k] is not None else 0.0) for k in range(2)], axis=1)
                    t[c, b * 128:(b + 1) * 128, :] = s
                    m8 = jnp.maximum(m8, jnp.max(s.reshape(16, 8, 256), axis=0) + cf[h, b:b + 1, cols])
                m = jnp.max(m8, axis=0, keepdims=True)
                acc = jnp.zeros((80, 256), jnp.float32)
                for g in range(nkey // 2):
                    ps = []
                    for b in (2 * g, 2 * g + 1):
                        ps.append(jnp.exp2(t[c, b * 128:(b + 1) * 128, :] - (m - cf[h, b:b + 1, cols])).astype(jnp.bfloat16))
                    lhs = jnp.concatenate([vt[hrows, g * 256:(g + 1) * 256], ones], axis=0)
                    acc = acc + nn(lhs, jnp.concatenate(ps, axis=0))
                l = acc[64:65, :]
                ot[hrows, cols] = (acc[:64, :] / l).astype(jnp.bfloat16)
                lse[h, 0:1, cols] = m + jnp.log2(l)
        return 0
    lax.fori_loop(0, kp.shape[0], pair, 0)

def attend_fwd(kcol, rrow, cf, vec, kp, vt, qt):
    pairs, seq, _ = kp.shape
    rows = qt.shape[1]
    nrow, nkey = rows // 256, seq // 128
    V = pl.BlockSpec(memory_space=pltpu.MemorySpace.VMEM)
    return pl.pallas_call(
        functools.partial(fwd_kernel, nrow, nkey),
        out_shape=(jax.ShapeDtypeStruct(qt.shape, jnp.bfloat16), jax.ShapeDtypeStruct((2 * pairs, 1, rows), jnp.float32)),
        in_specs=[V] * 7, out_specs=(V, V),
        scratch_shapes=[pltpu.VMEM((seq, rows), jnp.float32), pltpu.VMEM((rows // 256, seq, 256), jnp.float32), pltpu.VMEM((5, 128, 128), jnp.float32)],
        compiler_params=pltpu.CompilerParams(vmem_limit_bytes=VLIM),
        name="attend_fwd",
    )(kcol, rrow, cf, vec, kp, vt, qt)

def bwd_kernel(nrow, nkey, fused, *refs):
    if fused:
        kcol, rrow, cf, vec, kp, vp, kt, qt, ot, got, lse, g, gqt, gkt, gvt, far, diag, summed, mask, gq, bacc, band, *scratch = refs
        at = Place()
        at.greet()
        scatter = Scatter(at, g, *scratch)
        scatter.start()
    else:
        kcol, rrow, cf, vec, kp, vp, kt, qt, ot, got, lse, gqt, gkt, gvt, far, diag, mask, gq, bacc, band = refs
    build_mask(mask, kcol, rrow, nkey, nrow)

    def exchange(p):
        if not fused:
            return
        for k in range(4):
            @pl.when(p == 1)
            def _():
                scatter.stage0(k)
        for k in range(4):
            @pl.when(p == k + 2)
            def _():
                scatter.stage1(k)
                if k:
                    scatter.stage2(k - 1)
                    scatter.stage3(k)

    rows = 2 * nrow * 128
    nchunk = rows // 256
    full = slice(0, rows)
    block_of = lax.broadcasted_iota(jnp.int32, (16, 256), 0)
    half_of = lax.broadcasted_iota(jnp.int32, (16, 256), 1) // 128
    def pair(p, _):
        exchange(p)
        for hh in range(2):
            h = 2 * p + hh
            hrows = pl.ds(pl.multiple_of(h * 64, 64), 64)
            band_tiles(band, vec, h)
            q_h = qt[hrows, :]
            go_h = got[hrows, :]
            delta = jnp.sum(ot[hrows, :].astype(jnp.float32) * go_h.astype(jnp.float32), axis=0, keepdims=True)
            for k in range(5):
                bacc[k] = jnp.zeros((128, 128), jnp.float32)
            gq[...] = jnp.zeros_like(gq)
            qm = head_rows(qt, p, hh, full)
            gm = head_rows(got, p, hh, full)
            for g in range(nkey // 2):
                pp, gg = [], []
                for c in range(nchunk):
                    cols = slice(c * 256, (c + 1) * 256)
                    pc, gc = [], []
                    for b in (2 * g, 2 * g + 1):
                        keys = slice(b * 128, (b + 1) * 128)
                        s = nn(kp[p, keys, :], qm[:, cols])
                        dp = nn(vp[p, keys, :], gm[:, cols])
                        s = s + mask[keys, cols]
                        kinds = [band_kind((2 * c + k) % nrow, b, nrow, nkey) for k in range(2)]
                        if any(k is not None for k in kinds):
                            s = jnp.concatenate([s[:, k * 128:(k + 1) * 128] + (band[kinds[k]] if kinds[k] is not None else 0.0) for k in range(2)], axis=1)
                        pr = jnp.exp2(s - (lse[h, 0:1, cols] - cf[h, b:b + 1, cols]))
                        gs = pr * (dp - delta[:, cols])
                        for k in range(2):
                            if kinds[k] is not None:
                                bacc[kinds[k]] += gs[:, k * 128:(k + 1) * 128]
                        pc.append(pr.astype(jnp.bfloat16))
                        gc.append(gs.astype(jnp.bfloat16))
                    pp.append(jnp.concatenate(pc, axis=0))
                    gg.append(jnp.concatenate(gc, axis=0))
                pall = jnp.concatenate(pp, axis=1)
                gall = jnp.concatenate(gg, axis=1)
                keys = slice(g * 256, (g + 1) * 256)
                onehot = (block_of == 2 * g + half_of).astype(jnp.bfloat16)
                gq[...] += nn(jnp.concatenate([kt[hrows, keys], onehot], axis=0), gall)
                gkt[hrows, keys] = (nt(q_h, gall) * LN2).astype(jnp.bfloat16)
                gvt[hrows, keys] = nt(go_h, pall).astype(jnp.bfloat16)
            gqt[hrows, :] = (gq[:64, :] * 0.125).astype(jnp.bfloat16)
            far[h] = gq[64:80, :]
            for k in range(5):
                direct, wrapped = diagonal_sums(bacc[k])
                diag[h, 2 * k:2 * k + 1, :] = direct
                diag[h, 2 * k + 1:2 * k + 2, :] = wrapped
        return 0
    lax.fori_loop(0, kp.shape[0], pair, 0)
    if fused:
        scatter.stage2(3)
        scatter.finish(summed)


def attend_bwd(kcol, rrow, cf, vec, kp, vp, kt, qt, ot, got, lse, g=None):
    pairs, seq, _ = kp.shape
    rows = qt.shape[1]
    nrow, nkey = rows // 256, seq // 128
    V = pl.BlockSpec(memory_space=pltpu.MemorySpace.VMEM)
    S = jax.ShapeDtypeStruct
    fused = g is not None
    outs = [S(qt.shape, jnp.bfloat16), S(kt.shape, jnp.bfloat16), S(kt.shape, jnp.bfloat16), S((2 * pairs, 16, rows), jnp.float32), S((2 * pairs, 16, 128), jnp.float32)]
    scratch = [pltpu.VMEM((seq, rows), jnp.float32), pltpu.VMEM((80, rows), jnp.float32), pltpu.VMEM((5, 128, 128), jnp.float32), pltpu.VMEM((5, 128, 128), jnp.float32)]
    params = dict(vmem_limit_bytes=VLIM)
    args = (kcol, rrow, cf, vec, kp, vp, kt, qt, ot, got, lse)
    specs = [V] * 11
    if fused:
        outs.append(S((g.shape[4], g.shape[5]), jnp.float32))
        scratch += scatter_scratch(g.shape[0], g.shape[4], g.shape[5])
        params.update(collective_id=2, has_side_effects=True)
        args += (g,)
        specs = specs + [pl.BlockSpec(memory_space=pl.ANY)]
    return pl.pallas_call(
        functools.partial(bwd_kernel, nrow, nkey, fused),
        out_shape=tuple(outs), in_specs=specs, out_specs=(V,) * len(outs), scratch_shapes=scratch,
        compiler_params=pltpu.CompilerParams(**params), name="attend_bwd",
    )(*args)


HEAD = 64
NB = 32
PIC = 256
THRESHOLDS = (12, 16, 23, 32, 46, 64, 91)
EPSILON = 1e-05


def bucket_of(offsets):
    magnitude = jnp.abs(offsets)
    far_bucket = 8 + sum((magnitude >= threshold).astype(jnp.int32) for threshold in THRESHOLDS)
    return jnp.where(magnitude < 8, magnitude, far_bucket) + 16 * (offsets > 0).astype(jnp.int32)


def span_labels(starts, length):
    places = jnp.arange(length, dtype=jnp.int32)
    inside = (places[None, :] >= starts[:, None]) & (places[None, :] < starts[:, None] + PIC)
    labels = jnp.arange(starts.shape[0], dtype=jnp.int32)[:, None] + 1
    return jnp.sum(jnp.where(inside, labels, 0), axis=0) - 1


def dot(spec, a, b):
    return jnp.einsum(spec, a, b, preferred_element_type=jnp.float32)


def norm_stats(residual):
    centered = residual - jnp.mean(residual, axis=-1, keepdims=True)
    scale = lax.rsqrt(jnp.mean(centered * centered, axis=-1, keepdims=True) + EPSILON)
    return centered * scale, scale


def norm_back(cotangent, normal, scale, gain):
    inner = cotangent * gain
    mean_inner = jnp.mean(inner, axis=-1, keepdims=True)
    mean_cross = jnp.mean(inner * normal, axis=-1, keepdims=True)
    back = scale * (inner - mean_inner - normal * mean_cross)
    return back, jnp.sum(cotangent * normal, axis=0), jnp.sum(cotangent, axis=0)


def bucket_tables(nrow, nkey, tp_index, tp_size):
    lanes = jnp.arange(128, dtype=jnp.int32)
    rel = jnp.array([-1, -1, 0, 1, 1], jnp.int32)
    offsets = 128 * rel[:, None, None] + 128 * jnp.arange(2, dtype=jnp.int32)[None, :, None] - lanes
    buckets = bucket_of(offsets)
    far_right, far_left = bucket_of(jnp.int32(128)), bucket_of(jnp.int32(-128))
    buckets = buckets.at[0].set(jnp.where(tp_index == 0, far_right, buckets[0]))
    buckets = buckets.at[4].set(jnp.where(tp_index == tp_size - 1, far_left, buckets[4]))
    key_block = jnp.arange(16, dtype=jnp.int32)[:, None]
    row_block = jnp.arange(nrow, dtype=jnp.int32)[None, :]
    gap = (key_block - row_block) % nkey
    far = (gap != 0) & (gap != 1) & (gap != nkey - 1) & (key_block < nkey)
    key_place = (key_block + nrow * tp_index) % nkey
    left = far & (key_place < row_block + nrow * tp_index)
    right = far & (key_place > row_block + nrow * tp_index)
    return buckets.reshape(10, 128), left, right


def local(
    tp_size, own_exchange, content, query, w_query, w_key, w_value, w_out, w_in, w_down, gain_first, shift_first,
    gain_second, shift_second, bias_table, ranks, span_starts, upstream_content, upstream_query,
):
    rows, width = content.shape
    seq = ranks.shape[1]
    nrow, nkey = rows // 128, seq // 128
    heads = bias_table.shape[0]
    pairs = heads // 2
    tp_index = lax.axis_index("tp")
    both_axes = ("tp", "fsdp")
    narrow = w_query.shape[1]

    def gather(parts):
        shard = jnp.concatenate(parts, axis=1)
        return lax.all_gather(shard, both_axes, axis=0, tiled=True).reshape(tp_size, width, shard.shape[1])

    seq_content = lax.all_gather(content, "tp", axis=0, tiled=True)
    first = gather([w_query, w_key, w_value])
    second = gather([w_out.T, w_in, w_down.T])
    wq, wk, wv = (first[:, :, i * narrow:(i + 1) * narrow] for i in range(3))
    wide = w_in.shape[1]
    wo, wi, wd = second[:, :, :narrow], second[:, :, narrow:narrow + wide], second[:, :, narrow + wide:]

    shift = -rows * tp_index
    seq_rot = jnp.roll(seq_content, shift, axis=0)
    rank_all = ranks[0]
    span_all = span_labels(span_starts[0], seq)
    marks = jnp.roll(jnp.stack([rank_all, span_all]), shift, axis=1)
    kcol = jnp.broadcast_to(marks[:, :, None], (2, seq, 128))
    rrow = jnp.concatenate([marks[:, :rows], jnp.zeros((6, rows), jnp.int32)], axis=0)
    buckets, left, right = bucket_tables(nrow, nkey, tp_index, tp_size)
    one_hot = (buckets.reshape(-1)[None, :] == jnp.arange(NB, dtype=jnp.int32)[:, None]).astype(jnp.float32)
    table = bias_table * LOG2E
    vec = jnp.dot(table, one_hot, precision=lax.Precision.HIGHEST).reshape(heads, 10, 128)
    cf = jnp.where(left[None], table[:, 15, None, None], 0.0) + jnp.where(right[None], table[:, 31, None, None], 0.0)
    cf = jnp.broadcast_to(cf[:, :, None, :, None], (heads, 16, 2, nrow, 128)).reshape(heads, 16, 2 * rows)

    both = jnp.concatenate([content, query], axis=0)
    qt = (dot("tdc,rd->tcr", wq, both) * (HEAD ** -0.5 * LOG2E)).astype(jnp.bfloat16).reshape(width, 2 * rows)
    kt = dot("tdc,rd->tcr", wk, seq_rot).astype(jnp.bfloat16).reshape(width, seq)
    vt = dot("tdc,rd->tcr", wv, seq_rot).astype(jnp.bfloat16).reshape(width, seq)
    kp = jnp.swapaxes(kt.reshape(pairs, 128, seq), 1, 2)
    vp = jnp.swapaxes(vt.reshape(pairs, 128, seq), 1, 2)
    ot, lse = attend_fwd(kcol, rrow, cf, vec, kp, vt, qt)

    ot_blocks = ot.reshape(tp_size, narrow, 2 * rows)
    residual_first = both.astype(jnp.float32) + dot("tcr,tmc->rm", ot_blocks, wo)
    normal_first, scale_first = norm_stats(residual_first)
    normed_first = normal_first * gain_first + shift_first
    low_first = normed_first.astype(jnp.bfloat16)
    lifted = dot("rd,tdf->trf", low_first, wi)
    phi = 0.5 * (1.0 + lax.erf(lifted * (0.5 ** 0.5)))
    hidden = (lifted * phi).astype(jnp.bfloat16)
    slope = phi + lifted * jnp.exp(-0.5 * lifted * lifted) * 0.3989422804014327
    residual_second = normed_first + dot("trf,tmf->rm", hidden, wd)
    normal_second, scale_second = norm_stats(residual_second)
    normed_second = normal_second * gain_second + shift_second
    predicted = (marks[0, :rows] >= seq - seq * 15 // 100).astype(jnp.float32)
    upstream = jnp.concatenate(
        [upstream_content.astype(jnp.float32), upstream_query.astype(jnp.float32) * predicted[:, None]], axis=0
    )
    back_second, grad_gain_second, grad_shift_second = norm_back(upstream, normal_second, scale_second, gain_second)
    gf = back_second.astype(jnp.bfloat16)
    gu = (slope * dot("rm,tmf->trf", gf, wd)).astype(jnp.bfloat16)
    grad_down = dot("rm,trf->tmf", gf, hidden)
    grad_in = dot("rd,trf->tdf", low_first, gu)
    back_normed = back_second + dot("trf,tdf->rd", gu, wi)
    back_first, grad_gain_first, grad_shift_first = norm_back(back_normed, normal_first, scale_first, gain_first)
    ga = back_first.astype(jnp.bfloat16)
    grad_out = dot("rm,tcr->tmc", ga, ot_blocks)
    got = dot("rm,tmc->tcr", ga, wo).astype(jnp.bfloat16).reshape(width, 2 * rows)

    def scatter(blocks):
        flat = blocks.astype(jnp.bfloat16).reshape(tp_size * width, blocks.shape[2])
        return lax.psum_scatter(flat, both_axes, scatter_dimension=0, tiled=True).astype(jnp.float32)

    if own_exchange:
        grad_second = jnp.concatenate([g.astype(jnp.bfloat16) for g in (grad_out, grad_in, grad_down)], axis=2)
        grad_second = grad_second.reshape(4, 2, 2, 2, width // 8, grad_second.shape[2])
        gqt, gkt, gvt, far, diag, sum_second = attend_bwd(kcol, rrow, cf, vec, kp, vp, kt, qt, ot, got, lse, grad_second)
        sum_out, sum_in, sum_down = sum_second[:, :narrow], sum_second[:, narrow:narrow + wide], sum_second[:, narrow + wide:]
    else:
        sum_down, sum_in, sum_out = scatter(grad_down), scatter(grad_in), scatter(grad_out)
        gqt, gkt, gvt, far, diag = attend_bwd(kcol, rrow, cf, vec, kp, vp, kt, qt, ot, got, lse)
    gq_blocks, gk_blocks, gv_blocks = (g.reshape(tp_size, narrow, g.shape[1]) for g in (gqt, gkt, gvt))
    grads_first = (
        dot("rd,tcr->tdc", both, gq_blocks), dot("rd,tcr->tdc", seq_rot, gk_blocks), dot("rd,tcr->tdc", seq_rot, gv_blocks)
    )
    back_seq = dot("tcr,tdc->rd", gk_blocks, wk) + dot("tcr,tdc->rd", gv_blocks, wv)
    back_seq = jnp.roll(back_seq.astype(jnp.bfloat16), -shift, axis=0)
    back_content = lax.psum_scatter(back_seq, "tp", scatter_dimension=0, tiled=True).astype(jnp.float32)
    back_inputs = back_first + dot("tcr,tdc->rd", gq_blocks, wq)

    far_sums = jnp.sum(far.reshape(heads, 16, 2, nrow, 128), axis=(2, 4))
    columns = jnp.arange(NB, dtype=jnp.int32)[None, :]
    grad_table = jnp.dot(diag[:, :10].reshape(heads, 1280), one_hot.T, precision=lax.Precision.HIGHEST)
    for side, column in ((left, 15), (right, 31)):
        grad_table = grad_table + jnp.sum(jnp.where(side[None], far_sums, 0.0), axis=(1, 2))[:, None] * (columns == column)
    norm_stack = jnp.stack([grad_gain_first, grad_shift_first, grad_gain_second, grad_shift_second])
    if own_exchange:
        grad_first = jnp.concatenate([g.astype(jnp.bfloat16) for g in grads_first], axis=2)
        grad_first = grad_first.reshape(4, 2, 2, 2, width // 8, grad_first.shape[2])
        small = jnp.concatenate([norm_stack, jnp.zeros((4, width), jnp.float32).at[0, :heads * NB].set(grad_table.reshape(-1))], axis=0)
        sum_first, small = reduce_scatter(grad_first, small)
        sum_query, sum_key, sum_value = (sum_first[:, i * narrow:(i + 1) * narrow] for i in range(3))
        summed_norms, summed_table = small[:4], small[4, :heads * NB].reshape(heads, NB)
    else:
        sum_query, sum_key, sum_value = (scatter(g) for g in grads_first)
        summed_norms, summed_table = lax.psum((norm_stack, grad_table), ("fsdp", "tp"))
    return (
        normed_second[:rows].astype(jnp.bfloat16), normed_second[rows:].astype(jnp.bfloat16),
        back_inputs[:rows] + back_content, back_inputs[rows:],
        sum_query, sum_key, sum_value, sum_out.T, sum_in, sum_down.T,
        summed_norms[0], summed_norms[1], summed_norms[2], summed_norms[3], summed_table,
    )


def solution(mesh):
    in_specs = (
        P(("fsdp", "tp"), None),
        P(("fsdp", "tp"), None),
        P("fsdp", "tp"),
        P("fsdp", "tp"),
        P("fsdp", "tp"),
        P("tp", "fsdp"),
        P("fsdp", "tp"),
        P("tp", "fsdp"),
        P(),
        P(),
        P(),
        P(),
        P(),
        P("fsdp", None),
        P("fsdp", None),
        P(("fsdp", "tp"), None),
        P(("fsdp", "tp"), None),
    )
    out_specs = (
        P(("fsdp", "tp"), None),
        P(("fsdp", "tp"), None),
        P(("fsdp", "tp"), None),
        P(("fsdp", "tp"), None),
        P("fsdp", "tp"),
        P("fsdp", "tp"),
        P("fsdp", "tp"),
        P("tp", "fsdp"),
        P("fsdp", "tp"),
        P("tp", "fsdp"),
        P(),
        P(),
        P(),
        P(),
        P(),
    )
    return jax.shard_map(functools.partial(local, mesh.shape["tp"], mesh.shape["tp"] == 4 and mesh.shape["fsdp"] == 8), mesh=mesh, in_specs=in_specs, out_specs=out_specs, check_vma=False)
```

```python
import functools
import jax, jax.numpy as jnp
from jax import lax
from jax.sharding import PartitionSpec as P
from jax.experimental import pallas as pl
from jax.experimental.pallas import tpu as pltpu

NEG = -1e30
PIECES = 3
HEAD = 64
NB = 32
PIC = 256
THRESHOLDS = (12, 16, 23, 32, 46, 64, 91)
EPSILON = 1e-05
LOG2E = 1.4426950408889634
LN2 = 0.6931471805599453
VLIM = 60 * 2**20
MESH = pl.DeviceIdType.MESH

def pick(index, values):
    result = jnp.int32(values[-1])
    for place in range(len(values) - 2, -1, -1):
        result = jnp.where(index == place, jnp.int32(values[place]), result)
    return result


class Place:
    def __init__(self):
        f, t = lax.axis_index("fsdp"), lax.axis_index("tp")
        self.f, self.t = f, t
        self.y, self.x, self.c = f // 4, (f // 2) % 2, f % 2
        self.core = (f + 1 - 2 * self.c, t)
        self.xn = (f + 2 - 4 * self.x, t)
        self.yn = (f + 4 - 8 * self.y, t)
        self.up, self.down = (f, t + 1), (f, t - 1)
        self.order = [pick(t, row) for row in ((3, 3, 0, 0), (2, 0, 3, 1), (1, 2, 1, 2), (0, 1, 2, 3))]

    def greet(self):
        barrier = pltpu.get_barrier_semaphore()
        for there in (self.core, self.xn, self.yn):
            pl.semaphore_signal(barrier, inc=1, device_id=there, device_id_type=MESH)
        for there in ((self.f, jnp.where(self.t > 0, self.t - 1, 3)), (self.f, jnp.where(self.t < 3, self.t + 1, 0))):
            pl.semaphore_signal(barrier, inc=1, device_id=there, device_id_type=MESH)
        pl.semaphore_wait(barrier, 5)


def rdma(src, dst, ss, rs, there):
    return pltpu.make_async_remote_copy(src_ref=src, dst_ref=dst, send_sem=ss, recv_sem=rs, device_id=there, device_id_type=MESH)


class Scatter:
    def __init__(self, at, g, own, r0, r1a, r1b, r2a, r2b, zs, zr, sems, keep_sems):
        self.at, self.g, self.own, self.keep_sems = at, g, own, keep_sems
        self.r0, self.r1a, self.r1b, self.r2a, self.r2b, self.zs, self.zr = r0, r1a, r1b, r2a, r2b, zs, zr
        self.sems = sems
        self.wa = r1a.shape[-1]

    def sem(self, i):
        return self.sems.at[0, i], self.sems.at[1, i]

    def copy0(self, k):
        a = self.at; d = a.order[k]
        return rdma(self.g.at[d, :, :, 1 - a.c], self.r0.at[d], *self.sem(k), a.core)

    def copy1(self, k):
        a = self.at; d = a.order[k]; wa = self.wa
        return (rdma(self.r0.at[d, :, 1 - a.x, :, :wa], self.r1a.at[d], *self.sem(4 + k), a.xn),
                rdma(self.r0.at[d, 1 - a.y, :, :, wa:], self.r1b.at[d], *self.sem(8 + k), a.yn))

    def copy2(self, k):
        a = self.at; d = a.order[k]
        return (rdma(self.r1a.at[d, 1 - a.y], self.r2a.at[d], *self.sem(12 + k), a.yn),
                rdma(self.r1b.at[d, 1 - a.x], self.r2b.at[d], *self.sem(16 + k), a.xn))

    def hop(self, side, h):
        a = self.at
        return rdma(self.zs.at[side, h - 1], self.zr.at[side, h - 1], *self.sem(20 + 3 * side + h - 1), a.down if side else a.up)

    def keep(self, k):
        a = self.at; d = a.order[k]
        return pltpu.make_async_copy(self.g.at[d, :, :, a.c], self.own.at[d], self.keep_sems.at[k])

    def start(self):
        for k in range(4):
            self.copy0(k).start()
            self.keep(k).start()

    def stage0(self, k):
        a = self.at; d = a.order[k]
        self.keep(k).wait()
        self.copy0(k).wait()
        self.r0[d] = self.r0[d] + self.own[d]
        for c in self.copy1(k): c.start()

    def stage1(self, k):
        a = self.at; d = a.order[k]; wa = self.wa
        for c in self.copy1(k): c.wait()
        self.r1a[d] = self.r1a[d] + self.r0[d, :, a.x, :, :wa]
        self.r1b[d] = self.r1b[d] + self.r0[d, a.y, :, :, wa:]
        for c in self.copy2(k): c.start()

    def stage2(self, k):
        a = self.at; d = a.order[k]
        for c in self.copy2(k): c.wait()
        self.r2a[d] = self.r2a[d] + self.r1a[d, a.y]
        self.r2b[d] = self.r2b[d] + self.r1b[d, a.x]

    def stage3(self, h):
        wa = self.wa
        for side in range(2):
            u = 3 - self.at.t if side else self.at.t
            d = (self.at.t + h - 4) if side else (self.at.t + 4 - h)
            if h > 1:
                @pl.when((u > 0) & (u < 3) & (u <= h - 1))
                def _():
                    self.hop(side, h - 1).wait_recv()
                    self.zs[side, h - 1, :, :wa] = self.r2a[d] + self.zr[side, h - 2, :, :wa]
                    self.zs[side, h - 1, :, wa:] = self.r2b[d] + self.zr[side, h - 2, :, wa:]
                    self.hop(side, h).start()
            @pl.when(u == 0)
            def _():
                self.zs[side, h - 1, :, :wa] = self.r2a[d]
                self.zs[side, h - 1, :, wa:] = self.r2b[d]
                self.hop(side, h).start()

    def finish(self, out):
        a = self.at; wa = self.wa
        for side in range(2):
            u = 3 - a.t if side else a.t
            @pl.when(u > 0)
            def _():
                self.hop(side, 3).wait_recv()
        mine = jnp.concatenate([self.r2a[a.t], self.r2b[a.t]], axis=1).astype(jnp.float32)
        below = jnp.where(a.t > 0, self.zr[0, 2].astype(jnp.float32), 0.0)
        above = jnp.where(a.t < 3, self.zr[1, 2].astype(jnp.float32), 0.0)
        out[...] = mine + below + above
        for side in range(2):
            u = 3 - a.t if side else a.t
            for h in range(1, 4):
                @pl.when(u < h)
                def _():
                    self.hop(side, h).wait_send()

def scatter_scratch(T, R, W):
    wa = (W // 256) * 128
    B = jnp.bfloat16
    return [pltpu.VMEM((T, 2, 2, R, W), B), pltpu.VMEM((T, 2, 2, R, W), B), pltpu.VMEM((T, 2, R, wa), B), pltpu.VMEM((T, 2, R, W - wa), B),
            pltpu.VMEM((T, R, wa), B), pltpu.VMEM((T, R, W - wa), B), pltpu.VMEM((2, 3, R, W), B), pltpu.VMEM((2, 3, R, W), B),
            pltpu.SemaphoreType.DMA((2, 26)), pltpu.SemaphoreType.DMA((4,))]

class Total:
    def __init__(self, at, source, acc, got, sems):
        self.at, self.source, self.acc, self.got, self.sems = at, source, acc, got, sems
        t = at.t
        self.partners = [at.core, at.xn, at.yn, (at.f, t + 1 - 2 * (t % 2)), (at.f, 3 - t)]

    def copy(self, i):
        return rdma(self.acc.at[i], self.got.at[i], self.sems.at[0, i], self.sems.at[1, i], self.partners[i])

    def start(self):
        self.acc[0] = self.source[...]
        self.copy(0).start()

    def step(self, i):
        self.copy(i).wait_recv()
        self.acc[i + 1] = self.acc[i] + self.got[i]
        if i < 4:
            self.copy(i + 1).start()

    def finish(self, out):
        for i in range(5):
            self.copy(i).wait_send()
        out[...] = self.acc[5]


def total_scratch(rows, width):
    F = jnp.float32
    return [pltpu.VMEM((6, rows, width), F), pltpu.VMEM((5, rows, width), F), pltpu.SemaphoreType.DMA((2, 5))]


def tail_kernel(g, small, out, small_out, *scratch):
    at = Place()
    at.greet()
    s, total = Scatter(at, g, *scratch[:10]), Total(at, small, *scratch[10:])
    s.start()
    total.start()
    for k in range(4):
        s.stage0(k)
        total.step(k)
    for k in range(4):
        s.stage1(k)
        if k == 0:
            total.step(4)
        if k:
            s.stage2(k - 1)
            s.stage3(k)
    s.stage2(3)
    s.finish(out)
    total.finish(small_out)


def reduce_scatter(g, small):
    T, _, _, _, R, W = g.shape
    V = pl.BlockSpec(memory_space=pltpu.MemorySpace.VMEM)
    return pl.pallas_call(
        tail_kernel,
        out_shape=(jax.ShapeDtypeStruct((R, W), jnp.float32), jax.ShapeDtypeStruct(small.shape, jnp.float32)),
        in_specs=[pl.BlockSpec(memory_space=pl.ANY), V], out_specs=(V, V),
        scratch_shapes=scatter_scratch(T, R, W) + total_scratch(*small.shape),
        compiler_params=pltpu.CompilerParams(vmem_limit_bytes=VLIM, collective_id=1, has_side_effects=True),
        name="reduce_scatter",
    )(g, small)


def nn(a, b):
    return lax.dot_general(a, b, (((1,), (0,)), ((), ())), preferred_element_type=jnp.float32)
def nt(a, b):
    return lax.dot_general(a, b, (((1,), (1,)), ((), ())), preferred_element_type=jnp.float32)

def band_kind(i, b, nrow, nkey):
    rel = (b - i) % nkey
    if rel == 0: return 2
    if rel == nkey - 1: return 0 if i == 0 else 1
    if rel == 1: return 4 if i == nrow - 1 else 3
    return None

def wrap(value, size):
    return jnp.where(value >= size, value - size, value)


def bucket_of(offsets):
    magnitude = jnp.abs(offsets)
    far_bucket = 8 + sum((magnitude >= threshold).astype(jnp.int32) for threshold in THRESHOLDS)
    return jnp.where(magnitude < 8, magnitude, far_bucket) + jnp.where(offsets > 0, 16, 0)


def slot_bucket(slot, lanes, tp_index, tp_size):
    if slot >= 10:
        return jnp.full_like(lanes, 15 if slot == 10 else 31)
    kind, wrapped = slot // 2, slot % 2
    buckets = bucket_of(128 * ((-1, -1, 0, 1, 1)[kind] + wrapped) - lanes)
    if kind == 0:
        return jnp.where(tp_index == 0, 31, buckets)
    if kind == 4:
        return jnp.where(tp_index == tp_size - 1, 15, buckets)
    return buckets


def far_sides(nrow, nkey, tp_index):
    key_block = lax.broadcasted_iota(jnp.int32, (16, 2 * nrow * 128), 0)
    row_block = wrap(lax.broadcasted_iota(jnp.int32, (16, 2 * nrow * 128), 1) // 128, nrow)
    gap = key_block - row_block
    near = (gap == 0) | (gap == 1) | (gap == -1) | (gap == nkey - 1) | (gap == 1 - nkey) | (key_block >= nkey)
    key_place, row_place = wrap(key_block + nrow * tp_index, nkey), row_block + nrow * tp_index
    left = jnp.where(near, 0.0, jnp.where(key_place < row_place, 1.0, 0.0))
    return left, jnp.where(near, 0.0, 1.0 - left)


def prepare(nrow, nkey, tp_size, ranks, starts, table, mask, ring, vec, sides):
    tp_index = lax.axis_index("tp")
    rows, seq = nrow * 128, nkey * 128
    base = rows * tp_index
    rank_row = jnp.broadcast_to(ranks[...].astype(jnp.float32), (8, seq))
    ring[:, :seq] = rank_row
    ring[:, seq:] = rank_row

    def label(place):
        found = jnp.zeros(place.shape, jnp.int32)
        for k in range(starts.shape[1]):
            start = starts[0, k]
            found = found + jnp.where((place >= start) & (place < start + PIC), k + 1, 0)
        return found

    row_rank, row_label = [], []
    for i in range(nrow):
        row_rank.append(ring[0:1, pl.ds(pl.multiple_of(base + i * 128, 128), 128)])
        row_label.append(label(base + i * 128 + lax.broadcasted_iota(jnp.int32, (1, 128), 1)))

    def one(b, _):
        keys = pl.ds(pl.multiple_of(b * 128, 128), 128)
        rank_k = jnp.broadcast_to(ring[0:1, pl.ds(pl.multiple_of(base + b * 128, 128), 128)], (128, 128)).T
        kpos = b * 128 + lax.broadcasted_iota(jnp.int32, (128, 128), 0)
        label_k = label(wrap(base + kpos, seq))
        for i in range(nrow):
            rpos = i * 128 + lax.broadcasted_iota(jnp.int32, (128, 128), 1)
            same = (label_k == row_label[i]) & (label_k > 0)
            content = (rank_k <= row_rank[i]) | same
            strict = (rank_k < jnp.maximum(row_rank[i], 1.0)) | (same & (kpos != rpos))
            mask[keys, i * 128:(i + 1) * 128] = jnp.where(content, 0.0, NEG)
            mask[keys, rows + i * 128:rows + (i + 1) * 128] = jnp.where(strict, 0.0, NEG)
        return 0
    lax.fori_loop(0, nkey, one, 0)

    heads = table.shape[0]
    lanes = lax.broadcasted_iota(jnp.int32, (heads, 128), 1)
    columns = [jnp.broadcast_to(table[:, n:n + 1] * LOG2E, (heads, 128)) for n in range(NB)]
    for slot in range(12):
        buckets = slot_bucket(slot, lanes, tp_index, tp_size)
        values = columns[0]
        for n in range(1, NB):
            values = jnp.where(buckets == n, columns[n], values)
        for h in range(heads):
            vec[h, slot:slot + 1, :] = values[h:h + 1, :]
    sides[0], sides[1] = far_sides(nrow, nkey, tp_index)


def far_bias(vec, sides, cf, h):
    copies = cf.shape[1] // 128
    left, right = (jnp.concatenate([vec[h, slot:slot + 1, :]] * copies, axis=1) for slot in (10, 11))
    cf[...] = sides[0] * left + sides[1] * right


def prepare_scratch(nrow, nkey, heads):
    F, rows = jnp.float32, 2 * nrow * 128
    return [
        pltpu.VMEM((nkey * 128, rows), F), pltpu.VMEM((8, 2 * nkey * 128), F), pltpu.VMEM((heads, 12, 128), F),
        pltpu.VMEM((2, 16, rows), F), pltpu.VMEM((16, rows), F), pltpu.VMEM((5, 128, 128), F),
    ]


def band_tiles(band, vec, h):
    lane = lax.broadcasted_iota(jnp.int32, (128, 128), 1)
    sub = lax.broadcasted_iota(jnp.int32, (128, 128), 0)
    for k in range(5):
        direct, wrapped = (
            pltpu.roll(jnp.broadcast_to(vec[h, 2 * k + w:2 * k + w + 1, :], (128, 128)), 0, 1, stride=1, stride_axis=0)
            for w in range(2)
        )
        band[k] = jnp.where(lane >= sub, direct, wrapped)

def diagonal_sums(tile):
    lane = lax.broadcasted_iota(jnp.int32, (8, 128), 1)
    sub = lax.broadcasted_iota(jnp.int32, (8, 128), 0)
    direct = wrapped = jnp.zeros((8, 128), jnp.float32)
    for a in range(16):
        rows = tile[8 * a:8 * a + 8, :]
        kept = jnp.where(lane >= sub + 8 * a, rows, 0.0)
        left = rows - kept
        if a:
            kept, left = pltpu.roll(kept, 128 - 8 * a, 1), pltpu.roll(left, 128 - 8 * a, 1)
        direct, wrapped = direct + kept, wrapped + left
    for bit in (1, 2, 4):
        moved = (sub & bit) != 0
        direct = jnp.where(moved, pltpu.roll(direct, 128 - bit, 1), direct)
        wrapped = jnp.where(moved, pltpu.roll(wrapped, 128 - bit, 1), wrapped)
    return jnp.sum(direct, axis=0, keepdims=True), jnp.sum(wrapped, axis=0, keepdims=True)

def head_rows(ref, p, hh, cols):
    z = jnp.zeros((64, cols.stop - cols.start), jnp.bfloat16)
    rows = ref[pl.ds(pl.multiple_of((2 * p + hh) * 64, 64), 64), cols]
    return jnp.concatenate([rows, z] if hh == 0 else [z, rows], axis=0)

def attend_rows(nrow, nkey, kp, vt, qt, ot, lse, t, prepared, exchange):
    mask, _, vec, sides, cf, band = prepared
    ones = jnp.ones((16, 256), jnp.bfloat16)
    nchunk = 2 * nrow * 128 // 256
    def pair(p, _):
        for hh in range(2):
            h = 2 * p + hh
            exchange(h)
            hrows = pl.ds(pl.multiple_of(h * 64, 64), 64)
            band_tiles(band, vec, h)
            far_bias(vec, sides, cf, h)
            for c in range(nchunk):
                cols = slice(c * 256, (c + 1) * 256)
                qh = head_rows(qt, p, hh, cols)
                m8 = jnp.full((8, 256), -jnp.inf, jnp.float32)
                for b in range(nkey):
                    s = nn(kp[p, b * 128:(b + 1) * 128, :], qh)
                    s = s + mask[b * 128:(b + 1) * 128, cols]
                    kinds = [band_kind((2 * c + k) % nrow, b, nrow, nkey) for k in range(2)]
                    if any(k is not None for k in kinds):
                        s = jnp.concatenate([s[:, k * 128:(k + 1) * 128] + (band[kinds[k]] if kinds[k] is not None else 0.0) for k in range(2)], axis=1)
                    t[c, b * 128:(b + 1) * 128, :] = s
                    m8 = jnp.maximum(m8, jnp.max(s.reshape(16, 8, 256), axis=0) + cf[b:b + 1, cols])
                m = jnp.max(m8, axis=0, keepdims=True)
                acc = jnp.zeros((80, 256), jnp.float32)
                for g in range(nkey // 2):
                    ps = []
                    for b in (2 * g, 2 * g + 1):
                        ps.append(jnp.exp2(t[c, b * 128:(b + 1) * 128, :] - (m - cf[b:b + 1, cols])).astype(jnp.bfloat16))
                    lhs = jnp.concatenate([vt[hrows, g * 256:(g + 1) * 256], ones], axis=0)
                    acc = acc + nn(lhs, jnp.concatenate(ps, axis=0))
                l = acc[64:65, :]
                ot[hrows, cols] = (acc[:64, :] / l).astype(jnp.bfloat16)
                lse[h, 0:1, cols] = m + jnp.log2(l)
        return 0
    lax.fori_loop(0, kp.shape[0], pair, 0)

def fwd_kernel(nrow, nkey, tp_size, ranks, starts, table, kp, vt, qt, ot, lse, t, *prepared):
    prepare(nrow, nkey, tp_size, ranks, starts, table, *prepared[:4])
    attend_rows(nrow, nkey, kp, vt, qt, ot, lse, t, prepared, lambda h: None)


def attend_fwd(tp_size, ranks, starts, table, kp, vt, qt):
    pairs, seq, _ = kp.shape
    rows = qt.shape[1]
    nrow, nkey = rows // 256, seq // 128
    V, M = pl.BlockSpec(memory_space=pltpu.MemorySpace.VMEM), pl.BlockSpec(memory_space=pltpu.MemorySpace.SMEM)
    return pl.pallas_call(
        functools.partial(fwd_kernel, nrow, nkey, tp_size),
        out_shape=(jax.ShapeDtypeStruct(qt.shape, jnp.bfloat16), jax.ShapeDtypeStruct((2 * pairs, 1, rows), jnp.float32)),
        in_specs=[V, M, V, V, V, V], out_specs=(V, V),
        scratch_shapes=[pltpu.VMEM((rows // 256, seq, 256), jnp.float32)] + prepare_scratch(nrow, nkey, 2 * pairs),
        compiler_params=pltpu.CompilerParams(vmem_limit_bytes=VLIM),
        name="attend_fwd",
    )(ranks, starts, table, kp, vt, qt)


class Gather:
    def __init__(self, at, shard, g, wa, sems, own_sem):
        self.at, self.shard, self.g, self.wa, self.sems, self.own_sem = at, shard, g, wa, sems, own_sem
        self.blocks = at.order[::-1]

    def send(self, i, src, dst, there):
        return rdma(src, dst, self.sems.at[0, i], self.sems.at[1, i], there)

    def along_z(self, b, upward):
        a = self.at
        here = self.g.at[b, a.y, a.x, a.c]
        return self.send(b + (0 if upward else 4), here, here, a.up if upward else a.down)

    def first(self, b):
        a, wa = self.at, self.wa
        left, right = (self.g.at[b, a.y, a.x, a.c, :, cols] for cols in (slice(0, wa), slice(wa, None)))
        return self.send(8 + b, left, left, a.xn), self.send(12 + b, right, right, a.yn)

    def second(self, b):
        a, wa = self.at, self.wa
        left, right = self.g.at[b, a.y, :, a.c, :, :wa], self.g.at[b, :, a.x, a.c, :, wa:]
        return self.send(16 + b, left, left, a.yn), self.send(20 + b, right, right, a.xn)

    def across(self, b):
        a = self.at
        here = self.g.at[b, :, :, a.c]
        return self.send(24 + b, here, here, a.core)

    def own(self):
        a = self.at
        return pltpu.make_async_copy(self.shard, self.g.at[a.t, a.y, a.x, a.c], self.own_sem)

    def begin(self):
        self.own().start()
        self.own().wait()
        for c in self.first(self.at.t):
            c.start()

    def begin_z(self):
        a = self.at
        @pl.when(a.t < 3)
        def _():
            self.along_z(a.t, True).start()
        @pl.when(a.t > 0)
        def _():
            self.along_z(a.t, False).start()

    def arrive(self, j):
        a, b = self.at, self.blocks[j]
        @pl.when(b < a.t)
        def _():
            self.along_z(b, True).wait_recv()
        @pl.when(b > a.t)
        def _():
            self.along_z(b, False).wait_recv()
        @pl.when((b < a.t) & (a.t < 3))
        def _():
            self.along_z(b, True).start()
        @pl.when((b > a.t) & (a.t > 0))
        def _():
            self.along_z(b, False).start()
        for c in self.first(b):
            c.start()

    def step1(self, j):
        b = self.blocks[j]
        for c in self.first(b):
            c.wait_recv()
        for c in self.second(b):
            c.start()

    def step2(self, j):
        b = self.blocks[j]
        for c in self.second(b):
            c.wait_recv()
        self.across(b).start()

    def step3(self, j):
        self.across(self.blocks[j]).wait_recv()

    def finish(self):
        a = self.at
        for b in range(4):
            @pl.when((b <= a.t) & (a.t < 3))
            def _():
                self.along_z(b, True).wait_send()
            @pl.when((b >= a.t) & (a.t > 0))
            def _():
                self.along_z(b, False).wait_send()
            for c in (*self.first(b), *self.second(b), self.across(b)):
                c.wait_send()


class Chain:
    def __init__(self, at, seq, sems, pieces):
        self.at, self.seq, self.sems, self.pieces = at, seq, sems, pieces
        self.blocks = at.order[::-1]

    def move(self, b, upward, s):
        a = self.at
        i = (b + (0 if upward else 4)) * self.pieces + s
        there = a.t + 1 if upward else a.t - 1
        size = self.seq.shape[1] // self.pieces
        part = slice(s * size, (s + 1) * size)
        return rdma(self.seq.at[(b - a.t + 4) % 4, part], self.seq.at[(b - there + 4) % 4, part], self.sems.at[0, i], self.sems.at[1, i], (a.f, there))

    def begin(self):
        a = self.at
        for s in range(self.pieces):
            @pl.when(a.t < 3)
            def _():
                self.move(a.t, True, s).start()
            @pl.when(a.t > 0)
            def _():
                self.move(a.t, False, s).start()

    def arrive(self, j):
        a, b = self.at, self.blocks[j]
        for s in range(self.pieces):
            @pl.when(b < a.t)
            def _():
                self.move(b, True, s).wait_recv()
            @pl.when(b > a.t)
            def _():
                self.move(b, False, s).wait_recv()
            @pl.when((b < a.t) & (a.t < 3))
            def _():
                self.move(b, True, s).start()
            @pl.when((b > a.t) & (a.t > 0))
            def _():
                self.move(b, False, s).start()

    def finish(self):
        a = self.at
        for b in range(4):
            for s in range(self.pieces):
                @pl.when((b <= a.t) & (a.t < 3))
                def _():
                    self.move(b, True, s).wait_send()
                @pl.when((b >= a.t) & (a.t > 0))
                def _():
                    self.move(b, False, s).wait_send()


def front_kernel(nrow, nkey, content, query, shard1, shard2, ranks, starts, table,
                 ot, lse, seq_out, kp_out, vp_out, kt_out, qt_out, w1_out, w2_out,
                 seq, w1, w2, w1t, kp, vp, kt, vt, qt, t,
                 sems1, sems2, semsc, own_sems, out_sems, *prepared):
    at = Place()
    rows = nrow * 128
    pairs = kp.shape[0]
    narrow = shard1.shape[1] // 4
    width = content.shape[1]
    weights1 = Gather(at, shard1, w1, shard1.shape[1] // 2, sems1, own_sems.at[0])
    weights2 = Gather(at, shard2, w2, shard2.shape[1] // 2, sems2, own_sems.at[1])
    chain = Chain(at, seq, semsc, PIECES)
    seq[0] = content[...]
    at.greet()
    weights1.begin()
    weights1.begin_z()
    weights1.arrive(1)
    weights1.step1(0)
    weights1.arrive(2)
    weights1.step1(1)
    weights1.step2(0)
    weights1.arrive(3)
    chain.begin()
    weights1.step1(2)
    weights1.step2(1)
    weights1.step1(3)
    weights2.begin()
    prepare(nrow, nkey, 4, ranks, starts, table, *prepared[:4])
    weights1.step2(2)
    weights1.step2(3)
    for j in range(4):
        weights1.step3(j)

    scale = HEAD ** -0.5 * LOG2E
    for tt in range(4):
        block = w1[tt].reshape(width, 4 * narrow)
        w1t[tt] = block[:, narrow:].T
        for s, x in enumerate((content, query)):
            q = nt(w1t[tt, :narrow, :], x[...])
            qt[tt * narrow:(tt + 1) * narrow, s * rows:(s + 1) * rows] = (q * scale).astype(jnp.bfloat16)

    def project(r):
        x = seq[r]
        cols = pl.ds(pl.multiple_of(r * rows, 128), rows)
        for i, (across, upright) in enumerate(((kp, kt), (vp, vt))):
            for tt in range(4):
                out = nt(w1t[tt, (i + 1) * narrow:(i + 2) * narrow, :], x)
                upright[tt * narrow:(tt + 1) * narrow, cols] = out.astype(jnp.bfloat16)
            for u in range(2):
                halves = [
                    nn(x, w1[2 * u + v].reshape(width, 4 * narrow)[:, (i + 2) * narrow:(i + 3) * narrow]) for v in range(2)
                ]
                joined = jnp.concatenate(halves, axis=1).astype(jnp.bfloat16)
                for p in range(pairs // 2):
                    across[u * (pairs // 2) + p, cols, :] = joined[:, p * 128:(p + 1) * 128]

    project(0)
    for j in range(1, 4):
        chain.arrive(j)
        if j == 1:
            weights2.step1(0)
        if j == 2:
            weights2.begin_z()
            weights2.step2(0)
        project((chain.blocks[j] - at.t + 4) % 4)

    outs = [
        pltpu.make_async_copy(src, dst, out_sems.at[i])
        for i, (src, dst) in enumerate(((seq, seq_out), (kp, kp_out), (vp, vp_out), (kt, kt_out), (qt, qt_out), (w1, w1_out)))
    ]
    for c in outs:
        c.start()

    def second_out(j):
        b = weights2.blocks[j]
        return pltpu.make_async_copy(w2.at[b], w2_out.at[b], out_sems.at[6 + j])

    def exchange(h):
        steps = (
            (weights2.arrive, 1, 2), (weights2.step1, 1, 4), (weights2.arrive, 2, 5), (weights2.step2, 1, 6), (weights2.step1, 2, 7),
            (weights2.arrive, 3, 8), (weights2.step2, 2, 9), (weights2.step1, 3, 11),
        )
        for step, j, place in steps:
            @pl.when(h == place)
            def _():
                step(j)

    attend_rows(nrow, nkey, kp, vt, qt, ot, lse, t, prepared, exchange)
    weights2.step2(3)
    for j in range(4):
        weights2.step3(j)
        second_out(j).start()
    for c in outs:
        c.wait()
    for j in range(4):
        second_out(j).wait()
    weights1.finish()
    weights2.finish()
    chain.finish()


def front(content, query, shard1, shard2, ranks, starts, table):
    rows, width = content.shape
    heads, seq_len = table.shape[0], ranks.shape[1]
    pairs, R = heads // 2, shard1.shape[0]
    nrow, nkey = rows // 128, seq_len // 128
    narrow = shard1.shape[1] // 4
    V, A = pl.BlockSpec(memory_space=pltpu.MemorySpace.VMEM), pl.BlockSpec(memory_space=pl.ANY)
    B, F, S, DMA = jnp.bfloat16, jnp.float32, jax.ShapeDtypeStruct, pltpu.SemaphoreType.DMA
    full1, full2 = (4, 2, 2, 2) + shard1.shape, (4, 2, 2, 2) + shard2.shape
    kept = [((4, rows, width), B), ((pairs, seq_len, 128), B), ((pairs, seq_len, 128), B), ((width, seq_len), B), ((width, 2 * rows), B), (full1, B)]
    outs = [S((width, 2 * rows), B), S((heads, 1, 2 * rows), F)] + [S(*k) for k in kept] + [S(full2, B)]
    scratch = [pltpu.VMEM(*kept[0]), pltpu.VMEM(full1, B), pltpu.VMEM(full2, B), pltpu.VMEM((4, 3 * narrow, width), B), pltpu.VMEM(*kept[1]), pltpu.VMEM(*kept[2]),
               pltpu.VMEM(*kept[3]), pltpu.VMEM(*kept[3]), pltpu.VMEM(*kept[4]),
               pltpu.VMEM((2 * rows // 256, seq_len, 256), F),
               DMA((2, 28)), DMA((2, 28)), DMA((2, 8 * PIECES)), DMA((2,)), DMA((10,))] + prepare_scratch(nrow, nkey, heads)
    return pl.pallas_call(
        functools.partial(front_kernel, nrow, nkey),
        out_shape=tuple(outs), in_specs=[V, V, A, A, V, pl.BlockSpec(memory_space=pltpu.MemorySpace.SMEM), V], out_specs=tuple([V, V] + [A] * 7), scratch_shapes=scratch,
        compiler_params=pltpu.CompilerParams(vmem_limit_bytes=VLIM, collective_id=3, has_side_effects=True), name="front",
    )(content, query, shard1, shard2, ranks, starts, table)


def bwd_kernel(nrow, nkey, tp_size, fused, *refs):
    if fused:
        ranks, starts, table, kp, vp, kt, qt, ot, got, lse, g, gqt, gkt, gvt, back_table, summed, gq, bacc, diag, *scratch = refs
        prepared, scratch = scratch[:6], scratch[6:]
        at = Place()
        at.greet()
        scatter = Scatter(at, g, *scratch)
        scatter.start()
    else:
        ranks, starts, table, kp, vp, kt, qt, ot, got, lse, gqt, gkt, gvt, back_table, gq, bacc, diag, *prepared = refs
    mask, _, vec, sides, cf, band = prepared
    prepare(nrow, nkey, tp_size, ranks, starts, table, *prepared[:4])
    lane_row = lax.broadcasted_iota(jnp.int32, (1, 128), 1)

    def exchange(p):
        if not fused:
            return
        for k in range(4):
            @pl.when(p == 1)
            def _():
                scatter.stage0(k)
        for k in range(4):
            @pl.when(p == k + 2)
            def _():
                scatter.stage1(k)
                if k:
                    scatter.stage2(k - 1)
                    scatter.stage3(k)

    rows = 2 * nrow * 128
    nchunk = rows // 256
    full = slice(0, rows)
    block_of = lax.broadcasted_iota(jnp.int32, (16, 256), 0)
    half_of = lax.broadcasted_iota(jnp.int32, (16, 256), 1) // 128
    def pair(p, _):
        exchange(p)
        for hh in range(2):
            h = 2 * p + hh
            hrows = pl.ds(pl.multiple_of(h * 64, 64), 64)
            band_tiles(band, vec, h)
            far_bias(vec, sides, cf, h)
            q_h = qt[hrows, :]
            go_h = got[hrows, :]
            delta = jnp.sum(ot[hrows, :].astype(jnp.float32) * go_h.astype(jnp.float32), axis=0, keepdims=True)
            for k in range(5):
                bacc[k] = jnp.zeros((128, 128), jnp.float32)
            gq[...] = jnp.zeros_like(gq)
            qm = head_rows(qt, p, hh, full)
            gm = head_rows(got, p, hh, full)
            for g in range(nkey // 2):
                pp, gg = [], []
                for c in range(nchunk):
                    cols = slice(c * 256, (c + 1) * 256)
                    pc, gc = [], []
                    for b in (2 * g, 2 * g + 1):
                        keys = slice(b * 128, (b + 1) * 128)
                        s = nn(kp[p, keys, :], qm[:, cols])
                        dp = nn(vp[p, keys, :], gm[:, cols])
                        s = s + mask[keys, cols]
                        kinds = [band_kind((2 * c + k) % nrow, b, nrow, nkey) for k in range(2)]
                        if any(k is not None for k in kinds):
                            s = jnp.concatenate([s[:, k * 128:(k + 1) * 128] + (band[kinds[k]] if kinds[k] is not None else 0.0) for k in range(2)], axis=1)
                        pr = jnp.exp2(s - (lse[h, 0:1, cols] - cf[b:b + 1, cols]))
                        gs = pr * (dp - delta[:, cols])
                        for k in range(2):
                            if kinds[k] is not None:
                                bacc[kinds[k]] += gs[:, k * 128:(k + 1) * 128]
                        pc.append(pr.astype(jnp.bfloat16))
                        gc.append(gs.astype(jnp.bfloat16))
                    pp.append(jnp.concatenate(pc, axis=0))
                    gg.append(jnp.concatenate(gc, axis=0))
                pall = jnp.concatenate(pp, axis=1)
                gall = jnp.concatenate(gg, axis=1)
                keys = slice(g * 256, (g + 1) * 256)
                onehot = (block_of == 2 * g + half_of).astype(jnp.bfloat16)
                gq[...] += nn(jnp.concatenate([kt[hrows, keys], onehot], axis=0), gall)
                gkt[hrows, keys] = (nt(q_h, gall) * LN2).astype(jnp.bfloat16)
                gvt[hrows, keys] = nt(go_h, pall).astype(jnp.bfloat16)
            gqt[hrows, :] = (gq[:64, :] * 0.125).astype(jnp.bfloat16)
            for k in range(5):
                direct, wrapped = diagonal_sums(bacc[k])
                diag[h, 0:1, 256 * k:256 * k + 128] = direct
                diag[h, 0:1, 256 * k + 128:256 * k + 256] = wrapped
            for s in range(2):
                side = jnp.sum(jnp.sum(gq[64:80, :] * sides[s], axis=0, keepdims=True), axis=1, keepdims=True)
                diag[h, 0:1, 1280 + 128 * s:1408 + 128 * s] = jnp.where(lane_row == 0, side, 0.0)
        return 0
    lax.fori_loop(0, kp.shape[0], pair, 0)
    tp_index = lax.axis_index("tp")
    places = lax.broadcasted_iota(jnp.int32, (128, 128), 0)
    numbers = lax.broadcasted_iota(jnp.int32, (128, 128), 1)
    sums = jnp.concatenate([diag[h] for h in range(diag.shape[0])], axis=0)
    total = jnp.zeros((diag.shape[0], 128), jnp.float32)
    for slot in range(12):
        one_hot = jnp.where(slot_bucket(slot, places, tp_index, tp_size) == numbers, 1.0, 0.0)
        total = total + jnp.dot(
            sums[:, slot * 128:(slot + 1) * 128], one_hot, precision=lax.Precision.HIGHEST, preferred_element_type=jnp.float32
        )
    back_table[...] = total
    if fused:
        scatter.stage2(3)
        scatter.finish(summed)


def attend_bwd(tp_size, ranks, starts, table, kp, vp, kt, qt, ot, got, lse, g=None):
    pairs, seq, _ = kp.shape
    rows = qt.shape[1]
    heads = 2 * pairs
    nrow, nkey = rows // 256, seq // 128
    V, M = pl.BlockSpec(memory_space=pltpu.MemorySpace.VMEM), pl.BlockSpec(memory_space=pltpu.MemorySpace.SMEM)
    S, F = jax.ShapeDtypeStruct, jnp.float32
    fused = g is not None
    outs = [S(qt.shape, jnp.bfloat16), S(kt.shape, jnp.bfloat16), S(kt.shape, jnp.bfloat16), S((heads, 128), F)]
    scratch = [pltpu.VMEM((80, rows), F), pltpu.VMEM((5, 128, 128), F), pltpu.VMEM((heads, 1, 1536), F)] + prepare_scratch(nrow, nkey, heads)
    params = dict(vmem_limit_bytes=VLIM)
    args = (ranks, starts, table, kp, vp, kt, qt, ot, got, lse)
    specs = [V, M] + [V] * 8
    if fused:
        outs.append(S((g.shape[4], g.shape[5]), F))
        scratch += scatter_scratch(g.shape[0], g.shape[4], g.shape[5])
        params.update(collective_id=2, has_side_effects=True)
        args += (g,)
        specs = specs + [pl.BlockSpec(memory_space=pl.ANY)]
    return pl.pallas_call(
        functools.partial(bwd_kernel, nrow, nkey, tp_size, fused),
        out_shape=tuple(outs), in_specs=specs, out_specs=(V,) * len(outs), scratch_shapes=scratch,
        compiler_params=pltpu.CompilerParams(**params), name="attend_bwd",
    )(*args)


def norm(residual):
    centered = residual - jnp.mean(residual, axis=-1, keepdims=True)
    scale = lax.rsqrt(jnp.mean(centered * centered, axis=-1, keepdims=True) + EPSILON)
    return centered * scale, scale


def norm_step(cotangent, normal, scale, gain):
    inner = cotangent * gain
    mean_inner = jnp.mean(inner, axis=-1, keepdims=True)
    mean_cross = jnp.mean(inner * normal, axis=-1, keepdims=True)
    return scale * (inner - mean_inner - normal * mean_cross)


def middle_kernel(chunk, ot, content, query, first, second, gains, ranks, up_content, up_query,
                  content_out, query_out, grads, back, got, sums,
                  x, up, wot, wo_block, onat, n1bt, gft, gat, hidden, slope, gu, out2, stage, sems, out_sems):
    rows = content.shape[0]
    seq, width = ranks.shape[1], content.shape[1]
    narrow, wide = width // 4, second.shape[2] // 2
    blocks = [pltpu.make_async_copy(first.at[t, :, pl.ds(0, 256)], wo_block.at[t], sems.at[t]) for t in range(4)]
    for c in blocks:
        c.start()
    base = rows * lax.axis_index("tp")
    x[:rows] = content[...]
    x[rows:] = query[...]
    up[:rows] = up_content[...].astype(jnp.float32)
    for i in range(rows // 128):
        rank = ranks[0:1, pl.ds(pl.multiple_of(base + i * 128, 128), 128)].astype(jnp.float32)
        rank = jnp.broadcast_to(rank, (128, 128)).T
        kept = jnp.where(rank >= seq - seq * 15 // 100, 1.0, 0.0)
        up[rows + i * 128:rows + (i + 1) * 128, :] = up_query[i * 128:(i + 1) * 128, :].astype(jnp.float32) * jnp.concatenate([kept] * (width // 128), axis=1)
    for c in blocks:
        c.wait()
    wot[...] = jnp.concatenate([wo_block[t, :, :narrow] for t in range(4)], axis=1)
    sums[...] = jnp.zeros_like(sums)
    gain1, shift1, gain2, shift2 = (gains[i:i + 1, :] for i in range(4))

    def one(i, _):
        here = pl.ds(pl.multiple_of(i * chunk, chunk), chunk)
        mixed = ot[:, here].T
        onat[here, :] = mixed
        normal1, scale1 = norm(x[here, :].astype(jnp.float32) + nt(mixed, wot[...]))
        normed = normal1 * gain1 + shift1
        low = normed.astype(jnp.bfloat16)
        n1bt[:, here] = low.T
        total = normed
        for t in range(4):
            lifted = nn(low, second[t, :, :wide])
            phi = 0.5 + 0.5 * lax.erf(lifted * (0.5 ** 0.5))
            act = (lifted * phi).astype(jnp.bfloat16)
            hidden[t, here, :] = act
            slope[t] = phi + lifted * (jnp.exp(-0.5 * lifted * lifted) * 0.3989422804014327)
            total = total + nt(act, second[t, :, wide:])
        normal2, scale2 = norm(total)
        out2[here, :] = (normal2 * gain2 + shift2).astype(jnp.bfloat16)
        cotangent = up[here, :]
        sums[2:3, :] += jnp.sum(cotangent * normal2, axis=0, keepdims=True)
        sums[3:4, :] += jnp.sum(cotangent, axis=0, keepdims=True)
        back2 = norm_step(cotangent, normal2, scale2, gain2)
        gf = back2.astype(jnp.bfloat16)
        gft[:, here] = gf.T
        total = back2
        for t in range(4):
            g = (slope[t] * nn(gf, second[t, :, wide:])).astype(jnp.bfloat16)
            gu[t, here, :] = g
            total = total + nt(g, second[t, :, :wide])
        sums[0:1, :] += jnp.sum(total * normal1, axis=0, keepdims=True)
        sums[1:2, :] += jnp.sum(total, axis=0, keepdims=True)
        back1 = norm_step(total, normal1, scale1, gain1)
        back[here, :] = back1
        ga = back1.astype(jnp.bfloat16)
        gat[:, here] = ga.T
        got[:, here] = nn(ga, wot[...]).astype(jnp.bfloat16).T
        return 0

    lax.fori_loop(0, 2 * rows // chunk, one, 0)
    content_out[...] = out2[:rows]
    query_out[...] = out2[rows:]
    for t in range(4):
        wo_block[t, :, :narrow] = nn(gat[...], onat[:, t * narrow:(t + 1) * narrow]).astype(jnp.bfloat16)

    def send(t):
        return pltpu.make_async_copy(stage.at[t % 2], grads.at[t], out_sems.at[t % 2])

    for t in range(4):
        if t >= 2:
            send(t - 2).wait()
        stage[t % 2, :, :wide] = nn(n1bt[...], gu[t]).astype(jnp.bfloat16)
        stage[t % 2, :, wide:2 * wide] = nn(gft[...], hidden[t]).astype(jnp.bfloat16)
        stage[t % 2, :, 2 * wide:] = wo_block[t, :, :narrow]
        send(t).start()
    for t in (2, 3):
        send(t).wait()


def middle(ot, content, query, first, second, gains, ranks, up_content, up_query):
    rows, width = content.shape
    narrow, wide = width // 4, second.shape[2] // 2
    both, chunk = 2 * rows, 256
    V, A = pl.BlockSpec(memory_space=pltpu.MemorySpace.VMEM), pl.BlockSpec(memory_space=pl.ANY)
    B, F, S, DMA = jnp.bfloat16, jnp.float32, jax.ShapeDtypeStruct, pltpu.SemaphoreType.DMA
    return pl.pallas_call(
        functools.partial(middle_kernel, chunk),
        out_shape=(S((rows, width), B), S((rows, width), B), S((4, width, 2 * wide + narrow), B), S((both, width), F), S((width, both), B), S((8, width), F)),
        in_specs=[V, V, V, A, V, V, V, V, V], out_specs=(V, V, A, V, V, V),
        scratch_shapes=[
            pltpu.VMEM((both, width), B), pltpu.VMEM((both, width), F), pltpu.VMEM((width, width), B), pltpu.VMEM((4, width, 256), B),
            pltpu.VMEM((both, width), B), pltpu.VMEM((width, both), B), pltpu.VMEM((width, both), B), pltpu.VMEM((width, both), B),
            pltpu.VMEM((4, both, wide), B), pltpu.VMEM((4, chunk, wide), F), pltpu.VMEM((4, both, wide), B), pltpu.VMEM((both, width), B),
            pltpu.VMEM((2, width, 2 * wide + narrow), B), DMA((4,)), DMA((2,)),
        ],
        compiler_params=pltpu.CompilerParams(vmem_limit_bytes=VLIM), name="middle",
    )(ot, content, query, first, second, gains, ranks, up_content, up_query)


def dot(spec, a, b):
    return jnp.einsum(spec, a, b, preferred_element_type=jnp.float32)


def norm_stats(residual):
    centered = residual - jnp.mean(residual, axis=-1, keepdims=True)
    scale = lax.rsqrt(jnp.mean(centered * centered, axis=-1, keepdims=True) + EPSILON)
    return centered * scale, scale


def norm_back(cotangent, normal, scale, gain):
    inner = cotangent * gain
    mean_inner = jnp.mean(inner, axis=-1, keepdims=True)
    mean_cross = jnp.mean(inner * normal, axis=-1, keepdims=True)
    back = scale * (inner - mean_inner - normal * mean_cross)
    return back, jnp.sum(cotangent * normal, axis=0), jnp.sum(cotangent, axis=0)


def local(
    tp_size, own_exchange, content, query, w_query, w_key, w_value, w_out, w_in, w_down, gain_first, shift_first,
    gain_second, shift_second, bias_table, ranks, span_starts, upstream_content, upstream_query,
):
    rows, width = content.shape
    seq = ranks.shape[1]
    heads = bias_table.shape[0]
    pairs = heads // 2
    tp_index = lax.axis_index("tp")
    both_axes = ("tp", "fsdp")
    narrow = w_query.shape[1]

    def gather(parts):
        shard = jnp.concatenate(parts, axis=1)
        return lax.all_gather(shard, both_axes, axis=0, tiled=True).reshape(tp_size, width, shard.shape[1])

    wide = w_in.shape[1]
    shift = -rows * tp_index
    both = jnp.concatenate([content, query], axis=0)
    if own_exchange:
        shard1, shard2 = jnp.concatenate([w_out.T, w_query, w_key, w_value], axis=1), jnp.concatenate([w_in, w_down.T], axis=1)
        ot, lse, seq_rot, kp, vp, kt, qt, first, second = front(content, query, shard1, shard2, ranks, span_starts, bias_table)
        seq_rot = seq_rot.reshape(seq, width)
        first, second = first.reshape(tp_size, width, 4 * narrow), second.reshape(tp_size, width, 2 * wide)
    else:
        first, second = gather([w_out.T, w_query, w_key, w_value]), gather([w_in, w_down.T])
    wo, wq, wk, wv = (first[:, :, i * narrow:(i + 1) * narrow] for i in range(4))
    wi, wd = second[:, :, :wide], second[:, :, wide:]
    if not own_exchange:
        seq_rot = jnp.roll(lax.all_gather(content, "tp", axis=0, tiled=True), shift, axis=0)
        qt = (dot("tdc,rd->tcr", wq, both) * (HEAD ** -0.5 * LOG2E)).astype(jnp.bfloat16).reshape(width, 2 * rows)
        kt = dot("tdc,rd->tcr", wk, seq_rot).astype(jnp.bfloat16).reshape(width, seq)
        vt = dot("tdc,rd->tcr", wv, seq_rot).astype(jnp.bfloat16).reshape(width, seq)
        kp = jnp.swapaxes(kt.reshape(pairs, 128, seq), 1, 2)
        vp = jnp.swapaxes(vt.reshape(pairs, 128, seq), 1, 2)
        ot, lse = attend_fwd(tp_size, ranks, span_starts, bias_table, kp, vt, qt)

    if own_exchange:
        gains = jnp.concatenate([jnp.stack([gain_first, shift_first, gain_second, shift_second]), jnp.zeros((4, width), jnp.float32)], axis=0)
        content_out, query_out, grad_second, back_first, got, norm_stack = middle(
            ot, content, query, first, second, gains, ranks, upstream_content, upstream_query
        )
    else:
        ot_blocks = ot.reshape(tp_size, narrow, 2 * rows)
        residual_first = both.astype(jnp.float32) + dot("tcr,tmc->rm", ot_blocks, wo)
        normal_first, scale_first = norm_stats(residual_first)
        normed_first = normal_first * gain_first + shift_first
        low_first = normed_first.astype(jnp.bfloat16)
        lifted = dot("rd,tdf->trf", low_first, wi)
        phi = 0.5 * (1.0 + lax.erf(lifted * (0.5 ** 0.5)))
        hidden = (lifted * phi).astype(jnp.bfloat16)
        slope = phi + lifted * jnp.exp(-0.5 * lifted * lifted) * 0.3989422804014327
        residual_second = normed_first + dot("trf,tmf->rm", hidden, wd)
        normal_second, scale_second = norm_stats(residual_second)
        normed_second = normal_second * gain_second + shift_second
        rank_rows = lax.dynamic_slice_in_dim(ranks[0], rows * tp_index, rows)
        predicted = (rank_rows >= seq - seq * 15 // 100).astype(jnp.float32)
        upstream = jnp.concatenate(
            [upstream_content.astype(jnp.float32), upstream_query.astype(jnp.float32) * predicted[:, None]], axis=0
        )
        back_second, grad_gain_second, grad_shift_second = norm_back(upstream, normal_second, scale_second, gain_second)
        gf = back_second.astype(jnp.bfloat16)
        gu = (slope * dot("rm,tmf->trf", gf, wd)).astype(jnp.bfloat16)
        grad_down = dot("rm,trf->tmf", gf, hidden)
        grad_in = dot("rd,trf->tdf", low_first, gu)
        back_normed = back_second + dot("trf,tdf->rd", gu, wi)
        back_first, grad_gain_first, grad_shift_first = norm_back(back_normed, normal_first, scale_first, gain_first)
        ga = back_first.astype(jnp.bfloat16)
        grad_out = dot("rm,tcr->tmc", ga, ot_blocks)
        got = dot("rm,tmc->tcr", ga, wo).astype(jnp.bfloat16).reshape(width, 2 * rows)
        content_out, query_out = (normed_second[s * rows:(s + 1) * rows].astype(jnp.bfloat16) for s in range(2))
        norm_stack = jnp.stack([grad_gain_first, grad_shift_first, grad_gain_second, grad_shift_second])

    def scatter(blocks):
        flat = blocks.astype(jnp.bfloat16).reshape(tp_size * width, blocks.shape[2])
        return lax.psum_scatter(flat, both_axes, scatter_dimension=0, tiled=True).astype(jnp.float32)

    if own_exchange:
        grad_second = grad_second.reshape(4, 2, 2, 2, width // 8, grad_second.shape[2])
        gqt, gkt, gvt, grad_table, sum_second = attend_bwd(tp_size, ranks, span_starts, bias_table, kp, vp, kt, qt, ot, got, lse, grad_second)
        sum_in, sum_down, sum_out = sum_second[:, :wide], sum_second[:, wide:2 * wide], sum_second[:, 2 * wide:]
    else:
        sum_down, sum_in, sum_out = scatter(grad_down), scatter(grad_in), scatter(grad_out)
        gqt, gkt, gvt, grad_table = attend_bwd(tp_size, ranks, span_starts, bias_table, kp, vp, kt, qt, ot, got, lse)
    gq_blocks, gk_blocks, gv_blocks = (g.reshape(tp_size, narrow, g.shape[1]) for g in (gqt, gkt, gvt))
    grads_first = (
        dot("rd,tcr->tdc", both, gq_blocks), dot("rd,tcr->tdc", seq_rot, gk_blocks), dot("rd,tcr->tdc", seq_rot, gv_blocks)
    )
    back_seq = dot("tcr,tdc->rd", gk_blocks, wk) + dot("tcr,tdc->rd", gv_blocks, wv)
    back_seq = jnp.roll(back_seq.astype(jnp.bfloat16), -shift, axis=0)
    back_content = lax.psum_scatter(back_seq, "tp", scatter_dimension=0, tiled=True).astype(jnp.float32)
    back_inputs = back_first + dot("tcr,tdc->rd", gq_blocks, wq)

    grad_table = grad_table[:, :NB]
    if own_exchange:
        grad_first = jnp.concatenate([g.astype(jnp.bfloat16) for g in grads_first], axis=2)
        grad_first = grad_first.reshape(4, 2, 2, 2, width // 8, grad_first.shape[2])
        small = jnp.concatenate([norm_stack[:4], jnp.zeros((4, width), jnp.float32).at[0, :heads * NB].set(grad_table.reshape(-1))], axis=0)
        sum_first, small = reduce_scatter(grad_first, small)
        sum_query, sum_key, sum_value = (sum_first[:, i * narrow:(i + 1) * narrow] for i in range(3))
        summed_norms, summed_table = small[:4], small[4, :heads * NB].reshape(heads, NB)
    else:
        sum_query, sum_key, sum_value = (scatter(g) for g in grads_first)
        summed_norms, summed_table = lax.psum((norm_stack, grad_table), ("fsdp", "tp"))
    return (
        content_out, query_out,
        back_inputs[:rows] + back_content, back_inputs[rows:],
        sum_query, sum_key, sum_value, sum_out.T, sum_in, sum_down.T,
        summed_norms[0], summed_norms[1], summed_norms[2], summed_norms[3], summed_table,
    )


def solution(mesh):
    in_specs = (
        P(("fsdp", "tp"), None),
        P(("fsdp", "tp"), None),
        P("fsdp", "tp"),
        P("fsdp", "tp"),
        P("fsdp", "tp"),
        P("tp", "fsdp"),
        P("fsdp", "tp"),
        P("tp", "fsdp"),
        P(),
        P(),
        P(),
        P(),
        P(),
        P("fsdp", None),
        P("fsdp", None),
        P(("fsdp", "tp"), None),
        P(("fsdp", "tp"), None),
    )
    out_specs = (
        P(("fsdp", "tp"), None),
        P(("fsdp", "tp"), None),
        P(("fsdp", "tp"), None),
        P(("fsdp", "tp"), None),
        P("fsdp", "tp"),
        P("fsdp", "tp"),
        P("fsdp", "tp"),
        P("tp", "fsdp"),
        P("fsdp", "tp"),
        P("tp", "fsdp"),
        P(),
        P(),
        P(),
        P(),
        P(),
    )
    return jax.shard_map(functools.partial(local, mesh.shape["tp"], mesh.shape["tp"] == 4 and mesh.shape["fsdp"] == 8), mesh=mesh, in_specs=in_specs, out_specs=out_specs, check_vma=False)
```

```python
import functools
import jax, jax.numpy as jnp
from jax import lax
from jax.sharding import PartitionSpec as P
from jax.experimental import pallas as pl
from jax.experimental.pallas import tpu as pltpu

NEG = -1e30
PIECES = 3
HEAD = 64
NB = 32
PIC = 256
THRESHOLDS = (12, 16, 23, 32, 46, 64, 91)
EPSILON = 1e-05
LOG2E = 1.4426950408889634
LN2 = 0.6931471805599453
VLIM = 60 * 2**20
MESH = pl.DeviceIdType.MESH

def pick(index, values):
    result = jnp.int32(values[-1])
    for place in range(len(values) - 2, -1, -1):
        result = jnp.where(index == place, jnp.int32(values[place]), result)
    return result


class Place:
    def __init__(self):
        f, t = lax.axis_index("fsdp"), lax.axis_index("tp")
        self.f, self.t = f, t
        self.y, self.x, self.c = f // 4, (f // 2) % 2, f % 2
        self.core = (f + 1 - 2 * self.c, t)
        self.xn = (f + 2 - 4 * self.x, t)
        self.yn = (f + 4 - 8 * self.y, t)
        self.up, self.down = (f, t + 1), (f, t - 1)
        self.order = [pick(t, row) for row in ((3, 3, 0, 0), (2, 0, 3, 1), (1, 2, 1, 2), (0, 1, 2, 3))]

    def greet(self):
        barrier = pltpu.get_barrier_semaphore()
        for there in (self.core, self.xn, self.yn):
            pl.semaphore_signal(barrier, inc=1, device_id=there, device_id_type=MESH)
        for there in ((self.f, jnp.where(self.t > 0, self.t - 1, 3)), (self.f, jnp.where(self.t < 3, self.t + 1, 0))):
            pl.semaphore_signal(barrier, inc=1, device_id=there, device_id_type=MESH)
        pl.semaphore_wait(barrier, 5)


def rdma(src, dst, ss, rs, there):
    return pltpu.make_async_remote_copy(src_ref=src, dst_ref=dst, send_sem=ss, recv_sem=rs, device_id=there, device_id_type=MESH)


class Scatter:
    def __init__(self, at, g, own, r0, r1a, r1b, r2a, r2b, zs, zr, sems, keep_sems):
        self.at, self.g, self.own, self.keep_sems = at, g, own, keep_sems
        self.r0, self.r1a, self.r1b, self.r2a, self.r2b, self.zs, self.zr = r0, r1a, r1b, r2a, r2b, zs, zr
        self.sems = sems
        self.wa = r1a.shape[-1]

    def sem(self, i):
        return self.sems.at[0, i], self.sems.at[1, i]

    def copy0(self, k):
        a = self.at; d = a.order[k]
        return rdma(self.g.at[d, :, :, 1 - a.c], self.r0.at[d], *self.sem(k), a.core)

    def copy1(self, k):
        a = self.at; d = a.order[k]; wa = self.wa
        return (rdma(self.r0.at[d, :, 1 - a.x, :, :wa], self.r1a.at[d], *self.sem(4 + k), a.xn),
                rdma(self.r0.at[d, 1 - a.y, :, :, wa:], self.r1b.at[d], *self.sem(8 + k), a.yn))

    def copy2(self, k):
        a = self.at; d = a.order[k]
        return (rdma(self.r1a.at[d, 1 - a.y], self.r2a.at[d], *self.sem(12 + k), a.yn),
                rdma(self.r1b.at[d, 1 - a.x], self.r2b.at[d], *self.sem(16 + k), a.xn))

    def hop(self, side, h):
        a = self.at
        return rdma(self.zs.at[side, h - 1], self.zr.at[side, h - 1], *self.sem(20 + 3 * side + h - 1), a.down if side else a.up)

    def keep(self, k):
        a = self.at; d = a.order[k]
        return pltpu.make_async_copy(self.g.at[d, :, :, a.c], self.own.at[d], self.keep_sems.at[k])

    def start(self):
        for k in range(4):
            self.copy0(k).start()
            self.keep(k).start()

    def start_one(self, k):
        self.copy0(k).start()

    def stage0(self, k):
        a = self.at; d = a.order[k]
        if self.own is None:
            own = self.g[d, :, :, a.c]
        else:
            self.keep(k).wait()
            own = self.own[d]
        self.copy0(k).wait()
        self.r0[d] = self.r0[d] + own
        for c in self.copy1(k): c.start()

    def stage1(self, k):
        a = self.at; d = a.order[k]; wa = self.wa
        for c in self.copy1(k): c.wait()
        self.r1a[d] = self.r1a[d] + self.r0[d, :, a.x, :, :wa]
        self.r1b[d] = self.r1b[d] + self.r0[d, a.y, :, :, wa:]
        for c in self.copy2(k): c.start()

    def stage2(self, k):
        a = self.at; d = a.order[k]
        for c in self.copy2(k): c.wait()
        self.r2a[d] = self.r2a[d] + self.r1a[d, a.y]
        self.r2b[d] = self.r2b[d] + self.r1b[d, a.x]

    def stage3(self, h):
        wa = self.wa
        for side in range(2):
            u = 3 - self.at.t if side else self.at.t
            d = (self.at.t + h - 4) if side else (self.at.t + 4 - h)
            if h > 1:
                @pl.when((u > 0) & (u < 3) & (u <= h - 1))
                def _():
                    self.hop(side, h - 1).wait_recv()
                    self.zs[side, h - 1, :, :wa] = self.r2a[d] + self.zr[side, h - 2, :, :wa]
                    self.zs[side, h - 1, :, wa:] = self.r2b[d] + self.zr[side, h - 2, :, wa:]
                    self.hop(side, h).start()
            @pl.when(u == 0)
            def _():
                self.zs[side, h - 1, :, :wa] = self.r2a[d]
                self.zs[side, h - 1, :, wa:] = self.r2b[d]
                self.hop(side, h).start()

    def finish(self):
        a = self.at; wa = self.wa
        for side in range(2):
            u = 3 - a.t if side else a.t
            @pl.when(u > 0)
            def _():
                self.hop(side, 3).wait_recv()
        mine = jnp.concatenate([self.r2a[a.t], self.r2b[a.t]], axis=1).astype(jnp.float32)
        below = jnp.where(a.t > 0, self.zr[0, 2].astype(jnp.float32), 0.0)
        above = jnp.where(a.t < 3, self.zr[1, 2].astype(jnp.float32), 0.0)
        for side in range(2):
            u = 3 - a.t if side else a.t
            for h in range(1, 4):
                @pl.when(u < h)
                def _():
                    self.hop(side, h).wait_send()
        return mine + below + above


class Fold:
    def __init__(self, at, part, got, sems):
        self.at, self.part, self.got, self.sems = at, part, got, sems

    def hop(self, side, h):
        a = self.at
        d = jnp.clip((a.t + h - 4) if side else (a.t + 4 - h), 0, 3)
        i = 3 * side + h - 1
        return rdma(self.part.at[d], self.got.at[side, h - 1], self.sems.at[0, i], self.sems.at[1, i], a.down if side else a.up)

    def step(self, h):
        for side in range(2):
            u = 3 - self.at.t if side else self.at.t
            d = (self.at.t + h - 4) if side else (self.at.t + 4 - h)
            if h > 1:
                @pl.when((u > 0) & (u < 3) & (u <= h - 1))
                def _():
                    self.hop(side, h - 1).wait_recv()
                    self.part[d] = self.part[d] + self.got[side, h - 2]
                    self.hop(side, h).start()
            @pl.when(u == 0)
            def _():
                self.hop(side, h).start()

    def finish(self):
        a = self.at
        for side in range(2):
            u = 3 - a.t if side else a.t
            @pl.when(u > 0)
            def _():
                self.hop(side, 3).wait_recv()
            for h in range(1, 4):
                @pl.when(u < h)
                def _():
                    self.hop(side, h).wait_send()
        below = jnp.where(a.t > 0, self.got[0, 2].astype(jnp.float32), 0.0)
        above = jnp.where(a.t < 3, self.got[1, 2].astype(jnp.float32), 0.0)
        return self.part[a.t].astype(jnp.float32) + below + above

def scatter_scratch(T, R, W, kept=True):
    wa = (W // 256) * 128
    B = jnp.bfloat16
    return [pltpu.VMEM((T, 2, 2, R, W), B)] * (2 if kept else 1) + [pltpu.VMEM((T, 2, R, wa), B), pltpu.VMEM((T, 2, R, W - wa), B),
            pltpu.VMEM((T, R, wa), B), pltpu.VMEM((T, R, W - wa), B), pltpu.VMEM((2, 3, R, W), B), pltpu.VMEM((2, 3, R, W), B),
            pltpu.SemaphoreType.DMA((2, 26))] + [pltpu.SemaphoreType.DMA((4,))] * kept

class Total:
    def __init__(self, at, sources, acc, got, sems):
        self.at, self.sources, self.acc, self.got, self.sems = at, sources, acc, got, sems
        t = at.t
        self.partners = [at.core, at.xn, at.yn, (at.f, t + 1 - 2 * (t % 2)), (at.f, 3 - t)]

    def copy(self, i):
        return rdma(self.acc.at[i], self.got.at[i], self.sems.at[0, i], self.sems.at[1, i], self.partners[i])

    def start(self):
        norms, table = self.sources
        self.acc[0] = jnp.zeros_like(self.acc[0])
        self.acc[0, :8, :] = norms[...]
        self.acc[0, 8:8 + table.shape[0], :table.shape[1]] = table[...]
        self.copy(0).start()

    def step(self, i):
        self.copy(i).wait_recv()
        self.acc[i + 1] = self.acc[i] + self.got[i]
        if i < 4:
            self.copy(i + 1).start()

    def finish(self, norms_out, table_out):
        for i in range(5):
            self.copy(i).wait_send()
        norms_out[...] = self.acc[5, :8, :]
        table_out[...] = self.acc[5, 8:8 + table_out.shape[0], :table_out.shape[1]]


def total_scratch(rows, width):
    F = jnp.float32
    return [pltpu.VMEM((6, rows, width), F), pltpu.VMEM((5, rows, width), F), pltpu.SemaphoreType.DMA((2, 5))]


def tail_kernel(gqt, gkt, gvt, seqt, queryt, first, back, norms, table,
                grad_content, grad_query, sum_query, sum_key, sum_value, norms_out, table_out,
                weights, part, got, g1, weight_sems, fold_sems, *scratch):
    rows, width = grad_content.shape
    narrow, R = width // 4, sum_query.shape[0]
    at = Place()
    loads = [pltpu.make_async_copy(first.at[b, :, pl.ds(128, 640)], weights.at[b], weight_sems.at[b]) for b in range(4)]
    for c in loads:
        c.start()
    at.greet()
    scatter, fold, total = Scatter(at, g1, None, *scratch[:8], None), Fold(at, part, got, fold_sems), Total(at, (norms, table), *scratch[8:])
    total.start()
    for c in loads:
        c.wait()

    def partial(d):
        cols = pl.ds(pl.multiple_of(((d - at.t + 4) % 4) * rows, 128), rows)
        out = jnp.zeros((rows, width), jnp.float32)
        for b in range(4):
            here = slice(b * narrow, (b + 1) * narrow)
            out = out + nt(jnp.concatenate([gkt[here, cols], gvt[here, cols]], axis=0).T, weights[b, :, 256:])
        part[d] = out.astype(jnp.bfloat16)

    def weight_grads(k):
        d = at.order[k]
        here = pl.ds(pl.multiple_of(d * narrow, 64), narrow)
        query = nt(seqt[:, :rows], gqt[here, :rows]) + nt(queryt[...], gqt[here, rows:])
        block = jnp.concatenate([query, nt(seqt[...], gkt[here, :]), nt(seqt[...], gvt[here, :])], axis=1)
        g1[d] = block.astype(jnp.bfloat16).reshape(2, 2, 2, R, 3 * narrow)
        scatter.start_one(k)

    for k in range(4):
        partial(at.order[k])
        if k == 0:
            fold.step(1)
    for k in range(4):
        weight_grads(k)
        total.step(k)
    total.step(4)
    for k in range(4):
        scatter.stage0(k)
    for s, out in enumerate((grad_content, grad_query)):
        cols = slice(s * rows, (s + 1) * rows)
        value = back[cols, :]
        for b in range(4):
            value = value + nt(gqt[b * narrow:(b + 1) * narrow, cols].T, weights[b, :, 64:256])
        out[...] = value
    fold.step(2)
    for k in range(4):
        scatter.stage1(k)
        if k:
            scatter.stage2(k - 1)
    scatter.stage2(3)
    scatter.stage3(1)
    fold.step(3)
    scatter.stage3(2)
    scatter.stage3(3)
    sums = scatter.finish()
    for i, out in enumerate((sum_query, sum_key, sum_value)):
        out[...] = sums[:, i * narrow:(i + 1) * narrow]
    total.finish(norms_out, table_out)
    grad_content[...] += fold.finish()


def tail(gqt, gkt, gvt, seqt, queryt, first, back, norms, table):
    width, both = gqt.shape
    rows, narrow, R = both // 2, width // 4, width // 8
    V, A = pl.BlockSpec(memory_space=pltpu.MemorySpace.VMEM), pl.BlockSpec(memory_space=pl.ANY)
    B, F, S, DMA = jnp.bfloat16, jnp.float32, jax.ShapeDtypeStruct, pltpu.SemaphoreType.DMA
    outs = [S((rows, width), F)] * 2 + [S((R, narrow), F)] * 3 + [S(norms.shape, F), S(table.shape, F)]
    return pl.pallas_call(
        tail_kernel, out_shape=tuple(outs), in_specs=[V, V, V, V, V, A, V, V, V], out_specs=(V,) * 7,
        scratch_shapes=[
            pltpu.VMEM((4, width, 640), B), pltpu.VMEM((4, rows, width), B), pltpu.VMEM((2, 3, rows, width), B),
            pltpu.VMEM((4, 2, 2, 2, R, 3 * narrow), B), DMA((4,)), DMA((2, 6)),
        ] + scatter_scratch(4, R, 3 * narrow, False) + total_scratch(24, width),
        compiler_params=pltpu.CompilerParams(vmem_limit_bytes=VLIM, collective_id=1, has_side_effects=True), name="tail",
    )(gqt, gkt, gvt, seqt, queryt, first, back, norms, table)


def nn(a, b):
    return lax.dot_general(a, b, (((1,), (0,)), ((), ())), preferred_element_type=jnp.float32)
def nt(a, b):
    return lax.dot_general(a, b, (((1,), (1,)), ((), ())), preferred_element_type=jnp.float32)

def band_kind(i, b, nrow, nkey):
    rel = (b - i) % nkey
    if rel == 0: return 2
    if rel == nkey - 1: return 0 if i == 0 else 1
    if rel == 1: return 4 if i == nrow - 1 else 3
    return None

def wrap(value, size):
    return jnp.where(value >= size, value - size, value)


def bucket_of(offsets):
    magnitude = jnp.abs(offsets)
    far_bucket = 8 + sum((magnitude >= threshold).astype(jnp.int32) for threshold in THRESHOLDS)
    return jnp.where(magnitude < 8, magnitude, far_bucket) + jnp.where(offsets > 0, 16, 0)


def slot_bucket(slot, lanes, tp_index, tp_size):
    if slot >= 10:
        return jnp.full_like(lanes, 15 if slot == 10 else 31)
    kind, wrapped = slot // 2, slot % 2
    buckets = bucket_of(128 * ((-1, -1, 0, 1, 1)[kind] + wrapped) - lanes)
    if kind == 0:
        return jnp.where(tp_index == 0, 31, buckets)
    if kind == 4:
        return jnp.where(tp_index == tp_size - 1, 15, buckets)
    return buckets


def far_sides(nrow, nkey, tp_index):
    key_block = lax.broadcasted_iota(jnp.int32, (16, 2 * nrow * 128), 0)
    row_block = wrap(lax.broadcasted_iota(jnp.int32, (16, 2 * nrow * 128), 1) // 128, nrow)
    gap = key_block - row_block
    near = (gap == 0) | (gap == 1) | (gap == -1) | (gap == nkey - 1) | (gap == 1 - nkey) | (key_block >= nkey)
    key_place, row_place = wrap(key_block + nrow * tp_index, nkey), row_block + nrow * tp_index
    left = jnp.where(near, 0.0, jnp.where(key_place < row_place, 1.0, 0.0))
    return left, jnp.where(near, 0.0, 1.0 - left)


def prepare(nrow, nkey, tp_size, ranks, starts, table, mask, ring, vec, sides):
    tp_index = lax.axis_index("tp")
    rows, seq = nrow * 128, nkey * 128
    base = rows * tp_index
    rank_row = jnp.broadcast_to(ranks[...].astype(jnp.float32), (8, seq))
    ring[:, :seq] = rank_row
    ring[:, seq:] = rank_row

    def label(place):
        found = jnp.zeros(place.shape, jnp.int32)
        for k in range(starts.shape[1]):
            start = starts[0, k]
            found = found + jnp.where((place >= start) & (place < start + PIC), k + 1, 0)
        return found

    row_rank, row_label = [], []
    for i in range(nrow):
        row_rank.append(ring[0:1, pl.ds(pl.multiple_of(base + i * 128, 128), 128)])
        row_label.append(label(base + i * 128 + lax.broadcasted_iota(jnp.int32, (1, 128), 1)))

    def one(b, _):
        keys = pl.ds(pl.multiple_of(b * 128, 128), 128)
        rank_k = jnp.broadcast_to(ring[0:1, pl.ds(pl.multiple_of(base + b * 128, 128), 128)], (128, 128)).T
        kpos = b * 128 + lax.broadcasted_iota(jnp.int32, (128, 128), 0)
        label_k = label(wrap(base + kpos, seq))
        for i in range(nrow):
            rpos = i * 128 + lax.broadcasted_iota(jnp.int32, (128, 128), 1)
            same = (label_k == row_label[i]) & (label_k > 0)
            content = (rank_k <= row_rank[i]) | same
            strict = (rank_k < jnp.maximum(row_rank[i], 1.0)) | (same & (kpos != rpos))
            mask[keys, i * 128:(i + 1) * 128] = jnp.where(content, 0.0, NEG)
            mask[keys, rows + i * 128:rows + (i + 1) * 128] = jnp.where(strict, 0.0, NEG)
        return 0
    lax.fori_loop(0, nkey, one, 0)

    heads = table.shape[0]
    lanes = lax.broadcasted_iota(jnp.int32, (heads, 128), 1)
    columns = [jnp.broadcast_to(table[:, n:n + 1] * LOG2E, (heads, 128)) for n in range(NB)]
    for slot in range(12):
        buckets = slot_bucket(slot, lanes, tp_index, tp_size)
        values = columns[0]
        for n in range(1, NB):
            values = jnp.where(buckets == n, columns[n], values)
        for h in range(heads):
            vec[h, slot:slot + 1, :] = values[h:h + 1, :]
    sides[0], sides[1] = far_sides(nrow, nkey, tp_index)


def far_bias(vec, sides, cf, h):
    copies = cf.shape[1] // 128
    left, right = (jnp.concatenate([vec[h, slot:slot + 1, :]] * copies, axis=1) for slot in (10, 11))
    cf[...] = sides[0] * left + sides[1] * right


def prepare_scratch(nrow, nkey, heads):
    F, rows = jnp.float32, 2 * nrow * 128
    return [
        pltpu.VMEM((nkey * 128, rows), F), pltpu.VMEM((8, 2 * nkey * 128), F), pltpu.VMEM((heads, 12, 128), F),
        pltpu.VMEM((2, 16, rows), F), pltpu.VMEM((16, rows), F), pltpu.VMEM((5, 128, 128), F),
    ]


def band_tiles(band, vec, h):
    lane = lax.broadcasted_iota(jnp.int32, (128, 128), 1)
    sub = lax.broadcasted_iota(jnp.int32, (128, 128), 0)
    for k in range(5):
        direct, wrapped = (
            pltpu.roll(jnp.broadcast_to(vec[h, 2 * k + w:2 * k + w + 1, :], (128, 128)), 0, 1, stride=1, stride_axis=0)
            for w in range(2)
        )
        band[k] = jnp.where(lane >= sub, direct, wrapped)

def diagonal_sums(tile):
    lane = lax.broadcasted_iota(jnp.int32, (8, 128), 1)
    sub = lax.broadcasted_iota(jnp.int32, (8, 128), 0)
    direct = wrapped = jnp.zeros((8, 128), jnp.float32)
    for a in range(16):
        rows = tile[8 * a:8 * a + 8, :]
        kept = jnp.where(lane >= sub + 8 * a, rows, 0.0)
        left = rows - kept
        if a:
            kept, left = pltpu.roll(kept, 128 - 8 * a, 1), pltpu.roll(left, 128 - 8 * a, 1)
        direct, wrapped = direct + kept, wrapped + left
    for bit in (1, 2, 4):
        moved = (sub & bit) != 0
        direct = jnp.where(moved, pltpu.roll(direct, 128 - bit, 1), direct)
        wrapped = jnp.where(moved, pltpu.roll(wrapped, 128 - bit, 1), wrapped)
    return jnp.sum(direct, axis=0, keepdims=True), jnp.sum(wrapped, axis=0, keepdims=True)

def head_rows(ref, p, hh, cols):
    z = jnp.zeros((64, cols.stop - cols.start), jnp.bfloat16)
    rows = ref[pl.ds(pl.multiple_of((2 * p + hh) * 64, 64), 64), cols]
    return jnp.concatenate([rows, z] if hh == 0 else [z, rows], axis=0)

def attend_rows(nrow, nkey, kp, vt, qt, ot, lse, t, prepared, exchange):
    mask, _, vec, sides, cf, band = prepared
    ones = jnp.ones((16, 256), jnp.bfloat16)
    nchunk = 2 * nrow * 128 // 256
    def pair(p, _):
        for hh in range(2):
            h = 2 * p + hh
            exchange(h)
            hrows = pl.ds(pl.multiple_of(h * 64, 64), 64)
            band_tiles(band, vec, h)
            far_bias(vec, sides, cf, h)
            for c in range(nchunk):
                cols = slice(c * 256, (c + 1) * 256)
                qh = head_rows(qt, p, hh, cols)
                m8 = jnp.full((8, 256), -jnp.inf, jnp.float32)
                for b in range(nkey):
                    s = nn(kp[p, b * 128:(b + 1) * 128, :], qh)
                    s = s + mask[b * 128:(b + 1) * 128, cols]
                    kinds = [band_kind((2 * c + k) % nrow, b, nrow, nkey) for k in range(2)]
                    if any(k is not None for k in kinds):
                        s = jnp.concatenate([s[:, k * 128:(k + 1) * 128] + (band[kinds[k]] if kinds[k] is not None else 0.0) for k in range(2)], axis=1)
                    t[c, b * 128:(b + 1) * 128, :] = s
                    m8 = jnp.maximum(m8, jnp.max(s.reshape(16, 8, 256), axis=0) + cf[b:b + 1, cols])
                m = jnp.max(m8, axis=0, keepdims=True)
                acc = jnp.zeros((80, 256), jnp.float32)
                for g in range(nkey // 2):
                    ps = []
                    for b in (2 * g, 2 * g + 1):
                        ps.append(jnp.exp2(t[c, b * 128:(b + 1) * 128, :] - (m - cf[b:b + 1, cols])).astype(jnp.bfloat16))
                    lhs = jnp.concatenate([vt[hrows, g * 256:(g + 1) * 256], ones], axis=0)
                    acc = acc + nn(lhs, jnp.concatenate(ps, axis=0))
                l = acc[64:65, :]
                ot[hrows, cols] = (acc[:64, :] / l).astype(jnp.bfloat16)
                lse[h, 0:1, cols] = m + jnp.log2(l)
        return 0
    lax.fori_loop(0, kp.shape[0], pair, 0)

def fwd_kernel(nrow, nkey, tp_size, ranks, starts, table, kp, vt, qt, ot, lse, t, *prepared):
    prepare(nrow, nkey, tp_size, ranks, starts, table, *prepared[:4])
    attend_rows(nrow, nkey, kp, vt, qt, ot, lse, t, prepared, lambda h: None)


def attend_fwd(tp_size, ranks, starts, table, kp, vt, qt):
    pairs, seq, _ = kp.shape
    rows = qt.shape[1]
    nrow, nkey = rows // 256, seq // 128
    V, M = pl.BlockSpec(memory_space=pltpu.MemorySpace.VMEM), pl.BlockSpec(memory_space=pltpu.MemorySpace.SMEM)
    return pl.pallas_call(
        functools.partial(fwd_kernel, nrow, nkey, tp_size),
        out_shape=(jax.ShapeDtypeStruct(qt.shape, jnp.bfloat16), jax.ShapeDtypeStruct((2 * pairs, 1, rows), jnp.float32)),
        in_specs=[V, M, V, V, V, V], out_specs=(V, V),
        scratch_shapes=[pltpu.VMEM((rows // 256, seq, 256), jnp.float32)] + prepare_scratch(nrow, nkey, 2 * pairs),
        compiler_params=pltpu.CompilerParams(vmem_limit_bytes=VLIM),
        name="attend_fwd",
    )(ranks, starts, table, kp, vt, qt)


class Gather:
    def __init__(self, at, shard, g, wa, sems, own_sem):
        self.at, self.shard, self.g, self.wa, self.sems, self.own_sem = at, shard, g, wa, sems, own_sem
        self.blocks = at.order[::-1]

    def send(self, i, src, dst, there):
        return rdma(src, dst, self.sems.at[0, i], self.sems.at[1, i], there)

    def along_z(self, b, upward):
        a = self.at
        here = self.g.at[b, a.y, a.x, a.c]
        return self.send(b + (0 if upward else 4), here, here, a.up if upward else a.down)

    def first(self, b):
        a, wa = self.at, self.wa
        left, right = (self.g.at[b, a.y, a.x, a.c, :, cols] for cols in (slice(0, wa), slice(wa, None)))
        return self.send(8 + b, left, left, a.xn), self.send(12 + b, right, right, a.yn)

    def second(self, b):
        a, wa = self.at, self.wa
        left, right = self.g.at[b, a.y, :, a.c, :, :wa], self.g.at[b, :, a.x, a.c, :, wa:]
        return self.send(16 + b, left, left, a.yn), self.send(20 + b, right, right, a.xn)

    def across(self, b):
        a = self.at
        here = self.g.at[b, :, :, a.c]
        return self.send(24 + b, here, here, a.core)

    def own(self):
        a = self.at
        return pltpu.make_async_copy(self.shard, self.g.at[a.t, a.y, a.x, a.c], self.own_sem)

    def begin(self):
        self.own().start()
        self.own().wait()
        for c in self.first(self.at.t):
            c.start()

    def begin_z(self):
        a = self.at
        @pl.when(a.t < 3)
        def _():
            self.along_z(a.t, True).start()
        @pl.when(a.t > 0)
        def _():
            self.along_z(a.t, False).start()

    def arrive(self, j):
        a, b = self.at, self.blocks[j]
        @pl.when(b < a.t)
        def _():
            self.along_z(b, True).wait_recv()
        @pl.when(b > a.t)
        def _():
            self.along_z(b, False).wait_recv()
        @pl.when((b < a.t) & (a.t < 3))
        def _():
            self.along_z(b, True).start()
        @pl.when((b > a.t) & (a.t > 0))
        def _():
            self.along_z(b, False).start()
        for c in self.first(b):
            c.start()

    def step1(self, j):
        b = self.blocks[j]
        for c in self.first(b):
            c.wait_recv()
        for c in self.second(b):
            c.start()

    def step2(self, j):
        b = self.blocks[j]
        for c in self.second(b):
            c.wait_recv()
        self.across(b).start()

    def step3(self, j):
        self.across(self.blocks[j]).wait_recv()

    def finish(self):
        a = self.at
        for b in range(4):
            @pl.when((b <= a.t) & (a.t < 3))
            def _():
                self.along_z(b, True).wait_send()
            @pl.when((b >= a.t) & (a.t > 0))
            def _():
                self.along_z(b, False).wait_send()
            for c in (*self.first(b), *self.second(b), self.across(b)):
                c.wait_send()


class Chain:
    def __init__(self, at, seq, sems, pieces):
        self.at, self.seq, self.sems, self.pieces = at, seq, sems, pieces
        self.blocks = at.order[::-1]

    def move(self, b, upward, s):
        a = self.at
        i = (b + (0 if upward else 4)) * self.pieces + s
        there = a.t + 1 if upward else a.t - 1
        size = self.seq.shape[1] // self.pieces
        part = slice(s * size, (s + 1) * size)
        return rdma(self.seq.at[(b - a.t + 4) % 4, part], self.seq.at[(b - there + 4) % 4, part], self.sems.at[0, i], self.sems.at[1, i], (a.f, there))

    def begin(self):
        a = self.at
        for s in range(self.pieces):
            @pl.when(a.t < 3)
            def _():
                self.move(a.t, True, s).start()
            @pl.when(a.t > 0)
            def _():
                self.move(a.t, False, s).start()

    def arrive(self, j):
        a, b = self.at, self.blocks[j]
        for s in range(self.pieces):
            @pl.when(b < a.t)
            def _():
                self.move(b, True, s).wait_recv()
            @pl.when(b > a.t)
            def _():
                self.move(b, False, s).wait_recv()
            @pl.when((b < a.t) & (a.t < 3))
            def _():
                self.move(b, True, s).start()
            @pl.when((b > a.t) & (a.t > 0))
            def _():
                self.move(b, False, s).start()

    def finish(self):
        a = self.at
        for b in range(4):
            for s in range(self.pieces):
                @pl.when((b <= a.t) & (a.t < 3))
                def _():
                    self.move(b, True, s).wait_send()
                @pl.when((b >= a.t) & (a.t > 0))
                def _():
                    self.move(b, False, s).wait_send()


def front_kernel(nrow, nkey, content, query, shard1, shard2, ranks, starts, table,
                 ot, lse, seqt_out, queryt_out, kp_out, vp_out, kt_out, qt_out, w1_out, w2_out,
                 seq, seqt, queryt, w1, w2, w1t, kp, vp, kt, vt, qt, t,
                 sems1, sems2, semsc, own_sems, out_sems, *prepared):
    at = Place()
    rows = nrow * 128
    pairs = kp.shape[0]
    narrow = shard1.shape[1] // 4
    width = content.shape[1]
    weights1 = Gather(at, shard1, w1, shard1.shape[1] // 2, sems1, own_sems.at[0])
    weights2 = Gather(at, shard2, w2, shard2.shape[1] // 2, sems2, own_sems.at[1])
    chain = Chain(at, seq, semsc, PIECES)
    seq[0] = content[...]
    at.greet()
    weights1.begin()
    weights1.begin_z()
    weights1.arrive(1)
    weights1.step1(0)
    weights1.arrive(2)
    weights1.step1(1)
    weights1.step2(0)
    weights1.arrive(3)
    chain.begin()
    weights1.step1(2)
    weights1.step2(1)
    weights1.step1(3)
    weights2.begin()
    prepare(nrow, nkey, 4, ranks, starts, table, *prepared[:4])
    weights1.step2(2)
    weights1.step2(3)
    for j in range(4):
        weights1.step3(j)

    scale = HEAD ** -0.5 * LOG2E
    for tt in range(4):
        block = w1[tt].reshape(width, 4 * narrow)
        w1t[tt] = block[:, narrow:].T
        for s, x in enumerate((content, query)):
            q = nt(w1t[tt, :narrow, :], x[...])
            qt[tt * narrow:(tt + 1) * narrow, s * rows:(s + 1) * rows] = (q * scale).astype(jnp.bfloat16)

    def project(r):
        x = seq[r]
        cols = pl.ds(pl.multiple_of(r * rows, 128), rows)
        seqt[:, cols] = x.T
        for i, (across, upright) in enumerate(((kp, kt), (vp, vt))):
            for tt in range(4):
                out = nt(w1t[tt, (i + 1) * narrow:(i + 2) * narrow, :], x)
                upright[tt * narrow:(tt + 1) * narrow, cols] = out.astype(jnp.bfloat16)
            for u in range(2):
                halves = [
                    nn(x, w1[2 * u + v].reshape(width, 4 * narrow)[:, (i + 2) * narrow:(i + 3) * narrow]) for v in range(2)
                ]
                joined = jnp.concatenate(halves, axis=1).astype(jnp.bfloat16)
                for p in range(pairs // 2):
                    across[u * (pairs // 2) + p, cols, :] = joined[:, p * 128:(p + 1) * 128]

    queryt[...] = query[...].T
    project(0)
    for j in range(1, 4):
        chain.arrive(j)
        if j == 1:
            weights2.step1(0)
        if j == 2:
            weights2.begin_z()
            weights2.step2(0)
        project((chain.blocks[j] - at.t + 4) % 4)

    outs = [
        pltpu.make_async_copy(src, dst, out_sems.at[i])
        for i, (src, dst) in enumerate(((seqt, seqt_out), (queryt, queryt_out), (kp, kp_out), (vp, vp_out), (kt, kt_out), (qt, qt_out), (w1, w1_out)))
    ]
    for c in outs:
        c.start()

    def second_out(j):
        b = weights2.blocks[j]
        return pltpu.make_async_copy(w2.at[b], w2_out.at[b], out_sems.at[7 + j])

    def exchange(h):
        steps = (
            (weights2.arrive, 1, 2), (weights2.step1, 1, 4), (weights2.arrive, 2, 5), (weights2.step2, 1, 6), (weights2.step1, 2, 7),
            (weights2.arrive, 3, 8), (weights2.step2, 2, 9), (weights2.step1, 3, 11),
        )
        for step, j, place in steps:
            @pl.when(h == place)
            def _():
                step(j)

    attend_rows(nrow, nkey, kp, vt, qt, ot, lse, t, prepared, exchange)
    weights2.step2(3)
    for j in range(4):
        weights2.step3(j)
        second_out(j).start()
    for c in outs:
        c.wait()
    for j in range(4):
        second_out(j).wait()
    weights1.finish()
    weights2.finish()
    chain.finish()


def front(content, query, shard1, shard2, ranks, starts, table):
    rows, width = content.shape
    heads, seq_len = table.shape[0], ranks.shape[1]
    pairs, R = heads // 2, shard1.shape[0]
    nrow, nkey = rows // 128, seq_len // 128
    narrow = shard1.shape[1] // 4
    V, A = pl.BlockSpec(memory_space=pltpu.MemorySpace.VMEM), pl.BlockSpec(memory_space=pl.ANY)
    B, F, S, DMA = jnp.bfloat16, jnp.float32, jax.ShapeDtypeStruct, pltpu.SemaphoreType.DMA
    full1, full2 = (4, 2, 2, 2) + shard1.shape, (4, 2, 2, 2) + shard2.shape
    kept = [((width, seq_len), B), ((width, rows), B), ((pairs, seq_len, 128), B), ((pairs, seq_len, 128), B), ((width, seq_len), B), ((width, 2 * rows), B), (full1, B)]
    outs = [S((width, 2 * rows), B), S((heads, 1, 2 * rows), F)] + [S(*k) for k in kept] + [S(full2, B)]
    scratch = [pltpu.VMEM((4, rows, width), B), pltpu.VMEM(*kept[0]), pltpu.VMEM(*kept[1]), pltpu.VMEM(full1, B), pltpu.VMEM(full2, B),
               pltpu.VMEM((4, 3 * narrow, width), B), pltpu.VMEM(*kept[2]), pltpu.VMEM(*kept[3]),
               pltpu.VMEM(*kept[4]), pltpu.VMEM(*kept[4]), pltpu.VMEM(*kept[5]),
               pltpu.VMEM((2 * rows // 256, seq_len, 256), F),
               DMA((2, 28)), DMA((2, 28)), DMA((2, 8 * PIECES)), DMA((2,)), DMA((11,))] + prepare_scratch(nrow, nkey, heads)
    return pl.pallas_call(
        functools.partial(front_kernel, nrow, nkey),
        out_shape=tuple(outs), in_specs=[V, V, A, A, V, pl.BlockSpec(memory_space=pltpu.MemorySpace.SMEM), V], out_specs=tuple([V, V] + [A] * 8), scratch_shapes=scratch,
        compiler_params=pltpu.CompilerParams(vmem_limit_bytes=VLIM, collective_id=3, has_side_effects=True), name="front",
    )(content, query, shard1, shard2, ranks, starts, table)


def bwd_kernel(nrow, nkey, tp_size, fused, *refs):
    if fused:
        ranks, starts, table, kp, vp, kt, qt, ot, got, lse, g, gqt, gkt, gvt, back_table, sum_in, sum_down, sum_out, gq, bacc, diag, *scratch = refs
        prepared, scratch = scratch[:6], scratch[6:]
        at = Place()
        at.greet()
        scatter = Scatter(at, g, *scratch)
        scatter.start()
    else:
        ranks, starts, table, kp, vp, kt, qt, ot, got, lse, gqt, gkt, gvt, back_table, gq, bacc, diag, *prepared = refs
    mask, _, vec, sides, cf, band = prepared
    prepare(nrow, nkey, tp_size, ranks, starts, table, *prepared[:4])
    lane_row = lax.broadcasted_iota(jnp.int32, (1, 128), 1)

    def exchange(h):
        if not fused:
            return
        steps = (
            (scatter.stage0, 0, 0), (scatter.stage0, 1, 1), (scatter.stage1, 0, 3), (scatter.stage0, 2, 3), (scatter.stage2, 0, 6), (scatter.stage3, 1, 6),
            (scatter.stage1, 1, 6), (scatter.stage0, 3, 6), (scatter.stage1, 2, 8), (scatter.stage2, 1, 9), (scatter.stage3, 2, 9), (scatter.stage1, 3, 11),
        )
        for step, k, place in steps:
            @pl.when(h == place)
            def _():
                step(k)

    rows = 2 * nrow * 128
    nchunk = rows // 256
    full = slice(0, rows)
    block_of = lax.broadcasted_iota(jnp.int32, (16, 256), 0)
    half_of = lax.broadcasted_iota(jnp.int32, (16, 256), 1) // 128
    def pair(p, _):
        for hh in range(2):
            h = 2 * p + hh
            exchange(h)
            hrows = pl.ds(pl.multiple_of(h * 64, 64), 64)
            band_tiles(band, vec, h)
            far_bias(vec, sides, cf, h)
            q_h = qt[hrows, :]
            go_h = got[hrows, :]
            delta = jnp.sum(ot[hrows, :].astype(jnp.float32) * go_h.astype(jnp.float32), axis=0, keepdims=True)
            for k in range(5):
                bacc[k] = jnp.zeros((128, 128), jnp.float32)
            gq[...] = jnp.zeros_like(gq)
            qm = head_rows(qt, p, hh, full)
            gm = head_rows(got, p, hh, full)
            for g in range(nkey // 2):
                pp, gg = [], []
                for c in range(nchunk):
                    cols = slice(c * 256, (c + 1) * 256)
                    pc, gc = [], []
                    for b in (2 * g, 2 * g + 1):
                        keys = slice(b * 128, (b + 1) * 128)
                        s = nn(kp[p, keys, :], qm[:, cols])
                        dp = nn(vp[p, keys, :], gm[:, cols])
                        s = s + mask[keys, cols]
                        kinds = [band_kind((2 * c + k) % nrow, b, nrow, nkey) for k in range(2)]
                        if any(k is not None for k in kinds):
                            s = jnp.concatenate([s[:, k * 128:(k + 1) * 128] + (band[kinds[k]] if kinds[k] is not None else 0.0) for k in range(2)], axis=1)
                        pr = jnp.exp2(s - (lse[h, 0:1, cols] - cf[b:b + 1, cols]))
                        gs = pr * (dp - delta[:, cols])
                        for k in range(2):
                            if kinds[k] is not None:
                                bacc[kinds[k]] += gs[:, k * 128:(k + 1) * 128]
                        pc.append(pr.astype(jnp.bfloat16))
                        gc.append(gs.astype(jnp.bfloat16))
                    pp.append(jnp.concatenate(pc, axis=0))
                    gg.append(jnp.concatenate(gc, axis=0))
                pall = jnp.concatenate(pp, axis=1)
                gall = jnp.concatenate(gg, axis=1)
                keys = slice(g * 256, (g + 1) * 256)
                onehot = (block_of == 2 * g + half_of).astype(jnp.bfloat16)
                gq[...] += nn(jnp.concatenate([kt[hrows, keys], onehot], axis=0), gall)
                gkt[hrows, keys] = (nt(q_h, gall) * LN2).astype(jnp.bfloat16)
                gvt[hrows, keys] = nt(go_h, pall).astype(jnp.bfloat16)
            gqt[hrows, :] = (gq[:64, :] * 0.125).astype(jnp.bfloat16)
            for k in range(5):
                direct, wrapped = diagonal_sums(bacc[k])
                diag[h, 0:1, 256 * k:256 * k + 128] = direct
                diag[h, 0:1, 256 * k + 128:256 * k + 256] = wrapped
            for s in range(2):
                side = jnp.sum(jnp.sum(gq[64:80, :] * sides[s], axis=0, keepdims=True), axis=1, keepdims=True)
                diag[h, 0:1, 1280 + 128 * s:1408 + 128 * s] = jnp.where(lane_row == 0, side, 0.0)
        return 0
    lax.fori_loop(0, kp.shape[0], pair, 0)
    tp_index = lax.axis_index("tp")
    places = lax.broadcasted_iota(jnp.int32, (128, 128), 0)
    numbers = lax.broadcasted_iota(jnp.int32, (128, 128), 1)
    sums = jnp.concatenate([diag[h] for h in range(diag.shape[0])], axis=0)
    total = jnp.zeros((diag.shape[0], 128), jnp.float32)
    for slot in range(12):
        one_hot = jnp.where(slot_bucket(slot, places, tp_index, tp_size) == numbers, 1.0, 0.0)
        total = total + jnp.dot(
            sums[:, slot * 128:(slot + 1) * 128], one_hot, precision=lax.Precision.HIGHEST, preferred_element_type=jnp.float32
        )
    back_table[...] = total
    if fused:
        scatter.stage2(2)
        scatter.stage3(3)
        scatter.stage2(3)
        sums = scatter.finish()
        wide = sum_in.shape[1]
        sum_in[...] = sums[:, :wide]
        sum_down[...] = sums[:, wide:2 * wide].T
        sum_out[...] = sums[:, 2 * wide:].T


def attend_bwd(tp_size, ranks, starts, table, kp, vp, kt, qt, ot, got, lse, g=None):
    pairs, seq, _ = kp.shape
    rows = qt.shape[1]
    heads = 2 * pairs
    nrow, nkey = rows // 256, seq // 128
    V, M = pl.BlockSpec(memory_space=pltpu.MemorySpace.VMEM), pl.BlockSpec(memory_space=pltpu.MemorySpace.SMEM)
    S, F = jax.ShapeDtypeStruct, jnp.float32
    fused = g is not None
    outs = [S(qt.shape, jnp.bfloat16), S(kt.shape, jnp.bfloat16), S(kt.shape, jnp.bfloat16), S((heads, 128), F)]
    scratch = [pltpu.VMEM((80, rows), F), pltpu.VMEM((5, 128, 128), F), pltpu.VMEM((heads, 1, 1536), F)] + prepare_scratch(nrow, nkey, heads)
    params = dict(vmem_limit_bytes=VLIM)
    args = (ranks, starts, table, kp, vp, kt, qt, ot, got, lse)
    specs = [V, M] + [V] * 8
    if fused:
        narrow = kt.shape[0] // 4
        wide = (g.shape[5] - narrow) // 2
        outs += [S((g.shape[4], wide), F), S((wide, g.shape[4]), F), S((narrow, g.shape[4]), F)]
        scratch += scatter_scratch(g.shape[0], g.shape[4], g.shape[5])
        params.update(collective_id=2, has_side_effects=True)
        args += (g,)
        specs = specs + [pl.BlockSpec(memory_space=pl.ANY)]
    return pl.pallas_call(
        functools.partial(bwd_kernel, nrow, nkey, tp_size, fused),
        out_shape=tuple(outs), in_specs=specs, out_specs=(V,) * len(outs), scratch_shapes=scratch,
        compiler_params=pltpu.CompilerParams(**params), name="attend_bwd",
    )(*args)


def norm(residual):
    centered = residual - jnp.mean(residual, axis=-1, keepdims=True)
    scale = lax.rsqrt(jnp.mean(centered * centered, axis=-1, keepdims=True) + EPSILON)
    return centered * scale, scale


def norm_step(cotangent, normal, scale, gain):
    inner = cotangent * gain
    mean_inner = jnp.mean(inner, axis=-1, keepdims=True)
    mean_cross = jnp.mean(inner * normal, axis=-1, keepdims=True)
    return scale * (inner - mean_inner - normal * mean_cross)


def middle_kernel(chunk, ot, content, query, first, second, gains, ranks, up_content, up_query,
                  content_out, query_out, grads, back, got, sums,
                  x, up, wot, wo_block, onat, n1bt, gft, gat, hidden, slope, gu, out2, stage, sems, out_sems):
    rows = content.shape[0]
    seq, width = ranks.shape[1], content.shape[1]
    narrow, wide = width // 4, second.shape[2] // 2
    blocks = [pltpu.make_async_copy(first.at[t, :, pl.ds(0, 256)], wo_block.at[t], sems.at[t]) for t in range(4)]
    for c in blocks:
        c.start()
    base = rows * lax.axis_index("tp")
    x[:rows] = content[...]
    x[rows:] = query[...]
    up[:rows] = up_content[...].astype(jnp.float32)
    for i in range(rows // 128):
        rank = ranks[0:1, pl.ds(pl.multiple_of(base + i * 128, 128), 128)].astype(jnp.float32)
        rank = jnp.broadcast_to(rank, (128, 128)).T
        kept = jnp.where(rank >= seq - seq * 15 // 100, 1.0, 0.0)
        up[rows + i * 128:rows + (i + 1) * 128, :] = up_query[i * 128:(i + 1) * 128, :].astype(jnp.float32) * jnp.concatenate([kept] * (width // 128), axis=1)
    for c in blocks:
        c.wait()
    wot[...] = jnp.concatenate([wo_block[t, :, :narrow] for t in range(4)], axis=1)
    sums[...] = jnp.zeros_like(sums)
    gain1, shift1, gain2, shift2 = (gains[i:i + 1, :] for i in range(4))

    def one(i, _):
        here = pl.ds(pl.multiple_of(i * chunk, chunk), chunk)
        mixed = ot[:, here].T
        onat[here, :] = mixed
        normal1, scale1 = norm(x[here, :].astype(jnp.float32) + nt(mixed, wot[...]))
        normed = normal1 * gain1 + shift1
        low = normed.astype(jnp.bfloat16)
        n1bt[:, here] = low.T
        total = normed
        for t in range(4):
            lifted = nn(low, second[t, :, :wide])
            phi = 0.5 + 0.5 * lax.erf(lifted * (0.5 ** 0.5))
            act = (lifted * phi).astype(jnp.bfloat16)
            hidden[t, here, :] = act
            slope[t] = phi + lifted * (jnp.exp(-0.5 * lifted * lifted) * 0.3989422804014327)
            total = total + nt(act, second[t, :, wide:])
        normal2, scale2 = norm(total)
        out2[here, :] = (normal2 * gain2 + shift2).astype(jnp.bfloat16)
        cotangent = up[here, :]
        sums[2:3, :] += jnp.sum(cotangent * normal2, axis=0, keepdims=True)
        sums[3:4, :] += jnp.sum(cotangent, axis=0, keepdims=True)
        back2 = norm_step(cotangent, normal2, scale2, gain2)
        gf = back2.astype(jnp.bfloat16)
        gft[:, here] = gf.T
        total = back2
        for t in range(4):
            g = (slope[t] * nn(gf, second[t, :, wide:])).astype(jnp.bfloat16)
            gu[t, here, :] = g
            total = total + nt(g, second[t, :, :wide])
        sums[0:1, :] += jnp.sum(total * normal1, axis=0, keepdims=True)
        sums[1:2, :] += jnp.sum(total, axis=0, keepdims=True)
        back1 = norm_step(total, normal1, scale1, gain1)
        back[here, :] = back1
        ga = back1.astype(jnp.bfloat16)
        gat[:, here] = ga.T
        got[:, here] = nn(ga, wot[...]).astype(jnp.bfloat16).T
        return 0

    lax.fori_loop(0, 2 * rows // chunk, one, 0)
    content_out[...] = out2[:rows]
    query_out[...] = out2[rows:]
    for t in range(4):
        wo_block[t, :, :narrow] = nn(gat[...], onat[:, t * narrow:(t + 1) * narrow]).astype(jnp.bfloat16)

    def send(t):
        return pltpu.make_async_copy(stage.at[t % 2], grads.at[t], out_sems.at[t % 2])

    for t in range(4):
        if t >= 2:
            send(t - 2).wait()
        stage[t % 2, :, :wide] = nn(n1bt[...], gu[t]).astype(jnp.bfloat16)
        stage[t % 2, :, wide:2 * wide] = nn(gft[...], hidden[t]).astype(jnp.bfloat16)
        stage[t % 2, :, 2 * wide:] = wo_block[t, :, :narrow]
        send(t).start()
    for t in (2, 3):
        send(t).wait()


def middle(ot, content, query, first, second, gains, ranks, up_content, up_query):
    rows, width = content.shape
    narrow, wide = width // 4, second.shape[2] // 2
    both, chunk = 2 * rows, 256
    V, A = pl.BlockSpec(memory_space=pltpu.MemorySpace.VMEM), pl.BlockSpec(memory_space=pl.ANY)
    B, F, S, DMA = jnp.bfloat16, jnp.float32, jax.ShapeDtypeStruct, pltpu.SemaphoreType.DMA
    return pl.pallas_call(
        functools.partial(middle_kernel, chunk),
        out_shape=(S((rows, width), B), S((rows, width), B), S((4, width, 2 * wide + narrow), B), S((both, width), F), S((width, both), B), S((8, width), F)),
        in_specs=[V, V, V, A, V, V, V, V, V], out_specs=(V, V, A, V, V, V),
        scratch_shapes=[
            pltpu.VMEM((both, width), B), pltpu.VMEM((both, width), F), pltpu.VMEM((width, width), B), pltpu.VMEM((4, width, 256), B),
            pltpu.VMEM((both, width), B), pltpu.VMEM((width, both), B), pltpu.VMEM((width, both), B), pltpu.VMEM((width, both), B),
            pltpu.VMEM((4, both, wide), B), pltpu.VMEM((4, chunk, wide), F), pltpu.VMEM((4, both, wide), B), pltpu.VMEM((both, width), B),
            pltpu.VMEM((2, width, 2 * wide + narrow), B), DMA((4,)), DMA((2,)),
        ],
        compiler_params=pltpu.CompilerParams(vmem_limit_bytes=VLIM), name="middle",
    )(ot, content, query, first, second, gains, ranks, up_content, up_query)


def dot(spec, a, b):
    return jnp.einsum(spec, a, b, preferred_element_type=jnp.float32)


def norm_stats(residual):
    centered = residual - jnp.mean(residual, axis=-1, keepdims=True)
    scale = lax.rsqrt(jnp.mean(centered * centered, axis=-1, keepdims=True) + EPSILON)
    return centered * scale, scale


def norm_back(cotangent, normal, scale, gain):
    inner = cotangent * gain
    mean_inner = jnp.mean(inner, axis=-1, keepdims=True)
    mean_cross = jnp.mean(inner * normal, axis=-1, keepdims=True)
    back = scale * (inner - mean_inner - normal * mean_cross)
    return back, jnp.sum(cotangent * normal, axis=0), jnp.sum(cotangent, axis=0)


def local(
    tp_size, own_exchange, content, query, w_query, w_key, w_value, w_out, w_in, w_down, gain_first, shift_first,
    gain_second, shift_second, bias_table, ranks, span_starts, upstream_content, upstream_query,
):
    rows, width = content.shape
    seq = ranks.shape[1]
    heads = bias_table.shape[0]
    pairs = heads // 2
    tp_index = lax.axis_index("tp")
    both_axes = ("tp", "fsdp")
    narrow = w_query.shape[1]

    def gather(parts):
        shard = jnp.concatenate(parts, axis=1)
        return lax.all_gather(shard, both_axes, axis=0, tiled=True).reshape(tp_size, width, shard.shape[1])

    wide = w_in.shape[1]
    shift = -rows * tp_index
    both = jnp.concatenate([content, query], axis=0)
    if own_exchange:
        shard1, shard2 = jnp.concatenate([w_out.T, w_query, w_key, w_value], axis=1), jnp.concatenate([w_in, w_down.T], axis=1)
        ot, lse, seqt, queryt, kp, vp, kt, qt, first, second = front(content, query, shard1, shard2, ranks, span_starts, bias_table)
        first, second = first.reshape(tp_size, width, 4 * narrow), second.reshape(tp_size, width, 2 * wide)
    else:
        first, second = gather([w_out.T, w_query, w_key, w_value]), gather([w_in, w_down.T])
    wo, wq, wk, wv = (first[:, :, i * narrow:(i + 1) * narrow] for i in range(4))
    wi, wd = second[:, :, :wide], second[:, :, wide:]
    if not own_exchange:
        seq_rot = jnp.roll(lax.all_gather(content, "tp", axis=0, tiled=True), shift, axis=0)
        qt = (dot("tdc,rd->tcr", wq, both) * (HEAD ** -0.5 * LOG2E)).astype(jnp.bfloat16).reshape(width, 2 * rows)
        kt = dot("tdc,rd->tcr", wk, seq_rot).astype(jnp.bfloat16).reshape(width, seq)
        vt = dot("tdc,rd->tcr", wv, seq_rot).astype(jnp.bfloat16).reshape(width, seq)
        kp = jnp.swapaxes(kt.reshape(pairs, 128, seq), 1, 2)
        vp = jnp.swapaxes(vt.reshape(pairs, 128, seq), 1, 2)
        ot, lse = attend_fwd(tp_size, ranks, span_starts, bias_table, kp, vt, qt)

    if own_exchange:
        gains = jnp.concatenate([jnp.stack([gain_first, shift_first, gain_second, shift_second]), jnp.zeros((4, width), jnp.float32)], axis=0)
        content_out, query_out, grad_second, back_first, got, norm_stack = middle(
            ot, content, query, first, second, gains, ranks, upstream_content, upstream_query
        )
    else:
        ot_blocks = ot.reshape(tp_size, narrow, 2 * rows)
        residual_first = both.astype(jnp.float32) + dot("tcr,tmc->rm", ot_blocks, wo)
        normal_first, scale_first = norm_stats(residual_first)
        normed_first = normal_first * gain_first + shift_first
        low_first = normed_first.astype(jnp.bfloat16)
        lifted = dot("rd,tdf->trf", low_first, wi)
        phi = 0.5 * (1.0 + lax.erf(lifted * (0.5 ** 0.5)))
        hidden = (lifted * phi).astype(jnp.bfloat16)
        slope = phi + lifted * jnp.exp(-0.5 * lifted * lifted) * 0.3989422804014327
        residual_second = normed_first + dot("trf,tmf->rm", hidden, wd)
        normal_second, scale_second = norm_stats(residual_second)
        normed_second = normal_second * gain_second + shift_second
        rank_rows = lax.dynamic_slice_in_dim(ranks[0], rows * tp_index, rows)
        predicted = (rank_rows >= seq - seq * 15 // 100).astype(jnp.float32)
        upstream = jnp.concatenate(
            [upstream_content.astype(jnp.float32), upstream_query.astype(jnp.float32) * predicted[:, None]], axis=0
        )
        back_second, grad_gain_second, grad_shift_second = norm_back(upstream, normal_second, scale_second, gain_second)
        gf = back_second.astype(jnp.bfloat16)
        gu = (slope * dot("rm,tmf->trf", gf, wd)).astype(jnp.bfloat16)
        grad_down = dot("rm,trf->tmf", gf, hidden)
        grad_in = dot("rd,trf->tdf", low_first, gu)
        back_normed = back_second + dot("trf,tdf->rd", gu, wi)
        back_first, grad_gain_first, grad_shift_first = norm_back(back_normed, normal_first, scale_first, gain_first)
        ga = back_first.astype(jnp.bfloat16)
        grad_out = dot("rm,tcr->tmc", ga, ot_blocks)
        got = dot("rm,tmc->tcr", ga, wo).astype(jnp.bfloat16).reshape(width, 2 * rows)
        content_out, query_out = (normed_second[s * rows:(s + 1) * rows].astype(jnp.bfloat16) for s in range(2))
        norm_stack = jnp.stack([grad_gain_first, grad_shift_first, grad_gain_second, grad_shift_second])

    def scatter(blocks):
        flat = blocks.astype(jnp.bfloat16).reshape(tp_size * width, blocks.shape[2])
        return lax.psum_scatter(flat, both_axes, scatter_dimension=0, tiled=True).astype(jnp.float32)

    if own_exchange:
        grad_second = grad_second.reshape(4, 2, 2, 2, width // 8, grad_second.shape[2])
        gqt, gkt, gvt, grad_table, sum_in, sum_down, sum_out = attend_bwd(
            tp_size, ranks, span_starts, bias_table, kp, vp, kt, qt, ot, got, lse, grad_second
        )
        grad_content, grad_query, sum_query, sum_key, sum_value, norms, grad_table = tail(
            gqt, gkt, gvt, seqt, queryt, first, back_first, norm_stack, grad_table
        )
    else:
        sum_down, sum_in, sum_out = scatter(grad_down).T, scatter(grad_in), scatter(grad_out).T
        gqt, gkt, gvt, grad_table = attend_bwd(tp_size, ranks, span_starts, bias_table, kp, vp, kt, qt, ot, got, lse)
        gq_blocks, gk_blocks, gv_blocks = (g.reshape(tp_size, narrow, g.shape[1]) for g in (gqt, gkt, gvt))
        sum_query = scatter(dot("rd,tcr->tdc", both, gq_blocks))
        sum_key = scatter(dot("rd,tcr->tdc", seq_rot, gk_blocks))
        sum_value = scatter(dot("rd,tcr->tdc", seq_rot, gv_blocks))
        back_seq = dot("tcr,tdc->rd", gk_blocks, wk) + dot("tcr,tdc->rd", gv_blocks, wv)
        back_seq = jnp.roll(back_seq.astype(jnp.bfloat16), -shift, axis=0)
        back_content = lax.psum_scatter(back_seq, "tp", scatter_dimension=0, tiled=True).astype(jnp.float32)
        back_inputs = back_first + dot("tcr,tdc->rd", gq_blocks, wq)
        grad_content, grad_query = back_inputs[:rows] + back_content, back_inputs[rows:]
        norms, grad_table = lax.psum((norm_stack, grad_table), ("fsdp", "tp"))
    return (
        content_out, query_out, grad_content, grad_query, sum_query, sum_key, sum_value, sum_out, sum_in, sum_down,
        norms[0], norms[1], norms[2], norms[3], grad_table[:, :NB],
    )


def solution(mesh):
    in_specs = (
        P(("fsdp", "tp"), None),
        P(("fsdp", "tp"), None),
        P("fsdp", "tp"),
        P("fsdp", "tp"),
        P("fsdp", "tp"),
        P("tp", "fsdp"),
        P("fsdp", "tp"),
        P("tp", "fsdp"),
        P(),
        P(),
        P(),
        P(),
        P(),
        P("fsdp", None),
        P("fsdp", None),
        P(("fsdp", "tp"), None),
        P(("fsdp", "tp"), None),
    )
    out_specs = (
        P(("fsdp", "tp"), None),
        P(("fsdp", "tp"), None),
        P(("fsdp", "tp"), None),
        P(("fsdp", "tp"), None),
        P("fsdp", "tp"),
        P("fsdp", "tp"),
        P("fsdp", "tp"),
        P("tp", "fsdp"),
        P("fsdp", "tp"),
        P("tp", "fsdp"),
        P(),
        P(),
        P(),
        P(),
        P(),
    )
    return jax.shard_map(functools.partial(local, mesh.shape["tp"], mesh.shape["tp"] == 4 and mesh.shape["fsdp"] == 8), mesh=mesh, in_specs=in_specs, out_specs=out_specs, check_vma=False)
```

```python
import functools
import jax, jax.numpy as jnp
from jax import lax
from jax.sharding import PartitionSpec as P
from jax.experimental import pallas as pl
from jax.experimental.pallas import tpu as pltpu

NEG = -1e30
PIECES = 1
HEAD = 64
NB = 32
PIC = 256
THRESHOLDS = (12, 16, 23, 32, 46, 64, 91)
EPSILON = 1e-05
LOG2E = 1.4426950408889634
LN2 = 0.6931471805599453
VLIM = 60 * 2**20
MESH = pl.DeviceIdType.MESH

def pick(index, values):
    result = jnp.int32(values[-1])
    for place in range(len(values) - 2, -1, -1):
        result = jnp.where(index == place, jnp.int32(values[place]), result)
    return result


class Place:
    def __init__(self):
        f, t = lax.axis_index("fsdp"), lax.axis_index("tp")
        self.f, self.t = f, t
        self.y, self.x, self.c = f // 4, (f // 2) % 2, f % 2
        self.core = (f + 1 - 2 * self.c, t)
        self.xn = (f + 2 - 4 * self.x, t)
        self.yn = (f + 4 - 8 * self.y, t)
        self.up, self.down = (f, t + 1), (f, t - 1)
        self.order = [pick(t, row) for row in ((3, 3, 0, 0), (2, 0, 3, 1), (1, 2, 1, 2), (0, 1, 2, 3))]

    def greet(self):
        barrier = pltpu.get_barrier_semaphore()
        for there in (self.core, self.xn, self.yn):
            pl.semaphore_signal(barrier, inc=1, device_id=there, device_id_type=MESH)
        for there in ((self.f, jnp.where(self.t > 0, self.t - 1, 3)), (self.f, jnp.where(self.t < 3, self.t + 1, 0))):
            pl.semaphore_signal(barrier, inc=1, device_id=there, device_id_type=MESH)
        pl.semaphore_wait(barrier, 5)


def rdma(src, dst, ss, rs, there):
    return pltpu.make_async_remote_copy(src_ref=src, dst_ref=dst, send_sem=ss, recv_sem=rs, device_id=there, device_id_type=MESH)


class Loads:
    def __init__(self, pairs, sems):
        self.copies = [pltpu.make_async_copy(src, dst, sems.at[i]) for i, (src, dst) in enumerate(pairs)]
        for c in self.copies:
            c.start()

    def wait(self, *which):
        for i in which:
            self.copies[i].wait()


class Scatter:
    def __init__(self, at, g, own, r0, r1a, r1b, r2a, r2b, zs, zr, sems, keep_sems):
        self.at, self.g, self.own, self.keep_sems = at, g, own, keep_sems
        self.r0, self.r1a, self.r1b, self.r2a, self.r2b, self.zs, self.zr = r0, r1a, r1b, r2a, r2b, zs, zr
        self.sems = sems
        self.wa = r1a.shape[-1]

    def sem(self, i):
        return self.sems.at[0, i], self.sems.at[1, i]

    def copy0(self, k):
        a = self.at; d = a.order[k]
        return rdma(self.g.at[d, :, :, 1 - a.c], self.r0.at[d], *self.sem(k), a.core)

    def copy1(self, k):
        a = self.at; d = a.order[k]; wa = self.wa
        return (rdma(self.r0.at[d, :, 1 - a.x, :, :wa], self.r1a.at[d], *self.sem(4 + k), a.xn),
                rdma(self.r0.at[d, 1 - a.y, :, :, wa:], self.r1b.at[d], *self.sem(8 + k), a.yn))

    def copy2(self, k):
        a = self.at; d = a.order[k]
        return (rdma(self.r1a.at[d, 1 - a.y], self.r2a.at[d], *self.sem(12 + k), a.yn),
                rdma(self.r1b.at[d, 1 - a.x], self.r2b.at[d], *self.sem(16 + k), a.xn))

    def hop(self, side, h):
        a = self.at
        return rdma(self.zs.at[side, h - 1], self.zr.at[side, h - 1], *self.sem(20 + 3 * side + h - 1), a.down if side else a.up)

    def keep(self, k):
        a = self.at; d = a.order[k]
        return pltpu.make_async_copy(self.g.at[d, :, :, a.c], self.own.at[d], self.keep_sems.at[k])

    def start(self):
        for k in range(4):
            self.copy0(k).start()
            self.keep(k).start()

    def start_one(self, k):
        self.copy0(k).start()

    def stage0(self, k):
        a = self.at; d = a.order[k]
        if self.own is None:
            own = self.g[d, :, :, a.c]
        else:
            self.keep(k).wait()
            own = self.own[d]
        self.copy0(k).wait()
        self.r0[d] = self.r0[d] + own
        for c in self.copy1(k): c.start()

    def stage1(self, k):
        a = self.at; d = a.order[k]; wa = self.wa
        for c in self.copy1(k): c.wait()
        self.r1a[d] = self.r1a[d] + self.r0[d, :, a.x, :, :wa]
        self.r1b[d] = self.r1b[d] + self.r0[d, a.y, :, :, wa:]
        for c in self.copy2(k): c.start()

    def stage2(self, k):
        a = self.at; d = a.order[k]
        for c in self.copy2(k): c.wait()
        self.r2a[d] = self.r2a[d] + self.r1a[d, a.y]
        self.r2b[d] = self.r2b[d] + self.r1b[d, a.x]

    def stage3(self, h):
        wa = self.wa
        for side in range(2):
            u = 3 - self.at.t if side else self.at.t
            d = (self.at.t + h - 4) if side else (self.at.t + 4 - h)
            if h > 1:
                @pl.when((u > 0) & (u < 3) & (u <= h - 1))
                def _():
                    self.hop(side, h - 1).wait_recv()
                    self.zs[side, h - 1, :, :wa] = self.r2a[d] + self.zr[side, h - 2, :, :wa]
                    self.zs[side, h - 1, :, wa:] = self.r2b[d] + self.zr[side, h - 2, :, wa:]
                    self.hop(side, h).start()
            @pl.when(u == 0)
            def _():
                self.zs[side, h - 1, :, :wa] = self.r2a[d]
                self.zs[side, h - 1, :, wa:] = self.r2b[d]
                self.hop(side, h).start()

    def finish(self):
        a = self.at; wa = self.wa
        for side in range(2):
            u = 3 - a.t if side else a.t
            @pl.when(u > 0)
            def _():
                self.hop(side, 3).wait_recv()
        mine = jnp.concatenate([self.r2a[a.t], self.r2b[a.t]], axis=1).astype(jnp.float32)
        below = jnp.where(a.t > 0, self.zr[0, 2].astype(jnp.float32), 0.0)
        above = jnp.where(a.t < 3, self.zr[1, 2].astype(jnp.float32), 0.0)
        for side in range(2):
            u = 3 - a.t if side else a.t
            for h in range(1, 4):
                @pl.when(u < h)
                def _():
                    self.hop(side, h).wait_send()
        return mine + below + above


class Fold:
    def __init__(self, at, part, got, sems):
        self.at, self.part, self.got, self.sems = at, part, got, sems

    def hop(self, side, h):
        a = self.at
        d = jnp.clip((a.t + h - 4) if side else (a.t + 4 - h), 0, 3)
        i = 3 * side + h - 1
        return rdma(self.part.at[d], self.got.at[side, h - 1], self.sems.at[0, i], self.sems.at[1, i], a.down if side else a.up)

    def step(self, h):
        for side in range(2):
            u = 3 - self.at.t if side else self.at.t
            d = (self.at.t + h - 4) if side else (self.at.t + 4 - h)
            @pl.when(u == 0)
            def _():
                if h > 1:
                    self.hop(side, h - 1).wait_send()
                self.hop(side, h).start()
            if h > 1:
                @pl.when((u > 0) & (u < 3) & (u <= h - 1))
                def _():
                    self.hop(side, h - 1).wait_recv()
                    self.part[d] = self.part[d] + self.got[side, h - 2]
                    self.hop(side, h).start()

    def finish(self):
        a = self.at
        for side in range(2):
            u = 3 - a.t if side else a.t
            @pl.when(u > 0)
            def _():
                self.hop(side, 3).wait_recv()
            for h in range(1, 4):
                @pl.when((u < h) & ((u > 0) | (h == 3)))
                def _():
                    self.hop(side, h).wait_send()
        below = jnp.where(a.t > 0, self.got[0, 2].astype(jnp.float32), 0.0)
        above = jnp.where(a.t < 3, self.got[1, 2].astype(jnp.float32), 0.0)
        return self.part[a.t].astype(jnp.float32) + below + above

def scatter_scratch(T, R, W, kept=True):
    wa = (W // 256) * 128
    B = jnp.bfloat16
    return [pltpu.VMEM((T, 2, 2, R, W), B)] * (2 if kept else 1) + [pltpu.VMEM((T, 2, R, wa), B), pltpu.VMEM((T, 2, R, W - wa), B),
            pltpu.VMEM((T, R, wa), B), pltpu.VMEM((T, R, W - wa), B), pltpu.VMEM((2, 3, R, W), B), pltpu.VMEM((2, 3, R, W), B),
            pltpu.SemaphoreType.DMA((2, 26))] + [pltpu.SemaphoreType.DMA((4,))] * kept

class Total:
    def __init__(self, at, sources, acc, got, sems):
        self.at, self.sources, self.acc, self.got, self.sems = at, sources, acc, got, sems
        t = at.t
        self.partners = [at.core, at.xn, at.yn, (at.f, t + 1 - 2 * (t % 2)), (at.f, 3 - t)]

    def copy(self, i):
        return rdma(self.acc.at[i], self.got.at[i], self.sems.at[0, i], self.sems.at[1, i], self.partners[i])

    def start(self):
        norms, table = self.sources
        self.acc[0] = jnp.zeros_like(self.acc[0])
        self.acc[0, :8, :] = norms[...]
        self.acc[0, 8:8 + table.shape[0], :table.shape[1]] = table[...]
        self.copy(0).start()

    def step(self, i):
        self.copy(i).wait_recv()
        self.acc[i + 1] = self.acc[i] + self.got[i]
        if i < 4:
            self.copy(i + 1).start()

    def finish(self, norms_out, table_out):
        for i in range(5):
            self.copy(i).wait_send()
        norms_out[...] = self.acc[5, :8, :]
        table_out[...] = self.acc[5, 8:8 + table_out.shape[0], :table_out.shape[1]]


def total_scratch(rows, width):
    F = jnp.float32
    return [pltpu.VMEM((6, rows, width), F), pltpu.VMEM((5, rows, width), F), pltpu.SemaphoreType.DMA((2, 5))]


def tail_kernel(gqt_in, gkt_in, gvt_in, seqt_in, queryt_in, first, back_in, norms, table,
                grad_content, grad_query, sum_query, sum_key, sum_value, norms_out, table_out,
                gqt, gkt, gvt, seqt, queryt, back, weights, part, got, g1, load_sems, fold_sems, *scratch):
    rows, width = grad_content.shape
    narrow, R = width // 4, sum_query.shape[0]
    at = Place()
    loads = Loads(
        [(gkt_in, gkt), (gvt_in, gvt)] + [(first.at[b, :, pl.ds(128, 640)], weights.at[b]) for b in range(4)]
        + [(seqt_in, seqt), (queryt_in, queryt), (gqt_in, gqt), (back_in, back)], load_sems
    )
    at.greet()
    scatter, fold, total = Scatter(at, g1, None, *scratch[:8], None), Fold(at, part, got, fold_sems), Total(at, (norms, table), *scratch[8:])
    total.start()
    loads.wait(0, 1, 2, 3, 4, 5)

    def partial(d):
        cols = pl.ds(pl.multiple_of(((d - at.t + 4) % 4) * rows, 128), rows)
        out = jnp.zeros((rows, width), jnp.float32)
        for b in range(4):
            here = slice(b * narrow, (b + 1) * narrow)
            out = out + nt(jnp.concatenate([gkt[here, cols], gvt[here, cols]], axis=0).T, weights[b, :, 256:])
        part[d] = out.astype(jnp.bfloat16)

    def weight_grads(k):
        d = at.order[k]
        here = pl.ds(pl.multiple_of(d * narrow, 64), narrow)
        query = nt(seqt[:, :rows], gqt[here, :rows]) + nt(queryt[...], gqt[here, rows:])
        block = jnp.concatenate([query, nt(seqt[...], gkt[here, :]), nt(seqt[...], gvt[here, :])], axis=1)
        g1[d] = block.astype(jnp.bfloat16).reshape(2, 2, 2, R, 3 * narrow)
        scatter.start_one(k)

    for k in range(4):
        partial(at.order[k])
        if k == 0:
            fold.step(1)
    total.step(0)
    loads.wait(6, 7, 8)
    for k in range(4):
        weight_grads(k)
        if k == 1:
            total.step(1)
    scatter.stage0(0)
    scatter.stage0(1)
    total.step(2)
    scatter.stage0(2)
    scatter.stage0(3)
    loads.wait(9)
    for s, out in enumerate((grad_content, grad_query)):
        cols = slice(s * rows, (s + 1) * rows)
        value = back[cols, :]
        for b in range(4):
            value = value + nt(gqt[b * narrow:(b + 1) * narrow, cols].T, weights[b, :, 64:256])
        out[...] = value
    fold.step(2)
    scatter.stage1(0)
    scatter.stage1(1)
    total.step(3)
    scatter.stage1(2)
    scatter.stage1(3)
    scatter.stage2(0)
    scatter.stage3(1)
    scatter.stage2(1)
    total.step(4)
    fold.step(3)
    scatter.stage3(2)
    scatter.stage2(2)
    scatter.stage2(3)
    scatter.stage3(3)
    sums = scatter.finish()
    for i, out in enumerate((sum_query, sum_key, sum_value)):
        out[...] = sums[:, i * narrow:(i + 1) * narrow]
    total.finish(norms_out, table_out)
    grad_content[...] += fold.finish()


def tail(gqt, gkt, gvt, seqt, queryt, first, back, norms, table):
    width, both = gqt.shape
    rows, narrow, R = both // 2, width // 4, width // 8
    V, A = pl.BlockSpec(memory_space=pltpu.MemorySpace.VMEM), pl.BlockSpec(memory_space=pl.ANY)
    B, F, S, DMA = jnp.bfloat16, jnp.float32, jax.ShapeDtypeStruct, pltpu.SemaphoreType.DMA
    outs = [S((rows, width), F)] * 2 + [S((R, narrow), F)] * 3 + [S(norms.shape, F), S(table.shape, F)]
    return pl.pallas_call(
        tail_kernel, out_shape=tuple(outs), in_specs=[A] * 7 + [V, V], out_specs=(V,) * 7,
        scratch_shapes=[
            pltpu.VMEM(gqt.shape, B), pltpu.VMEM(gkt.shape, B), pltpu.VMEM(gvt.shape, B), pltpu.VMEM(seqt.shape, B), pltpu.VMEM(queryt.shape, B),
            pltpu.VMEM(back.shape, F),
            pltpu.VMEM((4, width, 640), B), pltpu.VMEM((4, rows, width), B), pltpu.VMEM((2, 3, rows, width), B),
            pltpu.VMEM((4, 2, 2, 2, R, 3 * narrow), B), DMA((10,)), DMA((2, 6)),
        ] + scatter_scratch(4, R, 3 * narrow, False) + total_scratch(24, width),
        compiler_params=pltpu.CompilerParams(vmem_limit_bytes=VLIM, collective_id=1, has_side_effects=True), name="tail",
    )(gqt, gkt, gvt, seqt, queryt, first, back, norms, table)


def nn(a, b):
    return lax.dot_general(a, b, (((1,), (0,)), ((), ())), preferred_element_type=jnp.float32)
def nt(a, b):
    return lax.dot_general(a, b, (((1,), (1,)), ((), ())), preferred_element_type=jnp.float32)

def band_kind(i, b, nrow, nkey):
    rel = (b - i) % nkey
    if rel == 0: return 2
    if rel == nkey - 1: return 0 if i == 0 else 1
    if rel == 1: return 4 if i == nrow - 1 else 3
    return None

def wrap(value, size):
    return jnp.where(value >= size, value - size, value)


def bucket_of(offsets):
    magnitude = jnp.abs(offsets)
    far_bucket = 8 + sum((magnitude >= threshold).astype(jnp.int32) for threshold in THRESHOLDS)
    return jnp.where(magnitude < 8, magnitude, far_bucket) + jnp.where(offsets > 0, 16, 0)


def slot_bucket(slot, lanes, tp_index, tp_size):
    if slot >= 10:
        return jnp.full_like(lanes, 15 if slot == 10 else 31)
    kind, wrapped = slot // 2, slot % 2
    buckets = bucket_of(128 * ((-1, -1, 0, 1, 1)[kind] + wrapped) - lanes)
    if kind == 0:
        return jnp.where(tp_index == 0, 31, buckets)
    if kind == 4:
        return jnp.where(tp_index == tp_size - 1, 15, buckets)
    return buckets


def far_sides(nrow, nkey, tp_index):
    key_block = lax.broadcasted_iota(jnp.int32, (16, 2 * nrow * 128), 0)
    row_block = wrap(lax.broadcasted_iota(jnp.int32, (16, 2 * nrow * 128), 1) // 128, nrow)
    gap = key_block - row_block
    near = (gap == 0) | (gap == 1) | (gap == -1) | (gap == nkey - 1) | (gap == 1 - nkey) | (key_block >= nkey)
    key_place, row_place = wrap(key_block + nrow * tp_index, nkey), row_block + nrow * tp_index
    left = jnp.where(near, 0.0, jnp.where(key_place < row_place, 1.0, 0.0))
    return left, jnp.where(near, 0.0, 1.0 - left)


def prepare(nrow, nkey, tp_size, ranks, starts, table, mask, ring, vec, sides):
    tp_index = lax.axis_index("tp")
    rows, seq = nrow * 128, nkey * 128
    base = rows * tp_index
    rank_row = jnp.broadcast_to(ranks[...].astype(jnp.float32), (8, seq))
    ring[:, :seq] = rank_row
    ring[:, seq:] = rank_row

    def label(place):
        found = jnp.zeros(place.shape, jnp.int32)
        for k in range(starts.shape[1]):
            start = starts[0, k]
            found = found + jnp.where((place >= start) & (place < start + PIC), k + 1, 0)
        return found

    row_rank, row_label = [], []
    for i in range(nrow):
        row_rank.append(ring[0:1, pl.ds(pl.multiple_of(base + i * 128, 128), 128)])
        row_label.append(label(base + i * 128 + lax.broadcasted_iota(jnp.int32, (1, 128), 1)))

    def one(b, _):
        keys = pl.ds(pl.multiple_of(b * 128, 128), 128)
        rank_k = jnp.broadcast_to(ring[0:1, pl.ds(pl.multiple_of(base + b * 128, 128), 128)], (128, 128)).T
        kpos = b * 128 + lax.broadcasted_iota(jnp.int32, (128, 128), 0)
        label_k = label(wrap(base + kpos, seq))
        for i in range(nrow):
            rpos = i * 128 + lax.broadcasted_iota(jnp.int32, (128, 128), 1)
            same = (label_k == row_label[i]) & (label_k > 0)
            content = (rank_k <= row_rank[i]) | same
            strict = (rank_k < jnp.maximum(row_rank[i], 1.0)) | (same & (kpos != rpos))
            mask[keys, i * 128:(i + 1) * 128] = jnp.where(content, 0.0, NEG)
            mask[keys, rows + i * 128:rows + (i + 1) * 128] = jnp.where(strict, 0.0, NEG)
        return 0
    lax.fori_loop(0, nkey, one, 0)

    heads = table.shape[0]
    lanes = lax.broadcasted_iota(jnp.int32, (heads, 128), 1)
    columns = [jnp.broadcast_to(table[:, n:n + 1] * LOG2E, (heads, 128)) for n in range(NB)]
    for slot in range(12):
        buckets = slot_bucket(slot, lanes, tp_index, tp_size)
        values = columns[0]
        for n in range(1, NB):
            values = jnp.where(buckets == n, columns[n], values)
        for h in range(heads):
            vec[h, slot:slot + 1, :] = values[h:h + 1, :]
    sides[0], sides[1] = far_sides(nrow, nkey, tp_index)


def far_bias(vec, sides, cf, h):
    copies = cf.shape[1] // 128
    left, right = (jnp.concatenate([vec[h, slot:slot + 1, :]] * copies, axis=1) for slot in (10, 11))
    cf[...] = sides[0] * left + sides[1] * right


def prepare_scratch(nrow, nkey, heads):
    F, rows = jnp.float32, 2 * nrow * 128
    return [
        pltpu.VMEM((nkey * 128, rows), F), pltpu.VMEM((8, 2 * nkey * 128), F), pltpu.VMEM((heads, 12, 128), F),
        pltpu.VMEM((2, 16, rows), F), pltpu.VMEM((16, rows), F), pltpu.VMEM((5, 128, 128), F),
    ]


def band_tiles(band, vec, h):
    lane = lax.broadcasted_iota(jnp.int32, (128, 128), 1)
    sub = lax.broadcasted_iota(jnp.int32, (128, 128), 0)
    for k in range(5):
        direct, wrapped = (
            pltpu.roll(jnp.broadcast_to(vec[h, 2 * k + w:2 * k + w + 1, :], (128, 128)), 0, 1, stride=1, stride_axis=0)
            for w in range(2)
        )
        band[k] = jnp.where(lane >= sub, direct, wrapped)

def diagonal_sums(tile):
    lane = lax.broadcasted_iota(jnp.int32, (8, 128), 1)
    sub = lax.broadcasted_iota(jnp.int32, (8, 128), 0)
    direct = wrapped = jnp.zeros((8, 128), jnp.float32)
    for a in range(16):
        rows = tile[8 * a:8 * a + 8, :]
        kept = jnp.where(lane >= sub + 8 * a, rows, 0.0)
        left = rows - kept
        if a:
            kept, left = pltpu.roll(kept, 128 - 8 * a, 1), pltpu.roll(left, 128 - 8 * a, 1)
        direct, wrapped = direct + kept, wrapped + left
    for bit in (1, 2, 4):
        moved = (sub & bit) != 0
        direct = jnp.where(moved, pltpu.roll(direct, 128 - bit, 1), direct)
        wrapped = jnp.where(moved, pltpu.roll(wrapped, 128 - bit, 1), wrapped)
    return jnp.sum(direct, axis=0, keepdims=True), jnp.sum(wrapped, axis=0, keepdims=True)

def head_rows(ref, p, hh, cols):
    z = jnp.zeros((64, cols.stop - cols.start), jnp.bfloat16)
    rows = ref[pl.ds(pl.multiple_of((2 * p + hh) * 64, 64), 64), cols]
    return jnp.concatenate([rows, z] if hh == 0 else [z, rows], axis=0)

def attend_rows(nrow, nkey, kp, vt, qt, ot, lse, t, prepared, exchange):
    mask, _, vec, sides, cf, band = prepared
    ones = jnp.ones((16, 256), jnp.bfloat16)
    nchunk = 2 * nrow * 128 // 256
    def pair(p, _):
        for hh in range(2):
            h = 2 * p + hh
            exchange(h)
            hrows = pl.ds(pl.multiple_of(h * 64, 64), 64)
            band_tiles(band, vec, h)
            far_bias(vec, sides, cf, h)
            for c in range(nchunk):
                cols = slice(c * 256, (c + 1) * 256)
                qh = head_rows(qt, p, hh, cols)
                m8 = jnp.full((8, 256), -jnp.inf, jnp.float32)
                for b in range(nkey):
                    s = nn(kp[p, b * 128:(b + 1) * 128, :], qh)
                    s = s + mask[b * 128:(b + 1) * 128, cols]
                    kinds = [band_kind((2 * c + k) % nrow, b, nrow, nkey) for k in range(2)]
                    if any(k is not None for k in kinds):
                        s = jnp.concatenate([s[:, k * 128:(k + 1) * 128] + (band[kinds[k]] if kinds[k] is not None else 0.0) for k in range(2)], axis=1)
                    t[c, b * 128:(b + 1) * 128, :] = s
                    m8 = jnp.maximum(m8, jnp.max(s.reshape(16, 8, 256), axis=0) + cf[b:b + 1, cols])
                m = jnp.max(m8, axis=0, keepdims=True)
                acc = jnp.zeros((80, 256), jnp.float32)
                for g in range(nkey // 2):
                    ps = []
                    for b in (2 * g, 2 * g + 1):
                        ps.append(jnp.exp2(t[c, b * 128:(b + 1) * 128, :] - (m - cf[b:b + 1, cols])).astype(jnp.bfloat16))
                    lhs = jnp.concatenate([vt[hrows, g * 256:(g + 1) * 256], ones], axis=0)
                    acc = acc + nn(lhs, jnp.concatenate(ps, axis=0))
                l = acc[64:65, :]
                ot[hrows, cols] = (acc[:64, :] / l).astype(jnp.bfloat16)
                lse[h, 0:1, cols] = m + jnp.log2(l)
        return 0
    lax.fori_loop(0, kp.shape[0], pair, 0)

def fwd_kernel(nrow, nkey, tp_size, ranks, starts, table, kp, vt, qt, ot, lse, t, *prepared):
    prepare(nrow, nkey, tp_size, ranks, starts, table, *prepared[:4])
    attend_rows(nrow, nkey, kp, vt, qt, ot, lse, t, prepared, lambda h: None)


def attend_fwd(tp_size, ranks, starts, table, kp, vt, qt):
    pairs, seq, _ = kp.shape
    rows = qt.shape[1]
    nrow, nkey = rows // 256, seq // 128
    V, M = pl.BlockSpec(memory_space=pltpu.MemorySpace.VMEM), pl.BlockSpec(memory_space=pltpu.MemorySpace.SMEM)
    return pl.pallas_call(
        functools.partial(fwd_kernel, nrow, nkey, tp_size),
        out_shape=(jax.ShapeDtypeStruct(qt.shape, jnp.bfloat16), jax.ShapeDtypeStruct((2 * pairs, 1, rows), jnp.float32)),
        in_specs=[V, M, V, V, V, V], out_specs=(V, V),
        scratch_shapes=[pltpu.VMEM((rows // 256, seq, 256), jnp.float32)] + prepare_scratch(nrow, nkey, 2 * pairs),
        compiler_params=pltpu.CompilerParams(vmem_limit_bytes=VLIM),
        name="attend_fwd",
    )(ranks, starts, table, kp, vt, qt)


class Gather:
    def __init__(self, at, shard, g, wa, sems, own_sem):
        self.at, self.shard, self.g, self.wa, self.sems, self.own_sem = at, shard, g, wa, sems, own_sem
        self.blocks = at.order[::-1]

    def send(self, i, src, dst, there):
        return rdma(src, dst, self.sems.at[0, i], self.sems.at[1, i], there)

    def along_z(self, b, upward):
        a = self.at
        here = self.g.at[b, a.y, a.x, a.c]
        return self.send(b + (0 if upward else 4), here, here, a.up if upward else a.down)

    def first(self, b):
        a, wa = self.at, self.wa
        left, right = (self.g.at[b, a.y, a.x, a.c, :, cols] for cols in (slice(0, wa), slice(wa, None)))
        return self.send(8 + b, left, left, a.xn), self.send(12 + b, right, right, a.yn)

    def second(self, b):
        a, wa = self.at, self.wa
        left, right = self.g.at[b, a.y, :, a.c, :, :wa], self.g.at[b, :, a.x, a.c, :, wa:]
        return self.send(16 + b, left, left, a.yn), self.send(20 + b, right, right, a.xn)

    def across(self, b):
        a = self.at
        here = self.g.at[b, :, :, a.c]
        return self.send(24 + b, here, here, a.core)

    def own(self):
        a = self.at
        return pltpu.make_async_copy(self.shard, self.g.at[a.t, a.y, a.x, a.c], self.own_sem)

    def begin(self):
        self.own().start()
        self.own().wait()
        for c in self.first(self.at.t):
            c.start()

    def begin_z(self):
        a = self.at
        @pl.when(a.t < 3)
        def _():
            self.along_z(a.t, True).start()
        @pl.when(a.t > 0)
        def _():
            self.along_z(a.t, False).start()

    def arrive(self, j):
        a, b = self.at, self.blocks[j]
        @pl.when(b < a.t)
        def _():
            self.along_z(b, True).wait_recv()
        @pl.when(b > a.t)
        def _():
            self.along_z(b, False).wait_recv()
        @pl.when((b < a.t) & (a.t < 3))
        def _():
            self.along_z(b, True).start()
        @pl.when((b > a.t) & (a.t > 0))
        def _():
            self.along_z(b, False).start()
        for c in self.first(b):
            c.start()

    def step1(self, j):
        b = self.blocks[j]
        for c in self.first(b):
            c.wait_recv()
        for c in self.second(b):
            c.start()

    def step2(self, j):
        b = self.blocks[j]
        for c in self.second(b):
            c.wait_recv()
        self.across(b).start()

    def step3(self, j):
        self.across(self.blocks[j]).wait_recv()

    def finish(self):
        a = self.at
        for b in range(4):
            @pl.when((b <= a.t) & (a.t < 3))
            def _():
                self.along_z(b, True).wait_send()
            @pl.when((b >= a.t) & (a.t > 0))
            def _():
                self.along_z(b, False).wait_send()
            for c in (*self.first(b), *self.second(b), self.across(b)):
                c.wait_send()


class Chain:
    def __init__(self, at, seq, sems, pieces):
        self.at, self.seq, self.sems, self.pieces = at, seq, sems, pieces
        self.blocks = at.order[::-1]

    def move(self, b, upward, s):
        a = self.at
        i = (b + (0 if upward else 4)) * self.pieces + s
        there = a.t + 1 if upward else a.t - 1
        size = self.seq.shape[1] // self.pieces
        part = slice(s * size, (s + 1) * size)
        return rdma(self.seq.at[(b - a.t + 4) % 4, part], self.seq.at[(b - there + 4) % 4, part], self.sems.at[0, i], self.sems.at[1, i], (a.f, there))

    def begin(self):
        a = self.at
        for s in range(self.pieces):
            @pl.when(a.t < 3)
            def _():
                self.move(a.t, True, s).start()
            @pl.when(a.t > 0)
            def _():
                self.move(a.t, False, s).start()

    def arrive(self, j):
        a, b = self.at, self.blocks[j]
        for s in range(self.pieces):
            @pl.when(b < a.t)
            def _():
                self.move(b, True, s).wait_recv()
            @pl.when(b > a.t)
            def _():
                self.move(b, False, s).wait_recv()
            @pl.when((b < a.t) & (a.t < 3))
            def _():
                self.move(b, True, s).start()
            @pl.when((b > a.t) & (a.t > 0))
            def _():
                self.move(b, False, s).start()

    def finish(self):
        a = self.at
        for b in range(4):
            for s in range(self.pieces):
                @pl.when((b <= a.t) & (a.t < 3))
                def _():
                    self.move(b, True, s).wait_send()
                @pl.when((b >= a.t) & (a.t > 0))
                def _():
                    self.move(b, False, s).wait_send()


def front_kernel(nrow, nkey, content, query, w_query, w_key, w_value, w_out, w_in, w_down, ranks, starts, table,
                 ot, lse, seqt_out, queryt_out, kp_out, vp_out, kt_out, qt_out, w1_out, w2_out,
                 shard1, shard2, seq, seqt, queryt, w1, w2, w1t, kp, vp, kt, vt, qt, t,
                 sems1, sems2, semsc, own_sems, out_sems, *prepared):
    at = Place()
    rows = nrow * 128
    pairs = kp.shape[0]
    narrow = shard1.shape[1] // 4
    width = content.shape[1]
    weights1 = Gather(at, shard1, w1, shard1.shape[1] // 2, sems1, own_sems.at[0])
    weights2 = Gather(at, shard2, w2, shard2.shape[1] // 2, sems2, own_sems.at[1])
    chain = Chain(at, seq, semsc, PIECES)
    shard1[...] = jnp.concatenate([w_out[...].T, w_query[...], w_key[...], w_value[...]], axis=1)
    shard2[:, :w_in.shape[1]] = w_in[...]
    shard2[:, w_in.shape[1]:] = w_down[...]
    seq[0] = content[...]
    at.greet()
    weights1.begin()
    weights1.begin_z()
    weights1.arrive(1)
    weights1.step1(0)
    weights1.arrive(2)
    weights1.step1(1)
    weights1.step2(0)
    weights1.arrive(3)
    chain.begin()
    weights2.begin()
    weights2.begin_z()
    weights1.step1(2)
    weights1.step2(1)
    weights1.step1(3)
    prepare(nrow, nkey, 4, ranks, starts, table, *prepared[:4])
    weights1.step2(2)
    weights1.step2(3)
    for j in range(4):
        weights1.step3(j)

    scale = HEAD ** -0.5 * LOG2E
    for tt in range(4):
        block = w1[tt].reshape(width, 4 * narrow)
        w1t[tt] = block[:, narrow:].T
        for s, x in enumerate((content, query)):
            q = nt(w1t[tt, :narrow, :], x[...])
            qt[tt * narrow:(tt + 1) * narrow, s * rows:(s + 1) * rows] = (q * scale).astype(jnp.bfloat16)

    def project(r):
        x = seq[r]
        cols = pl.ds(pl.multiple_of(r * rows, 128), rows)
        seqt[:, cols] = x.T
        for i, (across, upright) in enumerate(((kp, kt), (vp, vt))):
            for tt in range(4):
                out = nt(w1t[tt, (i + 1) * narrow:(i + 2) * narrow, :], x)
                upright[tt * narrow:(tt + 1) * narrow, cols] = out.astype(jnp.bfloat16)
            for u in range(2):
                halves = [
                    nn(x, w1[2 * u + v].reshape(width, 4 * narrow)[:, (i + 2) * narrow:(i + 3) * narrow]) for v in range(2)
                ]
                joined = jnp.concatenate(halves, axis=1).astype(jnp.bfloat16)
                for p in range(pairs // 2):
                    across[u * (pairs // 2) + p, cols, :] = joined[:, p * 128:(p + 1) * 128]

    queryt[...] = query[...].T
    project(0)
    chain.arrive(1)
    weights2.arrive(1)
    weights2.step1(0)
    project((chain.blocks[1] - at.t + 4) % 4)
    chain.arrive(2)
    weights2.step2(0)
    weights2.step1(1)
    weights2.arrive(2)
    project((chain.blocks[2] - at.t + 4) % 4)
    chain.arrive(3)
    weights2.step2(1)
    weights2.step1(2)
    project((chain.blocks[3] - at.t + 4) % 4)

    outs = [
        pltpu.make_async_copy(src, dst, out_sems.at[i])
        for i, (src, dst) in enumerate(((seqt, seqt_out), (queryt, queryt_out), (kp, kp_out), (vp, vp_out), (kt, kt_out), (qt, qt_out), (w1, w1_out)))
    ]
    for c in outs:
        c.start()

    def second_out(j):
        b = weights2.blocks[j]
        return pltpu.make_async_copy(w2.at[b], w2_out.at[b], out_sems.at[7 + j])

    def exchange(h):
        steps = (
            (weights2.arrive, 3, 0),
            (weights2.step2, 2, 1),
            (weights2.step1, 3, 4),
        )
        for step, j, place in steps:
            @pl.when(h == place)
            def _():
                step(j)

    attend_rows(nrow, nkey, kp, vt, qt, ot, lse, t, prepared, exchange)
    weights2.step2(3)
    for j in range(4):
        weights2.step3(j)
        second_out(j).start()
    for c in outs:
        c.wait()
    for j in range(4):
        second_out(j).wait()
    weights1.finish()
    weights2.finish()
    chain.finish()


def front(content, query, w_query, w_key, w_value, w_out, w_in, w_down, ranks, starts, table):
    rows, width = content.shape
    heads, seq_len = table.shape[0], ranks.shape[1]
    pairs, (R, narrow), wide = heads // 2, w_query.shape, w_in.shape[1]
    nrow, nkey = rows // 128, seq_len // 128
    V, A = pl.BlockSpec(memory_space=pltpu.MemorySpace.VMEM), pl.BlockSpec(memory_space=pl.ANY)
    B, F, S, DMA = jnp.bfloat16, jnp.float32, jax.ShapeDtypeStruct, pltpu.SemaphoreType.DMA
    full1, full2 = (4, 2, 2, 2, R, 4 * narrow), (4, 2, 2, 2, R, 2 * wide)
    kept = [((width, seq_len), B), ((width, rows), B), ((pairs, seq_len, 128), B), ((pairs, seq_len, 128), B), ((width, seq_len), B), ((width, 2 * rows), B), (full1, B)]
    outs = [S((width, 2 * rows), B), S((heads, 1, 2 * rows), F)] + [S(*k) for k in kept] + [S(full2, B)]
    scratch = [pltpu.VMEM((R, 4 * narrow), B), pltpu.VMEM((R, 2 * wide), B), pltpu.VMEM((4, rows, width), B), pltpu.VMEM(*kept[0]), pltpu.VMEM(*kept[1]), pltpu.VMEM(full1, B), pltpu.VMEM(full2, B),
               pltpu.VMEM((4, 3 * narrow, width), B), pltpu.VMEM(*kept[2]), pltpu.VMEM(*kept[3]),
               pltpu.VMEM(*kept[4]), pltpu.VMEM(*kept[4]), pltpu.VMEM(*kept[5]),
               pltpu.VMEM((2 * rows // 256, seq_len, 256), F),
               DMA((2, 28)), DMA((2, 28)), DMA((2, 8 * PIECES)), DMA((2,)), DMA((11,))] + prepare_scratch(nrow, nkey, heads)
    return pl.pallas_call(
        functools.partial(front_kernel, nrow, nkey),
        out_shape=tuple(outs), in_specs=[V] * 9 + [pl.BlockSpec(memory_space=pltpu.MemorySpace.SMEM), V], out_specs=tuple([V, V] + [A] * 8), scratch_shapes=scratch,
        compiler_params=pltpu.CompilerParams(vmem_limit_bytes=VLIM, collective_id=3, has_side_effects=True), name="front",
    )(content, query, w_query, w_key, w_value, w_out, w_in, w_down, ranks, starts, table)


def bwd_kernel(nrow, nkey, tp_size, fused, *refs):
    if fused:
        ranks, starts, table, kp, vp, kt, qt, ot, got, lse, g, gqt, gkt, gvt, back_table, sum_in, sum_down, sum_out, gq, bacc, diag, *scratch = refs
        prepared, kept, load_sems, scratch = scratch[:6], scratch[6:12], scratch[12], scratch[13:]
        loads = Loads(list(zip((kp, vp, kt, qt, ot, got), kept)), load_sems)
        kp, vp, kt, qt, ot, got = kept
        at = Place()
        at.greet()
        scatter = Scatter(at, g, *scratch)
        scatter.start()
    else:
        ranks, starts, table, kp, vp, kt, qt, ot, got, lse, gqt, gkt, gvt, back_table, gq, bacc, diag, *prepared = refs
    mask, _, vec, sides, cf, band = prepared
    prepare(nrow, nkey, tp_size, ranks, starts, table, *prepared[:4])
    lane_row = lax.broadcasted_iota(jnp.int32, (1, 128), 1)
    if fused:
        loads.wait(0, 1, 2, 3, 4, 5)

    def exchange(h):
        if not fused:
            return
        steps = (
            (scatter.stage0, 0, 0), (scatter.stage0, 1, 1), (scatter.stage1, 0, 3), (scatter.stage0, 2, 3), (scatter.stage2, 0, 6), (scatter.stage3, 1, 6),
            (scatter.stage1, 1, 6), (scatter.stage0, 3, 6), (scatter.stage1, 2, 8), (scatter.stage2, 1, 9), (scatter.stage3, 2, 9), (scatter.stage1, 3, 11),
        )
        for step, k, place in steps:
            @pl.when(h == place)
            def _():
                step(k)

    rows = 2 * nrow * 128
    nchunk = rows // 256
    full = slice(0, rows)
    block_of = lax.broadcasted_iota(jnp.int32, (16, 256), 0)
    half_of = lax.broadcasted_iota(jnp.int32, (16, 256), 1) // 128
    def pair(p, _):
        for hh in range(2):
            h = 2 * p + hh
            exchange(h)
            hrows = pl.ds(pl.multiple_of(h * 64, 64), 64)
            band_tiles(band, vec, h)
            far_bias(vec, sides, cf, h)
            q_h = qt[hrows, :]
            go_h = got[hrows, :]
            delta = jnp.sum(ot[hrows, :].astype(jnp.float32) * go_h.astype(jnp.float32), axis=0, keepdims=True)
            for k in range(5):
                bacc[k] = jnp.zeros((128, 128), jnp.float32)
            gq[...] = jnp.zeros_like(gq)
            qm = head_rows(qt, p, hh, full)
            gm = head_rows(got, p, hh, full)
            for g in range(nkey // 2):
                pp, gg = [], []
                for c in range(nchunk):
                    cols = slice(c * 256, (c + 1) * 256)
                    pc, gc = [], []
                    for b in (2 * g, 2 * g + 1):
                        keys = slice(b * 128, (b + 1) * 128)
                        s = nn(kp[p, keys, :], qm[:, cols])
                        dp = nn(vp[p, keys, :], gm[:, cols])
                        s = s + mask[keys, cols]
                        kinds = [band_kind((2 * c + k) % nrow, b, nrow, nkey) for k in range(2)]
                        if any(k is not None for k in kinds):
                            s = jnp.concatenate([s[:, k * 128:(k + 1) * 128] + (band[kinds[k]] if kinds[k] is not None else 0.0) for k in range(2)], axis=1)
                        pr = jnp.exp2(s - (lse[h, 0:1, cols] - cf[b:b + 1, cols]))
                        gs = pr * (dp - delta[:, cols])
                        for k in range(2):
                            if kinds[k] is not None:
                                bacc[kinds[k]] += gs[:, k * 128:(k + 1) * 128]
                        pc.append(pr.astype(jnp.bfloat16))
                        gc.append(gs.astype(jnp.bfloat16))
                    pp.append(jnp.concatenate(pc, axis=0))
                    gg.append(jnp.concatenate(gc, axis=0))
                pall = jnp.concatenate(pp, axis=1)
                gall = jnp.concatenate(gg, axis=1)
                keys = slice(g * 256, (g + 1) * 256)
                onehot = (block_of == 2 * g + half_of).astype(jnp.bfloat16)
                gq[...] += nn(jnp.concatenate([kt[hrows, keys], onehot], axis=0), gall)
                gkt[hrows, keys] = (nt(q_h, gall) * LN2).astype(jnp.bfloat16)
                gvt[hrows, keys] = nt(go_h, pall).astype(jnp.bfloat16)
            gqt[hrows, :] = (gq[:64, :] * 0.125).astype(jnp.bfloat16)
            for k in range(5):
                direct, wrapped = diagonal_sums(bacc[k])
                diag[h, 0:1, 256 * k:256 * k + 128] = direct
                diag[h, 0:1, 256 * k + 128:256 * k + 256] = wrapped
            for s in range(2):
                side = jnp.sum(jnp.sum(gq[64:80, :] * sides[s], axis=0, keepdims=True), axis=1, keepdims=True)
                diag[h, 0:1, 1280 + 128 * s:1408 + 128 * s] = jnp.where(lane_row == 0, side, 0.0)
        return 0
    lax.fori_loop(0, kp.shape[0], pair, 0)
    tp_index = lax.axis_index("tp")
    places = lax.broadcasted_iota(jnp.int32, (128, 128), 0)
    numbers = lax.broadcasted_iota(jnp.int32, (128, 128), 1)
    sums = jnp.concatenate([diag[h] for h in range(diag.shape[0])], axis=0)
    total = jnp.zeros((diag.shape[0], 128), jnp.float32)
    for slot in range(12):
        one_hot = jnp.where(slot_bucket(slot, places, tp_index, tp_size) == numbers, 1.0, 0.0)
        total = total + jnp.dot(
            sums[:, slot * 128:(slot + 1) * 128], one_hot, precision=lax.Precision.HIGHEST, preferred_element_type=jnp.float32
        )
    back_table[...] = total
    if fused:
        scatter.stage2(2)
        scatter.stage3(3)
        scatter.stage2(3)
        sums = scatter.finish()
        wide = sum_in.shape[1]
        sum_in[...] = sums[:, :wide]
        sum_down[...] = sums[:, wide:2 * wide]
        sum_out[...] = sums[:, 2 * wide:].T


def attend_bwd(tp_size, ranks, starts, table, kp, vp, kt, qt, ot, got, lse, g=None):
    pairs, seq, _ = kp.shape
    rows = qt.shape[1]
    heads = 2 * pairs
    nrow, nkey = rows // 256, seq // 128
    V, M = pl.BlockSpec(memory_space=pltpu.MemorySpace.VMEM), pl.BlockSpec(memory_space=pltpu.MemorySpace.SMEM)
    S, F = jax.ShapeDtypeStruct, jnp.float32
    fused = g is not None
    outs = [S(qt.shape, jnp.bfloat16), S(kt.shape, jnp.bfloat16), S(kt.shape, jnp.bfloat16), S((heads, 128), F)]
    scratch = [pltpu.VMEM((80, rows), F), pltpu.VMEM((5, 128, 128), F), pltpu.VMEM((heads, 1, 1536), F)] + prepare_scratch(nrow, nkey, heads)
    params = dict(vmem_limit_bytes=VLIM)
    args = (ranks, starts, table, kp, vp, kt, qt, ot, got, lse)
    specs = [V, M] + [V] * 8
    if fused:
        narrow = kt.shape[0] // 4
        wide = (g.shape[5] - narrow) // 2
        outs += [S((g.shape[4], wide), F), S((g.shape[4], wide), F), S((narrow, g.shape[4]), F)]
        scratch += [pltpu.VMEM(a.shape, a.dtype) for a in (kp, vp, kt, qt, ot, got)] + [pltpu.SemaphoreType.DMA((6,))]
        scratch += scatter_scratch(g.shape[0], g.shape[4], g.shape[5])
        params.update(collective_id=2, has_side_effects=True)
        args += (g,)
        A = pl.BlockSpec(memory_space=pl.ANY)
        specs = specs[:3] + [A] * 6 + [V, A]
    return pl.pallas_call(
        functools.partial(bwd_kernel, nrow, nkey, tp_size, fused),
        out_shape=tuple(outs), in_specs=specs, out_specs=(V,) * len(outs), scratch_shapes=scratch,
        compiler_params=pltpu.CompilerParams(**params), name="attend_bwd",
    )(*args)


def norm(residual):
    centered = residual - jnp.mean(residual, axis=-1, keepdims=True)
    scale = lax.rsqrt(jnp.mean(centered * centered, axis=-1, keepdims=True) + EPSILON)
    return centered * scale, scale


def norm_step(cotangent, normal, scale, gain):
    inner = cotangent * gain
    mean_inner = jnp.mean(inner, axis=-1, keepdims=True)
    mean_cross = jnp.mean(inner * normal, axis=-1, keepdims=True)
    return scale * (inner - mean_inner - normal * mean_cross)


def middle_kernel(chunk, ot_in, content, query, first, second_in, gain1, shift1, gain2, shift2, ranks, up_content, up_query,
                  content_out, query_out, grads, back, got, sums,
                  ot, second, x, up, wot, wo_block, onat, n1bt, gft, gat, hidden, slope, gu, out2, stage, sems, out_sems):
    rows = content.shape[0]
    seq, width = ranks.shape[1], content.shape[1]
    narrow, wide = width // 4, second.shape[2] // 2
    loads = Loads(
        [(first.at[t, :, pl.ds(0, 256)], wo_block.at[t]) for t in range(4)] + [(ot_in, ot)]
        + [(second_in.at[t], second.at[t]) for t in range(4)], sems
    )
    base = rows * lax.axis_index("tp")
    x[:rows] = content[...]
    x[rows:] = query[...]
    up[:rows] = up_content[...].astype(jnp.float32)
    for i in range(rows // 128):
        rank = ranks[0:1, pl.ds(pl.multiple_of(base + i * 128, 128), 128)].astype(jnp.float32)
        rank = jnp.broadcast_to(rank, (128, 128)).T
        kept = jnp.where(rank >= seq - seq * 15 // 100, 1.0, 0.0)
        up[rows + i * 128:rows + (i + 1) * 128, :] = up_query[i * 128:(i + 1) * 128, :].astype(jnp.float32) * jnp.concatenate([kept] * (width // 128), axis=1)
    loads.wait(0, 1, 2, 3, 4)
    wot[...] = jnp.concatenate([wo_block[t, :, :narrow] for t in range(4)], axis=1)
    sums[...] = jnp.zeros_like(sums)
    gain1, shift1, gain2, shift2 = (ref[...].reshape(1, width) for ref in (gain1, shift1, gain2, shift2))

    def one(i, _):
        here = pl.ds(pl.multiple_of(i * chunk, chunk), chunk)
        mixed = ot[:, here].T
        onat[here, :] = mixed
        normal1, scale1 = norm(x[here, :].astype(jnp.float32) + nt(mixed, wot[...]))
        normed = normal1 * gain1 + shift1
        low = normed.astype(jnp.bfloat16)
        n1bt[:, here] = low.T
        total = normed
        for t in range(4):
            @pl.when(i == 0)
            def _():
                loads.wait(5 + t)
            lifted = nn(low, second[t, :, :wide])
            phi = 0.5 + 0.5 * lax.erf(lifted * (0.5 ** 0.5))
            act = (lifted * phi).astype(jnp.bfloat16)
            hidden[t, here, :] = act
            slope[t] = phi + lifted * (jnp.exp(-0.5 * lifted * lifted) * 0.3989422804014327)
            total = total + nt(act, second[t, :, wide:])
        normal2, scale2 = norm(total)
        out2[here, :] = (normal2 * gain2 + shift2).astype(jnp.bfloat16)
        cotangent = up[here, :]
        sums[2:3, :] += jnp.sum(cotangent * normal2, axis=0, keepdims=True)
        sums[3:4, :] += jnp.sum(cotangent, axis=0, keepdims=True)
        back2 = norm_step(cotangent, normal2, scale2, gain2)
        gf = back2.astype(jnp.bfloat16)
        gft[:, here] = gf.T
        total = back2
        for t in range(4):
            g = (slope[t] * nn(gf, second[t, :, wide:])).astype(jnp.bfloat16)
            gu[t, here, :] = g
            total = total + nt(g, second[t, :, :wide])
        sums[0:1, :] += jnp.sum(total * normal1, axis=0, keepdims=True)
        sums[1:2, :] += jnp.sum(total, axis=0, keepdims=True)
        back1 = norm_step(total, normal1, scale1, gain1)
        back[here, :] = back1
        ga = back1.astype(jnp.bfloat16)
        gat[:, here] = ga.T
        got[:, here] = nn(ga, wot[...]).astype(jnp.bfloat16).T
        return 0

    lax.fori_loop(0, 2 * rows // chunk, one, 0)
    content_out[...] = out2[:rows]
    query_out[...] = out2[rows:]
    for t in range(4):
        wo_block[t, :, :narrow] = nn(gat[...], onat[:, t * narrow:(t + 1) * narrow]).astype(jnp.bfloat16)

    def send(t):
        return pltpu.make_async_copy(stage.at[t % 2], grads.at[t], out_sems.at[t % 2])

    for t in range(4):
        if t >= 2:
            send(t - 2).wait()
        stage[t % 2, :, :wide] = nn(n1bt[...], gu[t]).astype(jnp.bfloat16)
        stage[t % 2, :, wide:2 * wide] = nn(gft[...], hidden[t]).astype(jnp.bfloat16)
        stage[t % 2, :, 2 * wide:] = wo_block[t, :, :narrow]
        send(t).start()
    for t in (2, 3):
        send(t).wait()


def middle(ot, content, query, first, second, norms, ranks, up_content, up_query):
    rows, width = content.shape
    narrow, wide = width // 4, second.shape[2] // 2
    both, chunk = 2 * rows, 256
    V, A = pl.BlockSpec(memory_space=pltpu.MemorySpace.VMEM), pl.BlockSpec(memory_space=pl.ANY)
    B, F, S, DMA = jnp.bfloat16, jnp.float32, jax.ShapeDtypeStruct, pltpu.SemaphoreType.DMA
    return pl.pallas_call(
        functools.partial(middle_kernel, chunk),
        out_shape=(S((rows, width), B), S((rows, width), B), S((4, width, 2 * wide + narrow), B), S((both, width), F), S((width, both), B), S((8, width), F)),
        in_specs=[A, V, V, A, A] + [V] * 7, out_specs=(V, V, A, V, V, V),
        scratch_shapes=[
            pltpu.VMEM(ot.shape, B), pltpu.VMEM(second.shape, B),
            pltpu.VMEM((both, width), B), pltpu.VMEM((both, width), F), pltpu.VMEM((width, width), B), pltpu.VMEM((4, width, 256), B),
            pltpu.VMEM((both, width), B), pltpu.VMEM((width, both), B), pltpu.VMEM((width, both), B), pltpu.VMEM((width, both), B),
            pltpu.VMEM((4, both, wide), B), pltpu.VMEM((4, chunk, wide), F), pltpu.VMEM((4, both, wide), B), pltpu.VMEM((both, width), B),
            pltpu.VMEM((2, width, 2 * wide + narrow), B), DMA((9,)), DMA((2,)),
        ],
        compiler_params=pltpu.CompilerParams(vmem_limit_bytes=VLIM), name="middle",
    )(ot, content, query, first, second, *norms, ranks, up_content, up_query)


def finish_kernel(count, *refs):
    sources, norms, outs, sems = refs[:count], refs[count], refs[count + 1:], refs[-1]
    copies = [pltpu.make_async_copy(src, dst, sems.at[i]) for i, (src, dst) in enumerate(zip(sources, outs))]
    for c in copies:
        c.start()
    for i in range(4):
        outs[count + i][...] = norms[i:i + 1, :].reshape(norms.shape[1])
    for c in copies:
        c.wait()


def finish(arrays, norms):
    V, A, S = pl.BlockSpec(memory_space=pltpu.MemorySpace.VMEM), pl.BlockSpec(memory_space=pl.ANY), jax.ShapeDtypeStruct
    count = len(arrays)
    return pl.pallas_call(
        functools.partial(finish_kernel, count),
        out_shape=tuple(S(a.shape, a.dtype) for a in arrays) + tuple(S((norms.shape[1],), norms.dtype) for _ in range(4)),
        in_specs=[A] * count + [V], out_specs=(A,) * count + (V,) * 4, scratch_shapes=[pltpu.SemaphoreType.DMA((count,))],
        compiler_params=pltpu.CompilerParams(vmem_limit_bytes=VLIM), name="finish",
    )(*arrays, norms)


def dot(spec, a, b):
    return jnp.einsum(spec, a, b, preferred_element_type=jnp.float32)


def norm_stats(residual):
    centered = residual - jnp.mean(residual, axis=-1, keepdims=True)
    scale = lax.rsqrt(jnp.mean(centered * centered, axis=-1, keepdims=True) + EPSILON)
    return centered * scale, scale


def norm_back(cotangent, normal, scale, gain):
    inner = cotangent * gain
    mean_inner = jnp.mean(inner, axis=-1, keepdims=True)
    mean_cross = jnp.mean(inner * normal, axis=-1, keepdims=True)
    back = scale * (inner - mean_inner - normal * mean_cross)
    return back, jnp.sum(cotangent * normal, axis=0), jnp.sum(cotangent, axis=0)


def local(
    tp_size, own_exchange, content, query, w_query, w_key, w_value, w_out, w_in, w_down, gain_first, shift_first,
    gain_second, shift_second, bias_table, ranks, span_starts, upstream_content, upstream_query,
):
    rows, width = content.shape
    seq = ranks.shape[1]
    heads = bias_table.shape[0]
    pairs = heads // 2
    tp_index = lax.axis_index("tp")
    both_axes = ("tp", "fsdp")
    narrow = w_query.shape[1]

    def gather(parts):
        shard = jnp.concatenate(parts, axis=1)
        return lax.all_gather(shard, both_axes, axis=0, tiled=True).reshape(tp_size, width, shard.shape[1])

    wide = w_in.shape[1]
    shift = -rows * tp_index
    both = jnp.concatenate([content, query], axis=0)
    if own_exchange:
        ot, lse, seqt, queryt, kp, vp, kt, qt, first, second = front(
            content, query, w_query, w_key, w_value, w_out, w_in, w_down.T, ranks, span_starts, bias_table
        )
        first, second = first.reshape(tp_size, width, 4 * narrow), second.reshape(tp_size, width, 2 * wide)
    else:
        first, second = gather([w_out.T, w_query, w_key, w_value]), gather([w_in, w_down.T])
    wo, wq, wk, wv = (first[:, :, i * narrow:(i + 1) * narrow] for i in range(4))
    wi, wd = second[:, :, :wide], second[:, :, wide:]
    if not own_exchange:
        seq_rot = jnp.roll(lax.all_gather(content, "tp", axis=0, tiled=True), shift, axis=0)
        qt = (dot("tdc,rd->tcr", wq, both) * (HEAD ** -0.5 * LOG2E)).astype(jnp.bfloat16).reshape(width, 2 * rows)
        kt = dot("tdc,rd->tcr", wk, seq_rot).astype(jnp.bfloat16).reshape(width, seq)
        vt = dot("tdc,rd->tcr", wv, seq_rot).astype(jnp.bfloat16).reshape(width, seq)
        kp = jnp.swapaxes(kt.reshape(pairs, 128, seq), 1, 2)
        vp = jnp.swapaxes(vt.reshape(pairs, 128, seq), 1, 2)
        ot, lse = attend_fwd(tp_size, ranks, span_starts, bias_table, kp, vt, qt)

    if own_exchange:
        norms = [gain_first, shift_first, gain_second, shift_second]
        content_out, query_out, grad_second, back_first, got, norm_stack = middle(
            ot, content, query, first, second, norms, ranks, upstream_content, upstream_query
        )
    else:
        ot_blocks = ot.reshape(tp_size, narrow, 2 * rows)
        residual_first = both.astype(jnp.float32) + dot("tcr,tmc->rm", ot_blocks, wo)
        normal_first, scale_first = norm_stats(residual_first)
        normed_first = normal_first * gain_first + shift_first
        low_first = normed_first.astype(jnp.bfloat16)
        lifted = dot("rd,tdf->trf", low_first, wi)
        phi = 0.5 * (1.0 + lax.erf(lifted * (0.5 ** 0.5)))
        hidden = (lifted * phi).astype(jnp.bfloat16)
        slope = phi + lifted * jnp.exp(-0.5 * lifted * lifted) * 0.3989422804014327
        residual_second = normed_first + dot("trf,tmf->rm", hidden, wd)
        normal_second, scale_second = norm_stats(residual_second)
        normed_second = normal_second * gain_second + shift_second
        rank_rows = lax.dynamic_slice_in_dim(ranks[0], rows * tp_index, rows)
        predicted = (rank_rows >= seq - seq * 15 // 100).astype(jnp.float32)
        upstream = jnp.concatenate(
            [upstream_content.astype(jnp.float32), upstream_query.astype(jnp.float32) * predicted[:, None]], axis=0
        )
        back_second, grad_gain_second, grad_shift_second = norm_back(upstream, normal_second, scale_second, gain_second)
        gf = back_second.astype(jnp.bfloat16)
        gu = (slope * dot("rm,tmf->trf", gf, wd)).astype(jnp.bfloat16)
        grad_down = dot("rm,trf->tmf", gf, hidden)
        grad_in = dot("rd,trf->tdf", low_first, gu)
        back_normed = back_second + dot("trf,tdf->rd", gu, wi)
        back_first, grad_gain_first, grad_shift_first = norm_back(back_normed, normal_first, scale_first, gain_first)
        ga = back_first.astype(jnp.bfloat16)
        grad_out = dot("rm,tcr->tmc", ga, ot_blocks)
        got = dot("rm,tmc->tcr", ga, wo).astype(jnp.bfloat16).reshape(width, 2 * rows)
        content_out, query_out = (normed_second[s * rows:(s + 1) * rows].astype(jnp.bfloat16) for s in range(2))
        norm_stack = jnp.stack([grad_gain_first, grad_shift_first, grad_gain_second, grad_shift_second])

    def scatter(blocks):
        flat = blocks.astype(jnp.bfloat16).reshape(tp_size * width, blocks.shape[2])
        return lax.psum_scatter(flat, both_axes, scatter_dimension=0, tiled=True).astype(jnp.float32)

    if own_exchange:
        grad_second = grad_second.reshape(4, 2, 2, 2, width // 8, grad_second.shape[2])
        gqt, gkt, gvt, grad_table, sum_in, sum_down, sum_out = attend_bwd(
            tp_size, ranks, span_starts, bias_table, kp, vp, kt, qt, ot, got, lse, grad_second
        )
        grad_content, grad_query, sum_query, sum_key, sum_value, norms, grad_table = tail(
            gqt, gkt, gvt, seqt, queryt, first, back_first, norm_stack, grad_table
        )
        (grad_content, grad_query, sum_query, sum_key, sum_value, sum_out, sum_in, sum_down, *norms) = finish(
            (grad_content, grad_query, sum_query, sum_key, sum_value, sum_out, sum_in, sum_down), norms
        )
    else:
        sum_down, sum_in, sum_out = scatter(grad_down), scatter(grad_in), scatter(grad_out).T
        gqt, gkt, gvt, grad_table = attend_bwd(tp_size, ranks, span_starts, bias_table, kp, vp, kt, qt, ot, got, lse)
        gq_blocks, gk_blocks, gv_blocks = (g.reshape(tp_size, narrow, g.shape[1]) for g in (gqt, gkt, gvt))
        sum_query = scatter(dot("rd,tcr->tdc", both, gq_blocks))
        sum_key = scatter(dot("rd,tcr->tdc", seq_rot, gk_blocks))
        sum_value = scatter(dot("rd,tcr->tdc", seq_rot, gv_blocks))
        back_seq = dot("tcr,tdc->rd", gk_blocks, wk) + dot("tcr,tdc->rd", gv_blocks, wv)
        back_seq = jnp.roll(back_seq.astype(jnp.bfloat16), -shift, axis=0)
        back_content = lax.psum_scatter(back_seq, "tp", scatter_dimension=0, tiled=True).astype(jnp.float32)
        back_inputs = back_first + dot("tcr,tdc->rd", gq_blocks, wq)
        grad_content, grad_query = back_inputs[:rows] + back_content, back_inputs[rows:]
        norms, grad_table = lax.psum((norm_stack, grad_table), ("fsdp", "tp"))
    return (
        content_out, query_out, grad_content, grad_query, sum_query, sum_key, sum_value, sum_out, sum_in, sum_down.T,
        norms[0], norms[1], norms[2], norms[3], grad_table[:, :NB],
    )


def solution(mesh):
    in_specs = (
        P(("fsdp", "tp"), None),
        P(("fsdp", "tp"), None),
        P("fsdp", "tp"),
        P("fsdp", "tp"),
        P("fsdp", "tp"),
        P("tp", "fsdp"),
        P("fsdp", "tp"),
        P("tp", "fsdp"),
        P(),
        P(),
        P(),
        P(),
        P(),
        P("fsdp", None),
        P("fsdp", None),
        P(("fsdp", "tp"), None),
        P(("fsdp", "tp"), None),
    )
    out_specs = (
        P(("fsdp", "tp"), None),
        P(("fsdp", "tp"), None),
        P(("fsdp", "tp"), None),
        P(("fsdp", "tp"), None),
        P("fsdp", "tp"),
        P("fsdp", "tp"),
        P("fsdp", "tp"),
        P("tp", "fsdp"),
        P("fsdp", "tp"),
        P("tp", "fsdp"),
        P(),
        P(),
        P(),
        P(),
        P(),
    )
    return jax.shard_map(functools.partial(local, mesh.shape["tp"], mesh.shape["tp"] == 4 and mesh.shape["fsdp"] == 8), mesh=mesh, in_specs=in_specs, out_specs=out_specs, check_vma=False)
```

```python
import functools
import jax, jax.numpy as jnp
from jax import lax
from jax.sharding import PartitionSpec as P
from jax.experimental import pallas as pl
from jax.experimental.pallas import tpu as pltpu

NEG = -1e30
PIECES = 1
HEAD = 64
NB = 32
PIC = 256
THRESHOLDS = (12, 16, 23, 32, 46, 64, 91)
EPSILON = 1e-05
LOG2E = 1.4426950408889634
LN2 = 0.6931471805599453
VLIM = 60 * 2**20
MESH = pl.DeviceIdType.MESH

def pick(index, values):
    result = jnp.int32(values[-1])
    for place in range(len(values) - 2, -1, -1):
        result = jnp.where(index == place, jnp.int32(values[place]), result)
    return result


class Place:
    def __init__(self):
        f, t = lax.axis_index("fsdp"), lax.axis_index("tp")
        self.f, self.t = f, t
        self.y, self.x, self.c = f // 4, (f // 2) % 2, f % 2
        self.core = (f + 1 - 2 * self.c, t)
        self.xn = (f + 2 - 4 * self.x, t)
        self.yn = (f + 4 - 8 * self.y, t)
        self.up, self.down = (f, t + 1), (f, t - 1)
        self.order = [pick(t, row) for row in ((3, 3, 0, 0), (2, 0, 3, 1), (1, 2, 1, 2), (0, 1, 2, 3))]

    def greet(self):
        barrier = pltpu.get_barrier_semaphore()
        for there in (self.core, self.xn, self.yn):
            pl.semaphore_signal(barrier, inc=1, device_id=there, device_id_type=MESH)
        for there in ((self.f, jnp.where(self.t > 0, self.t - 1, 3)), (self.f, jnp.where(self.t < 3, self.t + 1, 0))):
            pl.semaphore_signal(barrier, inc=1, device_id=there, device_id_type=MESH)
        pl.semaphore_wait(barrier, 5)


def rdma(src, dst, ss, rs, there):
    return pltpu.make_async_remote_copy(src_ref=src, dst_ref=dst, send_sem=ss, recv_sem=rs, device_id=there, device_id_type=MESH)


class Loads:
    def __init__(self, pairs, sems):
        self.copies = [pltpu.make_async_copy(src, dst, sems.at[i]) for i, (src, dst) in enumerate(pairs)]
        for c in self.copies:
            c.start()

    def wait(self, *which):
        for i in which:
            self.copies[i].wait()


class Scatter:
    def __init__(self, at, g, own, r0, r1a, r1b, r2a, r2b, zs, zr, sems, keep_sems):
        self.at, self.g, self.own, self.keep_sems = at, g, own, keep_sems
        self.r0, self.r1a, self.r1b, self.r2a, self.r2b, self.zs, self.zr = r0, r1a, r1b, r2a, r2b, zs, zr
        self.sems = sems
        self.wa = r1a.shape[-1]

    def sem(self, i):
        return self.sems.at[0, i], self.sems.at[1, i]

    def copy0(self, k):
        a = self.at; d = a.order[k]
        return rdma(self.g.at[d, :, :, 1 - a.c], self.r0.at[d], *self.sem(k), a.core)

    def copy1(self, k):
        a = self.at; d = a.order[k]; wa = self.wa
        return (rdma(self.r0.at[d, :, 1 - a.x, :, :wa], self.r1a.at[d], *self.sem(4 + k), a.xn),
                rdma(self.r0.at[d, 1 - a.y, :, :, wa:], self.r1b.at[d], *self.sem(8 + k), a.yn))

    def copy2(self, k):
        a = self.at; d = a.order[k]
        return (rdma(self.r1a.at[d, 1 - a.y], self.r2a.at[d], *self.sem(12 + k), a.yn),
                rdma(self.r1b.at[d, 1 - a.x], self.r2b.at[d], *self.sem(16 + k), a.xn))

    def hop(self, side, h):
        a = self.at
        return rdma(self.zs.at[side, h - 1], self.zr.at[side, h - 1], *self.sem(20 + 3 * side + h - 1), a.down if side else a.up)

    def keep(self, k):
        a = self.at; d = a.order[k]
        return pltpu.make_async_copy(self.g.at[d, :, :, a.c], self.own.at[d], self.keep_sems.at[k])

    def start(self):
        for k in range(4):
            self.copy0(k).start()
            self.keep(k).start()

    def start_one(self, k):
        self.copy0(k).start()

    def stage0(self, k):
        a = self.at; d = a.order[k]
        if self.own is None:
            own = self.g[d, :, :, a.c]
        else:
            self.keep(k).wait()
            own = self.own[d]
        self.copy0(k).wait()
        self.r0[d] = self.r0[d] + own
        for c in self.copy1(k): c.start()

    def stage1(self, k):
        a = self.at; d = a.order[k]; wa = self.wa
        for c in self.copy1(k): c.wait()
        self.r1a[d] = self.r1a[d] + self.r0[d, :, a.x, :, :wa]
        self.r1b[d] = self.r1b[d] + self.r0[d, a.y, :, :, wa:]
        for c in self.copy2(k): c.start()

    def stage2(self, k):
        a = self.at; d = a.order[k]
        for c in self.copy2(k): c.wait()
        self.r2a[d] = self.r2a[d] + self.r1a[d, a.y]
        self.r2b[d] = self.r2b[d] + self.r1b[d, a.x]

    def stage3(self, h):
        wa = self.wa
        for side in range(2):
            u = 3 - self.at.t if side else self.at.t
            d = (self.at.t + h - 4) if side else (self.at.t + 4 - h)
            if h > 1:
                @pl.when((u > 0) & (u < 3) & (u <= h - 1))
                def _():
                    self.hop(side, h - 1).wait_recv()
                    self.zs[side, h - 1, :, :wa] = self.r2a[d] + self.zr[side, h - 2, :, :wa]
                    self.zs[side, h - 1, :, wa:] = self.r2b[d] + self.zr[side, h - 2, :, wa:]
                    self.hop(side, h).start()
            @pl.when(u == 0)
            def _():
                self.zs[side, h - 1, :, :wa] = self.r2a[d]
                self.zs[side, h - 1, :, wa:] = self.r2b[d]
                self.hop(side, h).start()

    def finish(self):
        a = self.at; wa = self.wa
        for side in range(2):
            u = 3 - a.t if side else a.t
            @pl.when(u > 0)
            def _():
                self.hop(side, 3).wait_recv()
        mine = jnp.concatenate([self.r2a[a.t], self.r2b[a.t]], axis=1).astype(jnp.float32)
        below = jnp.where(a.t > 0, self.zr[0, 2].astype(jnp.float32), 0.0)
        above = jnp.where(a.t < 3, self.zr[1, 2].astype(jnp.float32), 0.0)
        for side in range(2):
            u = 3 - a.t if side else a.t
            for h in range(1, 4):
                @pl.when(u < h)
                def _():
                    self.hop(side, h).wait_send()
        return mine + below + above


class Fold:
    def __init__(self, at, part, got, sems):
        self.at, self.part, self.got, self.sems = at, part, got, sems

    def hop(self, side, h):
        a = self.at
        d = jnp.clip((a.t + h - 4) if side else (a.t + 4 - h), 0, 3)
        i = 3 * side + h - 1
        return rdma(self.part.at[d], self.got.at[side, h - 1], self.sems.at[0, i], self.sems.at[1, i], a.down if side else a.up)

    def step(self, h):
        for side in range(2):
            u = 3 - self.at.t if side else self.at.t
            d = (self.at.t + h - 4) if side else (self.at.t + 4 - h)
            @pl.when(u == 0)
            def _():
                if h > 1:
                    self.hop(side, h - 1).wait_send()
                self.hop(side, h).start()
            if h > 1:
                @pl.when((u > 0) & (u < 3) & (u <= h - 1))
                def _():
                    self.hop(side, h - 1).wait_recv()
                    self.part[d] = self.part[d] + self.got[side, h - 2]
                    self.hop(side, h).start()

    def finish(self):
        a = self.at
        for side in range(2):
            u = 3 - a.t if side else a.t
            @pl.when(u > 0)
            def _():
                self.hop(side, 3).wait_recv()
            for h in range(1, 4):
                @pl.when((u < h) & ((u > 0) | (h == 3)))
                def _():
                    self.hop(side, h).wait_send()
        below = jnp.where(a.t > 0, self.got[0, 2].astype(jnp.float32), 0.0)
        above = jnp.where(a.t < 3, self.got[1, 2].astype(jnp.float32), 0.0)
        return self.part[a.t].astype(jnp.float32) + below + above

def scatter_scratch(T, R, W, kept=True):
    wa = (W // 256) * 128
    B = jnp.bfloat16
    return [pltpu.VMEM((T, 2, 2, R, W), B)] * (2 if kept else 1) + [pltpu.VMEM((T, 2, R, wa), B), pltpu.VMEM((T, 2, R, W - wa), B),
            pltpu.VMEM((T, R, wa), B), pltpu.VMEM((T, R, W - wa), B), pltpu.VMEM((2, 3, R, W), B), pltpu.VMEM((2, 3, R, W), B),
            pltpu.SemaphoreType.DMA((2, 26))] + [pltpu.SemaphoreType.DMA((4,))] * kept

class Total:
    def __init__(self, at, sources, acc, got, sems):
        self.at, self.sources, self.acc, self.got, self.sems = at, sources, acc, got, sems
        t = at.t
        self.partners = [at.core, at.xn, at.yn, (at.f, t + 1 - 2 * (t % 2)), (at.f, 3 - t)]

    def copy(self, i):
        return rdma(self.acc.at[i], self.got.at[i], self.sems.at[0, i], self.sems.at[1, i], self.partners[i])

    def start(self):
        norms, table = self.sources
        self.acc[0] = jnp.zeros_like(self.acc[0])
        self.acc[0, :8, :] = norms[...]
        self.acc[0, 8:8 + table.shape[0], :table.shape[1]] = table[...]
        self.copy(0).start()

    def step(self, i):
        self.copy(i).wait_recv()
        self.acc[i + 1] = self.acc[i] + self.got[i]
        if i < 4:
            self.copy(i + 1).start()

    def finish(self, norms_out, table_out):
        for i in range(5):
            self.copy(i).wait_send()
        norms_out[...] = self.acc[5, :8, :]
        table_out[...] = self.acc[5, 8:8 + table_out.shape[0], :table_out.shape[1]]


def total_scratch(rows, width):
    F = jnp.float32
    return [pltpu.VMEM((6, rows, width), F), pltpu.VMEM((5, rows, width), F), pltpu.SemaphoreType.DMA((2, 5))]


def tail_kernel(gqt_in, gkt_in, gvt_in, seqt_in, queryt_in, first, back_in, norms, table,
                grad_content, grad_query, sum_query, sum_key, sum_value, norms_out, table_out,
                gqt, gkt, gvt, seqt, queryt, back, weights, part, got, g1, load_sems, fold_sems, *scratch):
    rows, width = grad_content.shape
    narrow, R = width // 4, sum_query.shape[0]
    at = Place()
    loads = Loads(
        [(gkt_in, gkt), (gvt_in, gvt)] + [(first.at[b, :, pl.ds(128, 640)], weights.at[b]) for b in range(4)]
        + [(seqt_in, seqt), (queryt_in, queryt), (gqt_in, gqt), (back_in, back)], load_sems
    )
    at.greet()
    scatter, fold, total = Scatter(at, g1, None, *scratch[:8], None), Fold(at, part, got, fold_sems), Total(at, (norms, table), *scratch[8:])
    total.start()
    loads.wait(0, 1, 2, 3, 4, 5)

    def partial(d):
        cols = pl.ds(pl.multiple_of(((d - at.t + 4) % 4) * rows, 128), rows)
        out = jnp.zeros((rows, width), jnp.float32)
        for b in range(4):
            here = slice(b * narrow, (b + 1) * narrow)
            out = out + nt(jnp.concatenate([gkt[here, cols], gvt[here, cols]], axis=0).T, weights[b, :, 256:])
        part[d] = out.astype(jnp.bfloat16)

    def weight_grads(k):
        d = at.order[k]
        here = pl.ds(pl.multiple_of(d * narrow, 64), narrow)
        query = nt(seqt[:, :rows], gqt[here, :rows]) + nt(queryt[...], gqt[here, rows:])
        block = jnp.concatenate([query, nt(seqt[...], gkt[here, :]), nt(seqt[...], gvt[here, :])], axis=1)
        g1[d] = block.astype(jnp.bfloat16).reshape(2, 2, 2, R, 3 * narrow)
        scatter.start_one(k)

    for k in range(4):
        partial(at.order[k])
        if k == 0:
            fold.step(1)
    total.step(0)
    loads.wait(6, 7, 8)
    for k in range(4):
        weight_grads(k)
        if k == 1:
            total.step(1)
    scatter.stage0(0)
    scatter.stage0(1)
    total.step(2)
    scatter.stage0(2)
    scatter.stage0(3)
    loads.wait(9)
    for s, out in enumerate((grad_content, grad_query)):
        cols = slice(s * rows, (s + 1) * rows)
        value = back[cols, :]
        for b in range(4):
            value = value + nt(gqt[b * narrow:(b + 1) * narrow, cols].T, weights[b, :, 64:256])
        out[...] = value
    fold.step(2)
    scatter.stage1(0)
    scatter.stage1(1)
    total.step(3)
    scatter.stage1(2)
    scatter.stage1(3)
    scatter.stage2(0)
    scatter.stage3(1)
    scatter.stage2(1)
    total.step(4)
    fold.step(3)
    scatter.stage3(2)
    scatter.stage2(2)
    scatter.stage2(3)
    scatter.stage3(3)
    sums = scatter.finish()
    for i, out in enumerate((sum_query, sum_key, sum_value)):
        out[...] = sums[:, i * narrow:(i + 1) * narrow]
    total.finish(norms_out, table_out)
    grad_content[...] += fold.finish()


def tail(gqt, gkt, gvt, seqt, queryt, first, back, norms, table):
    width, both = gqt.shape
    rows, narrow, R = both // 2, width // 4, width // 8
    V, A = pl.BlockSpec(memory_space=pltpu.MemorySpace.VMEM), pl.BlockSpec(memory_space=pl.ANY)
    B, F, S, DMA = jnp.bfloat16, jnp.float32, jax.ShapeDtypeStruct, pltpu.SemaphoreType.DMA
    outs = [S((rows, width), F)] * 2 + [S((R, narrow), F)] * 3 + [S(norms.shape, F), S(table.shape, F)]
    return pl.pallas_call(
        tail_kernel, out_shape=tuple(outs), in_specs=[A] * 7 + [V, V], out_specs=(V,) * 7,
        scratch_shapes=[
            pltpu.VMEM(gqt.shape, B), pltpu.VMEM(gkt.shape, B), pltpu.VMEM(gvt.shape, B), pltpu.VMEM(seqt.shape, B), pltpu.VMEM(queryt.shape, B),
            pltpu.VMEM(back.shape, F),
            pltpu.VMEM((4, width, 640), B), pltpu.VMEM((4, rows, width), B), pltpu.VMEM((2, 3, rows, width), B),
            pltpu.VMEM((4, 2, 2, 2, R, 3 * narrow), B), DMA((10,)), DMA((2, 6)),
        ] + scatter_scratch(4, R, 3 * narrow, False) + total_scratch(24, width),
        compiler_params=pltpu.CompilerParams(vmem_limit_bytes=VLIM, collective_id=1, has_side_effects=True), name="tail",
    )(gqt, gkt, gvt, seqt, queryt, first, back, norms, table)


def nn(a, b):
    return lax.dot_general(a, b, (((1,), (0,)), ((), ())), preferred_element_type=jnp.float32)
def nt(a, b):
    return lax.dot_general(a, b, (((1,), (1,)), ((), ())), preferred_element_type=jnp.float32)

def band_kind(i, b, nrow, nkey):
    rel = (b - i) % nkey
    if rel == 0: return 2
    if rel == nkey - 1: return 0 if i == 0 else 1
    if rel == 1: return 4 if i == nrow - 1 else 3
    return None

def wrap(value, size):
    return jnp.where(value >= size, value - size, value)


def bucket_of(offsets):
    magnitude = jnp.abs(offsets)
    far_bucket = 8 + sum((magnitude >= threshold).astype(jnp.int32) for threshold in THRESHOLDS)
    return jnp.where(magnitude < 8, magnitude, far_bucket) + jnp.where(offsets > 0, 16, 0)


def slot_bucket(slot, lanes, tp_index, tp_size):
    if slot >= 10:
        return jnp.full_like(lanes, 15 if slot == 10 else 31)
    kind, wrapped = slot // 2, slot % 2
    buckets = bucket_of(128 * ((-1, -1, 0, 1, 1)[kind] + wrapped) - lanes)
    if kind == 0:
        return jnp.where(tp_index == 0, 31, buckets)
    if kind == 4:
        return jnp.where(tp_index == tp_size - 1, 15, buckets)
    return buckets


def far_sides(nrow, nkey, tp_index):
    key_block = lax.broadcasted_iota(jnp.int32, (16, 2 * nrow * 128), 0)
    row_block = wrap(lax.broadcasted_iota(jnp.int32, (16, 2 * nrow * 128), 1) // 128, nrow)
    gap = key_block - row_block
    near = (gap == 0) | (gap == 1) | (gap == -1) | (gap == nkey - 1) | (gap == 1 - nkey) | (key_block >= nkey)
    key_place, row_place = wrap(key_block + nrow * tp_index, nkey), row_block + nrow * tp_index
    left = jnp.where(near, 0.0, jnp.where(key_place < row_place, 1.0, 0.0))
    return left, jnp.where(near, 0.0, 1.0 - left)


def prepare(nrow, nkey, tp_size, ranks, starts, table, mask, ring, vec, sides):
    tp_index = lax.axis_index("tp")
    rows, seq = nrow * 128, nkey * 128
    base = rows * tp_index
    rank_row = jnp.broadcast_to(ranks[...].astype(jnp.float32), (8, seq))
    ring[:, :seq] = rank_row
    ring[:, seq:] = rank_row

    def label(place):
        found = jnp.zeros(place.shape, jnp.int32)
        for k in range(starts.shape[1]):
            start = starts[0, k]
            found = found + jnp.where((place >= start) & (place < start + PIC), k + 1, 0)
        return found

    row_rank, row_label = [], []
    for i in range(nrow):
        row_rank.append(ring[0:1, pl.ds(pl.multiple_of(base + i * 128, 128), 128)])
        row_label.append(label(base + i * 128 + lax.broadcasted_iota(jnp.int32, (1, 128), 1)))

    def one(b, _):
        keys = pl.ds(pl.multiple_of(b * 128, 128), 128)
        rank_k = jnp.broadcast_to(ring[0:1, pl.ds(pl.multiple_of(base + b * 128, 128), 128)], (128, 128)).T
        kpos = b * 128 + lax.broadcasted_iota(jnp.int32, (128, 128), 0)
        label_k = label(wrap(base + kpos, seq))
        for i in range(nrow):
            rpos = i * 128 + lax.broadcasted_iota(jnp.int32, (128, 128), 1)
            same = (label_k == row_label[i]) & (label_k > 0)
            content = (rank_k <= row_rank[i]) | same
            strict = (rank_k < jnp.maximum(row_rank[i], 1.0)) | (same & (kpos != rpos))
            mask[keys, i * 128:(i + 1) * 128] = jnp.where(content, 0.0, NEG)
            mask[keys, rows + i * 128:rows + (i + 1) * 128] = jnp.where(strict, 0.0, NEG)
        return 0
    lax.fori_loop(0, nkey, one, 0)

    heads = table.shape[0]
    lanes = lax.broadcasted_iota(jnp.int32, (heads, 128), 1)
    columns = [jnp.broadcast_to(table[:, n:n + 1] * LOG2E, (heads, 128)) for n in range(NB)]
    for slot in range(12):
        buckets = slot_bucket(slot, lanes, tp_index, tp_size)
        values = columns[0]
        for n in range(1, NB):
            values = jnp.where(buckets == n, columns[n], values)
        for h in range(heads):
            vec[h, slot:slot + 1, :] = values[h:h + 1, :]
    sides[0], sides[1] = far_sides(nrow, nkey, tp_index)


def far_bias(vec, sides, cf, h):
    copies = cf.shape[1] // 128
    left, right = (jnp.concatenate([vec[h, slot:slot + 1, :]] * copies, axis=1) for slot in (10, 11))
    cf[...] = sides[0] * left + sides[1] * right


def prepare_scratch(nrow, nkey, heads):
    F, rows = jnp.float32, 2 * nrow * 128
    return [
        pltpu.VMEM((nkey * 128, rows), F), pltpu.VMEM((8, 2 * nkey * 128), F), pltpu.VMEM((heads, 12, 128), F),
        pltpu.VMEM((2, 16, rows), F), pltpu.VMEM((16, rows), F), pltpu.VMEM((5, 128, 128), F),
    ]


def band_tiles(band, vec, h):
    lane = lax.broadcasted_iota(jnp.int32, (128, 128), 1)
    sub = lax.broadcasted_iota(jnp.int32, (128, 128), 0)
    for k in range(5):
        direct, wrapped = (
            pltpu.roll(jnp.broadcast_to(vec[h, 2 * k + w:2 * k + w + 1, :], (128, 128)), 0, 1, stride=1, stride_axis=0)
            for w in range(2)
        )
        band[k] = jnp.where(lane >= sub, direct, wrapped)

def diagonal_sums(tile):
    lane = lax.broadcasted_iota(jnp.int32, (8, 128), 1)
    sub = lax.broadcasted_iota(jnp.int32, (8, 128), 0)
    direct = wrapped = jnp.zeros((8, 128), jnp.float32)
    for a in range(16):
        rows = tile[8 * a:8 * a + 8, :]
        kept = jnp.where(lane >= sub + 8 * a, rows, 0.0)
        left = rows - kept
        if a:
            kept, left = pltpu.roll(kept, 128 - 8 * a, 1), pltpu.roll(left, 128 - 8 * a, 1)
        direct, wrapped = direct + kept, wrapped + left
    for bit in (1, 2, 4):
        moved = (sub & bit) != 0
        direct = jnp.where(moved, pltpu.roll(direct, 128 - bit, 1), direct)
        wrapped = jnp.where(moved, pltpu.roll(wrapped, 128 - bit, 1), wrapped)
    return jnp.sum(direct, axis=0, keepdims=True), jnp.sum(wrapped, axis=0, keepdims=True)

def head_rows(ref, p, hh, cols):
    z = jnp.zeros((64, cols.stop - cols.start), jnp.bfloat16)
    rows = ref[pl.ds(pl.multiple_of((2 * p + hh) * 64, 64), 64), cols]
    return jnp.concatenate([rows, z] if hh == 0 else [z, rows], axis=0)

def attend_rows(nrow, nkey, kp, vt, qt, ot, lse, t, prepared, exchange):
    mask, _, vec, sides, cf, band = prepared
    ones = jnp.ones((16, 256), jnp.bfloat16)
    nchunk = 2 * nrow * 128 // 256
    def pair(p, _):
        for hh in range(2):
            h = 2 * p + hh
            exchange(h)
            hrows = pl.ds(pl.multiple_of(h * 64, 64), 64)
            band_tiles(band, vec, h)
            far_bias(vec, sides, cf, h)
            for c in range(nchunk):
                cols = slice(c * 256, (c + 1) * 256)
                qh = head_rows(qt, p, hh, cols)
                m8 = jnp.full((8, 256), -jnp.inf, jnp.float32)
                for b in range(nkey):
                    s = nn(kp[p, b * 128:(b + 1) * 128, :], qh)
                    s = s + mask[b * 128:(b + 1) * 128, cols]
                    kinds = [band_kind((2 * c + k) % nrow, b, nrow, nkey) for k in range(2)]
                    if any(k is not None for k in kinds):
                        s = jnp.concatenate([s[:, k * 128:(k + 1) * 128] + (band[kinds[k]] if kinds[k] is not None else 0.0) for k in range(2)], axis=1)
                    t[c, b * 128:(b + 1) * 128, :] = s
                    m8 = jnp.maximum(m8, jnp.max(s.reshape(16, 8, 256), axis=0) + cf[b:b + 1, cols])
                m = jnp.max(m8, axis=0, keepdims=True)
                acc = jnp.zeros((80, 256), jnp.float32)
                for g in range(nkey // 2):
                    ps = []
                    for b in (2 * g, 2 * g + 1):
                        ps.append(jnp.exp2(t[c, b * 128:(b + 1) * 128, :] - (m - cf[b:b + 1, cols])).astype(jnp.bfloat16))
                    lhs = jnp.concatenate([vt[hrows, g * 256:(g + 1) * 256], ones], axis=0)
                    acc = acc + nn(lhs, jnp.concatenate(ps, axis=0))
                l = acc[64:65, :]
                ot[hrows, cols] = (acc[:64, :] / l).astype(jnp.bfloat16)
                lse[h, 0:1, cols] = m + jnp.log2(l)
        return 0
    lax.fori_loop(0, kp.shape[0], pair, 0)

def fwd_kernel(nrow, nkey, tp_size, ranks, starts, table, kp, vt, qt, ot, lse, t, *prepared):
    prepare(nrow, nkey, tp_size, ranks, starts, table, *prepared[:4])
    attend_rows(nrow, nkey, kp, vt, qt, ot, lse, t, prepared, lambda h: None)


def attend_fwd(tp_size, ranks, starts, table, kp, vt, qt):
    pairs, seq, _ = kp.shape
    rows = qt.shape[1]
    nrow, nkey = rows // 256, seq // 128
    V, M = pl.BlockSpec(memory_space=pltpu.MemorySpace.VMEM), pl.BlockSpec(memory_space=pltpu.MemorySpace.SMEM)
    return pl.pallas_call(
        functools.partial(fwd_kernel, nrow, nkey, tp_size),
        out_shape=(jax.ShapeDtypeStruct(qt.shape, jnp.bfloat16), jax.ShapeDtypeStruct((2 * pairs, 1, rows), jnp.float32)),
        in_specs=[V, M, V, V, V, V], out_specs=(V, V),
        scratch_shapes=[pltpu.VMEM((rows // 256, seq, 256), jnp.float32)] + prepare_scratch(nrow, nkey, 2 * pairs),
        compiler_params=pltpu.CompilerParams(vmem_limit_bytes=VLIM),
        name="attend_fwd",
    )(ranks, starts, table, kp, vt, qt)


class Gather:
    def __init__(self, at, shard, g, wa, sems, own_sem):
        self.at, self.shard, self.g, self.wa, self.sems, self.own_sem = at, shard, g, wa, sems, own_sem
        self.blocks = at.order[::-1]

    def send(self, i, src, dst, there):
        return rdma(src, dst, self.sems.at[0, i], self.sems.at[1, i], there)

    def along_z(self, b, upward):
        a = self.at
        here = self.g.at[b, a.y, a.x, a.c]
        return self.send(b + (0 if upward else 4), here, here, a.up if upward else a.down)

    def first(self, b):
        a, wa = self.at, self.wa
        left, right = (self.g.at[b, a.y, a.x, a.c, :, cols] for cols in (slice(0, wa), slice(wa, None)))
        return self.send(8 + b, left, left, a.xn), self.send(12 + b, right, right, a.yn)

    def second(self, b):
        a, wa = self.at, self.wa
        left, right = self.g.at[b, a.y, :, a.c, :, :wa], self.g.at[b, :, a.x, a.c, :, wa:]
        return self.send(16 + b, left, left, a.yn), self.send(20 + b, right, right, a.xn)

    def across(self, b):
        a = self.at
        here = self.g.at[b, :, :, a.c]
        return self.send(24 + b, here, here, a.core)

    def own(self):
        a = self.at
        return pltpu.make_async_copy(self.shard, self.g.at[a.t, a.y, a.x, a.c], self.own_sem)

    def begin(self):
        self.own().start()
        self.own().wait()
        for c in self.first(self.at.t):
            c.start()

    def begin_z(self):
        a = self.at
        @pl.when(a.t < 3)
        def _():
            self.along_z(a.t, True).start()
        @pl.when(a.t > 0)
        def _():
            self.along_z(a.t, False).start()

    def arrive(self, j):
        a, b = self.at, self.blocks[j]
        @pl.when(b < a.t)
        def _():
            self.along_z(b, True).wait_recv()
        @pl.when(b > a.t)
        def _():
            self.along_z(b, False).wait_recv()
        @pl.when((b < a.t) & (a.t < 3))
        def _():
            self.along_z(b, True).start()
        @pl.when((b > a.t) & (a.t > 0))
        def _():
            self.along_z(b, False).start()
        for c in self.first(b):
            c.start()

    def step1(self, j):
        b = self.blocks[j]
        for c in self.first(b):
            c.wait_recv()
        for c in self.second(b):
            c.start()

    def step2(self, j):
        b = self.blocks[j]
        for c in self.second(b):
            c.wait_recv()
        self.across(b).start()

    def step3(self, j):
        self.across(self.blocks[j]).wait_recv()

    def finish(self):
        a = self.at
        for b in range(4):
            @pl.when((b <= a.t) & (a.t < 3))
            def _():
                self.along_z(b, True).wait_send()
            @pl.when((b >= a.t) & (a.t > 0))
            def _():
                self.along_z(b, False).wait_send()
            for c in (*self.first(b), *self.second(b), self.across(b)):
                c.wait_send()


class Chain:
    def __init__(self, at, seq, sems, pieces):
        self.at, self.seq, self.sems, self.pieces = at, seq, sems, pieces
        self.blocks = at.order[::-1]

    def move(self, b, upward, s):
        a = self.at
        i = (b + (0 if upward else 4)) * self.pieces + s
        there = a.t + 1 if upward else a.t - 1
        size = self.seq.shape[1] // self.pieces
        part = slice(s * size, (s + 1) * size)
        return rdma(self.seq.at[(b - a.t + 4) % 4, part], self.seq.at[(b - there + 4) % 4, part], self.sems.at[0, i], self.sems.at[1, i], (a.f, there))

    def begin(self):
        a = self.at
        for s in range(self.pieces):
            @pl.when(a.t < 3)
            def _():
                self.move(a.t, True, s).start()
            @pl.when(a.t > 0)
            def _():
                self.move(a.t, False, s).start()

    def arrive(self, j):
        a, b = self.at, self.blocks[j]
        for s in range(self.pieces):
            @pl.when(b < a.t)
            def _():
                self.move(b, True, s).wait_recv()
            @pl.when(b > a.t)
            def _():
                self.move(b, False, s).wait_recv()
            @pl.when((b < a.t) & (a.t < 3))
            def _():
                self.move(b, True, s).start()
            @pl.when((b > a.t) & (a.t > 0))
            def _():
                self.move(b, False, s).start()

    def finish(self):
        a = self.at
        for b in range(4):
            for s in range(self.pieces):
                @pl.when((b <= a.t) & (a.t < 3))
                def _():
                    self.move(b, True, s).wait_send()
                @pl.when((b >= a.t) & (a.t > 0))
                def _():
                    self.move(b, False, s).wait_send()


def front_kernel(nrow, nkey, content, query, w_query, w_key, w_value, w_out, w_in, w_down, ranks, starts, table,
                 ot, lse, seqt_out, queryt_out, kp_out, vp_out, kt_out, qt_out, w1_out, w2_out,
                 shard1, shard2, seq, seqt, queryt, w1, w2, w1t, kp, vp, kt, vt, qt, t,
                 sems1, sems2, semsc, own_sems, out_sems, *prepared):
    at = Place()
    rows = nrow * 128
    pairs = kp.shape[0]
    narrow = shard1.shape[1] // 4
    width = content.shape[1]
    weights1 = Gather(at, shard1, w1, shard1.shape[1] // 2, sems1, own_sems.at[0])
    weights2 = Gather(at, shard2, w2, shard2.shape[1] // 2, sems2, own_sems.at[1])
    chain = Chain(at, seq, semsc, PIECES)
    shard1[...] = jnp.concatenate([w_out[...].T, w_query[...], w_key[...], w_value[...]], axis=1)
    shard2[:, :w_in.shape[1]] = w_in[...]
    shard2[:, w_in.shape[1]:] = w_down[...]
    seq[0] = content[...]
    at.greet()
    weights1.begin()
    weights1.begin_z()
    weights1.arrive(1)
    weights1.step1(0)
    weights1.arrive(2)
    weights1.step1(1)
    weights1.step2(0)
    weights1.arrive(3)
    chain.begin()
    weights2.begin()
    weights2.begin_z()
    weights1.step1(2)
    weights1.step2(1)
    weights1.step1(3)
    prepare(nrow, nkey, 4, ranks, starts, table, *prepared[:4])
    weights1.step2(2)
    weights1.step2(3)
    for j in range(4):
        weights1.step3(j)

    scale = HEAD ** -0.5 * LOG2E
    for tt in range(4):
        block = w1[tt].reshape(width, 4 * narrow)
        w1t[tt] = block[:, narrow:].T
        for s, x in enumerate((content, query)):
            q = nt(w1t[tt, :narrow, :], x[...])
            qt[tt * narrow:(tt + 1) * narrow, s * rows:(s + 1) * rows] = (q * scale).astype(jnp.bfloat16)

    def project(r):
        x = seq[r]
        cols = pl.ds(pl.multiple_of(r * rows, 128), rows)
        seqt[:, cols] = x.T
        for i, (across, upright) in enumerate(((kp, kt), (vp, vt))):
            for tt in range(4):
                out = nt(w1t[tt, (i + 1) * narrow:(i + 2) * narrow, :], x)
                upright[tt * narrow:(tt + 1) * narrow, cols] = out.astype(jnp.bfloat16)
            for u in range(2):
                halves = [
                    nn(x, w1[2 * u + v].reshape(width, 4 * narrow)[:, (i + 2) * narrow:(i + 3) * narrow]) for v in range(2)
                ]
                joined = jnp.concatenate(halves, axis=1).astype(jnp.bfloat16)
                for p in range(pairs // 2):
                    across[u * (pairs // 2) + p, cols, :] = joined[:, p * 128:(p + 1) * 128]

    queryt[...] = query[...].T
    project(0)
    chain.arrive(1)
    weights2.arrive(1)
    weights2.step1(0)
    project((chain.blocks[1] - at.t + 4) % 4)
    chain.arrive(2)
    weights2.step2(0)
    weights2.step1(1)
    weights2.arrive(2)
    project((chain.blocks[2] - at.t + 4) % 4)
    chain.arrive(3)
    weights2.step2(1)
    weights2.step1(2)
    project((chain.blocks[3] - at.t + 4) % 4)

    outs = [
        pltpu.make_async_copy(src, dst, out_sems.at[i])
        for i, (src, dst) in enumerate(((seqt, seqt_out), (queryt, queryt_out), (kp, kp_out), (vp, vp_out), (kt, kt_out), (qt, qt_out), (w1, w1_out)))
    ]
    for c in outs:
        c.start()

    def second_out(j):
        b = weights2.blocks[j]
        return pltpu.make_async_copy(w2.at[b], w2_out.at[b], out_sems.at[7 + j])

    def exchange(h):
        steps = (
            (weights2.arrive, 3, 1),
            (weights2.step2, 2, 3),
            (weights2.step1, 3, 6),
            (weights2.step2, 3, 10),
        )
        for step, j, place in steps:
            @pl.when(h == place)
            def _():
                step(j)

    attend_rows(nrow, nkey, kp, vt, qt, ot, lse, t, prepared, exchange)
    for j in range(4):
        weights2.step3(j)
        second_out(j).start()
    for c in outs:
        c.wait()
    for j in range(4):
        second_out(j).wait()
    weights1.finish()
    weights2.finish()
    chain.finish()


def front(content, query, w_query, w_key, w_value, w_out, w_in, w_down, ranks, starts, table):
    rows, width = content.shape
    heads, seq_len = table.shape[0], ranks.shape[1]
    pairs, (R, narrow), wide = heads // 2, w_query.shape, w_in.shape[1]
    nrow, nkey = rows // 128, seq_len // 128
    V, A = pl.BlockSpec(memory_space=pltpu.MemorySpace.VMEM), pl.BlockSpec(memory_space=pl.ANY)
    B, F, S, DMA = jnp.bfloat16, jnp.float32, jax.ShapeDtypeStruct, pltpu.SemaphoreType.DMA
    full1, full2 = (4, 2, 2, 2, R, 4 * narrow), (4, 2, 2, 2, R, 2 * wide)
    kept = [((width, seq_len), B), ((width, rows), B), ((pairs, seq_len, 128), B), ((pairs, seq_len, 128), B), ((width, seq_len), B), ((width, 2 * rows), B), (full1, B)]
    outs = [S((width, 2 * rows), B), S((heads, 1, 2 * rows), F)] + [S(*k) for k in kept] + [S(full2, B)]
    scratch = [pltpu.VMEM((R, 4 * narrow), B), pltpu.VMEM((R, 2 * wide), B), pltpu.VMEM((4, rows, width), B), pltpu.VMEM(*kept[0]), pltpu.VMEM(*kept[1]), pltpu.VMEM(full1, B), pltpu.VMEM(full2, B),
               pltpu.VMEM((4, 3 * narrow, width), B), pltpu.VMEM(*kept[2]), pltpu.VMEM(*kept[3]),
               pltpu.VMEM(*kept[4]), pltpu.VMEM(*kept[4]), pltpu.VMEM(*kept[5]),
               pltpu.VMEM((2 * rows // 256, seq_len, 256), F),
               DMA((2, 28)), DMA((2, 28)), DMA((2, 8 * PIECES)), DMA((2,)), DMA((11,))] + prepare_scratch(nrow, nkey, heads)
    return pl.pallas_call(
        functools.partial(front_kernel, nrow, nkey),
        out_shape=tuple(outs), in_specs=[V] * 9 + [pl.BlockSpec(memory_space=pltpu.MemorySpace.SMEM), V], out_specs=tuple([V, V] + [A] * 8), scratch_shapes=scratch,
        compiler_params=pltpu.CompilerParams(vmem_limit_bytes=VLIM, collective_id=3, has_side_effects=True), name="front",
    )(content, query, w_query, w_key, w_value, w_out, w_in, w_down, ranks, starts, table)


def bwd_kernel(nrow, nkey, tp_size, fused, *refs):
    if fused:
        ranks, starts, table, kp, vp, kt, qt, ot, got, lse, g, gqt, gkt, gvt, back_table, sum_in, sum_down, sum_out, gq, bacc, diag, *scratch = refs
        prepared, kept, load_sems, scratch = scratch[:6], scratch[6:12], scratch[12], scratch[13:]
        loads = Loads(list(zip((kp, vp, kt, qt, ot, got), kept)), load_sems)
        kp, vp, kt, qt, ot, got = kept
        at = Place()
        at.greet()
        scatter = Scatter(at, g, *scratch)
        scatter.start()
    else:
        ranks, starts, table, kp, vp, kt, qt, ot, got, lse, gqt, gkt, gvt, back_table, gq, bacc, diag, *prepared = refs
    mask, _, vec, sides, cf, band = prepared
    prepare(nrow, nkey, tp_size, ranks, starts, table, *prepared[:4])
    lane_row = lax.broadcasted_iota(jnp.int32, (1, 128), 1)
    if fused:
        loads.wait(0, 1, 2, 3, 4, 5)

    def exchange(h):
        if not fused:
            return
        steps = (
            (scatter.stage0, 0, 0), (scatter.stage0, 1, 1), (scatter.stage1, 0, 3), (scatter.stage0, 2, 3), (scatter.stage2, 0, 6), (scatter.stage3, 1, 6),
            (scatter.stage1, 1, 6), (scatter.stage0, 3, 6), (scatter.stage1, 2, 8), (scatter.stage2, 1, 9), (scatter.stage3, 2, 9), (scatter.stage1, 3, 11),
        )
        for step, k, place in steps:
            @pl.when(h == place)
            def _():
                step(k)

    rows = 2 * nrow * 128
    nchunk = rows // 256
    full = slice(0, rows)
    block_of = lax.broadcasted_iota(jnp.int32, (16, 256), 0)
    half_of = lax.broadcasted_iota(jnp.int32, (16, 256), 1) // 128
    def pair(p, _):
        for hh in range(2):
            h = 2 * p + hh
            exchange(h)
            hrows = pl.ds(pl.multiple_of(h * 64, 64), 64)
            band_tiles(band, vec, h)
            far_bias(vec, sides, cf, h)
            q_h = qt[hrows, :]
            go_h = got[hrows, :]
            delta = jnp.sum(ot[hrows, :].astype(jnp.float32) * go_h.astype(jnp.float32), axis=0, keepdims=True)
            for k in range(5):
                bacc[k] = jnp.zeros((128, 128), jnp.float32)
            gq[...] = jnp.zeros_like(gq)
            qm = head_rows(qt, p, hh, full)
            gm = head_rows(got, p, hh, full)
            for g in range(nkey // 2):
                pp, gg = [], []
                for c in range(nchunk):
                    cols = slice(c * 256, (c + 1) * 256)
                    pc, gc = [], []
                    for b in (2 * g, 2 * g + 1):
                        keys = slice(b * 128, (b + 1) * 128)
                        s = nn(kp[p, keys, :], qm[:, cols])
                        dp = nn(vp[p, keys, :], gm[:, cols])
                        s = s + mask[keys, cols]
                        kinds = [band_kind((2 * c + k) % nrow, b, nrow, nkey) for k in range(2)]
                        if any(k is not None for k in kinds):
                            s = jnp.concatenate([s[:, k * 128:(k + 1) * 128] + (band[kinds[k]] if kinds[k] is not None else 0.0) for k in range(2)], axis=1)
                        pr = jnp.exp2(s - (lse[h, 0:1, cols] - cf[b:b + 1, cols]))
                        gs = pr * (dp - delta[:, cols])
                        for k in range(2):
                            if kinds[k] is not None:
                                bacc[kinds[k]] += gs[:, k * 128:(k + 1) * 128]
                        pc.append(pr.astype(jnp.bfloat16))
                        gc.append(gs.astype(jnp.bfloat16))
                    pp.append(jnp.concatenate(pc, axis=0))
                    gg.append(jnp.concatenate(gc, axis=0))
                pall = jnp.concatenate(pp, axis=1)
                gall = jnp.concatenate(gg, axis=1)
                keys = slice(g * 256, (g + 1) * 256)
                onehot = (block_of == 2 * g + half_of).astype(jnp.bfloat16)
                gq[...] += nn(jnp.concatenate([kt[hrows, keys], onehot], axis=0), gall)
                gkt[hrows, keys] = (nt(q_h, gall) * LN2).astype(jnp.bfloat16)
                gvt[hrows, keys] = nt(go_h, pall).astype(jnp.bfloat16)
            gqt[hrows, :] = (gq[:64, :] * 0.125).astype(jnp.bfloat16)
            for k in range(5):
                direct, wrapped = diagonal_sums(bacc[k])
                diag[h, 0:1, 256 * k:256 * k + 128] = direct
                diag[h, 0:1, 256 * k + 128:256 * k + 256] = wrapped
            for s in range(2):
                side = jnp.sum(jnp.sum(gq[64:80, :] * sides[s], axis=0, keepdims=True), axis=1, keepdims=True)
                diag[h, 0:1, 1280 + 128 * s:1408 + 128 * s] = jnp.where(lane_row == 0, side, 0.0)
        return 0
    lax.fori_loop(0, kp.shape[0], pair, 0)
    tp_index = lax.axis_index("tp")
    places = lax.broadcasted_iota(jnp.int32, (128, 128), 0)
    numbers = lax.broadcasted_iota(jnp.int32, (128, 128), 1)
    sums = jnp.concatenate([diag[h] for h in range(diag.shape[0])], axis=0)
    total = jnp.zeros((diag.shape[0], 128), jnp.float32)
    for slot in range(12):
        one_hot = jnp.where(slot_bucket(slot, places, tp_index, tp_size) == numbers, 1.0, 0.0)
        total = total + jnp.dot(
            sums[:, slot * 128:(slot + 1) * 128], one_hot, precision=lax.Precision.HIGHEST, preferred_element_type=jnp.float32
        )
    back_table[...] = total
    if fused:
        scatter.stage2(2)
        scatter.stage3(3)
        scatter.stage2(3)
        sums = scatter.finish()
        wide = sum_in.shape[1]
        sum_in[...] = sums[:, :wide]
        sum_down[...] = sums[:, wide:2 * wide]
        sum_out[...] = sums[:, 2 * wide:].T


def attend_bwd(tp_size, ranks, starts, table, kp, vp, kt, qt, ot, got, lse, g=None):
    pairs, seq, _ = kp.shape
    rows = qt.shape[1]
    heads = 2 * pairs
    nrow, nkey = rows // 256, seq // 128
    V, M = pl.BlockSpec(memory_space=pltpu.MemorySpace.VMEM), pl.BlockSpec(memory_space=pltpu.MemorySpace.SMEM)
    S, F = jax.ShapeDtypeStruct, jnp.float32
    fused = g is not None
    outs = [S(qt.shape, jnp.bfloat16), S(kt.shape, jnp.bfloat16), S(kt.shape, jnp.bfloat16), S((heads, 128), F)]
    scratch = [pltpu.VMEM((80, rows), F), pltpu.VMEM((5, 128, 128), F), pltpu.VMEM((heads, 1, 1536), F)] + prepare_scratch(nrow, nkey, heads)
    params = dict(vmem_limit_bytes=VLIM)
    args = (ranks, starts, table, kp, vp, kt, qt, ot, got, lse)
    specs = [V, M] + [V] * 8
    if fused:
        narrow = kt.shape[0] // 4
        wide = (g.shape[5] - narrow) // 2
        outs += [S((g.shape[4], wide), F), S((g.shape[4], wide), F), S((narrow, g.shape[4]), F)]
        scratch += [pltpu.VMEM(a.shape, a.dtype) for a in (kp, vp, kt, qt, ot, got)] + [pltpu.SemaphoreType.DMA((6,))]
        scratch += scatter_scratch(g.shape[0], g.shape[4], g.shape[5])
        params.update(collective_id=2, has_side_effects=True)
        args += (g,)
        A = pl.BlockSpec(memory_space=pl.ANY)
        specs = specs[:3] + [A] * 6 + [V, A]
    return pl.pallas_call(
        functools.partial(bwd_kernel, nrow, nkey, tp_size, fused),
        out_shape=tuple(outs), in_specs=specs, out_specs=(V,) * len(outs), scratch_shapes=scratch,
        compiler_params=pltpu.CompilerParams(**params), name="attend_bwd",
    )(*args)


def norm(residual):
    centered = residual - jnp.mean(residual, axis=-1, keepdims=True)
    scale = lax.rsqrt(jnp.mean(centered * centered, axis=-1, keepdims=True) + EPSILON)
    return centered * scale, scale


def norm_step(cotangent, normal, scale, gain):
    inner = cotangent * gain
    mean_inner = jnp.mean(inner, axis=-1, keepdims=True)
    mean_cross = jnp.mean(inner * normal, axis=-1, keepdims=True)
    return scale * (inner - mean_inner - normal * mean_cross)


def middle_kernel(chunk, ot_in, content, query, first, second_in, gain1, shift1, gain2, shift2, ranks, up_content, up_query,
                  content_out, query_out, grads, back, got, sums,
                  ot, second, x, up, wot, wo_block, onat, n1bt, gft, gat, hidden, slope, gu, out2, stage, sems, out_sems):
    rows = content.shape[0]
    seq, width = ranks.shape[1], content.shape[1]
    narrow, wide = width // 4, second.shape[2] // 2
    loads = Loads(
        [(first.at[t, :, pl.ds(0, 256)], wo_block.at[t]) for t in range(4)] + [(ot_in, ot)]
        + [(second_in.at[t], second.at[t]) for t in range(4)], sems
    )
    base = rows * lax.axis_index("tp")
    x[:rows] = content[...]
    x[rows:] = query[...]
    up[:rows] = up_content[...].astype(jnp.float32)
    for i in range(rows // 128):
        rank = ranks[0:1, pl.ds(pl.multiple_of(base + i * 128, 128), 128)].astype(jnp.float32)
        rank = jnp.broadcast_to(rank, (128, 128)).T
        kept = jnp.where(rank >= seq - seq * 15 // 100, 1.0, 0.0)
        up[rows + i * 128:rows + (i + 1) * 128, :] = up_query[i * 128:(i + 1) * 128, :].astype(jnp.float32) * jnp.concatenate([kept] * (width // 128), axis=1)
    loads.wait(0, 1, 2, 3, 4)
    wot[...] = jnp.concatenate([wo_block[t, :, :narrow] for t in range(4)], axis=1)
    sums[...] = jnp.zeros_like(sums)
    gain1, shift1, gain2, shift2 = (ref[...].reshape(1, width) for ref in (gain1, shift1, gain2, shift2))

    def one(i, _):
        here = pl.ds(pl.multiple_of(i * chunk, chunk), chunk)
        mixed = ot[:, here].T
        onat[here, :] = mixed
        normal1, scale1 = norm(x[here, :].astype(jnp.float32) + nt(mixed, wot[...]))
        normed = normal1 * gain1 + shift1
        low = normed.astype(jnp.bfloat16)
        n1bt[:, here] = low.T
        total = normed
        for t in range(4):
            @pl.when(i == 0)
            def _():
                loads.wait(5 + t)
            lifted = nn(low, second[t, :, :wide])
            phi = 0.5 + 0.5 * lax.erf(lifted * (0.5 ** 0.5))
            act = (lifted * phi).astype(jnp.bfloat16)
            hidden[t, here, :] = act
            slope[t] = phi + lifted * (jnp.exp(-0.5 * lifted * lifted) * 0.3989422804014327)
            total = total + nt(act, second[t, :, wide:])
        normal2, scale2 = norm(total)
        out2[here, :] = (normal2 * gain2 + shift2).astype(jnp.bfloat16)
        cotangent = up[here, :]
        sums[2:3, :] += jnp.sum(cotangent * normal2, axis=0, keepdims=True)
        sums[3:4, :] += jnp.sum(cotangent, axis=0, keepdims=True)
        back2 = norm_step(cotangent, normal2, scale2, gain2)
        gf = back2.astype(jnp.bfloat16)
        gft[:, here] = gf.T
        total = back2
        for t in range(4):
            g = (slope[t] * nn(gf, second[t, :, wide:])).astype(jnp.bfloat16)
            gu[t, here, :] = g
            total = total + nt(g, second[t, :, :wide])
        sums[0:1, :] += jnp.sum(total * normal1, axis=0, keepdims=True)
        sums[1:2, :] += jnp.sum(total, axis=0, keepdims=True)
        back1 = norm_step(total, normal1, scale1, gain1)
        back[here, :] = back1
        ga = back1.astype(jnp.bfloat16)
        gat[:, here] = ga.T
        got[:, here] = nn(ga, wot[...]).astype(jnp.bfloat16).T
        return 0

    lax.fori_loop(0, 2 * rows // chunk, one, 0)
    content_out[...] = out2[:rows]
    query_out[...] = out2[rows:]
    for t in range(4):
        wo_block[t, :, :narrow] = nn(gat[...], onat[:, t * narrow:(t + 1) * narrow]).astype(jnp.bfloat16)

    def send(t):
        return pltpu.make_async_copy(stage.at[t % 2], grads.at[t], out_sems.at[t % 2])

    for t in range(4):
        if t >= 2:
            send(t - 2).wait()
        stage[t % 2, :, :wide] = nn(n1bt[...], gu[t]).astype(jnp.bfloat16)
        stage[t % 2, :, wide:2 * wide] = nn(gft[...], hidden[t]).astype(jnp.bfloat16)
        stage[t % 2, :, 2 * wide:] = wo_block[t, :, :narrow]
        send(t).start()
    for t in (2, 3):
        send(t).wait()


def middle(ot, content, query, first, second, norms, ranks, up_content, up_query):
    rows, width = content.shape
    narrow, wide = width // 4, second.shape[2] // 2
    both, chunk = 2 * rows, 256
    V, A = pl.BlockSpec(memory_space=pltpu.MemorySpace.VMEM), pl.BlockSpec(memory_space=pl.ANY)
    B, F, S, DMA = jnp.bfloat16, jnp.float32, jax.ShapeDtypeStruct, pltpu.SemaphoreType.DMA
    return pl.pallas_call(
        functools.partial(middle_kernel, chunk),
        out_shape=(S((rows, width), B), S((rows, width), B), S((4, width, 2 * wide + narrow), B), S((both, width), F), S((width, both), B), S((8, width), F)),
        in_specs=[A, V, V, A, A] + [V] * 7, out_specs=(V, V, A, V, V, V),
        scratch_shapes=[
            pltpu.VMEM(ot.shape, B), pltpu.VMEM(second.shape, B),
            pltpu.VMEM((both, width), B), pltpu.VMEM((both, width), F), pltpu.VMEM((width, width), B), pltpu.VMEM((4, width, 256), B),
            pltpu.VMEM((both, width), B), pltpu.VMEM((width, both), B), pltpu.VMEM((width, both), B), pltpu.VMEM((width, both), B),
            pltpu.VMEM((4, both, wide), B), pltpu.VMEM((4, chunk, wide), F), pltpu.VMEM((4, both, wide), B), pltpu.VMEM((both, width), B),
            pltpu.VMEM((2, width, 2 * wide + narrow), B), DMA((9,)), DMA((2,)),
        ],
        compiler_params=pltpu.CompilerParams(vmem_limit_bytes=VLIM), name="middle",
    )(ot, content, query, first, second, *norms, ranks, up_content, up_query)


def finish_kernel(count, *refs):
    sources, norms, outs, held, sems = refs[:count], refs[count], refs[count + 1:2 * count + 5], refs[2 * count + 5:-1], refs[-1]
    loads = [pltpu.make_async_copy(src, mid, sems.at[0, i]) for i, (src, mid) in enumerate(zip(sources, held))]
    stores = [pltpu.make_async_copy(mid, dst, sems.at[1, i]) for i, (mid, dst) in enumerate(zip(held, outs))]
    for c in loads:
        c.start()
    for i in range(4):
        outs[count + i][...] = norms[i:i + 1, :].reshape(norms.shape[1])
    for load, store in zip(loads, stores):
        load.wait()
        store.start()
    for c in stores:
        c.wait()


def finish(arrays, norms):
    V, A, S = pl.BlockSpec(memory_space=pltpu.MemorySpace.VMEM), pl.BlockSpec(memory_space=pl.ANY), jax.ShapeDtypeStruct
    count = len(arrays)
    return pl.pallas_call(
        functools.partial(finish_kernel, count),
        out_shape=tuple(S(a.shape, a.dtype) for a in arrays) + tuple(S((norms.shape[1],), norms.dtype) for _ in range(4)),
        in_specs=[A] * count + [V], out_specs=(A,) * count + (V,) * 4, scratch_shapes=[pltpu.VMEM(a.shape, a.dtype) for a in arrays] + [pltpu.SemaphoreType.DMA((2, count))],
        compiler_params=pltpu.CompilerParams(vmem_limit_bytes=VLIM), name="finish",
    )(*arrays, norms)


def dot(spec, a, b):
    return jnp.einsum(spec, a, b, preferred_element_type=jnp.float32)


def norm_stats(residual):
    centered = residual - jnp.mean(residual, axis=-1, keepdims=True)
    scale = lax.rsqrt(jnp.mean(centered * centered, axis=-1, keepdims=True) + EPSILON)
    return centered * scale, scale


def norm_back(cotangent, normal, scale, gain):
    inner = cotangent * gain
    mean_inner = jnp.mean(inner, axis=-1, keepdims=True)
    mean_cross = jnp.mean(inner * normal, axis=-1, keepdims=True)
    back = scale * (inner - mean_inner - normal * mean_cross)
    return back, jnp.sum(cotangent * normal, axis=0), jnp.sum(cotangent, axis=0)


def local(
    tp_size, own_exchange, content, query, w_query, w_key, w_value, w_out, w_in, w_down, gain_first, shift_first,
    gain_second, shift_second, bias_table, ranks, span_starts, upstream_content, upstream_query,
):
    rows, width = content.shape
    seq = ranks.shape[1]
    heads = bias_table.shape[0]
    pairs = heads // 2
    tp_index = lax.axis_index("tp")
    both_axes = ("tp", "fsdp")
    narrow = w_query.shape[1]

    def gather(parts):
        shard = jnp.concatenate(parts, axis=1)
        return lax.all_gather(shard, both_axes, axis=0, tiled=True).reshape(tp_size, width, shard.shape[1])

    wide = w_in.shape[1]
    shift = -rows * tp_index
    both = jnp.concatenate([content, query], axis=0)
    if own_exchange:
        ot, lse, seqt, queryt, kp, vp, kt, qt, first, second = front(
            content, query, w_query, w_key, w_value, w_out, w_in, w_down.T, ranks, span_starts, bias_table
        )
        first, second = first.reshape(tp_size, width, 4 * narrow), second.reshape(tp_size, width, 2 * wide)
    else:
        first, second = gather([w_out.T, w_query, w_key, w_value]), gather([w_in, w_down.T])
    wo, wq, wk, wv = (first[:, :, i * narrow:(i + 1) * narrow] for i in range(4))
    wi, wd = second[:, :, :wide], second[:, :, wide:]
    if not own_exchange:
        seq_rot = jnp.roll(lax.all_gather(content, "tp", axis=0, tiled=True), shift, axis=0)
        qt = (dot("tdc,rd->tcr", wq, both) * (HEAD ** -0.5 * LOG2E)).astype(jnp.bfloat16).reshape(width, 2 * rows)
        kt = dot("tdc,rd->tcr", wk, seq_rot).astype(jnp.bfloat16).reshape(width, seq)
        vt = dot("tdc,rd->tcr", wv, seq_rot).astype(jnp.bfloat16).reshape(width, seq)
        kp = jnp.swapaxes(kt.reshape(pairs, 128, seq), 1, 2)
        vp = jnp.swapaxes(vt.reshape(pairs, 128, seq), 1, 2)
        ot, lse = attend_fwd(tp_size, ranks, span_starts, bias_table, kp, vt, qt)

    if own_exchange:
        norms = [gain_first, shift_first, gain_second, shift_second]
        content_out, query_out, grad_second, back_first, got, norm_stack = middle(
            ot, content, query, first, second, norms, ranks, upstream_content, upstream_query
        )
    else:
        ot_blocks = ot.reshape(tp_size, narrow, 2 * rows)
        residual_first = both.astype(jnp.float32) + dot("tcr,tmc->rm", ot_blocks, wo)
        normal_first, scale_first = norm_stats(residual_first)
        normed_first = normal_first * gain_first + shift_first
        low_first = normed_first.astype(jnp.bfloat16)
        lifted = dot("rd,tdf->trf", low_first, wi)
        phi = 0.5 * (1.0 + lax.erf(lifted * (0.5 ** 0.5)))
        hidden = (lifted * phi).astype(jnp.bfloat16)
        slope = phi + lifted * jnp.exp(-0.5 * lifted * lifted) * 0.3989422804014327
        residual_second = normed_first + dot("trf,tmf->rm", hidden, wd)
        normal_second, scale_second = norm_stats(residual_second)
        normed_second = normal_second * gain_second + shift_second
        rank_rows = lax.dynamic_slice_in_dim(ranks[0], rows * tp_index, rows)
        predicted = (rank_rows >= seq - seq * 15 // 100).astype(jnp.float32)
        upstream = jnp.concatenate(
            [upstream_content.astype(jnp.float32), upstream_query.astype(jnp.float32) * predicted[:, None]], axis=0
        )
        back_second, grad_gain_second, grad_shift_second = norm_back(upstream, normal_second, scale_second, gain_second)
        gf = back_second.astype(jnp.bfloat16)
        gu = (slope * dot("rm,tmf->trf", gf, wd)).astype(jnp.bfloat16)
        grad_down = dot("rm,trf->tmf", gf, hidden)
        grad_in = dot("rd,trf->tdf", low_first, gu)
        back_normed = back_second + dot("trf,tdf->rd", gu, wi)
        back_first, grad_gain_first, grad_shift_first = norm_back(back_normed, normal_first, scale_first, gain_first)
        ga = back_first.astype(jnp.bfloat16)
        grad_out = dot("rm,tcr->tmc", ga, ot_blocks)
        got = dot("rm,tmc->tcr", ga, wo).astype(jnp.bfloat16).reshape(width, 2 * rows)
        content_out, query_out = (normed_second[s * rows:(s + 1) * rows].astype(jnp.bfloat16) for s in range(2))
        norm_stack = jnp.stack([grad_gain_first, grad_shift_first, grad_gain_second, grad_shift_second])

    def scatter(blocks):
        flat = blocks.astype(jnp.bfloat16).reshape(tp_size * width, blocks.shape[2])
        return lax.psum_scatter(flat, both_axes, scatter_dimension=0, tiled=True).astype(jnp.float32)

    if own_exchange:
        grad_second = grad_second.reshape(4, 2, 2, 2, width // 8, grad_second.shape[2])
        gqt, gkt, gvt, grad_table, sum_in, sum_down, sum_out = attend_bwd(
            tp_size, ranks, span_starts, bias_table, kp, vp, kt, qt, ot, got, lse, grad_second
        )
        grad_content, grad_query, sum_query, sum_key, sum_value, norms, grad_table = tail(
            gqt, gkt, gvt, seqt, queryt, first, back_first, norm_stack, grad_table
        )
        (grad_content, grad_query, sum_query, sum_key, sum_value, sum_out, sum_in, sum_down, *norms) = finish(
            (grad_content, grad_query, sum_query, sum_key, sum_value, sum_out, sum_in, sum_down), norms
        )
    else:
        sum_down, sum_in, sum_out = scatter(grad_down), scatter(grad_in), scatter(grad_out).T
        gqt, gkt, gvt, grad_table = attend_bwd(tp_size, ranks, span_starts, bias_table, kp, vp, kt, qt, ot, got, lse)
        gq_blocks, gk_blocks, gv_blocks = (g.reshape(tp_size, narrow, g.shape[1]) for g in (gqt, gkt, gvt))
        sum_query = scatter(dot("rd,tcr->tdc", both, gq_blocks))
        sum_key = scatter(dot("rd,tcr->tdc", seq_rot, gk_blocks))
        sum_value = scatter(dot("rd,tcr->tdc", seq_rot, gv_blocks))
        back_seq = dot("tcr,tdc->rd", gk_blocks, wk) + dot("tcr,tdc->rd", gv_blocks, wv)
        back_seq = jnp.roll(back_seq.astype(jnp.bfloat16), -shift, axis=0)
        back_content = lax.psum_scatter(back_seq, "tp", scatter_dimension=0, tiled=True).astype(jnp.float32)
        back_inputs = back_first + dot("tcr,tdc->rd", gq_blocks, wq)
        grad_content, grad_query = back_inputs[:rows] + back_content, back_inputs[rows:]
        norms, grad_table = lax.psum((norm_stack, grad_table), ("fsdp", "tp"))
    return (
        content_out, query_out, grad_content, grad_query, sum_query, sum_key, sum_value, sum_out, sum_in, sum_down.T,
        norms[0], norms[1], norms[2], norms[3], grad_table[:, :NB],
    )


def solution(mesh):
    in_specs = (
        P(("fsdp", "tp"), None),
        P(("fsdp", "tp"), None),
        P("fsdp", "tp"),
        P("fsdp", "tp"),
        P("fsdp", "tp"),
        P("tp", "fsdp"),
        P("fsdp", "tp"),
        P("tp", "fsdp"),
        P(),
        P(),
        P(),
        P(),
        P(),
        P("fsdp", None),
        P("fsdp", None),
        P(("fsdp", "tp"), None),
        P(("fsdp", "tp"), None),
    )
    out_specs = (
        P(("fsdp", "tp"), None),
        P(("fsdp", "tp"), None),
        P(("fsdp", "tp"), None),
        P(("fsdp", "tp"), None),
        P("fsdp", "tp"),
        P("fsdp", "tp"),
        P("fsdp", "tp"),
        P("tp", "fsdp"),
        P("fsdp", "tp"),
        P("tp", "fsdp"),
        P(),
        P(),
        P(),
        P(),
        P(),
    )
    return jax.shard_map(functools.partial(local, mesh.shape["tp"], mesh.shape["tp"] == 4 and mesh.shape["fsdp"] == 8), mesh=mesh, in_specs=in_specs, out_specs=out_specs, check_vma=False)
```

```python
import functools
import jax, jax.numpy as jnp
from jax import lax
from jax.sharding import PartitionSpec as P
from jax.experimental import pallas as pl
from jax.experimental.pallas import tpu as pltpu

NEG = -1e30
PIECES = 1
HEAD = 64
NB = 32
PIC = 256
THRESHOLDS = (12, 16, 23, 32, 46, 64, 91)
EPSILON = 1e-05
LOG2E = 1.4426950408889634
LN2 = 0.6931471805599453
VLIM = 60 * 2**20
MESH = pl.DeviceIdType.MESH

def pick(index, values):
    result = jnp.int32(values[-1])
    for place in range(len(values) - 2, -1, -1):
        result = jnp.where(index == place, jnp.int32(values[place]), result)
    return result


class Place:
    def __init__(self):
        f, t = lax.axis_index("fsdp"), lax.axis_index("tp")
        self.f, self.t = f, t
        self.y, self.x, self.c = f // 4, (f // 2) % 2, f % 2
        self.core = (f + 1 - 2 * self.c, t)
        self.xn = (f + 2 - 4 * self.x, t)
        self.yn = (f + 4 - 8 * self.y, t)
        self.up, self.down = (f, t + 1), (f, t - 1)
        self.order = [pick(t, row) for row in ((3, 3, 0, 0), (2, 0, 3, 1), (1, 2, 1, 2), (0, 1, 2, 3))]

    def greet(self):
        barrier = pltpu.get_barrier_semaphore()
        for there in (self.core, self.xn, self.yn):
            pl.semaphore_signal(barrier, inc=1, device_id=there, device_id_type=MESH)
        for there in ((self.f, jnp.where(self.t > 0, self.t - 1, 3)), (self.f, jnp.where(self.t < 3, self.t + 1, 0))):
            pl.semaphore_signal(barrier, inc=1, device_id=there, device_id_type=MESH)
        pl.semaphore_wait(barrier, 5)


def rdma(src, dst, ss, rs, there):
    return pltpu.make_async_remote_copy(src_ref=src, dst_ref=dst, send_sem=ss, recv_sem=rs, device_id=there, device_id_type=MESH)


class Loads:
    def __init__(self, pairs, sems):
        self.copies = [pltpu.make_async_copy(src, dst, sems.at[i]) for i, (src, dst) in enumerate(pairs)]
        for c in self.copies:
            c.start()

    def wait(self, *which):
        for i in which:
            self.copies[i].wait()


class Scatter:
    def __init__(self, at, g, own, r0, r1a, r1b, r2a, r2b, zs, zr, sems, keep_sems):
        self.at, self.g, self.own, self.keep_sems = at, g, own, keep_sems
        self.r0, self.r1a, self.r1b, self.r2a, self.r2b, self.zs, self.zr = r0, r1a, r1b, r2a, r2b, zs, zr
        self.sems = sems
        self.wa = r1a.shape[-1]

    def sem(self, i):
        return self.sems.at[0, i], self.sems.at[1, i]

    def copy0(self, k):
        a = self.at; d = a.order[k]
        return rdma(self.g.at[d, :, :, 1 - a.c], self.r0.at[d], *self.sem(k), a.core)

    def copy1(self, k):
        a = self.at; d = a.order[k]; wa = self.wa
        return (rdma(self.r0.at[d, :, 1 - a.x, :, :wa], self.r1a.at[d], *self.sem(4 + k), a.xn),
                rdma(self.r0.at[d, 1 - a.y, :, :, wa:], self.r1b.at[d], *self.sem(8 + k), a.yn))

    def copy2(self, k):
        a = self.at; d = a.order[k]
        return (rdma(self.r1a.at[d, 1 - a.y], self.r2a.at[d], *self.sem(12 + k), a.yn),
                rdma(self.r1b.at[d, 1 - a.x], self.r2b.at[d], *self.sem(16 + k), a.xn))

    def hop(self, side, h):
        a = self.at
        return rdma(self.zs.at[side, h - 1], self.zr.at[side, h - 1], *self.sem(20 + 3 * side + h - 1), a.down if side else a.up)

    def keep(self, k):
        a = self.at; d = a.order[k]
        return pltpu.make_async_copy(self.g.at[d, :, :, a.c], self.own.at[d], self.keep_sems.at[k])

    def start(self):
        for k in range(4):
            self.copy0(k).start()
            self.keep(k).start()

    def start_one(self, k):
        self.copy0(k).start()

    def stage0(self, k):
        a = self.at; d = a.order[k]
        if self.own is None:
            own = self.g[d, :, :, a.c]
        else:
            self.keep(k).wait()
            own = self.own[d]
        self.copy0(k).wait()
        self.r0[d] = self.r0[d] + own
        for c in self.copy1(k): c.start()

    def stage1(self, k):
        a = self.at; d = a.order[k]; wa = self.wa
        for c in self.copy1(k): c.wait()
        self.r1a[d] = self.r1a[d] + self.r0[d, :, a.x, :, :wa]
        self.r1b[d] = self.r1b[d] + self.r0[d, a.y, :, :, wa:]
        for c in self.copy2(k): c.start()

    def stage2(self, k):
        a = self.at; d = a.order[k]
        for c in self.copy2(k): c.wait()
        self.r2a[d] = self.r2a[d] + self.r1a[d, a.y]
        self.r2b[d] = self.r2b[d] + self.r1b[d, a.x]

    def stage3(self, h):
        wa = self.wa
        for side in range(2):
            u = 3 - self.at.t if side else self.at.t
            d = (self.at.t + h - 4) if side else (self.at.t + 4 - h)
            if h > 1:
                @pl.when((u > 0) & (u < 3) & (u <= h - 1))
                def _():
                    self.hop(side, h - 1).wait_recv()
                    self.zs[side, h - 1, :, :wa] = self.r2a[d] + self.zr[side, h - 2, :, :wa]
                    self.zs[side, h - 1, :, wa:] = self.r2b[d] + self.zr[side, h - 2, :, wa:]
                    self.hop(side, h).start()
            @pl.when(u == 0)
            def _():
                self.zs[side, h - 1, :, :wa] = self.r2a[d]
                self.zs[side, h - 1, :, wa:] = self.r2b[d]
                self.hop(side, h).start()

    def finish(self):
        a = self.at; wa = self.wa
        for side in range(2):
            u = 3 - a.t if side else a.t
            @pl.when(u > 0)
            def _():
                self.hop(side, 3).wait_recv()
        mine = jnp.concatenate([self.r2a[a.t], self.r2b[a.t]], axis=1).astype(jnp.float32)
        below = jnp.where(a.t > 0, self.zr[0, 2].astype(jnp.float32), 0.0)
        above = jnp.where(a.t < 3, self.zr[1, 2].astype(jnp.float32), 0.0)
        for side in range(2):
            u = 3 - a.t if side else a.t
            for h in range(1, 4):
                @pl.when(u < h)
                def _():
                    self.hop(side, h).wait_send()
        return mine + below + above


class Fold:
    def __init__(self, at, part, got, sems):
        self.at, self.part, self.got, self.sems = at, part, got, sems

    def hop(self, side, h):
        a = self.at
        d = jnp.clip((a.t + h - 4) if side else (a.t + 4 - h), 0, 3)
        i = 3 * side + h - 1
        return rdma(self.part.at[d], self.got.at[side, h - 1], self.sems.at[0, i], self.sems.at[1, i], a.down if side else a.up)

    def step(self, h):
        for side in range(2):
            u = 3 - self.at.t if side else self.at.t
            d = (self.at.t + h - 4) if side else (self.at.t + 4 - h)
            @pl.when(u == 0)
            def _():
                if h > 1:
                    self.hop(side, h - 1).wait_send()
                self.hop(side, h).start()
            if h > 1:
                @pl.when((u > 0) & (u < 3) & (u <= h - 1))
                def _():
                    self.hop(side, h - 1).wait_recv()
                    self.part[d] = self.part[d] + self.got[side, h - 2]
                    self.hop(side, h).start()

    def finish(self):
        a = self.at
        for side in range(2):
            u = 3 - a.t if side else a.t
            @pl.when(u > 0)
            def _():
                self.hop(side, 3).wait_recv()
            for h in range(1, 4):
                @pl.when((u < h) & ((u > 0) | (h == 3)))
                def _():
                    self.hop(side, h).wait_send()
        below = jnp.where(a.t > 0, self.got[0, 2].astype(jnp.float32), 0.0)
        above = jnp.where(a.t < 3, self.got[1, 2].astype(jnp.float32), 0.0)
        return self.part[a.t].astype(jnp.float32) + below + above

def scatter_scratch(T, R, W, kept=True):
    wa = (W + 128) // 256 * 128
    B = jnp.bfloat16
    return [pltpu.VMEM((T, 2, 2, R, W), B)] * (2 if kept else 1) + [pltpu.VMEM((T, 2, R, wa), B), pltpu.VMEM((T, 2, R, W - wa), B),
            pltpu.VMEM((T, R, wa), B), pltpu.VMEM((T, R, W - wa), B), pltpu.VMEM((2, 3, R, W), B), pltpu.VMEM((2, 3, R, W), B),
            pltpu.SemaphoreType.DMA((2, 26))] + [pltpu.SemaphoreType.DMA((4,))] * kept

class Total:
    def __init__(self, at, sources, acc, got, sems):
        self.at, self.sources, self.acc, self.got, self.sems = at, sources, acc, got, sems
        t = at.t
        self.partners = [at.core, at.xn, at.yn, (at.f, t + 1 - 2 * (t % 2)), (at.f, 3 - t)]

    def copy(self, i):
        return rdma(self.acc.at[i], self.got.at[i], self.sems.at[0, i], self.sems.at[1, i], self.partners[i])

    def start(self):
        norms, table = self.sources
        self.acc[0] = jnp.zeros_like(self.acc[0])
        self.acc[0, :8, :] = norms[...]
        self.acc[0, 8:8 + table.shape[0], :table.shape[1]] = table[...]
        self.copy(0).start()

    def step(self, i):
        self.copy(i).wait_recv()
        self.acc[i + 1] = self.acc[i] + self.got[i]
        if i < 4:
            self.copy(i + 1).start()

    def finish(self, norms_out, table_out):
        for i in range(5):
            self.copy(i).wait_send()
        norms_out[...] = self.acc[5, :8, :]
        table_out[...] = self.acc[5, 8:8 + table_out.shape[0], :table_out.shape[1]]


def total_scratch(rows, width):
    F = jnp.float32
    return [pltpu.VMEM((6, rows, width), F), pltpu.VMEM((5, rows, width), F), pltpu.SemaphoreType.DMA((2, 5))]


def tail_kernel(part_in, gqt_in, gkt_in, gvt_in, seqt_in, queryt_in, first, back_in, norms, table,
                grad_content, grad_query, sum_query, sum_key, sum_value, norms_out, table_out,
                gqt, gkt, gvt, seqt, queryt, back, weights, part, got, g1, load_sems, fold_sems, *scratch):
    rows, width = grad_content.shape
    narrow, R = width // 4, sum_query.shape[0]
    at = Place()
    loads = Loads(
        [(part_in, part), (gkt_in, gkt), (gvt_in, gvt), (seqt_in, seqt), (queryt_in, queryt), (gqt_in, gqt), (back_in, back)]
        + [(first.at[b, :, pl.ds(128, 256)], weights.at[b]) for b in range(4)], load_sems
    )
    at.greet()
    scatter, fold, total = Scatter(at, g1, None, *scratch[:8], None), Fold(at, part, got, fold_sems), Total(at, (norms, table), *scratch[8:])
    loads.wait(0)
    fold.step(1)
    total.start()

    def weight_grads(k):
        d = at.order[k]
        here = pl.ds(pl.multiple_of(d * narrow, 64), narrow)
        query = nt(seqt[:, :rows], gqt[here, :rows]) + nt(queryt[...], gqt[here, rows:])
        block = jnp.concatenate([query, nt(seqt[...], gkt[here, :]), nt(seqt[...], gvt[here, :])], axis=1)
        g1[d] = block.astype(jnp.bfloat16).reshape(2, 2, 2, R, 3 * narrow)
        scatter.start_one(k)

    loads.wait(1, 2, 3, 4, 5)
    total.step(0)
    for k in range(4):
        weight_grads(k)
        if k == 1:
            total.step(1)
    scatter.stage0(0)
    scatter.stage0(1)
    total.step(2)
    scatter.stage0(2)
    scatter.stage0(3)
    loads.wait(6, 7, 8, 9, 10)
    for s, out in enumerate((grad_content, grad_query)):
        cols = slice(s * rows, (s + 1) * rows)
        value = back[cols, :]
        for b in range(4):
            value = value + nt(gqt[b * narrow:(b + 1) * narrow, cols].T, weights[b, :, 64:256])
        out[...] = value
    fold.step(2)
    scatter.stage1(0)
    scatter.stage1(1)
    total.step(3)
    scatter.stage1(2)
    scatter.stage1(3)
    scatter.stage2(0)
    scatter.stage3(1)
    scatter.stage2(1)
    total.step(4)
    fold.step(3)
    scatter.stage3(2)
    scatter.stage2(2)
    scatter.stage2(3)
    scatter.stage3(3)
    sums = scatter.finish()
    for i, out in enumerate((sum_query, sum_key, sum_value)):
        out[...] = sums[:, i * narrow:(i + 1) * narrow]
    total.finish(norms_out, table_out)
    grad_content[...] += fold.finish()


def tail(parts, gqt, gkt, gvt, seqt, queryt, first, back, norms, table):
    width, both = gqt.shape
    rows, narrow, R = both // 2, width // 4, width // 8
    V, A = pl.BlockSpec(memory_space=pltpu.MemorySpace.VMEM), pl.BlockSpec(memory_space=pl.ANY)
    B, F, S, DMA = jnp.bfloat16, jnp.float32, jax.ShapeDtypeStruct, pltpu.SemaphoreType.DMA
    outs = [S((rows, width), F)] * 2 + [S((R, narrow), F)] * 3 + [S(norms.shape, F), S(table.shape, F)]
    return pl.pallas_call(
        tail_kernel, out_shape=tuple(outs), in_specs=[A] * 8 + [V, V], out_specs=(V,) * 7,
        scratch_shapes=[
            pltpu.VMEM(gqt.shape, B), pltpu.VMEM(gkt.shape, B), pltpu.VMEM(gvt.shape, B), pltpu.VMEM(seqt.shape, B), pltpu.VMEM(queryt.shape, B),
            pltpu.VMEM(back.shape, F),
            pltpu.VMEM((4, width, 256), B), pltpu.VMEM((4, rows, width), B), pltpu.VMEM((2, 3, rows, width), B),
            pltpu.VMEM((4, 2, 2, 2, R, 3 * narrow), B), DMA((11,)), DMA((2, 6)),
        ] + scatter_scratch(4, R, 3 * narrow, False) + total_scratch(24, width),
        compiler_params=pltpu.CompilerParams(vmem_limit_bytes=VLIM, collective_id=1, has_side_effects=True), name="tail",
    )(parts, gqt, gkt, gvt, seqt, queryt, first, back, norms, table)


def nn(a, b):
    return lax.dot_general(a, b, (((1,), (0,)), ((), ())), preferred_element_type=jnp.float32)
def nt(a, b):
    return lax.dot_general(a, b, (((1,), (1,)), ((), ())), preferred_element_type=jnp.float32)

def band_kind(i, b, nrow, nkey):
    rel = (b - i) % nkey
    if rel == 0: return 2
    if rel == nkey - 1: return 0 if i == 0 else 1
    if rel == 1: return 4 if i == nrow - 1 else 3
    return None

def wrap(value, size):
    return jnp.where(value >= size, value - size, value)


def bucket_of(offsets):
    magnitude = jnp.abs(offsets)
    far_bucket = 8 + sum((magnitude >= threshold).astype(jnp.int32) for threshold in THRESHOLDS)
    return jnp.where(magnitude < 8, magnitude, far_bucket) + jnp.where(offsets > 0, 16, 0)


def slot_bucket(slot, lanes, tp_index, tp_size):
    if slot >= 10:
        return jnp.full_like(lanes, 15 if slot == 10 else 31)
    kind, wrapped = slot // 2, slot % 2
    buckets = bucket_of(128 * ((-1, -1, 0, 1, 1)[kind] + wrapped) - lanes)
    if kind == 0:
        return jnp.where(tp_index == 0, 31, buckets)
    if kind == 4:
        return jnp.where(tp_index == tp_size - 1, 15, buckets)
    return buckets


def far_sides(nrow, nkey, tp_index):
    key_block = lax.broadcasted_iota(jnp.int32, (16, 2 * nrow * 128), 0)
    row_block = wrap(lax.broadcasted_iota(jnp.int32, (16, 2 * nrow * 128), 1) // 128, nrow)
    gap = key_block - row_block
    near = (gap == 0) | (gap == 1) | (gap == -1) | (gap == nkey - 1) | (gap == 1 - nkey) | (key_block >= nkey)
    key_place, row_place = wrap(key_block + nrow * tp_index, nkey), row_block + nrow * tp_index
    left = jnp.where(near, 0.0, jnp.where(key_place < row_place, 1.0, 0.0))
    return left, jnp.where(near, 0.0, 1.0 - left)


def prepare(nrow, nkey, tp_size, ranks, starts, table, mask, ring, vec, sides):
    tp_index = lax.axis_index("tp")
    rows, seq = nrow * 128, nkey * 128
    base = rows * tp_index
    rank_row = jnp.broadcast_to(ranks[...].astype(jnp.float32), (8, seq))
    ring[:, :seq] = rank_row
    ring[:, seq:] = rank_row

    def label(place):
        found = jnp.zeros(place.shape, jnp.int32)
        for k in range(starts.shape[1]):
            start = starts[0, k]
            found = found + jnp.where((place >= start) & (place < start + PIC), k + 1, 0)
        return found

    row_rank, row_label = [], []
    for i in range(nrow):
        row_rank.append(ring[0:1, pl.ds(pl.multiple_of(base + i * 128, 128), 128)])
        row_label.append(label(base + i * 128 + lax.broadcasted_iota(jnp.int32, (1, 128), 1)))

    def one(b, _):
        keys = pl.ds(pl.multiple_of(b * 128, 128), 128)
        rank_k = jnp.broadcast_to(ring[0:1, pl.ds(pl.multiple_of(base + b * 128, 128), 128)], (128, 128)).T
        kpos = b * 128 + lax.broadcasted_iota(jnp.int32, (128, 128), 0)
        label_k = label(wrap(base + kpos, seq))
        for i in range(nrow):
            rpos = i * 128 + lax.broadcasted_iota(jnp.int32, (128, 128), 1)
            same = (label_k == row_label[i]) & (label_k > 0)
            content = (rank_k <= row_rank[i]) | same
            strict = (rank_k < jnp.maximum(row_rank[i], 1.0)) | (same & (kpos != rpos))
            mask[keys, i * 128:(i + 1) * 128] = jnp.where(content, 0.0, NEG)
            mask[keys, rows + i * 128:rows + (i + 1) * 128] = jnp.where(strict, 0.0, NEG)
        return 0
    lax.fori_loop(0, nkey, one, 0)

    heads = table.shape[0]
    lanes = lax.broadcasted_iota(jnp.int32, (heads, 128), 1)
    columns = [jnp.broadcast_to(table[:, n:n + 1] * LOG2E, (heads, 128)) for n in range(NB)]
    for slot in range(12):
        buckets = slot_bucket(slot, lanes, tp_index, tp_size)
        values = columns[0]
        for n in range(1, NB):
            values = jnp.where(buckets == n, columns[n], values)
        for h in range(heads):
            vec[h, slot:slot + 1, :] = values[h:h + 1, :]
    sides[0], sides[1] = far_sides(nrow, nkey, tp_index)


def far_bias(vec, sides, cf, h):
    copies = cf.shape[1] // 128
    left, right = (jnp.concatenate([vec[h, slot:slot + 1, :]] * copies, axis=1) for slot in (10, 11))
    cf[...] = sides[0] * left + sides[1] * right


def prepare_scratch(nrow, nkey, heads):
    F, rows = jnp.float32, 2 * nrow * 128
    return [
        pltpu.VMEM((nkey * 128, rows), F), pltpu.VMEM((8, 2 * nkey * 128), F), pltpu.VMEM((heads, 12, 128), F),
        pltpu.VMEM((2, 16, rows), F), pltpu.VMEM((16, rows), F), pltpu.VMEM((5, 128, 128), F),
    ]


def band_tiles(band, vec, h):
    lane = lax.broadcasted_iota(jnp.int32, (128, 128), 1)
    sub = lax.broadcasted_iota(jnp.int32, (128, 128), 0)
    for k in range(5):
        direct, wrapped = (
            pltpu.roll(jnp.broadcast_to(vec[h, 2 * k + w:2 * k + w + 1, :], (128, 128)), 0, 1, stride=1, stride_axis=0)
            for w in range(2)
        )
        band[k] = jnp.where(lane >= sub, direct, wrapped)

def diagonal_sums(tile):
    lane = lax.broadcasted_iota(jnp.int32, (8, 128), 1)
    sub = lax.broadcasted_iota(jnp.int32, (8, 128), 0)
    direct = wrapped = jnp.zeros((8, 128), jnp.float32)
    for a in range(16):
        rows = tile[8 * a:8 * a + 8, :]
        kept = jnp.where(lane >= sub + 8 * a, rows, 0.0)
        left = rows - kept
        if a:
            kept, left = pltpu.roll(kept, 128 - 8 * a, 1), pltpu.roll(left, 128 - 8 * a, 1)
        direct, wrapped = direct + kept, wrapped + left
    for bit in (1, 2, 4):
        moved = (sub & bit) != 0
        direct = jnp.where(moved, pltpu.roll(direct, 128 - bit, 1), direct)
        wrapped = jnp.where(moved, pltpu.roll(wrapped, 128 - bit, 1), wrapped)
    return jnp.sum(direct, axis=0, keepdims=True), jnp.sum(wrapped, axis=0, keepdims=True)

def head_rows(ref, p, hh, cols):
    z = jnp.zeros((64, cols.stop - cols.start), jnp.bfloat16)
    rows = ref[pl.ds(pl.multiple_of((2 * p + hh) * 64, 64), 64), cols]
    return jnp.concatenate([rows, z] if hh == 0 else [z, rows], axis=0)

def attend_rows(nrow, nkey, kp, vt, qt, ot, lse, t, prepared, exchange):
    mask, _, vec, sides, cf, band = prepared
    ones = jnp.ones((16, 256), jnp.bfloat16)
    nchunk = 2 * nrow * 128 // 256
    def pair(p, _):
        for hh in range(2):
            h = 2 * p + hh
            exchange(h)
            hrows = pl.ds(pl.multiple_of(h * 64, 64), 64)
            band_tiles(band, vec, h)
            far_bias(vec, sides, cf, h)
            for c in range(nchunk):
                cols = slice(c * 256, (c + 1) * 256)
                qh = head_rows(qt, p, hh, cols)
                m8 = jnp.full((8, 256), -jnp.inf, jnp.float32)
                for b in range(nkey):
                    s = nn(kp[p, b * 128:(b + 1) * 128, :], qh)
                    s = s + mask[b * 128:(b + 1) * 128, cols]
                    kinds = [band_kind((2 * c + k) % nrow, b, nrow, nkey) for k in range(2)]
                    if any(k is not None for k in kinds):
                        s = jnp.concatenate([s[:, k * 128:(k + 1) * 128] + (band[kinds[k]] if kinds[k] is not None else 0.0) for k in range(2)], axis=1)
                    t[c, b * 128:(b + 1) * 128, :] = s
                    m8 = jnp.maximum(m8, jnp.max(s.reshape(16, 8, 256), axis=0) + cf[b:b + 1, cols])
                m = jnp.max(m8, axis=0, keepdims=True)
                acc = jnp.zeros((80, 256), jnp.float32)
                for g in range(nkey // 2):
                    ps = []
                    for b in (2 * g, 2 * g + 1):
                        ps.append(jnp.exp2(t[c, b * 128:(b + 1) * 128, :] - (m - cf[b:b + 1, cols])).astype(jnp.bfloat16))
                    lhs = jnp.concatenate([vt[hrows, g * 256:(g + 1) * 256], ones], axis=0)
                    acc = acc + nn(lhs, jnp.concatenate(ps, axis=0))
                l = acc[64:65, :]
                ot[hrows, cols] = (acc[:64, :] / l).astype(jnp.bfloat16)
                lse[h, 0:1, cols] = m + jnp.log2(l)
        return 0
    lax.fori_loop(0, kp.shape[0], pair, 0)

def fwd_kernel(nrow, nkey, tp_size, ranks, starts, table, kp, vt, qt, ot, lse, t, *prepared):
    prepare(nrow, nkey, tp_size, ranks, starts, table, *prepared[:4])
    attend_rows(nrow, nkey, kp, vt, qt, ot, lse, t, prepared, lambda h: None)


def attend_fwd(tp_size, ranks, starts, table, kp, vt, qt):
    pairs, seq, _ = kp.shape
    rows = qt.shape[1]
    nrow, nkey = rows // 256, seq // 128
    V, M = pl.BlockSpec(memory_space=pltpu.MemorySpace.VMEM), pl.BlockSpec(memory_space=pltpu.MemorySpace.SMEM)
    return pl.pallas_call(
        functools.partial(fwd_kernel, nrow, nkey, tp_size),
        out_shape=(jax.ShapeDtypeStruct(qt.shape, jnp.bfloat16), jax.ShapeDtypeStruct((2 * pairs, 1, rows), jnp.float32)),
        in_specs=[V, M, V, V, V, V], out_specs=(V, V),
        scratch_shapes=[pltpu.VMEM((rows // 256, seq, 256), jnp.float32)] + prepare_scratch(nrow, nkey, 2 * pairs),
        compiler_params=pltpu.CompilerParams(vmem_limit_bytes=VLIM),
        name="attend_fwd",
    )(ranks, starts, table, kp, vt, qt)


class Gather:
    def __init__(self, at, shard, g, wa, sems, own_sem):
        self.at, self.shard, self.g, self.wa, self.sems, self.own_sem = at, shard, g, wa, sems, own_sem
        self.blocks = at.order[::-1]

    def send(self, i, src, dst, there):
        return rdma(src, dst, self.sems.at[0, i], self.sems.at[1, i], there)

    def along_z(self, b, upward):
        a = self.at
        here = self.g.at[b, a.y, a.x, a.c]
        return self.send(b + (0 if upward else 4), here, here, a.up if upward else a.down)

    def first(self, b):
        a, wa = self.at, self.wa
        left, right = (self.g.at[b, a.y, a.x, a.c, :, cols] for cols in (slice(0, wa), slice(wa, None)))
        return self.send(8 + b, left, left, a.xn), self.send(12 + b, right, right, a.yn)

    def second(self, b):
        a, wa = self.at, self.wa
        left, right = self.g.at[b, a.y, :, a.c, :, :wa], self.g.at[b, :, a.x, a.c, :, wa:]
        return self.send(16 + b, left, left, a.yn), self.send(20 + b, right, right, a.xn)

    def across(self, b):
        a = self.at
        here = self.g.at[b, :, :, a.c]
        return self.send(24 + b, here, here, a.core)

    def own(self):
        a = self.at
        return pltpu.make_async_copy(self.shard, self.g.at[a.t, a.y, a.x, a.c], self.own_sem)

    def begin(self):
        self.own().start()
        self.own().wait()
        for c in self.first(self.at.t):
            c.start()

    def begin_z(self):
        a = self.at
        @pl.when(a.t < 3)
        def _():
            self.along_z(a.t, True).start()
        @pl.when(a.t > 0)
        def _():
            self.along_z(a.t, False).start()

    def arrive(self, j):
        a, b = self.at, self.blocks[j]
        @pl.when(b < a.t)
        def _():
            self.along_z(b, True).wait_recv()
        @pl.when(b > a.t)
        def _():
            self.along_z(b, False).wait_recv()
        @pl.when((b < a.t) & (a.t < 3))
        def _():
            self.along_z(b, True).start()
        @pl.when((b > a.t) & (a.t > 0))
        def _():
            self.along_z(b, False).start()
        for c in self.first(b):
            c.start()

    def step1(self, j):
        b = self.blocks[j]
        for c in self.first(b):
            c.wait_recv()
        for c in self.second(b):
            c.start()

    def step2(self, j):
        b = self.blocks[j]
        for c in self.second(b):
            c.wait_recv()
        self.across(b).start()

    def step3(self, j):
        self.across(self.blocks[j]).wait_recv()

    def finish(self):
        a = self.at
        for b in range(4):
            @pl.when((b <= a.t) & (a.t < 3))
            def _():
                self.along_z(b, True).wait_send()
            @pl.when((b >= a.t) & (a.t > 0))
            def _():
                self.along_z(b, False).wait_send()
            for c in (*self.first(b), *self.second(b), self.across(b)):
                c.wait_send()


class Chain:
    def __init__(self, at, seq, sems, pieces):
        self.at, self.seq, self.sems, self.pieces = at, seq, sems, pieces
        self.blocks = at.order[::-1]

    def move(self, b, upward, s):
        a = self.at
        i = (b + (0 if upward else 4)) * self.pieces + s
        there = a.t + 1 if upward else a.t - 1
        size = self.seq.shape[1] // self.pieces
        part = slice(s * size, (s + 1) * size)
        return rdma(self.seq.at[(b - a.t + 4) % 4, part], self.seq.at[(b - there + 4) % 4, part], self.sems.at[0, i], self.sems.at[1, i], (a.f, there))

    def begin(self):
        a = self.at
        for s in range(self.pieces):
            @pl.when(a.t < 3)
            def _():
                self.move(a.t, True, s).start()
            @pl.when(a.t > 0)
            def _():
                self.move(a.t, False, s).start()

    def arrive(self, j):
        a, b = self.at, self.blocks[j]
        for s in range(self.pieces):
            @pl.when(b < a.t)
            def _():
                self.move(b, True, s).wait_recv()
            @pl.when(b > a.t)
            def _():
                self.move(b, False, s).wait_recv()
            @pl.when((b < a.t) & (a.t < 3))
            def _():
                self.move(b, True, s).start()
            @pl.when((b > a.t) & (a.t > 0))
            def _():
                self.move(b, False, s).start()

    def finish(self):
        a = self.at
        for b in range(4):
            for s in range(self.pieces):
                @pl.when((b <= a.t) & (a.t < 3))
                def _():
                    self.move(b, True, s).wait_send()
                @pl.when((b >= a.t) & (a.t > 0))
                def _():
                    self.move(b, False, s).wait_send()


def front_kernel(nrow, nkey, content, query, w_query, w_key, w_value, w_out, w_in, w_down, ranks, starts, table,
                 ot, lse, seqt_out, queryt_out, kp_out, vp_out, kt_out, qt_out, w1_out, w2_out,
                 shard1, shard2, seq, seqt, queryt, w1, w2, w1t, kp, vp, kt, vt, qt, t,
                 sems1, sems2, semsc, own_sems, out_sems, *prepared):
    at = Place()
    rows = nrow * 128
    pairs = kp.shape[0]
    narrow = shard1.shape[1] // 4
    width = content.shape[1]
    weights1 = Gather(at, shard1, w1, shard1.shape[1] // 2, sems1, own_sems.at[0])
    weights2 = Gather(at, shard2, w2, shard2.shape[1] // 2, sems2, own_sems.at[1])
    chain = Chain(at, seq, semsc, PIECES)
    shard1[...] = jnp.concatenate([w_out[...].T, w_query[...], w_key[...], w_value[...]], axis=1)
    shard2[:, :w_in.shape[1]] = w_in[...]
    shard2[:, w_in.shape[1]:] = w_down[...]
    seq[0] = content[...]
    at.greet()
    weights1.begin()
    weights1.begin_z()
    weights1.arrive(1)
    weights1.step1(0)
    weights1.arrive(2)
    weights1.step1(1)
    weights1.step2(0)
    weights1.arrive(3)
    chain.begin()
    weights2.begin()
    weights2.begin_z()
    weights1.step1(2)
    weights1.step2(1)
    weights1.step1(3)
    prepare(nrow, nkey, 4, ranks, starts, table, *prepared[:4])
    weights1.step2(2)
    weights1.step2(3)
    for j in range(4):
        weights1.step3(j)

    scale = HEAD ** -0.5 * LOG2E
    for tt in range(4):
        block = w1[tt].reshape(width, 4 * narrow)
        w1t[tt] = block[:, narrow:].T
        for s, x in enumerate((content, query)):
            q = nt(w1t[tt, :narrow, :], x[...])
            qt[tt * narrow:(tt + 1) * narrow, s * rows:(s + 1) * rows] = (q * scale).astype(jnp.bfloat16)

    def project(r):
        x = seq[r]
        cols = pl.ds(pl.multiple_of(r * rows, 128), rows)
        seqt[:, cols] = x.T
        for i, (across, upright) in enumerate(((kp, kt), (vp, vt))):
            for tt in range(4):
                out = nt(w1t[tt, (i + 1) * narrow:(i + 2) * narrow, :], x)
                upright[tt * narrow:(tt + 1) * narrow, cols] = out.astype(jnp.bfloat16)
            for u in range(2):
                halves = [
                    nn(x, w1[2 * u + v].reshape(width, 4 * narrow)[:, (i + 2) * narrow:(i + 3) * narrow]) for v in range(2)
                ]
                joined = jnp.concatenate(halves, axis=1).astype(jnp.bfloat16)
                for p in range(pairs // 2):
                    across[u * (pairs // 2) + p, cols, :] = joined[:, p * 128:(p + 1) * 128]

    queryt[...] = query[...].T
    project(0)
    chain.arrive(1)
    weights2.arrive(1)
    weights2.step1(0)
    project((chain.blocks[1] - at.t + 4) % 4)
    chain.arrive(2)
    weights2.step2(0)
    weights2.step1(1)
    weights2.arrive(2)
    project((chain.blocks[2] - at.t + 4) % 4)
    chain.arrive(3)
    weights2.step2(1)
    weights2.step1(2)
    project((chain.blocks[3] - at.t + 4) % 4)

    outs = [
        pltpu.make_async_copy(src, dst, out_sems.at[i])
        for i, (src, dst) in enumerate(((seqt, seqt_out), (queryt, queryt_out), (kp, kp_out), (vp, vp_out), (kt, kt_out), (qt, qt_out), (w1, w1_out)))
    ]
    for c in outs:
        c.start()

    def second_out(j):
        b = weights2.blocks[j]
        return pltpu.make_async_copy(w2.at[b], w2_out.at[b], out_sems.at[7 + j])

    def exchange(h):
        steps = (
            (weights2.arrive, 3, 1),
            (weights2.step2, 2, 3),
            (weights2.step1, 3, 6),
            (weights2.step2, 3, 10),
        )
        for step, j, place in steps:
            @pl.when(h == place)
            def _():
                step(j)

    attend_rows(nrow, nkey, kp, vt, qt, ot, lse, t, prepared, exchange)
    for j in range(4):
        weights2.step3(j)
        second_out(j).start()
    for c in outs:
        c.wait()
    for j in range(4):
        second_out(j).wait()
    weights1.finish()
    weights2.finish()
    chain.finish()


def front(content, query, w_query, w_key, w_value, w_out, w_in, w_down, ranks, starts, table):
    rows, width = content.shape
    heads, seq_len = table.shape[0], ranks.shape[1]
    pairs, (R, narrow), wide = heads // 2, w_query.shape, w_in.shape[1]
    nrow, nkey = rows // 128, seq_len // 128
    V, A = pl.BlockSpec(memory_space=pltpu.MemorySpace.VMEM), pl.BlockSpec(memory_space=pl.ANY)
    B, F, S, DMA = jnp.bfloat16, jnp.float32, jax.ShapeDtypeStruct, pltpu.SemaphoreType.DMA
    full1, full2 = (4, 2, 2, 2, R, 4 * narrow), (4, 2, 2, 2, R, 2 * wide)
    kept = [((width, seq_len), B), ((width, rows), B), ((pairs, seq_len, 128), B), ((pairs, seq_len, 128), B), ((width, seq_len), B), ((width, 2 * rows), B), (full1, B)]
    outs = [S((width, 2 * rows), B), S((heads, 1, 2 * rows), F)] + [S(*k) for k in kept] + [S(full2, B)]
    scratch = [pltpu.VMEM((R, 4 * narrow), B), pltpu.VMEM((R, 2 * wide), B), pltpu.VMEM((4, rows, width), B), pltpu.VMEM(*kept[0]), pltpu.VMEM(*kept[1]), pltpu.VMEM(full1, B), pltpu.VMEM(full2, B),
               pltpu.VMEM((4, 3 * narrow, width), B), pltpu.VMEM(*kept[2]), pltpu.VMEM(*kept[3]),
               pltpu.VMEM(*kept[4]), pltpu.VMEM(*kept[4]), pltpu.VMEM(*kept[5]),
               pltpu.VMEM((2 * rows // 256, seq_len, 256), F),
               DMA((2, 28)), DMA((2, 28)), DMA((2, 8 * PIECES)), DMA((2,)), DMA((11,))] + prepare_scratch(nrow, nkey, heads)
    return pl.pallas_call(
        functools.partial(front_kernel, nrow, nkey),
        out_shape=tuple(outs), in_specs=[V] * 9 + [pl.BlockSpec(memory_space=pltpu.MemorySpace.SMEM), V], out_specs=tuple([V, V] + [A] * 8), scratch_shapes=scratch,
        compiler_params=pltpu.CompilerParams(vmem_limit_bytes=VLIM, collective_id=3, has_side_effects=True), name="front",
    )(content, query, w_query, w_key, w_value, w_out, w_in, w_down, ranks, starts, table)


def bwd_kernel(nrow, nkey, tp_size, fused, *refs):
    if fused:
        ranks, starts, table, kp, vp, kt, qt, ot, got, lse, g, first, gqt, gkt, gvt, back_table, sum_in, sum_down, sum_out, part, gq, bacc, diag, weights, *scratch = refs
        prepared, kept, load_sems, scratch = scratch[:6], scratch[6:12], scratch[12], scratch[13:]
        loads = Loads(list(zip((kp, vp, kt, qt, ot, got), kept)) + [(first.at[b, :, pl.ds(384, 384)], weights.at[b]) for b in range(4)], load_sems)
        kp, vp, kt, qt, ot, got = kept
        at = Place()
        at.greet()
        scatter = Scatter(at, g, *scratch)
        scatter.start()
    else:
        ranks, starts, table, kp, vp, kt, qt, ot, got, lse, gqt, gkt, gvt, back_table, gq, bacc, diag, *prepared = refs
    mask, _, vec, sides, cf, band = prepared
    prepare(nrow, nkey, tp_size, ranks, starts, table, *prepared[:4])
    lane_row = lax.broadcasted_iota(jnp.int32, (1, 128), 1)
    if fused:
        loads.wait(0, 1, 2, 3, 4, 5)

    def exchange(h):
        if not fused:
            return
        steps = (
            (scatter.stage0, 0, 0), (scatter.stage0, 1, 1), (scatter.stage1, 0, 3), (scatter.stage0, 2, 3), (scatter.stage2, 0, 6), (scatter.stage3, 1, 6),
            (scatter.stage1, 1, 6), (scatter.stage0, 3, 6), (scatter.stage1, 2, 8), (scatter.stage2, 1, 9), (scatter.stage3, 2, 9), (scatter.stage1, 3, 11),
        )
        for step, k, place in steps:
            @pl.when(h == place)
            def _():
                step(k)

    rows = 2 * nrow * 128
    nchunk = rows // 256
    full = slice(0, rows)
    block_of = lax.broadcasted_iota(jnp.int32, (16, 256), 0)
    half_of = lax.broadcasted_iota(jnp.int32, (16, 256), 1) // 128
    def pair(p, _):
        for hh in range(2):
            h = 2 * p + hh
            exchange(h)
            hrows = pl.ds(pl.multiple_of(h * 64, 64), 64)
            band_tiles(band, vec, h)
            far_bias(vec, sides, cf, h)
            q_h = qt[hrows, :]
            go_h = got[hrows, :]
            delta = jnp.sum(ot[hrows, :].astype(jnp.float32) * go_h.astype(jnp.float32), axis=0, keepdims=True)
            for k in range(5):
                bacc[k] = jnp.zeros((128, 128), jnp.float32)
            gq[...] = jnp.zeros_like(gq)
            qm = head_rows(qt, p, hh, full)
            gm = head_rows(got, p, hh, full)
            for g in range(nkey // 2):
                pp, gg = [], []
                for c in range(nchunk):
                    cols = slice(c * 256, (c + 1) * 256)
                    pc, gc = [], []
                    for b in (2 * g, 2 * g + 1):
                        keys = slice(b * 128, (b + 1) * 128)
                        s = nn(kp[p, keys, :], qm[:, cols])
                        dp = nn(vp[p, keys, :], gm[:, cols])
                        s = s + mask[keys, cols]
                        kinds = [band_kind((2 * c + k) % nrow, b, nrow, nkey) for k in range(2)]
                        if any(k is not None for k in kinds):
                            s = jnp.concatenate([s[:, k * 128:(k + 1) * 128] + (band[kinds[k]] if kinds[k] is not None else 0.0) for k in range(2)], axis=1)
                        pr = jnp.exp2(s - (lse[h, 0:1, cols] - cf[b:b + 1, cols]))
                        gs = pr * (dp - delta[:, cols])
                        for k in range(2):
                            if kinds[k] is not None:
                                bacc[kinds[k]] += gs[:, k * 128:(k + 1) * 128]
                        pc.append(pr.astype(jnp.bfloat16))
                        gc.append(gs.astype(jnp.bfloat16))
                    pp.append(jnp.concatenate(pc, axis=0))
                    gg.append(jnp.concatenate(gc, axis=0))
                pall = jnp.concatenate(pp, axis=1)
                gall = jnp.concatenate(gg, axis=1)
                keys = slice(g * 256, (g + 1) * 256)
                onehot = (block_of == 2 * g + half_of).astype(jnp.bfloat16)
                gq[...] += nn(jnp.concatenate([kt[hrows, keys], onehot], axis=0), gall)
                gkt[hrows, keys] = (nt(q_h, gall) * LN2).astype(jnp.bfloat16)
                gvt[hrows, keys] = nt(go_h, pall).astype(jnp.bfloat16)
            gqt[hrows, :] = (gq[:64, :] * 0.125).astype(jnp.bfloat16)
            for k in range(5):
                direct, wrapped = diagonal_sums(bacc[k])
                diag[h, 0:1, 256 * k:256 * k + 128] = direct
                diag[h, 0:1, 256 * k + 128:256 * k + 256] = wrapped
            for s in range(2):
                side = jnp.sum(jnp.sum(gq[64:80, :] * sides[s], axis=0, keepdims=True), axis=1, keepdims=True)
                diag[h, 0:1, 1280 + 128 * s:1408 + 128 * s] = jnp.where(lane_row == 0, side, 0.0)
        return 0
    lax.fori_loop(0, kp.shape[0], pair, 0)
    tp_index = lax.axis_index("tp")
    places = lax.broadcasted_iota(jnp.int32, (128, 128), 0)
    numbers = lax.broadcasted_iota(jnp.int32, (128, 128), 1)
    sums = jnp.concatenate([diag[h] for h in range(diag.shape[0])], axis=0)
    total = jnp.zeros((diag.shape[0], 128), jnp.float32)
    for slot in range(12):
        one_hot = jnp.where(slot_bucket(slot, places, tp_index, tp_size) == numbers, 1.0, 0.0)
        total = total + jnp.dot(
            sums[:, slot * 128:(slot + 1) * 128], one_hot, precision=lax.Precision.HIGHEST, preferred_element_type=jnp.float32
        )
    back_table[...] = total
    if fused:
        scatter.stage2(2)
        scatter.stage3(3)
        loads.wait(6, 7, 8, 9)
        span, narrow = part.shape[1], kt.shape[0] // 4
        for d in range(4):
            here = pl.ds(pl.multiple_of(((d - at.t + 4) % 4) * span, 128), span)
            value = jnp.zeros(part.shape[1:], jnp.float32)
            for b in range(4):
                block = slice(b * narrow, (b + 1) * narrow)
                value = value + nt(jnp.concatenate([gkt[block, here], gvt[block, here]], axis=0).T, weights[b])
            part[d] = value.astype(jnp.bfloat16)
        scatter.stage2(3)
        sums = scatter.finish()
        wide = sum_in.shape[1]
        sum_in[...] = sums[:, :wide]
        sum_down[...] = sums[:, wide:2 * wide]
        sum_out[...] = sums[:, 2 * wide:].T


def attend_bwd(tp_size, ranks, starts, table, kp, vp, kt, qt, ot, got, lse, g=None, first=None):
    pairs, seq, _ = kp.shape
    rows = qt.shape[1]
    heads = 2 * pairs
    nrow, nkey = rows // 256, seq // 128
    V, M = pl.BlockSpec(memory_space=pltpu.MemorySpace.VMEM), pl.BlockSpec(memory_space=pltpu.MemorySpace.SMEM)
    S, F = jax.ShapeDtypeStruct, jnp.float32
    fused = g is not None
    outs = [S(qt.shape, jnp.bfloat16), S(kt.shape, jnp.bfloat16), S(kt.shape, jnp.bfloat16), S((heads, 128), F)]
    scratch = [pltpu.VMEM((80, rows), F), pltpu.VMEM((5, 128, 128), F), pltpu.VMEM((heads, 1, 1536), F)] + prepare_scratch(nrow, nkey, heads)
    params = dict(vmem_limit_bytes=VLIM)
    args = (ranks, starts, table, kp, vp, kt, qt, ot, got, lse)
    specs = [V, M] + [V] * 8
    if fused:
        narrow = kt.shape[0] // 4
        wide = (g.shape[5] - narrow) // 2
        outs += [S((g.shape[4], wide), F), S((g.shape[4], wide), F), S((narrow, g.shape[4]), F), S((4, rows // 2, kt.shape[0]), jnp.bfloat16)]
        scratch[3:3] = [pltpu.VMEM((4, kt.shape[0], 2 * narrow), jnp.bfloat16)]
        scratch += [pltpu.VMEM(a.shape, a.dtype) for a in (kp, vp, kt, qt, ot, got)] + [pltpu.SemaphoreType.DMA((10,))]
        scratch += scatter_scratch(g.shape[0], g.shape[4], g.shape[5])
        params.update(collective_id=2, has_side_effects=True)
        args += (g, first)
        A = pl.BlockSpec(memory_space=pl.ANY)
        specs = specs[:3] + [A] * 6 + [V, A, A]
    return pl.pallas_call(
        functools.partial(bwd_kernel, nrow, nkey, tp_size, fused),
        out_shape=tuple(outs), in_specs=specs, out_specs=(V,) * len(outs), scratch_shapes=scratch,
        compiler_params=pltpu.CompilerParams(**params), name="attend_bwd",
    )(*args)


def norm(residual):
    centered = residual - jnp.mean(residual, axis=-1, keepdims=True)
    scale = lax.rsqrt(jnp.mean(centered * centered, axis=-1, keepdims=True) + EPSILON)
    return centered * scale, scale


def norm_step(cotangent, normal, scale, gain):
    inner = cotangent * gain
    mean_inner = jnp.mean(inner, axis=-1, keepdims=True)
    mean_cross = jnp.mean(inner * normal, axis=-1, keepdims=True)
    return scale * (inner - mean_inner - normal * mean_cross)


def middle_kernel(chunk, ot_in, content, query, first, second_in, gain1, shift1, gain2, shift2, ranks, up_content, up_query,
                  content_out, query_out, grads, back, got, sums,
                  ot, second, x, up, wot, wo_block, onat, n1bt, gft, gat, hidden, slope, gu, out2, stage, sems, out_sems):
    rows = content.shape[0]
    seq, width = ranks.shape[1], content.shape[1]
    narrow, wide = width // 4, second.shape[2] // 2
    loads = Loads(
        [(first.at[t, :, pl.ds(0, 256)], wo_block.at[t]) for t in range(4)] + [(ot_in, ot)]
        + [(second_in.at[t], second.at[t]) for t in range(4)], sems
    )
    base = rows * lax.axis_index("tp")
    x[:rows] = content[...]
    x[rows:] = query[...]
    up[:rows] = up_content[...].astype(jnp.float32)
    for i in range(rows // 128):
        rank = ranks[0:1, pl.ds(pl.multiple_of(base + i * 128, 128), 128)].astype(jnp.float32)
        rank = jnp.broadcast_to(rank, (128, 128)).T
        kept = jnp.where(rank >= seq - seq * 15 // 100, 1.0, 0.0)
        up[rows + i * 128:rows + (i + 1) * 128, :] = up_query[i * 128:(i + 1) * 128, :].astype(jnp.float32) * jnp.concatenate([kept] * (width // 128), axis=1)
    loads.wait(0, 1, 2, 3, 4)
    wot[...] = jnp.concatenate([wo_block[t, :, :narrow] for t in range(4)], axis=1)
    sums[...] = jnp.zeros_like(sums)
    gain1, shift1, gain2, shift2 = (ref[...].reshape(1, width) for ref in (gain1, shift1, gain2, shift2))

    def one(i, _):
        here = pl.ds(pl.multiple_of(i * chunk, chunk), chunk)
        mixed = ot[:, here].T
        onat[here, :] = mixed
        normal1, scale1 = norm(x[here, :].astype(jnp.float32) + nt(mixed, wot[...]))
        normed = normal1 * gain1 + shift1
        low = normed.astype(jnp.bfloat16)
        n1bt[:, here] = low.T
        total = normed
        for t in range(4):
            @pl.when(i == 0)
            def _():
                loads.wait(5 + t)
            lifted = nn(low, second[t, :, :wide])
            phi = 0.5 + 0.5 * lax.erf(lifted * (0.5 ** 0.5))
            act = (lifted * phi).astype(jnp.bfloat16)
            hidden[t, here, :] = act
            slope[t] = phi + lifted * (jnp.exp(-0.5 * lifted * lifted) * 0.3989422804014327)
            total = total + nt(act, second[t, :, wide:])
        normal2, scale2 = norm(total)
        out2[here, :] = (normal2 * gain2 + shift2).astype(jnp.bfloat16)
        cotangent = up[here, :]
        sums[2:3, :] += jnp.sum(cotangent * normal2, axis=0, keepdims=True)
        sums[3:4, :] += jnp.sum(cotangent, axis=0, keepdims=True)
        back2 = norm_step(cotangent, normal2, scale2, gain2)
        gf = back2.astype(jnp.bfloat16)
        gft[:, here] = gf.T
        total = back2
        for t in range(4):
            g = (slope[t] * nn(gf, second[t, :, wide:])).astype(jnp.bfloat16)
            gu[t, here, :] = g
            total = total + nt(g, second[t, :, :wide])
        sums[0:1, :] += jnp.sum(total * normal1, axis=0, keepdims=True)
        sums[1:2, :] += jnp.sum(total, axis=0, keepdims=True)
        back1 = norm_step(total, normal1, scale1, gain1)
        back[here, :] = back1
        ga = back1.astype(jnp.bfloat16)
        gat[:, here] = ga.T
        got[:, here] = nn(ga, wot[...]).astype(jnp.bfloat16).T
        return 0

    lax.fori_loop(0, 2 * rows // chunk, one, 0)
    content_out[...] = out2[:rows]
    query_out[...] = out2[rows:]
    for t in range(4):
        wo_block[t, :, :narrow] = nn(gat[...], onat[:, t * narrow:(t + 1) * narrow]).astype(jnp.bfloat16)

    def send(t):
        return pltpu.make_async_copy(stage.at[t % 2], grads.at[t], out_sems.at[t % 2])

    for t in range(4):
        if t >= 2:
            send(t - 2).wait()
        stage[t % 2, :, :wide] = nn(n1bt[...], gu[t]).astype(jnp.bfloat16)
        stage[t % 2, :, wide:2 * wide] = nn(gft[...], hidden[t]).astype(jnp.bfloat16)
        stage[t % 2, :, 2 * wide:] = wo_block[t, :, :narrow]
        send(t).start()
    for t in (2, 3):
        send(t).wait()


def middle(ot, content, query, first, second, norms, ranks, up_content, up_query):
    rows, width = content.shape
    narrow, wide = width // 4, second.shape[2] // 2
    both, chunk = 2 * rows, rows
    V, A = pl.BlockSpec(memory_space=pltpu.MemorySpace.VMEM), pl.BlockSpec(memory_space=pl.ANY)
    B, F, S, DMA = jnp.bfloat16, jnp.float32, jax.ShapeDtypeStruct, pltpu.SemaphoreType.DMA
    return pl.pallas_call(
        functools.partial(middle_kernel, chunk),
        out_shape=(S((rows, width), B), S((rows, width), B), S((4, width, 2 * wide + narrow), B), S((both, width), F), S((width, both), B), S((8, width), F)),
        in_specs=[A, V, V, A, A] + [V] * 7, out_specs=(V, V, A, V, V, V),
        scratch_shapes=[
            pltpu.VMEM(ot.shape, B), pltpu.VMEM(second.shape, B),
            pltpu.VMEM((both, width), B), pltpu.VMEM((both, width), F), pltpu.VMEM((width, width), B), pltpu.VMEM((4, width, 256), B),
            pltpu.VMEM((both, width), B), pltpu.VMEM((width, both), B), pltpu.VMEM((width, both), B), pltpu.VMEM((width, both), B),
            pltpu.VMEM((4, both, wide), B), pltpu.VMEM((4, chunk, wide), F), pltpu.VMEM((4, both, wide), B), pltpu.VMEM((both, width), B),
            pltpu.VMEM((2, width, 2 * wide + narrow), B), DMA((9,)), DMA((2,)),
        ],
        compiler_params=pltpu.CompilerParams(vmem_limit_bytes=VLIM), name="middle",
    )(ot, content, query, first, second, *norms, ranks, up_content, up_query)


def finish_kernel(count, *refs):
    sources, norms, outs, held, sems = refs[:count], refs[count], refs[count + 1:2 * count + 5], refs[2 * count + 5:-1], refs[-1]
    loads = [pltpu.make_async_copy(src, mid, sems.at[0, i]) for i, (src, mid) in enumerate(zip(sources, held))]
    stores = [pltpu.make_async_copy(mid, dst, sems.at[1, i]) for i, (mid, dst) in enumerate(zip(held, outs))]
    for c in loads:
        c.start()
    for i in range(4):
        outs[count + i][...] = norms[i:i + 1, :].reshape(norms.shape[1])
    for load, store in zip(loads, stores):
        load.wait()
        store.start()
    for c in stores:
        c.wait()


def finish(arrays, norms):
    V, A, S = pl.BlockSpec(memory_space=pltpu.MemorySpace.VMEM), pl.BlockSpec(memory_space=pl.ANY), jax.ShapeDtypeStruct
    count = len(arrays)
    return pl.pallas_call(
        functools.partial(finish_kernel, count),
        out_shape=tuple(S(a.shape, a.dtype) for a in arrays) + tuple(S((norms.shape[1],), norms.dtype) for _ in range(4)),
        in_specs=[A] * count + [V], out_specs=(A,) * count + (V,) * 4, scratch_shapes=[pltpu.VMEM(a.shape, a.dtype) for a in arrays] + [pltpu.SemaphoreType.DMA((2, count))],
        compiler_params=pltpu.CompilerParams(vmem_limit_bytes=VLIM), name="finish",
    )(*arrays, norms)


def dot(spec, a, b):
    return jnp.einsum(spec, a, b, preferred_element_type=jnp.float32)


def norm_stats(residual):
    centered = residual - jnp.mean(residual, axis=-1, keepdims=True)
    scale = lax.rsqrt(jnp.mean(centered * centered, axis=-1, keepdims=True) + EPSILON)
    return centered * scale, scale


def norm_back(cotangent, normal, scale, gain):
    inner = cotangent * gain
    mean_inner = jnp.mean(inner, axis=-1, keepdims=True)
    mean_cross = jnp.mean(inner * normal, axis=-1, keepdims=True)
    back = scale * (inner - mean_inner - normal * mean_cross)
    return back, jnp.sum(cotangent * normal, axis=0), jnp.sum(cotangent, axis=0)


def local(
    tp_size, own_exchange, content, query, w_query, w_key, w_value, w_out, w_in, w_down, gain_first, shift_first,
    gain_second, shift_second, bias_table, ranks, span_starts, upstream_content, upstream_query,
):
    rows, width = content.shape
    seq = ranks.shape[1]
    heads = bias_table.shape[0]
    pairs = heads // 2
    tp_index = lax.axis_index("tp")
    both_axes = ("tp", "fsdp")
    narrow = w_query.shape[1]

    def gather(parts):
        shard = jnp.concatenate(parts, axis=1)
        return lax.all_gather(shard, both_axes, axis=0, tiled=True).reshape(tp_size, width, shard.shape[1])

    wide = w_in.shape[1]
    shift = -rows * tp_index
    both = jnp.concatenate([content, query], axis=0)
    if own_exchange:
        ot, lse, seqt, queryt, kp, vp, kt, qt, first, second = front(
            content, query, w_query, w_key, w_value, w_out, w_in, w_down.T, ranks, span_starts, bias_table
        )
        first, second = first.reshape(tp_size, width, 4 * narrow), second.reshape(tp_size, width, 2 * wide)
    else:
        first, second = gather([w_out.T, w_query, w_key, w_value]), gather([w_in, w_down.T])
    wo, wq, wk, wv = (first[:, :, i * narrow:(i + 1) * narrow] for i in range(4))
    wi, wd = second[:, :, :wide], second[:, :, wide:]
    if not own_exchange:
        seq_rot = jnp.roll(lax.all_gather(content, "tp", axis=0, tiled=True), shift, axis=0)
        qt = (dot("tdc,rd->tcr", wq, both) * (HEAD ** -0.5 * LOG2E)).astype(jnp.bfloat16).reshape(width, 2 * rows)
        kt = dot("tdc,rd->tcr", wk, seq_rot).astype(jnp.bfloat16).reshape(width, seq)
        vt = dot("tdc,rd->tcr", wv, seq_rot).astype(jnp.bfloat16).reshape(width, seq)
        kp = jnp.swapaxes(kt.reshape(pairs, 128, seq), 1, 2)
        vp = jnp.swapaxes(vt.reshape(pairs, 128, seq), 1, 2)
        ot, lse = attend_fwd(tp_size, ranks, span_starts, bias_table, kp, vt, qt)

    if own_exchange:
        norms = [gain_first, shift_first, gain_second, shift_second]
        content_out, query_out, grad_second, back_first, got, norm_stack = middle(
            ot, content, query, first, second, norms, ranks, upstream_content, upstream_query
        )
    else:
        ot_blocks = ot.reshape(tp_size, narrow, 2 * rows)
        residual_first = both.astype(jnp.float32) + dot("tcr,tmc->rm", ot_blocks, wo)
        normal_first, scale_first = norm_stats(residual_first)
        normed_first = normal_first * gain_first + shift_first
        low_first = normed_first.astype(jnp.bfloat16)
        lifted = dot("rd,tdf->trf", low_first, wi)
        phi = 0.5 * (1.0 + lax.erf(lifted * (0.5 ** 0.5)))
        hidden = (lifted * phi).astype(jnp.bfloat16)
        slope = phi + lifted * jnp.exp(-0.5 * lifted * lifted) * 0.3989422804014327
        residual_second = normed_first + dot("trf,tmf->rm", hidden, wd)
        normal_second, scale_second = norm_stats(residual_second)
        normed_second = normal_second * gain_second + shift_second
        rank_rows = lax.dynamic_slice_in_dim(ranks[0], rows * tp_index, rows)
        predicted = (rank_rows >= seq - seq * 15 // 100).astype(jnp.float32)
        upstream = jnp.concatenate(
            [upstream_content.astype(jnp.float32), upstream_query.astype(jnp.float32) * predicted[:, None]], axis=0
        )
        back_second, grad_gain_second, grad_shift_second = norm_back(upstream, normal_second, scale_second, gain_second)
        gf = back_second.astype(jnp.bfloat16)
        gu = (slope * dot("rm,tmf->trf", gf, wd)).astype(jnp.bfloat16)
        grad_down = dot("rm,trf->tmf", gf, hidden)
        grad_in = dot("rd,trf->tdf", low_first, gu)
        back_normed = back_second + dot("trf,tdf->rd", gu, wi)
        back_first, grad_gain_first, grad_shift_first = norm_back(back_normed, normal_first, scale_first, gain_first)
        ga = back_first.astype(jnp.bfloat16)
        grad_out = dot("rm,tcr->tmc", ga, ot_blocks)
        got = dot("rm,tmc->tcr", ga, wo).astype(jnp.bfloat16).reshape(width, 2 * rows)
        content_out, query_out = (normed_second[s * rows:(s + 1) * rows].astype(jnp.bfloat16) for s in range(2))
        norm_stack = jnp.stack([grad_gain_first, grad_shift_first, grad_gain_second, grad_shift_second])

    def scatter(blocks):
        flat = blocks.astype(jnp.bfloat16).reshape(tp_size * width, blocks.shape[2])
        return lax.psum_scatter(flat, both_axes, scatter_dimension=0, tiled=True).astype(jnp.float32)

    if own_exchange:
        grad_second = grad_second.reshape(4, 2, 2, 2, width // 8, grad_second.shape[2])
        gqt, gkt, gvt, grad_table, sum_in, sum_down, sum_out, parts = attend_bwd(
            tp_size, ranks, span_starts, bias_table, kp, vp, kt, qt, ot, got, lse, grad_second, first
        )
        grad_content, grad_query, sum_query, sum_key, sum_value, norms, grad_table = tail(
            parts, gqt, gkt, gvt, seqt, queryt, first, back_first, norm_stack, grad_table
        )
        (grad_content, grad_query, sum_query, sum_key, sum_value, sum_out, sum_in, sum_down, *norms) = finish(
            (grad_content, grad_query, sum_query, sum_key, sum_value, sum_out, sum_in, sum_down), norms
        )
    else:
        sum_down, sum_in, sum_out = scatter(grad_down), scatter(grad_in), scatter(grad_out).T
        gqt, gkt, gvt, grad_table = attend_bwd(tp_size, ranks, span_starts, bias_table, kp, vp, kt, qt, ot, got, lse)
        gq_blocks, gk_blocks, gv_blocks = (g.reshape(tp_size, narrow, g.shape[1]) for g in (gqt, gkt, gvt))
        sum_query = scatter(dot("rd,tcr->tdc", both, gq_blocks))
        sum_key = scatter(dot("rd,tcr->tdc", seq_rot, gk_blocks))
        sum_value = scatter(dot("rd,tcr->tdc", seq_rot, gv_blocks))
        back_seq = dot("tcr,tdc->rd", gk_blocks, wk) + dot("tcr,tdc->rd", gv_blocks, wv)
        back_seq = jnp.roll(back_seq.astype(jnp.bfloat16), -shift, axis=0)
        back_content = lax.psum_scatter(back_seq, "tp", scatter_dimension=0, tiled=True).astype(jnp.float32)
        back_inputs = back_first + dot("tcr,tdc->rd", gq_blocks, wq)
        grad_content, grad_query = back_inputs[:rows] + back_content, back_inputs[rows:]
        norms, grad_table = lax.psum((norm_stack, grad_table), ("fsdp", "tp"))
    return (
        content_out, query_out, grad_content, grad_query, sum_query, sum_key, sum_value, sum_out, sum_in, sum_down.T,
        norms[0], norms[1], norms[2], norms[3], grad_table[:, :NB],
    )


def solution(mesh):
    in_specs = (
        P(("fsdp", "tp"), None),
        P(("fsdp", "tp"), None),
        P("fsdp", "tp"),
        P("fsdp", "tp"),
        P("fsdp", "tp"),
        P("tp", "fsdp"),
        P("fsdp", "tp"),
        P("tp", "fsdp"),
        P(),
        P(),
        P(),
        P(),
        P(),
        P("fsdp", None),
        P("fsdp", None),
        P(("fsdp", "tp"), None),
        P(("fsdp", "tp"), None),
    )
    out_specs = (
        P(("fsdp", "tp"), None),
        P(("fsdp", "tp"), None),
        P(("fsdp", "tp"), None),
        P(("fsdp", "tp"), None),
        P("fsdp", "tp"),
        P("fsdp", "tp"),
        P("fsdp", "tp"),
        P("tp", "fsdp"),
        P("fsdp", "tp"),
        P("tp", "fsdp"),
        P(),
        P(),
        P(),
        P(),
        P(),
    )
    return jax.shard_map(functools.partial(local, mesh.shape["tp"], mesh.shape["tp"] == 4 and mesh.shape["fsdp"] == 8), mesh=mesh, in_specs=in_specs, out_specs=out_specs, check_vma=False)
```

```python
import functools
import jax, jax.numpy as jnp
from jax import lax
from jax.sharding import PartitionSpec as P
from jax.experimental import pallas as pl
from jax.experimental.pallas import tpu as pltpu

NEG = -1e30
PIECES = 1
HEAD = 64
NB = 32
PIC = 256
THRESHOLDS = (12, 16, 23, 32, 46, 64, 91)
EPSILON = 1e-05
LOG2E = 1.4426950408889634
LN2 = 0.6931471805599453
VLIM = 60 * 2**20
MESH = pl.DeviceIdType.MESH

def pick(index, values):
    result = jnp.int32(values[-1])
    for place in range(len(values) - 2, -1, -1):
        result = jnp.where(index == place, jnp.int32(values[place]), result)
    return result


class Place:
    def __init__(self):
        f, t = lax.axis_index("fsdp"), lax.axis_index("tp")
        self.f, self.t = f, t
        self.y, self.x, self.c = f // 4, (f // 2) % 2, f % 2
        self.core = (f + 1 - 2 * self.c, t)
        self.xn = (f + 2 - 4 * self.x, t)
        self.yn = (f + 4 - 8 * self.y, t)
        self.up, self.down = (f, t + 1), (f, t - 1)
        self.order = [pick(t, row) for row in ((3, 3, 0, 0), (2, 0, 3, 1), (1, 2, 1, 2), (0, 1, 2, 3))]

    def greet(self):
        barrier = pltpu.get_barrier_semaphore()
        for there in (self.core, self.xn, self.yn):
            pl.semaphore_signal(barrier, inc=1, device_id=there, device_id_type=MESH)
        for there in ((self.f, jnp.where(self.t > 0, self.t - 1, 3)), (self.f, jnp.where(self.t < 3, self.t + 1, 0))):
            pl.semaphore_signal(barrier, inc=1, device_id=there, device_id_type=MESH)
        pl.semaphore_wait(barrier, 5)


def rdma(src, dst, ss, rs, there):
    return pltpu.make_async_remote_copy(src_ref=src, dst_ref=dst, send_sem=ss, recv_sem=rs, device_id=there, device_id_type=MESH)


class Loads:
    def __init__(self, pairs, sems):
        self.copies = [pltpu.make_async_copy(src, dst, sems.at[i]) for i, (src, dst) in enumerate(pairs)]
        for c in self.copies:
            c.start()

    def wait(self, *which):
        for i in which:
            self.copies[i].wait()


class Scatter:
    def __init__(self, at, g, own, r0, r1a, r1b, r2a, r2b, zs, zr, sems, keep_sems):
        self.at, self.g, self.own, self.keep_sems = at, g, own, keep_sems
        self.r0, self.r1a, self.r1b, self.r2a, self.r2b, self.zs, self.zr = r0, r1a, r1b, r2a, r2b, zs, zr
        self.sems = sems
        self.wa = r1a.shape[-1]

    def sem(self, i):
        return self.sems.at[0, i], self.sems.at[1, i]

    def copy0(self, k):
        a = self.at; d = a.order[k]
        return rdma(self.g.at[d, :, :, 1 - a.c], self.r0.at[d], *self.sem(k), a.core)

    def copy1(self, k):
        a = self.at; d = a.order[k]; wa = self.wa
        return (rdma(self.r0.at[d, :, 1 - a.x, :, :wa], self.r1a.at[d], *self.sem(4 + k), a.xn),
                rdma(self.r0.at[d, 1 - a.y, :, :, wa:], self.r1b.at[d], *self.sem(8 + k), a.yn))

    def copy2(self, k):
        a = self.at; d = a.order[k]
        return (rdma(self.r1a.at[d, 1 - a.y], self.r2a.at[d], *self.sem(12 + k), a.yn),
                rdma(self.r1b.at[d, 1 - a.x], self.r2b.at[d], *self.sem(16 + k), a.xn))

    def hop(self, side, h):
        a = self.at
        return rdma(self.zs.at[side, h - 1], self.zr.at[side, h - 1], *self.sem(20 + 3 * side + h - 1), a.down if side else a.up)

    def keep(self, k):
        a = self.at; d = a.order[k]
        return pltpu.make_async_copy(self.g.at[d, :, :, a.c], self.own.at[d], self.keep_sems.at[k])

    def start(self):
        for k in range(4):
            self.copy0(k).start()
            self.keep(k).start()

    def start_one(self, k):
        self.copy0(k).start()

    def stage0(self, k):
        a = self.at; d = a.order[k]
        if self.own is None:
            own = self.g[d, :, :, a.c]
        else:
            self.keep(k).wait()
            own = self.own[d]
        self.copy0(k).wait()
        self.r0[d] = self.r0[d] + own
        for c in self.copy1(k): c.start()

    def stage1(self, k):
        a = self.at; d = a.order[k]; wa = self.wa
        for c in self.copy1(k): c.wait()
        self.r1a[d] = self.r1a[d] + self.r0[d, :, a.x, :, :wa]
        self.r1b[d] = self.r1b[d] + self.r0[d, a.y, :, :, wa:]
        for c in self.copy2(k): c.start()

    def stage2(self, k):
        a = self.at; d = a.order[k]
        for c in self.copy2(k): c.wait()
        self.r2a[d] = self.r2a[d] + self.r1a[d, a.y]
        self.r2b[d] = self.r2b[d] + self.r1b[d, a.x]

    def stage3(self, h):
        wa = self.wa
        for side in range(2):
            u = 3 - self.at.t if side else self.at.t
            d = (self.at.t + h - 4) if side else (self.at.t + 4 - h)
            if h > 1:
                @pl.when((u > 0) & (u < 3) & (u <= h - 1))
                def _():
                    self.hop(side, h - 1).wait_recv()
                    self.zs[side, h - 1, :, :wa] = self.r2a[d] + self.zr[side, h - 2, :, :wa]
                    self.zs[side, h - 1, :, wa:] = self.r2b[d] + self.zr[side, h - 2, :, wa:]
                    self.hop(side, h).start()
            @pl.when(u == 0)
            def _():
                self.zs[side, h - 1, :, :wa] = self.r2a[d]
                self.zs[side, h - 1, :, wa:] = self.r2b[d]
                self.hop(side, h).start()

    def finish(self):
        a = self.at; wa = self.wa
        for side in range(2):
            u = 3 - a.t if side else a.t
            @pl.when(u > 0)
            def _():
                self.hop(side, 3).wait_recv()
        mine = jnp.concatenate([self.r2a[a.t], self.r2b[a.t]], axis=1).astype(jnp.float32)
        below = jnp.where(a.t > 0, self.zr[0, 2].astype(jnp.float32), 0.0)
        above = jnp.where(a.t < 3, self.zr[1, 2].astype(jnp.float32), 0.0)
        for side in range(2):
            u = 3 - a.t if side else a.t
            for h in range(1, 4):
                @pl.when(u < h)
                def _():
                    self.hop(side, h).wait_send()
        return mine + below + above


class Fold:
    def __init__(self, at, part, got, sems):
        self.at, self.part, self.got, self.sems = at, part, got, sems

    def hop(self, side, h):
        a = self.at
        d = jnp.clip((a.t + h - 4) if side else (a.t + 4 - h), 0, 3)
        i = 3 * side + h - 1
        return rdma(self.part.at[d], self.got.at[side, h - 1], self.sems.at[0, i], self.sems.at[1, i], a.down if side else a.up)

    def step(self, h):
        for side in range(2):
            u = 3 - self.at.t if side else self.at.t
            d = (self.at.t + h - 4) if side else (self.at.t + 4 - h)
            @pl.when(u == 0)
            def _():
                if h > 1:
                    self.hop(side, h - 1).wait_send()
                self.hop(side, h).start()
            if h > 1:
                @pl.when((u > 0) & (u < 3) & (u <= h - 1))
                def _():
                    self.hop(side, h - 1).wait_recv()
                    self.part[d] = self.part[d] + self.got[side, h - 2]
                    self.hop(side, h).start()

    def finish(self):
        a = self.at
        for side in range(2):
            u = 3 - a.t if side else a.t
            @pl.when(u > 0)
            def _():
                self.hop(side, 3).wait_recv()
            for h in range(1, 4):
                @pl.when((u < h) & ((u > 0) | (h == 3)))
                def _():
                    self.hop(side, h).wait_send()
        below = jnp.where(a.t > 0, self.got[0, 2].astype(jnp.float32), 0.0)
        above = jnp.where(a.t < 3, self.got[1, 2].astype(jnp.float32), 0.0)
        return self.part[a.t].astype(jnp.float32) + below + above

def scatter_scratch(T, R, W, kept=True):
    wa = (W + 128) // 256 * 128
    B = jnp.bfloat16
    return [pltpu.VMEM((T, 2, 2, R, W), B)] * (2 if kept else 1) + [pltpu.VMEM((T, 2, R, wa), B), pltpu.VMEM((T, 2, R, W - wa), B),
            pltpu.VMEM((T, R, wa), B), pltpu.VMEM((T, R, W - wa), B), pltpu.VMEM((2, 3, R, W), B), pltpu.VMEM((2, 3, R, W), B),
            pltpu.SemaphoreType.DMA((2, 26))] + [pltpu.SemaphoreType.DMA((4,))] * kept

class Total:
    def __init__(self, at, sources, acc, got, sems):
        self.at, self.sources, self.acc, self.got, self.sems = at, sources, acc, got, sems
        t = at.t
        self.partners = [at.core, at.xn, at.yn, (at.f, t + 1 - 2 * (t % 2)), (at.f, 3 - t)]

    def copy(self, i):
        return rdma(self.acc.at[i], self.got.at[i], self.sems.at[0, i], self.sems.at[1, i], self.partners[i])

    def start(self):
        norms, table = self.sources
        self.acc[0] = jnp.zeros_like(self.acc[0])
        self.acc[0, :8, :] = norms[...]
        self.acc[0, 8:8 + table.shape[0], :table.shape[1]] = table[...]
        self.copy(0).start()

    def step(self, i):
        self.copy(i).wait_recv()
        self.acc[i + 1] = self.acc[i] + self.got[i]
        if i < 4:
            self.copy(i + 1).start()

    def finish(self, norms_out, table_out):
        for i in range(5):
            self.copy(i).wait_send()
        norms_out[...] = self.acc[5, :8, :]
        table_out[...] = self.acc[5, 8:8 + table_out.shape[0], :table_out.shape[1]]


def total_scratch(rows, width):
    F = jnp.float32
    return [pltpu.VMEM((6, rows, width), F), pltpu.VMEM((5, rows, width), F), pltpu.SemaphoreType.DMA((2, 5))]


def tail_kernel(part_in, gqt_in, gkt_in, gvt_in, seqt_in, queryt_in, first, back_in, norms, table,
                grad_content, grad_query, sum_query, sum_key, sum_value, norms_out, table_out,
                gqt, gkt, gvt, seqt, queryt, back, weights, part, got, g1, load_sems, fold_sems, *scratch):
    rows, width = grad_content.shape
    narrow, R = width // 4, sum_query.shape[0]
    at = Place()
    loads = Loads(
        [(part_in, part), (gkt_in, gkt), (gvt_in, gvt), (seqt_in, seqt), (queryt_in, queryt), (gqt_in, gqt), (back_in, back)]
        + [(first.at[b, :, pl.ds(128, 256)], weights.at[b]) for b in range(4)], load_sems
    )
    at.greet()
    scatter, fold, total = Scatter(at, g1, None, *scratch[:8], None), Fold(at, part, got, fold_sems), Total(at, (norms, table), *scratch[8:])
    loads.wait(0)
    fold.step(1)
    total.start()

    def weight_grads(k):
        d = at.order[k]
        here = pl.ds(pl.multiple_of(d * narrow, 64), narrow)
        query = nt(seqt[:, :rows], gqt[here, :rows]) + nt(queryt[...], gqt[here, rows:])
        block = jnp.concatenate([query, nt(seqt[...], gkt[here, :]), nt(seqt[...], gvt[here, :])], axis=1)
        g1[d] = block.astype(jnp.bfloat16).reshape(2, 2, 2, R, 3 * narrow)
        scatter.start_one(k)

    loads.wait(1, 2, 3, 4, 5)
    total.step(0)
    for k in range(4):
        weight_grads(k)
        if k == 1:
            total.step(1)
    scatter.stage0(0)
    scatter.stage0(1)
    total.step(2)
    scatter.stage0(2)
    scatter.stage0(3)
    loads.wait(6, 7, 8, 9, 10)
    for s, out in enumerate((grad_content, grad_query)):
        cols = slice(s * rows, (s + 1) * rows)
        value = back[cols, :]
        for b in range(4):
            value = value + nt(gqt[b * narrow:(b + 1) * narrow, cols].T, weights[b, :, 64:256])
        out[...] = value
    fold.step(2)
    scatter.stage1(0)
    scatter.stage1(1)
    total.step(3)
    scatter.stage1(2)
    scatter.stage1(3)
    scatter.stage2(0)
    scatter.stage3(1)
    scatter.stage2(1)
    total.step(4)
    fold.step(3)
    scatter.stage3(2)
    scatter.stage2(2)
    scatter.stage2(3)
    scatter.stage3(3)
    sums = scatter.finish()
    for i, out in enumerate((sum_query, sum_key, sum_value)):
        out[...] = sums[:, i * narrow:(i + 1) * narrow]
    total.finish(norms_out, table_out)
    grad_content[...] += fold.finish()


def tail(parts, gqt, gkt, gvt, seqt, queryt, first, back, norms, table):
    width, both = gqt.shape
    rows, narrow, R = both // 2, width // 4, width // 8
    V, A = pl.BlockSpec(memory_space=pltpu.MemorySpace.VMEM), pl.BlockSpec(memory_space=pl.ANY)
    B, F, S, DMA = jnp.bfloat16, jnp.float32, jax.ShapeDtypeStruct, pltpu.SemaphoreType.DMA
    outs = [S((rows, width), F)] * 2 + [S((R, narrow), F)] * 3 + [S(norms.shape, F), S(table.shape, F)]
    return pl.pallas_call(
        tail_kernel, out_shape=tuple(outs), in_specs=[A] * 8 + [V, V], out_specs=(V,) * 7,
        scratch_shapes=[
            pltpu.VMEM(gqt.shape, B), pltpu.VMEM(gkt.shape, B), pltpu.VMEM(gvt.shape, B), pltpu.VMEM(seqt.shape, B), pltpu.VMEM(queryt.shape, B),
            pltpu.VMEM(back.shape, F),
            pltpu.VMEM((4, width, 256), B), pltpu.VMEM((4, rows, width), B), pltpu.VMEM((2, 3, rows, width), B),
            pltpu.VMEM((4, 2, 2, 2, R, 3 * narrow), B), DMA((11,)), DMA((2, 6)),
        ] + scatter_scratch(4, R, 3 * narrow, False) + total_scratch(24, width),
        compiler_params=pltpu.CompilerParams(vmem_limit_bytes=VLIM, collective_id=1, has_side_effects=True), name="tail",
    )(parts, gqt, gkt, gvt, seqt, queryt, first, back, norms, table)


def nn(a, b):
    return lax.dot_general(a, b, (((1,), (0,)), ((), ())), preferred_element_type=jnp.float32)
def nt(a, b):
    return lax.dot_general(a, b, (((1,), (1,)), ((), ())), preferred_element_type=jnp.float32)

def band_kind(i, b, nrow, nkey):
    rel = (b - i) % nkey
    if rel == 0: return 2
    if rel == nkey - 1: return 0 if i == 0 else 1
    if rel == 1: return 4 if i == nrow - 1 else 3
    return None

def wrap(value, size):
    return jnp.where(value >= size, value - size, value)


def bucket_of(offsets):
    magnitude = jnp.abs(offsets)
    far_bucket = 8 + sum((magnitude >= threshold).astype(jnp.int32) for threshold in THRESHOLDS)
    return jnp.where(magnitude < 8, magnitude, far_bucket) + jnp.where(offsets > 0, 16, 0)


def slot_bucket(slot, lanes, tp_index, tp_size):
    if slot >= 10:
        return jnp.full_like(lanes, 15 if slot == 10 else 31)
    kind, wrapped = slot // 2, slot % 2
    buckets = bucket_of(128 * ((-1, -1, 0, 1, 1)[kind] + wrapped) - lanes)
    if kind == 0:
        return jnp.where(tp_index == 0, 31, buckets)
    if kind == 4:
        return jnp.where(tp_index == tp_size - 1, 15, buckets)
    return buckets


def far_sides(nrow, nkey, tp_index):
    key_block = lax.broadcasted_iota(jnp.int32, (16, 2 * nrow * 128), 0)
    row_block = wrap(lax.broadcasted_iota(jnp.int32, (16, 2 * nrow * 128), 1) // 128, nrow)
    gap = key_block - row_block
    near = (gap == 0) | (gap == 1) | (gap == -1) | (gap == nkey - 1) | (gap == 1 - nkey) | (key_block >= nkey)
    key_place, row_place = wrap(key_block + nrow * tp_index, nkey), row_block + nrow * tp_index
    left = jnp.where(near, 0.0, jnp.where(key_place < row_place, 1.0, 0.0))
    return left, jnp.where(near, 0.0, 1.0 - left)


def prepare(nrow, nkey, tp_size, ranks, starts, table, mask, ring, vec, sides):
    tp_index = lax.axis_index("tp")
    rows, seq = nrow * 128, nkey * 128
    base = rows * tp_index
    rank_row = jnp.broadcast_to(ranks[...].astype(jnp.float32), (8, seq))
    ring[:, :seq] = rank_row
    ring[:, seq:] = rank_row

    def label(place):
        found = jnp.zeros(place.shape, jnp.int32)
        for k in range(starts.shape[1]):
            start = starts[0, k]
            found = found + jnp.where((place >= start) & (place < start + PIC), k + 1, 0)
        return found

    row_rank, row_label = [], []
    for i in range(nrow):
        row_rank.append(ring[0:1, pl.ds(pl.multiple_of(base + i * 128, 128), 128)])
        row_label.append(label(base + i * 128 + lax.broadcasted_iota(jnp.int32, (1, 128), 1)))

    def one(b, _):
        keys = pl.ds(pl.multiple_of(b * 128, 128), 128)
        rank_k = jnp.broadcast_to(ring[0:1, pl.ds(pl.multiple_of(base + b * 128, 128), 128)], (128, 128)).T
        kpos = b * 128 + lax.broadcasted_iota(jnp.int32, (128, 128), 0)
        label_k = label(wrap(base + kpos, seq))
        for i in range(nrow):
            rpos = i * 128 + lax.broadcasted_iota(jnp.int32, (128, 128), 1)
            same = (label_k == row_label[i]) & (label_k > 0)
            content = (rank_k <= row_rank[i]) | same
            strict = (rank_k < jnp.maximum(row_rank[i], 1.0)) | (same & (kpos != rpos))
            mask[keys, i * 128:(i + 1) * 128] = jnp.where(content, 0.0, NEG)
            mask[keys, rows + i * 128:rows + (i + 1) * 128] = jnp.where(strict, 0.0, NEG)
        return 0
    lax.fori_loop(0, nkey, one, 0)

    heads = table.shape[0]
    lanes = lax.broadcasted_iota(jnp.int32, (heads, 128), 1)
    columns = [jnp.broadcast_to(table[:, n:n + 1] * LOG2E, (heads, 128)) for n in range(NB)]
    for slot in range(12):
        buckets = slot_bucket(slot, lanes, tp_index, tp_size)
        values = columns[0]
        for n in range(1, NB):
            values = jnp.where(buckets == n, columns[n], values)
        for h in range(heads):
            vec[h, slot:slot + 1, :] = values[h:h + 1, :]
    sides[0], sides[1] = far_sides(nrow, nkey, tp_index)


def far_bias(vec, sides, cf, h):
    copies = cf.shape[1] // 128
    left, right = (jnp.concatenate([vec[h, slot:slot + 1, :]] * copies, axis=1) for slot in (10, 11))
    cf[...] = sides[0] * left + sides[1] * right


def prepare_scratch(nrow, nkey, heads):
    F, rows = jnp.float32, 2 * nrow * 128
    return [
        pltpu.VMEM((nkey * 128, rows), F), pltpu.VMEM((8, 2 * nkey * 128), F), pltpu.VMEM((heads, 12, 128), F),
        pltpu.VMEM((2, 16, rows), F), pltpu.VMEM((16, rows), F), pltpu.VMEM((5, 128, 128), F),
    ]


def band_tiles(band, vec, h):
    lane = lax.broadcasted_iota(jnp.int32, (128, 128), 1)
    sub = lax.broadcasted_iota(jnp.int32, (128, 128), 0)
    for k in range(5):
        direct, wrapped = (
            pltpu.roll(jnp.broadcast_to(vec[h, 2 * k + w:2 * k + w + 1, :], (128, 128)), 0, 1, stride=1, stride_axis=0)
            for w in range(2)
        )
        band[k] = jnp.where(lane >= sub, direct, wrapped)

def diagonal_sums(tile):
    lane = lax.broadcasted_iota(jnp.int32, (8, 128), 1)
    sub = lax.broadcasted_iota(jnp.int32, (8, 128), 0)
    direct = wrapped = jnp.zeros((8, 128), jnp.float32)
    for a in range(16):
        rows = tile[8 * a:8 * a + 8, :]
        kept = jnp.where(lane >= sub + 8 * a, rows, 0.0)
        left = rows - kept
        if a:
            kept, left = pltpu.roll(kept, 128 - 8 * a, 1), pltpu.roll(left, 128 - 8 * a, 1)
        direct, wrapped = direct + kept, wrapped + left
    for bit in (1, 2, 4):
        moved = (sub & bit) != 0
        direct = jnp.where(moved, pltpu.roll(direct, 128 - bit, 1), direct)
        wrapped = jnp.where(moved, pltpu.roll(wrapped, 128 - bit, 1), wrapped)
    return jnp.sum(direct, axis=0, keepdims=True), jnp.sum(wrapped, axis=0, keepdims=True)

def head_rows(ref, p, hh, cols):
    z = jnp.zeros((64, cols.stop - cols.start), jnp.bfloat16)
    rows = ref[pl.ds(pl.multiple_of((2 * p + hh) * 64, 64), 64), cols]
    return jnp.concatenate([rows, z] if hh == 0 else [z, rows], axis=0)

def attend_rows(nrow, nkey, kp, vt, qt, ot, lse, t, prepared, exchange):
    mask, _, vec, sides, cf, band = prepared
    ones = jnp.ones((16, 256), jnp.bfloat16)
    nchunk = 2 * nrow * 128 // 256
    def pair(p, _):
        for hh in range(2):
            h = 2 * p + hh
            exchange(h)
            hrows = pl.ds(pl.multiple_of(h * 64, 64), 64)
            band_tiles(band, vec, h)
            far_bias(vec, sides, cf, h)
            for c in range(nchunk):
                cols = slice(c * 256, (c + 1) * 256)
                qh = head_rows(qt, p, hh, cols)
                m8 = jnp.full((8, 256), -jnp.inf, jnp.float32)
                for b in range(nkey):
                    s = nn(kp[p, b * 128:(b + 1) * 128, :], qh)
                    s = s + mask[b * 128:(b + 1) * 128, cols]
                    kinds = [band_kind((2 * c + k) % nrow, b, nrow, nkey) for k in range(2)]
                    if any(k is not None for k in kinds):
                        s = jnp.concatenate([s[:, k * 128:(k + 1) * 128] + (band[kinds[k]] if kinds[k] is not None else 0.0) for k in range(2)], axis=1)
                    t[c, b * 128:(b + 1) * 128, :] = s
                    m8 = jnp.maximum(m8, jnp.max(s.reshape(16, 8, 256), axis=0) + cf[b:b + 1, cols])
                m = jnp.max(m8, axis=0, keepdims=True)
                acc = jnp.zeros((80, 256), jnp.float32)
                for g in range(nkey // 2):
                    ps = []
                    for b in (2 * g, 2 * g + 1):
                        ps.append(jnp.exp2(t[c, b * 128:(b + 1) * 128, :] - (m - cf[b:b + 1, cols])).astype(jnp.bfloat16))
                    lhs = jnp.concatenate([vt[hrows, g * 256:(g + 1) * 256], ones], axis=0)
                    acc = acc + nn(lhs, jnp.concatenate(ps, axis=0))
                l = acc[64:65, :]
                ot[hrows, cols] = (acc[:64, :] / l).astype(jnp.bfloat16)
                lse[h, 0:1, cols] = m + jnp.log2(l)
        return 0
    lax.fori_loop(0, kp.shape[0], pair, 0)

def fwd_kernel(nrow, nkey, tp_size, ranks, starts, table, kp, vt, qt, ot, lse, t, *prepared):
    prepare(nrow, nkey, tp_size, ranks, starts, table, *prepared[:4])
    attend_rows(nrow, nkey, kp, vt, qt, ot, lse, t, prepared, lambda h: None)


def attend_fwd(tp_size, ranks, starts, table, kp, vt, qt):
    pairs, seq, _ = kp.shape
    rows = qt.shape[1]
    nrow, nkey = rows // 256, seq // 128
    V, M = pl.BlockSpec(memory_space=pltpu.MemorySpace.VMEM), pl.BlockSpec(memory_space=pltpu.MemorySpace.SMEM)
    return pl.pallas_call(
        functools.partial(fwd_kernel, nrow, nkey, tp_size),
        out_shape=(jax.ShapeDtypeStruct(qt.shape, jnp.bfloat16), jax.ShapeDtypeStruct((2 * pairs, 1, rows), jnp.float32)),
        in_specs=[V, M, V, V, V, V], out_specs=(V, V),
        scratch_shapes=[pltpu.VMEM((rows // 256, seq, 256), jnp.float32)] + prepare_scratch(nrow, nkey, 2 * pairs),
        compiler_params=pltpu.CompilerParams(vmem_limit_bytes=VLIM),
        name="attend_fwd",
    )(ranks, starts, table, kp, vt, qt)


class Gather:
    def __init__(self, at, shard, g, wa, sems, own_sem):
        self.at, self.shard, self.g, self.wa, self.sems, self.own_sem = at, shard, g, wa, sems, own_sem
        self.blocks = at.order[::-1]

    def send(self, i, src, dst, there):
        return rdma(src, dst, self.sems.at[0, i], self.sems.at[1, i], there)

    def along_z(self, b, upward):
        a = self.at
        here = self.g.at[b, a.y, a.x, a.c]
        return self.send(b + (0 if upward else 4), here, here, a.up if upward else a.down)

    def first(self, b):
        a, wa = self.at, self.wa
        left, right = (self.g.at[b, a.y, a.x, a.c, :, cols] for cols in (slice(0, wa), slice(wa, None)))
        return self.send(8 + b, left, left, a.xn), self.send(12 + b, right, right, a.yn)

    def second(self, b):
        a, wa = self.at, self.wa
        left, right = self.g.at[b, a.y, :, a.c, :, :wa], self.g.at[b, :, a.x, a.c, :, wa:]
        return self.send(16 + b, left, left, a.yn), self.send(20 + b, right, right, a.xn)

    def across(self, b):
        a = self.at
        here = self.g.at[b, :, :, a.c]
        return self.send(24 + b, here, here, a.core)

    def own(self):
        a = self.at
        return pltpu.make_async_copy(self.shard, self.g.at[a.t, a.y, a.x, a.c], self.own_sem)

    def begin(self):
        self.own().start()
        self.own().wait()
        for c in self.first(self.at.t):
            c.start()

    def begin_z(self):
        a = self.at
        @pl.when(a.t < 3)
        def _():
            self.along_z(a.t, True).start()
        @pl.when(a.t > 0)
        def _():
            self.along_z(a.t, False).start()

    def arrive(self, j):
        a, b = self.at, self.blocks[j]
        @pl.when(b < a.t)
        def _():
            self.along_z(b, True).wait_recv()
        @pl.when(b > a.t)
        def _():
            self.along_z(b, False).wait_recv()
        @pl.when((b < a.t) & (a.t < 3))
        def _():
            self.along_z(b, True).start()
        @pl.when((b > a.t) & (a.t > 0))
        def _():
            self.along_z(b, False).start()
        for c in self.first(b):
            c.start()

    def step1(self, j):
        b = self.blocks[j]
        for c in self.first(b):
            c.wait_recv()
        for c in self.second(b):
            c.start()

    def step2(self, j):
        b = self.blocks[j]
        for c in self.second(b):
            c.wait_recv()
        self.across(b).start()

    def step3(self, j):
        self.across(self.blocks[j]).wait_recv()

    def finish(self):
        a = self.at
        for b in range(4):
            @pl.when((b <= a.t) & (a.t < 3))
            def _():
                self.along_z(b, True).wait_send()
            @pl.when((b >= a.t) & (a.t > 0))
            def _():
                self.along_z(b, False).wait_send()
            for c in (*self.first(b), *self.second(b), self.across(b)):
                c.wait_send()


class Chain:
    def __init__(self, at, seq, sems, pieces):
        self.at, self.seq, self.sems, self.pieces = at, seq, sems, pieces
        self.blocks = at.order[::-1]

    def move(self, b, upward, s):
        a = self.at
        i = (b + (0 if upward else 4)) * self.pieces + s
        there = a.t + 1 if upward else a.t - 1
        size = self.seq.shape[1] // self.pieces
        part = slice(s * size, (s + 1) * size)
        return rdma(self.seq.at[(b - a.t + 4) % 4, part], self.seq.at[(b - there + 4) % 4, part], self.sems.at[0, i], self.sems.at[1, i], (a.f, there))

    def begin(self):
        a = self.at
        for s in range(self.pieces):
            @pl.when(a.t < 3)
            def _():
                self.move(a.t, True, s).start()
            @pl.when(a.t > 0)
            def _():
                self.move(a.t, False, s).start()

    def arrive(self, j):
        a, b = self.at, self.blocks[j]
        for s in range(self.pieces):
            @pl.when(b < a.t)
            def _():
                self.move(b, True, s).wait_recv()
            @pl.when(b > a.t)
            def _():
                self.move(b, False, s).wait_recv()
            @pl.when((b < a.t) & (a.t < 3))
            def _():
                self.move(b, True, s).start()
            @pl.when((b > a.t) & (a.t > 0))
            def _():
                self.move(b, False, s).start()

    def finish(self):
        a = self.at
        for b in range(4):
            for s in range(self.pieces):
                @pl.when((b <= a.t) & (a.t < 3))
                def _():
                    self.move(b, True, s).wait_send()
                @pl.when((b >= a.t) & (a.t > 0))
                def _():
                    self.move(b, False, s).wait_send()


def front_kernel(nrow, nkey, content, query, w_query, w_key, w_value, w_out, w_in, w_down, ranks, starts, table,
                 ot, lse, seqt_out, queryt_out, kp_out, vp_out, kt_out, qt_out, w1_out, w2_out,
                 shard1, shard2, seq, seqt, queryt, w1, w2, w1t, kp, vp, kt, vt, qt, t,
                 sems1, sems2, semsc, own_sems, out_sems, *prepared):
    at = Place()
    rows = nrow * 128
    pairs = kp.shape[0]
    narrow = shard1.shape[1] // 4
    width = content.shape[1]
    weights1 = Gather(at, shard1, w1, shard1.shape[1] // 2, sems1, own_sems.at[0])
    weights2 = Gather(at, shard2, w2, shard2.shape[1] // 2, sems2, own_sems.at[1])
    chain = Chain(at, seq, semsc, PIECES)
    shard1[...] = jnp.concatenate([w_out[...].T, w_query[...], w_key[...], w_value[...]], axis=1)
    shard2[:, :w_in.shape[1]] = w_in[...]
    shard2[:, w_in.shape[1]:] = w_down[...]
    seq[0] = content[...]
    at.greet()
    weights1.begin()
    weights1.begin_z()
    weights1.arrive(1)
    weights1.step1(0)
    weights1.arrive(2)
    weights1.step1(1)
    weights1.step2(0)
    weights1.arrive(3)
    chain.begin()
    weights2.begin()
    weights2.begin_z()
    weights1.step1(2)
    weights1.step2(1)
    weights1.step1(3)
    prepare(nrow, nkey, 4, ranks, starts, table, *prepared[:4])
    weights1.step2(2)
    weights1.step2(3)
    for j in range(4):
        weights1.step3(j)

    scale = HEAD ** -0.5 * LOG2E
    for tt in range(4):
        block = w1[tt].reshape(width, 4 * narrow)
        w1t[tt] = block[:, narrow:].T
        for s, x in enumerate((content, query)):
            q = nt(w1t[tt, :narrow, :], x[...])
            qt[tt * narrow:(tt + 1) * narrow, s * rows:(s + 1) * rows] = (q * scale).astype(jnp.bfloat16)

    def project(r):
        x = seq[r]
        cols = pl.ds(pl.multiple_of(r * rows, 128), rows)
        seqt[:, cols] = x.T
        for i, (across, upright) in enumerate(((kp, kt), (vp, vt))):
            for tt in range(4):
                out = nt(w1t[tt, (i + 1) * narrow:(i + 2) * narrow, :], x)
                upright[tt * narrow:(tt + 1) * narrow, cols] = out.astype(jnp.bfloat16)
            for u in range(2):
                halves = [
                    nn(x, w1[2 * u + v].reshape(width, 4 * narrow)[:, (i + 2) * narrow:(i + 3) * narrow]) for v in range(2)
                ]
                joined = jnp.concatenate(halves, axis=1).astype(jnp.bfloat16)
                for p in range(pairs // 2):
                    across[u * (pairs // 2) + p, cols, :] = joined[:, p * 128:(p + 1) * 128]

    queryt[...] = query[...].T
    project(0)
    chain.arrive(1)
    weights2.arrive(1)
    weights2.step1(0)
    project((chain.blocks[1] - at.t + 4) % 4)
    chain.arrive(2)
    weights2.step2(0)
    weights2.step1(1)
    weights2.arrive(2)
    project((chain.blocks[2] - at.t + 4) % 4)
    chain.arrive(3)
    weights2.step2(1)
    weights2.step1(2)
    project((chain.blocks[3] - at.t + 4) % 4)

    outs = [
        pltpu.make_async_copy(src, dst, out_sems.at[i])
        for i, (src, dst) in enumerate(((seqt, seqt_out), (queryt, queryt_out), (kp, kp_out), (vp, vp_out), (kt, kt_out), (qt, qt_out), (w1, w1_out)))
    ]
    for c in outs:
        c.start()

    def second_out(j):
        b = weights2.blocks[j]
        return pltpu.make_async_copy(w2.at[b], w2_out.at[b], out_sems.at[7 + j])

    def exchange(h):
        steps = (
            (weights2.arrive, 3, 2),
            (weights2.step2, 2, 4),
            (weights2.step1, 3, 7),
            (weights2.step2, 3, 11),
        )
        for step, j, place in steps:
            @pl.when(h == place)
            def _():
                step(j)

    attend_rows(nrow, nkey, kp, vt, qt, ot, lse, t, prepared, exchange)
    for j in range(4):
        weights2.step3(j)
        second_out(j).start()
    for c in outs:
        c.wait()
    for j in range(4):
        second_out(j).wait()
    weights1.finish()
    weights2.finish()
    chain.finish()


def front(content, query, w_query, w_key, w_value, w_out, w_in, w_down, ranks, starts, table):
    rows, width = content.shape
    heads, seq_len = table.shape[0], ranks.shape[1]
    pairs, (R, narrow), wide = heads // 2, w_query.shape, w_in.shape[1]
    nrow, nkey = rows // 128, seq_len // 128
    V, A = pl.BlockSpec(memory_space=pltpu.MemorySpace.VMEM), pl.BlockSpec(memory_space=pl.ANY)
    B, F, S, DMA = jnp.bfloat16, jnp.float32, jax.ShapeDtypeStruct, pltpu.SemaphoreType.DMA
    full1, full2 = (4, 2, 2, 2, R, 4 * narrow), (4, 2, 2, 2, R, 2 * wide)
    kept = [((width, seq_len), B), ((width, rows), B), ((pairs, seq_len, 128), B), ((pairs, seq_len, 128), B), ((width, seq_len), B), ((width, 2 * rows), B), (full1, B)]
    outs = [S((width, 2 * rows), B), S((heads, 1, 2 * rows), F)] + [S(*k) for k in kept] + [S(full2, B)]
    scratch = [pltpu.VMEM((R, 4 * narrow), B), pltpu.VMEM((R, 2 * wide), B), pltpu.VMEM((4, rows, width), B), pltpu.VMEM(*kept[0]), pltpu.VMEM(*kept[1]), pltpu.VMEM(full1, B), pltpu.VMEM(full2, B),
               pltpu.VMEM((4, 3 * narrow, width), B), pltpu.VMEM(*kept[2]), pltpu.VMEM(*kept[3]),
               pltpu.VMEM(*kept[4]), pltpu.VMEM(*kept[4]), pltpu.VMEM(*kept[5]),
               pltpu.VMEM((2 * rows // 256, seq_len, 256), F),
               DMA((2, 28)), DMA((2, 28)), DMA((2, 8 * PIECES)), DMA((2,)), DMA((11,))] + prepare_scratch(nrow, nkey, heads)
    return pl.pallas_call(
        functools.partial(front_kernel, nrow, nkey),
        out_shape=tuple(outs), in_specs=[V] * 9 + [pl.BlockSpec(memory_space=pltpu.MemorySpace.SMEM), V], out_specs=tuple([V, V] + [A] * 8), scratch_shapes=scratch,
        compiler_params=pltpu.CompilerParams(vmem_limit_bytes=VLIM, collective_id=3, has_side_effects=True), name="front",
    )(content, query, w_query, w_key, w_value, w_out, w_in, w_down, ranks, starts, table)


def bwd_kernel(nrow, nkey, tp_size, fused, *refs):
    if fused:
        ranks, starts, table, kp, vp, kt, qt, ot, got, lse, g, first, gqt_out, gkt_out, gvt_out, back_table, sum_in, sum_down, sum_out, part, gq, bacc, diag, weights, gqt, gkt, gvt, out_sems, *scratch = refs
        prepared, kept, load_sems, scratch = scratch[:6], scratch[6:12], scratch[12], scratch[13:]
        loads = Loads(list(zip((kp, vp, kt, qt, ot, got), kept)) + [(first.at[b, :, pl.ds(384, 384)], weights.at[b]) for b in range(4)], load_sems)
        kp, vp, kt, qt, ot, got = kept
        at = Place()
        at.greet()
        scatter = Scatter(at, g, *scratch)
        scatter.start()
    else:
        ranks, starts, table, kp, vp, kt, qt, ot, got, lse, gqt, gkt, gvt, back_table, gq, bacc, diag, *prepared = refs
    mask, _, vec, sides, cf, band = prepared
    prepare(nrow, nkey, tp_size, ranks, starts, table, *prepared[:4])
    lane_row = lax.broadcasted_iota(jnp.int32, (1, 128), 1)
    if fused:
        loads.wait(0, 1, 2, 3, 4, 5)

    def exchange(h):
        if not fused:
            return
        steps = (
            (scatter.stage0, 0, 0), (scatter.stage0, 1, 1), (scatter.stage1, 0, 3), (scatter.stage0, 2, 3), (scatter.stage2, 0, 6), (scatter.stage3, 1, 6),
            (scatter.stage1, 1, 6), (scatter.stage0, 3, 6), (scatter.stage1, 2, 8), (scatter.stage2, 1, 9), (scatter.stage3, 2, 9), (scatter.stage1, 3, 11),
        )
        for step, k, place in steps:
            @pl.when(h == place)
            def _():
                step(k)

    rows = 2 * nrow * 128
    nchunk = rows // 256
    full = slice(0, rows)
    block_of = lax.broadcasted_iota(jnp.int32, (16, 256), 0)
    half_of = lax.broadcasted_iota(jnp.int32, (16, 256), 1) // 128
    def pair(p, _):
        for hh in range(2):
            h = 2 * p + hh
            exchange(h)
            hrows = pl.ds(pl.multiple_of(h * 64, 64), 64)
            band_tiles(band, vec, h)
            far_bias(vec, sides, cf, h)
            q_h = qt[hrows, :]
            go_h = got[hrows, :]
            delta = jnp.sum(ot[hrows, :].astype(jnp.float32) * go_h.astype(jnp.float32), axis=0, keepdims=True)
            for k in range(5):
                bacc[k] = jnp.zeros((128, 128), jnp.float32)
            gq[...] = jnp.zeros_like(gq)
            qm = head_rows(qt, p, hh, full)
            gm = head_rows(got, p, hh, full)
            for g in range(nkey // 2):
                pp, gg = [], []
                for c in range(nchunk):
                    cols = slice(c * 256, (c + 1) * 256)
                    pc, gc = [], []
                    for b in (2 * g, 2 * g + 1):
                        keys = slice(b * 128, (b + 1) * 128)
                        s = nn(kp[p, keys, :], qm[:, cols])
                        dp = nn(vp[p, keys, :], gm[:, cols])
                        s = s + mask[keys, cols]
                        kinds = [band_kind((2 * c + k) % nrow, b, nrow, nkey) for k in range(2)]
                        if any(k is not None for k in kinds):
                            s = jnp.concatenate([s[:, k * 128:(k + 1) * 128] + (band[kinds[k]] if kinds[k] is not None else 0.0) for k in range(2)], axis=1)
                        pr = jnp.exp2(s - (lse[h, 0:1, cols] - cf[b:b + 1, cols]))
                        gs = pr * (dp - delta[:, cols])
                        for k in range(2):
                            if kinds[k] is not None:
                                bacc[kinds[k]] += gs[:, k * 128:(k + 1) * 128]
                        pc.append(pr.astype(jnp.bfloat16))
                        gc.append(gs.astype(jnp.bfloat16))
                    pp.append(jnp.concatenate(pc, axis=0))
                    gg.append(jnp.concatenate(gc, axis=0))
                pall = jnp.concatenate(pp, axis=1)
                gall = jnp.concatenate(gg, axis=1)
                keys = slice(g * 256, (g + 1) * 256)
                onehot = (block_of == 2 * g + half_of).astype(jnp.bfloat16)
                gq[...] += nn(jnp.concatenate([kt[hrows, keys], onehot], axis=0), gall)
                gkt[hrows, keys] = (nt(q_h, gall) * LN2).astype(jnp.bfloat16)
                gvt[hrows, keys] = nt(go_h, pall).astype(jnp.bfloat16)
            gqt[hrows, :] = (gq[:64, :] * 0.125).astype(jnp.bfloat16)
            for k in range(5):
                direct, wrapped = diagonal_sums(bacc[k])
                diag[h, 0:1, 256 * k:256 * k + 128] = direct
                diag[h, 0:1, 256 * k + 128:256 * k + 256] = wrapped
            for s in range(2):
                side = jnp.sum(jnp.sum(gq[64:80, :] * sides[s], axis=0, keepdims=True), axis=1, keepdims=True)
                diag[h, 0:1, 1280 + 128 * s:1408 + 128 * s] = jnp.where(lane_row == 0, side, 0.0)
        return 0
    lax.fori_loop(0, kp.shape[0], pair, 0)
    tp_index = lax.axis_index("tp")
    places = lax.broadcasted_iota(jnp.int32, (128, 128), 0)
    numbers = lax.broadcasted_iota(jnp.int32, (128, 128), 1)
    sums = jnp.concatenate([diag[h] for h in range(diag.shape[0])], axis=0)
    total = jnp.zeros((diag.shape[0], 128), jnp.float32)
    for slot in range(12):
        one_hot = jnp.where(slot_bucket(slot, places, tp_index, tp_size) == numbers, 1.0, 0.0)
        total = total + jnp.dot(
            sums[:, slot * 128:(slot + 1) * 128], one_hot, precision=lax.Precision.HIGHEST, preferred_element_type=jnp.float32
        )
    back_table[...] = total
    if fused:
        stores = Loads([(gqt, gqt_out), (gkt, gkt_out), (gvt, gvt_out)], out_sems)
        scatter.stage2(2)
        scatter.stage3(3)
        loads.wait(6, 7, 8, 9)
        span, narrow = part.shape[1], kt.shape[0] // 4
        for d in range(4):
            here = pl.ds(pl.multiple_of(((d - at.t + 4) % 4) * span, 128), span)
            value = jnp.zeros(part.shape[1:], jnp.float32)
            for b in range(4):
                block = slice(b * narrow, (b + 1) * narrow)
                value = value + nt(jnp.concatenate([gkt[block, here], gvt[block, here]], axis=0).T, weights[b])
            part[d] = value.astype(jnp.bfloat16)
        scatter.stage2(3)
        sums = scatter.finish()
        wide = sum_in.shape[1]
        sum_in[...] = sums[:, :wide]
        sum_down[...] = sums[:, wide:2 * wide]
        sum_out[...] = sums[:, 2 * wide:].T
        stores.wait(0, 1, 2)


def attend_bwd(tp_size, ranks, starts, table, kp, vp, kt, qt, ot, got, lse, g=None, first=None):
    pairs, seq, _ = kp.shape
    rows = qt.shape[1]
    heads = 2 * pairs
    nrow, nkey = rows // 256, seq // 128
    V, M = pl.BlockSpec(memory_space=pltpu.MemorySpace.VMEM), pl.BlockSpec(memory_space=pltpu.MemorySpace.SMEM)
    S, F = jax.ShapeDtypeStruct, jnp.float32
    fused = g is not None
    out_specs = [V] * 4
    outs = [S(qt.shape, jnp.bfloat16), S(kt.shape, jnp.bfloat16), S(kt.shape, jnp.bfloat16), S((heads, 128), F)]
    scratch = [pltpu.VMEM((80, rows), F), pltpu.VMEM((5, 128, 128), F), pltpu.VMEM((heads, 1, 1536), F)] + prepare_scratch(nrow, nkey, heads)
    params = dict(vmem_limit_bytes=VLIM)
    args = (ranks, starts, table, kp, vp, kt, qt, ot, got, lse)
    specs = [V, M] + [V] * 8
    if fused:
        narrow = kt.shape[0] // 4
        wide = (g.shape[5] - narrow) // 2
        outs += [S((g.shape[4], wide), F), S((g.shape[4], wide), F), S((narrow, g.shape[4]), F), S((4, rows // 2, kt.shape[0]), jnp.bfloat16)]
        scratch[3:3] = [pltpu.VMEM((4, kt.shape[0], 2 * narrow), jnp.bfloat16)] + [pltpu.VMEM(o.shape, o.dtype) for o in outs[:3]] + [pltpu.SemaphoreType.DMA((3,))]
        scratch += [pltpu.VMEM(a.shape, a.dtype) for a in (kp, vp, kt, qt, ot, got)] + [pltpu.SemaphoreType.DMA((10,))]
        scratch += scatter_scratch(g.shape[0], g.shape[4], g.shape[5])
        params.update(collective_id=2, has_side_effects=True)
        args += (g, first)
        A = pl.BlockSpec(memory_space=pl.ANY)
        specs = specs[:3] + [A] * 6 + [V, A, A]
        out_specs = [A] * 3 + [V] * 5
    return pl.pallas_call(
        functools.partial(bwd_kernel, nrow, nkey, tp_size, fused),
        out_shape=tuple(outs), in_specs=specs, out_specs=tuple(out_specs), scratch_shapes=scratch,
        compiler_params=pltpu.CompilerParams(**params), name="attend_bwd",
    )(*args)


def norm(residual):
    centered = residual - jnp.mean(residual, axis=-1, keepdims=True)
    scale = lax.rsqrt(jnp.mean(centered * centered, axis=-1, keepdims=True) + EPSILON)
    return centered * scale, scale


def norm_step(cotangent, normal, scale, gain):
    inner = cotangent * gain
    mean_inner = jnp.mean(inner, axis=-1, keepdims=True)
    mean_cross = jnp.mean(inner * normal, axis=-1, keepdims=True)
    return scale * (inner - mean_inner - normal * mean_cross)


def middle_kernel(chunk, ot_in, content, query, first, second_in, gain1, shift1, gain2, shift2, ranks, up_content, up_query,
                  content_out, query_out, grads, back_out, got_out, sums,
                  back, got, store_sems, ot, second, x, up, wot, wo_block, onat, n1bt, gft, gat, hidden, slope, gu, out2, stage, sems, out_sems):
    rows = content.shape[0]
    seq, width = ranks.shape[1], content.shape[1]
    narrow, wide = width // 4, second.shape[2] // 2
    loads = Loads(
        [(first.at[t, :, pl.ds(0, 256)], wo_block.at[t]) for t in range(4)] + [(ot_in, ot)]
        + [(second_in.at[t], second.at[t]) for t in range(4)], sems
    )
    base = rows * lax.axis_index("tp")
    x[:rows] = content[...]
    x[rows:] = query[...]
    up[:rows] = up_content[...].astype(jnp.float32)
    for i in range(rows // 128):
        rank = ranks[0:1, pl.ds(pl.multiple_of(base + i * 128, 128), 128)].astype(jnp.float32)
        rank = jnp.broadcast_to(rank, (128, 128)).T
        kept = jnp.where(rank >= seq - seq * 15 // 100, 1.0, 0.0)
        up[rows + i * 128:rows + (i + 1) * 128, :] = up_query[i * 128:(i + 1) * 128, :].astype(jnp.float32) * jnp.concatenate([kept] * (width // 128), axis=1)
    loads.wait(0, 1, 2, 3, 4)
    wot[...] = jnp.concatenate([wo_block[t, :, :narrow] for t in range(4)], axis=1)
    sums[...] = jnp.zeros_like(sums)
    gain1, shift1, gain2, shift2 = (ref[...].reshape(1, width) for ref in (gain1, shift1, gain2, shift2))

    def one(i, _):
        here = pl.ds(pl.multiple_of(i * chunk, chunk), chunk)
        mixed = ot[:, here].T
        onat[here, :] = mixed
        normal1, scale1 = norm(x[here, :].astype(jnp.float32) + nt(mixed, wot[...]))
        normed = normal1 * gain1 + shift1
        low = normed.astype(jnp.bfloat16)
        n1bt[:, here] = low.T
        total = normed
        for t in range(4):
            @pl.when(i == 0)
            def _():
                loads.wait(5 + t)
            lifted = nn(low, second[t, :, :wide])
            phi = 0.5 + 0.5 * lax.erf(lifted * (0.5 ** 0.5))
            act = (lifted * phi).astype(jnp.bfloat16)
            hidden[t, here, :] = act
            slope[t] = phi + lifted * (jnp.exp(-0.5 * lifted * lifted) * 0.3989422804014327)
            total = total + nt(act, second[t, :, wide:])
        normal2, scale2 = norm(total)
        out2[here, :] = (normal2 * gain2 + shift2).astype(jnp.bfloat16)
        cotangent = up[here, :]
        sums[2:3, :] += jnp.sum(cotangent * normal2, axis=0, keepdims=True)
        sums[3:4, :] += jnp.sum(cotangent, axis=0, keepdims=True)
        back2 = norm_step(cotangent, normal2, scale2, gain2)
        gf = back2.astype(jnp.bfloat16)
        gft[:, here] = gf.T
        total = back2
        for t in range(4):
            g = (slope[t] * nn(gf, second[t, :, wide:])).astype(jnp.bfloat16)
            gu[t, here, :] = g
            total = total + nt(g, second[t, :, :wide])
        sums[0:1, :] += jnp.sum(total * normal1, axis=0, keepdims=True)
        sums[1:2, :] += jnp.sum(total, axis=0, keepdims=True)
        back1 = norm_step(total, normal1, scale1, gain1)
        back[here, :] = back1
        ga = back1.astype(jnp.bfloat16)
        gat[:, here] = ga.T
        got[:, here] = nn(ga, wot[...]).astype(jnp.bfloat16).T
        return 0

    lax.fori_loop(0, 2 * rows // chunk, one, 0)
    stores = Loads([(out2.at[:rows], content_out), (out2.at[rows:], query_out), (back, back_out), (got, got_out)], store_sems)
    for t in range(4):
        wo_block[t, :, :narrow] = nn(gat[...], onat[:, t * narrow:(t + 1) * narrow]).astype(jnp.bfloat16)

    def send(t):
        return pltpu.make_async_copy(stage.at[t % 2], grads.at[t], out_sems.at[t % 2])

    for t in range(4):
        if t >= 2:
            send(t - 2).wait()
        stage[t % 2, :, :wide] = nn(n1bt[...], gu[t]).astype(jnp.bfloat16)
        stage[t % 2, :, wide:2 * wide] = nn(gft[...], hidden[t]).astype(jnp.bfloat16)
        stage[t % 2, :, 2 * wide:] = wo_block[t, :, :narrow]
        send(t).start()
    for t in (2, 3):
        send(t).wait()
    stores.wait(0, 1, 2, 3)


def middle(ot, content, query, first, second, norms, ranks, up_content, up_query):
    rows, width = content.shape
    narrow, wide = width // 4, second.shape[2] // 2
    both, chunk = 2 * rows, rows
    V, A = pl.BlockSpec(memory_space=pltpu.MemorySpace.VMEM), pl.BlockSpec(memory_space=pl.ANY)
    B, F, S, DMA = jnp.bfloat16, jnp.float32, jax.ShapeDtypeStruct, pltpu.SemaphoreType.DMA
    return pl.pallas_call(
        functools.partial(middle_kernel, chunk),
        out_shape=(S((rows, width), B), S((rows, width), B), S((4, width, 2 * wide + narrow), B), S((both, width), F), S((width, both), B), S((8, width), F)),
        in_specs=[A, V, V, A, A] + [V] * 7, out_specs=(A, A, A, A, A, V),
        scratch_shapes=[
            pltpu.VMEM((both, width), F), pltpu.VMEM((width, both), B), DMA((4,)), pltpu.VMEM(ot.shape, B), pltpu.VMEM(second.shape, B),
            pltpu.VMEM((both, width), B), pltpu.VMEM((both, width), F), pltpu.VMEM((width, width), B), pltpu.VMEM((4, width, 256), B),
            pltpu.VMEM((both, width), B), pltpu.VMEM((width, both), B), pltpu.VMEM((width, both), B), pltpu.VMEM((width, both), B),
            pltpu.VMEM((4, both, wide), B), pltpu.VMEM((4, chunk, wide), F), pltpu.VMEM((4, both, wide), B), pltpu.VMEM((both, width), B),
            pltpu.VMEM((2, width, 2 * wide + narrow), B), DMA((9,)), DMA((2,)),
        ],
        compiler_params=pltpu.CompilerParams(vmem_limit_bytes=VLIM), name="middle",
    )(ot, content, query, first, second, *norms, ranks, up_content, up_query)


def finish_kernel(count, *refs):
    sources, norms, outs, held, sems = refs[:count], refs[count], refs[count + 1:2 * count + 5], refs[2 * count + 5:-1], refs[-1]
    loads = [pltpu.make_async_copy(src, mid, sems.at[0, i]) for i, (src, mid) in enumerate(zip(sources, held))]
    stores = [pltpu.make_async_copy(mid, dst, sems.at[1, i]) for i, (mid, dst) in enumerate(zip(held, outs))]
    for c in loads:
        c.start()
    for i in range(4):
        outs[count + i][...] = norms[i:i + 1, :].reshape(norms.shape[1])
    for load, store in zip(loads, stores):
        load.wait()
        store.start()
    for c in stores:
        c.wait()


def finish(arrays, norms):
    V, A, S = pl.BlockSpec(memory_space=pltpu.MemorySpace.VMEM), pl.BlockSpec(memory_space=pl.ANY), jax.ShapeDtypeStruct
    count = len(arrays)
    return pl.pallas_call(
        functools.partial(finish_kernel, count),
        out_shape=tuple(S(a.shape, a.dtype) for a in arrays) + tuple(S((norms.shape[1],), norms.dtype) for _ in range(4)),
        in_specs=[A] * count + [V], out_specs=(A,) * count + (V,) * 4, scratch_shapes=[pltpu.VMEM(a.shape, a.dtype) for a in arrays] + [pltpu.SemaphoreType.DMA((2, count))],
        compiler_params=pltpu.CompilerParams(vmem_limit_bytes=VLIM), name="finish",
    )(*arrays, norms)


def dot(spec, a, b):
    return jnp.einsum(spec, a, b, preferred_element_type=jnp.float32)


def norm_stats(residual):
    centered = residual - jnp.mean(residual, axis=-1, keepdims=True)
    scale = lax.rsqrt(jnp.mean(centered * centered, axis=-1, keepdims=True) + EPSILON)
    return centered * scale, scale


def norm_back(cotangent, normal, scale, gain):
    inner = cotangent * gain
    mean_inner = jnp.mean(inner, axis=-1, keepdims=True)
    mean_cross = jnp.mean(inner * normal, axis=-1, keepdims=True)
    back = scale * (inner - mean_inner - normal * mean_cross)
    return back, jnp.sum(cotangent * normal, axis=0), jnp.sum(cotangent, axis=0)


def local(
    tp_size, own_exchange, content, query, w_query, w_key, w_value, w_out, w_in, w_down, gain_first, shift_first,
    gain_second, shift_second, bias_table, ranks, span_starts, upstream_content, upstream_query,
):
    rows, width = content.shape
    seq = ranks.shape[1]
    heads = bias_table.shape[0]
    pairs = heads // 2
    tp_index = lax.axis_index("tp")
    both_axes = ("tp", "fsdp")
    narrow = w_query.shape[1]

    def gather(parts):
        shard = jnp.concatenate(parts, axis=1)
        return lax.all_gather(shard, both_axes, axis=0, tiled=True).reshape(tp_size, width, shard.shape[1])

    wide = w_in.shape[1]
    shift = -rows * tp_index
    both = jnp.concatenate([content, query], axis=0)
    if own_exchange:
        ot, lse, seqt, queryt, kp, vp, kt, qt, first, second = front(
            content, query, w_query, w_key, w_value, w_out, w_in, w_down.T, ranks, span_starts, bias_table
        )
        first, second = first.reshape(tp_size, width, 4 * narrow), second.reshape(tp_size, width, 2 * wide)
    else:
        first, second = gather([w_out.T, w_query, w_key, w_value]), gather([w_in, w_down.T])
    wo, wq, wk, wv = (first[:, :, i * narrow:(i + 1) * narrow] for i in range(4))
    wi, wd = second[:, :, :wide], second[:, :, wide:]
    if not own_exchange:
        seq_rot = jnp.roll(lax.all_gather(content, "tp", axis=0, tiled=True), shift, axis=0)
        qt = (dot("tdc,rd->tcr", wq, both) * (HEAD ** -0.5 * LOG2E)).astype(jnp.bfloat16).reshape(width, 2 * rows)
        kt = dot("tdc,rd->tcr", wk, seq_rot).astype(jnp.bfloat16).reshape(width, seq)
        vt = dot("tdc,rd->tcr", wv, seq_rot).astype(jnp.bfloat16).reshape(width, seq)
        kp = jnp.swapaxes(kt.reshape(pairs, 128, seq), 1, 2)
        vp = jnp.swapaxes(vt.reshape(pairs, 128, seq), 1, 2)
        ot, lse = attend_fwd(tp_size, ranks, span_starts, bias_table, kp, vt, qt)

    if own_exchange:
        norms = [gain_first, shift_first, gain_second, shift_second]
        content_out, query_out, grad_second, back_first, got, norm_stack = middle(
            ot, content, query, first, second, norms, ranks, upstream_content, upstream_query
        )
    else:
        ot_blocks = ot.reshape(tp_size, narrow, 2 * rows)
        residual_first = both.astype(jnp.float32) + dot("tcr,tmc->rm", ot_blocks, wo)
        normal_first, scale_first = norm_stats(residual_first)
        normed_first = normal_first * gain_first + shift_first
        low_first = normed_first.astype(jnp.bfloat16)
        lifted = dot("rd,tdf->trf", low_first, wi)
        phi = 0.5 * (1.0 + lax.erf(lifted * (0.5 ** 0.5)))
        hidden = (lifted * phi).astype(jnp.bfloat16)
        slope = phi + lifted * jnp.exp(-0.5 * lifted * lifted) * 0.3989422804014327
        residual_second = normed_first + dot("trf,tmf->rm", hidden, wd)
        normal_second, scale_second = norm_stats(residual_second)
        normed_second = normal_second * gain_second + shift_second
        rank_rows = lax.dynamic_slice_in_dim(ranks[0], rows * tp_index, rows)
        predicted = (rank_rows >= seq - seq * 15 // 100).astype(jnp.float32)
        upstream = jnp.concatenate(
            [upstream_content.astype(jnp.float32), upstream_query.astype(jnp.float32) * predicted[:, None]], axis=0
        )
        back_second, grad_gain_second, grad_shift_second = norm_back(upstream, normal_second, scale_second, gain_second)
        gf = back_second.astype(jnp.bfloat16)
        gu = (slope * dot("rm,tmf->trf", gf, wd)).astype(jnp.bfloat16)
        grad_down = dot("rm,trf->tmf", gf, hidden)
        grad_in = dot("rd,trf->tdf", low_first, gu)
        back_normed = back_second + dot("trf,tdf->rd", gu, wi)
        back_first, grad_gain_first, grad_shift_first = norm_back(back_normed, normal_first, scale_first, gain_first)
        ga = back_first.astype(jnp.bfloat16)
        grad_out = dot("rm,tcr->tmc", ga, ot_blocks)
        got = dot("rm,tmc->tcr", ga, wo).astype(jnp.bfloat16).reshape(width, 2 * rows)
        content_out, query_out = (normed_second[s * rows:(s + 1) * rows].astype(jnp.bfloat16) for s in range(2))
        norm_stack = jnp.stack([grad_gain_first, grad_shift_first, grad_gain_second, grad_shift_second])

    def scatter(blocks):
        flat = blocks.astype(jnp.bfloat16).reshape(tp_size * width, blocks.shape[2])
        return lax.psum_scatter(flat, both_axes, scatter_dimension=0, tiled=True).astype(jnp.float32)

    if own_exchange:
        grad_second = grad_second.reshape(4, 2, 2, 2, width // 8, grad_second.shape[2])
        gqt, gkt, gvt, grad_table, sum_in, sum_down, sum_out, parts = attend_bwd(
            tp_size, ranks, span_starts, bias_table, kp, vp, kt, qt, ot, got, lse, grad_second, first
        )
        grad_content, grad_query, sum_query, sum_key, sum_value, norms, grad_table = tail(
            parts, gqt, gkt, gvt, seqt, queryt, first, back_first, norm_stack, grad_table
        )
        (grad_content, grad_query, sum_query, sum_key, sum_value, sum_out, sum_in, sum_down, *norms) = finish(
            (grad_content, grad_query, sum_query, sum_key, sum_value, sum_out, sum_in, sum_down), norms
        )
    else:
        sum_down, sum_in, sum_out = scatter(grad_down), scatter(grad_in), scatter(grad_out).T
        gqt, gkt, gvt, grad_table = attend_bwd(tp_size, ranks, span_starts, bias_table, kp, vp, kt, qt, ot, got, lse)
        gq_blocks, gk_blocks, gv_blocks = (g.reshape(tp_size, narrow, g.shape[1]) for g in (gqt, gkt, gvt))
        sum_query = scatter(dot("rd,tcr->tdc", both, gq_blocks))
        sum_key = scatter(dot("rd,tcr->tdc", seq_rot, gk_blocks))
        sum_value = scatter(dot("rd,tcr->tdc", seq_rot, gv_blocks))
        back_seq = dot("tcr,tdc->rd", gk_blocks, wk) + dot("tcr,tdc->rd", gv_blocks, wv)
        back_seq = jnp.roll(back_seq.astype(jnp.bfloat16), -shift, axis=0)
        back_content = lax.psum_scatter(back_seq, "tp", scatter_dimension=0, tiled=True).astype(jnp.float32)
        back_inputs = back_first + dot("tcr,tdc->rd", gq_blocks, wq)
        grad_content, grad_query = back_inputs[:rows] + back_content, back_inputs[rows:]
        norms, grad_table = lax.psum((norm_stack, grad_table), ("fsdp", "tp"))
    return (
        content_out, query_out, grad_content, grad_query, sum_query, sum_key, sum_value, sum_out, sum_in, sum_down.T,
        norms[0], norms[1], norms[2], norms[3], grad_table[:, :NB],
    )


def solution(mesh):
    in_specs = (
        P(("fsdp", "tp"), None),
        P(("fsdp", "tp"), None),
        P("fsdp", "tp"),
        P("fsdp", "tp"),
        P("fsdp", "tp"),
        P("tp", "fsdp"),
        P("fsdp", "tp"),
        P("tp", "fsdp"),
        P(),
        P(),
        P(),
        P(),
        P(),
        P("fsdp", None),
        P("fsdp", None),
        P(("fsdp", "tp"), None),
        P(("fsdp", "tp"), None),
    )
    out_specs = (
        P(("fsdp", "tp"), None),
        P(("fsdp", "tp"), None),
        P(("fsdp", "tp"), None),
        P(("fsdp", "tp"), None),
        P("fsdp", "tp"),
        P("fsdp", "tp"),
        P("fsdp", "tp"),
        P("tp", "fsdp"),
        P("fsdp", "tp"),
        P("tp", "fsdp"),
        P(),
        P(),
        P(),
        P(),
        P(),
    )
    return jax.shard_map(functools.partial(local, mesh.shape["tp"], mesh.shape["tp"] == 4 and mesh.shape["fsdp"] == 8), mesh=mesh, in_specs=in_specs, out_specs=out_specs, check_vma=False)
```

```python
import functools
import jax, jax.numpy as jnp
from jax import lax
from jax.sharding import PartitionSpec as P
from jax.experimental import pallas as pl
from jax.experimental.pallas import tpu as pltpu

NEG = -1e30
PIECES = 1
HEAD = 64
NB = 32
PIC = 256
THRESHOLDS = (12, 16, 23, 32, 46, 64, 91)
EPSILON = 1e-05
LOG2E = 1.4426950408889634
LN2 = 0.6931471805599453
VLIM = 60 * 2**20
MESH = pl.DeviceIdType.MESH

def pick(index, values):
    result = jnp.int32(values[-1])
    for place in range(len(values) - 2, -1, -1):
        result = jnp.where(index == place, jnp.int32(values[place]), result)
    return result


class Place:
    def __init__(self):
        f, t = lax.axis_index("fsdp"), lax.axis_index("tp")
        self.f, self.t = f, t
        self.y, self.x, self.c = f // 4, (f // 2) % 2, f % 2
        self.core = (f + 1 - 2 * self.c, t)
        self.xn = (f + 2 - 4 * self.x, t)
        self.yn = (f + 4 - 8 * self.y, t)
        self.up, self.down = (f, t + 1), (f, t - 1)
        self.order = [pick(t, row) for row in ((3, 3, 0, 0), (2, 0, 3, 1), (1, 2, 1, 2), (0, 1, 2, 3))]

    def greet(self):
        barrier = pltpu.get_barrier_semaphore()
        for there in (self.core, self.xn, self.yn):
            pl.semaphore_signal(barrier, inc=1, device_id=there, device_id_type=MESH)
        for there in ((self.f, jnp.where(self.t > 0, self.t - 1, 3)), (self.f, jnp.where(self.t < 3, self.t + 1, 0))):
            pl.semaphore_signal(barrier, inc=1, device_id=there, device_id_type=MESH)
        pl.semaphore_wait(barrier, 5)


def rdma(src, dst, ss, rs, there):
    return pltpu.make_async_remote_copy(src_ref=src, dst_ref=dst, send_sem=ss, recv_sem=rs, device_id=there, device_id_type=MESH)


class Loads:
    def __init__(self, pairs, sems):
        self.copies = [pltpu.make_async_copy(src, dst, sems.at[i]) for i, (src, dst) in enumerate(pairs)]
        for c in self.copies:
            c.start()

    def wait(self, *which):
        for i in which:
            self.copies[i].wait()


class Scatter:
    def __init__(self, at, g, own, r0, r1a, r1b, r2a, r2b, zs, zr, sems, keep_sems):
        self.at, self.g, self.own, self.keep_sems = at, g, own, keep_sems
        self.r0, self.r1a, self.r1b, self.r2a, self.r2b, self.zs, self.zr = r0, r1a, r1b, r2a, r2b, zs, zr
        self.sems = sems
        self.wa = r1a.shape[-1]

    def sem(self, i):
        return self.sems.at[0, i], self.sems.at[1, i]

    def copy0(self, k):
        a = self.at; d = a.order[k]
        return rdma(self.g.at[d, :, :, 1 - a.c], self.r0.at[d], *self.sem(k), a.core)

    def copy1(self, k):
        a = self.at; d = a.order[k]; wa = self.wa
        return (rdma(self.r0.at[d, :, 1 - a.x, :, :wa], self.r1a.at[d], *self.sem(4 + k), a.xn),
                rdma(self.r0.at[d, 1 - a.y, :, :, wa:], self.r1b.at[d], *self.sem(8 + k), a.yn))

    def copy2(self, k):
        a = self.at; d = a.order[k]
        return (rdma(self.r1a.at[d, 1 - a.y], self.r2a.at[d], *self.sem(12 + k), a.yn),
                rdma(self.r1b.at[d, 1 - a.x], self.r2b.at[d], *self.sem(16 + k), a.xn))

    def hop(self, side, h):
        a = self.at
        return rdma(self.zs.at[side, h - 1], self.zr.at[side, h - 1], *self.sem(20 + 3 * side + h - 1), a.down if side else a.up)

    def keep(self, k):
        a = self.at; d = a.order[k]
        return pltpu.make_async_copy(self.g.at[d, :, :, a.c], self.own.at[d], self.keep_sems.at[k])

    def start(self):
        for k in range(4):
            self.copy0(k).start()
            self.keep(k).start()

    def start_one(self, k):
        self.copy0(k).start()

    def stage0(self, k):
        a = self.at; d = a.order[k]
        if self.own is None:
            own = self.g[d, :, :, a.c]
        else:
            self.keep(k).wait()
            own = self.own[d]
        self.copy0(k).wait()
        self.r0[d] = self.r0[d] + own
        for c in self.copy1(k): c.start()

    def stage1(self, k):
        a = self.at; d = a.order[k]; wa = self.wa
        for c in self.copy1(k): c.wait()
        self.r1a[d] = self.r1a[d] + self.r0[d, :, a.x, :, :wa]
        self.r1b[d] = self.r1b[d] + self.r0[d, a.y, :, :, wa:]
        for c in self.copy2(k): c.start()

    def stage2(self, k):
        a = self.at; d = a.order[k]
        for c in self.copy2(k): c.wait()
        self.r2a[d] = self.r2a[d] + self.r1a[d, a.y]
        self.r2b[d] = self.r2b[d] + self.r1b[d, a.x]

    def stage3(self, h):
        wa = self.wa
        for side in range(2):
            u = 3 - self.at.t if side else self.at.t
            d = (self.at.t + h - 4) if side else (self.at.t + 4 - h)
            if h > 1:
                @pl.when((u > 0) & (u < 3) & (u <= h - 1))
                def _():
                    self.hop(side, h - 1).wait_recv()
                    self.zs[side, h - 1, :, :wa] = self.r2a[d] + self.zr[side, h - 2, :, :wa]
                    self.zs[side, h - 1, :, wa:] = self.r2b[d] + self.zr[side, h - 2, :, wa:]
                    self.hop(side, h).start()
            @pl.when(u == 0)
            def _():
                self.zs[side, h - 1, :, :wa] = self.r2a[d]
                self.zs[side, h - 1, :, wa:] = self.r2b[d]
                self.hop(side, h).start()

    def finish(self):
        a = self.at; wa = self.wa
        for side in range(2):
            u = 3 - a.t if side else a.t
            @pl.when(u > 0)
            def _():
                self.hop(side, 3).wait_recv()
        mine = jnp.concatenate([self.r2a[a.t], self.r2b[a.t]], axis=1).astype(jnp.float32)
        below = jnp.where(a.t > 0, self.zr[0, 2].astype(jnp.float32), 0.0)
        above = jnp.where(a.t < 3, self.zr[1, 2].astype(jnp.float32), 0.0)
        for side in range(2):
            u = 3 - a.t if side else a.t
            for h in range(1, 4):
                @pl.when(u < h)
                def _():
                    self.hop(side, h).wait_send()
        return mine + below + above


class Fold:
    def __init__(self, at, part, got, sems):
        self.at, self.part, self.got, self.sems = at, part, got, sems

    def hop(self, side, h):
        a = self.at
        d = jnp.clip((a.t + h - 4) if side else (a.t + 4 - h), 0, 3)
        i = 3 * side + h - 1
        return rdma(self.part.at[d], self.got.at[side, h - 1], self.sems.at[0, i], self.sems.at[1, i], a.down if side else a.up)

    def step(self, h):
        for side in range(2):
            u = 3 - self.at.t if side else self.at.t
            d = (self.at.t + h - 4) if side else (self.at.t + 4 - h)
            @pl.when(u == 0)
            def _():
                if h > 1:
                    self.hop(side, h - 1).wait_send()
                self.hop(side, h).start()
            if h > 1:
                @pl.when((u > 0) & (u < 3) & (u <= h - 1))
                def _():
                    self.hop(side, h - 1).wait_recv()
                    self.part[d] = self.part[d] + self.got[side, h - 2]
                    self.hop(side, h).start()

    def finish(self):
        a = self.at
        for side in range(2):
            u = 3 - a.t if side else a.t
            @pl.when(u > 0)
            def _():
                self.hop(side, 3).wait_recv()
            for h in range(1, 4):
                @pl.when((u < h) & ((u > 0) | (h == 3)))
                def _():
                    self.hop(side, h).wait_send()
        below = jnp.where(a.t > 0, self.got[0, 2].astype(jnp.float32), 0.0)
        above = jnp.where(a.t < 3, self.got[1, 2].astype(jnp.float32), 0.0)
        return self.part[a.t].astype(jnp.float32) + below + above

def scatter_scratch(T, R, W, kept=True):
    wa = (W + 128) // 256 * 128
    B = jnp.bfloat16
    return [pltpu.VMEM((T, 2, 2, R, W), B)] * (2 if kept else 1) + [pltpu.VMEM((T, 2, R, wa), B), pltpu.VMEM((T, 2, R, W - wa), B),
            pltpu.VMEM((T, R, wa), B), pltpu.VMEM((T, R, W - wa), B), pltpu.VMEM((2, 3, R, W), B), pltpu.VMEM((2, 3, R, W), B),
            pltpu.SemaphoreType.DMA((2, 26))] + [pltpu.SemaphoreType.DMA((4,))] * kept

class Total:
    def __init__(self, at, sources, acc, got, sems):
        self.at, self.sources, self.acc, self.got, self.sems = at, sources, acc, got, sems
        t = at.t
        self.partners = [at.core, at.xn, at.yn, (at.f, t + 1 - 2 * (t % 2)), (at.f, 3 - t)]

    def copy(self, i):
        return rdma(self.acc.at[i], self.got.at[i], self.sems.at[0, i], self.sems.at[1, i], self.partners[i])

    def start(self):
        norms, table = self.sources
        self.acc[0] = jnp.zeros_like(self.acc[0])
        self.acc[0, :8, :] = norms[...]
        self.acc[0, 8:8 + table.shape[0], :table.shape[1]] = table[...]
        self.copy(0).start()

    def step(self, i):
        self.copy(i).wait_recv()
        self.acc[i + 1] = self.acc[i] + self.got[i]
        if i < 4:
            self.copy(i + 1).start()

    def finish(self, norms_out, table_out):
        for i in range(5):
            self.copy(i).wait_send()
        norms_out[...] = self.acc[5, :8, :]
        table_out[...] = self.acc[5, 8:8 + table_out.shape[0], :table_out.shape[1]]


def total_scratch(rows, width):
    F = jnp.float32
    return [pltpu.VMEM((6, rows, width), F), pltpu.VMEM((5, rows, width), F), pltpu.SemaphoreType.DMA((2, 5))]


def tail_kernel(part_in, gqt_in, gkt_in, gvt_in, seqt_in, queryt_in, first, back_in, norms, table,
                grad_content, grad_query, sum_query, sum_key, sum_value, norms_out, table_out,
                gqt, gkt, gvt, seqt, queryt, back, weights, part, got, g1, load_sems, fold_sems, *scratch):
    rows, width = grad_content.shape
    narrow, R = width // 4, sum_query.shape[0]
    at = Place()
    leading = pltpu.make_async_copy(part_in, part, load_sems.at[10])
    leading.start()
    at.greet()
    scatter, fold, total = Scatter(at, g1, None, *scratch[:8], None), Fold(at, part, got, fold_sems), Total(at, (norms, table), *scratch[8:])
    leading.wait()
    fold.step(1)
    loads = Loads(
        [(gkt_in, gkt), (gvt_in, gvt), (seqt_in, seqt), (queryt_in, queryt), (gqt_in, gqt), (back_in, back)]
        + [(first.at[b, :, pl.ds(128, 256)], weights.at[b]) for b in range(4)], load_sems
    )
    total.start()

    def weight_grads(k):
        d = at.order[k]
        here = pl.ds(pl.multiple_of(d * narrow, 64), narrow)
        query = nt(seqt[:, :rows], gqt[here, :rows]) + nt(queryt[...], gqt[here, rows:])
        block = jnp.concatenate([query, nt(seqt[...], gkt[here, :]), nt(seqt[...], gvt[here, :])], axis=1)
        g1[d] = block.astype(jnp.bfloat16).reshape(2, 2, 2, R, 3 * narrow)
        scatter.start_one(k)

    loads.wait(0, 1, 2, 3, 4)
    total.step(0)
    for k in range(4):
        weight_grads(k)
        if k == 1:
            total.step(1)
    scatter.stage0(0)
    scatter.stage0(1)
    total.step(2)
    scatter.stage0(2)
    scatter.stage0(3)
    loads.wait(5, 6, 7, 8, 9)
    for s, out in enumerate((grad_content, grad_query)):
        cols = slice(s * rows, (s + 1) * rows)
        value = back[cols, :]
        for b in range(4):
            value = value + nt(gqt[b * narrow:(b + 1) * narrow, cols].T, weights[b, :, 64:256])
        out[...] = value
    fold.step(2)
    scatter.stage1(0)
    scatter.stage1(1)
    total.step(3)
    scatter.stage1(2)
    scatter.stage1(3)
    scatter.stage2(0)
    scatter.stage3(1)
    scatter.stage2(1)
    total.step(4)
    fold.step(3)
    scatter.stage3(2)
    scatter.stage2(2)
    scatter.stage2(3)
    scatter.stage3(3)
    sums = scatter.finish()
    for i, out in enumerate((sum_query, sum_key, sum_value)):
        out[...] = sums[:, i * narrow:(i + 1) * narrow]
    total.finish(norms_out, table_out)
    grad_content[...] += fold.finish()


def tail(parts, gqt, gkt, gvt, seqt, queryt, first, back, norms, table):
    width, both = gqt.shape
    rows, narrow, R = both // 2, width // 4, width // 8
    V, A = pl.BlockSpec(memory_space=pltpu.MemorySpace.VMEM), pl.BlockSpec(memory_space=pl.ANY)
    B, F, S, DMA = jnp.bfloat16, jnp.float32, jax.ShapeDtypeStruct, pltpu.SemaphoreType.DMA
    outs = [S((rows, width), F)] * 2 + [S((R, narrow), F)] * 3 + [S(norms.shape, F), S(table.shape, F)]
    return pl.pallas_call(
        tail_kernel, out_shape=tuple(outs), in_specs=[A] * 8 + [V, V], out_specs=(V,) * 7,
        scratch_shapes=[
            pltpu.VMEM(gqt.shape, B), pltpu.VMEM(gkt.shape, B), pltpu.VMEM(gvt.shape, B), pltpu.VMEM(seqt.shape, B), pltpu.VMEM(queryt.shape, B),
            pltpu.VMEM(back.shape, F),
            pltpu.VMEM((4, width, 256), B), pltpu.VMEM((4, rows, width), B), pltpu.VMEM((2, 3, rows, width), B),
            pltpu.VMEM((4, 2, 2, 2, R, 3 * narrow), B), DMA((11,)), DMA((2, 6)),
        ] + scatter_scratch(4, R, 3 * narrow, False) + total_scratch(24, width),
        compiler_params=pltpu.CompilerParams(vmem_limit_bytes=VLIM, collective_id=1, has_side_effects=True), name="tail",
    )(parts, gqt, gkt, gvt, seqt, queryt, first, back, norms, table)


def nn(a, b):
    return lax.dot_general(a, b, (((1,), (0,)), ((), ())), preferred_element_type=jnp.float32)
def nt(a, b):
    return lax.dot_general(a, b, (((1,), (1,)), ((), ())), preferred_element_type=jnp.float32)

def band_kind(i, b, nrow, nkey):
    rel = (b - i) % nkey
    if rel == 0: return 2
    if rel == nkey - 1: return 0 if i == 0 else 1
    if rel == 1: return 4 if i == nrow - 1 else 3
    return None

def wrap(value, size):
    return jnp.where(value >= size, value - size, value)


def bucket_of(offsets):
    magnitude = jnp.abs(offsets)
    far_bucket = 8 + sum((magnitude >= threshold).astype(jnp.int32) for threshold in THRESHOLDS)
    return jnp.where(magnitude < 8, magnitude, far_bucket) + jnp.where(offsets > 0, 16, 0)


def slot_bucket(slot, lanes, tp_index, tp_size):
    if slot >= 10:
        return jnp.full_like(lanes, 15 if slot == 10 else 31)
    kind, wrapped = slot // 2, slot % 2
    buckets = bucket_of(128 * ((-1, -1, 0, 1, 1)[kind] + wrapped) - lanes)
    if kind == 0:
        return jnp.where(tp_index == 0, 31, buckets)
    if kind == 4:
        return jnp.where(tp_index == tp_size - 1, 15, buckets)
    return buckets


def far_sides(nrow, nkey, tp_index):
    key_block = lax.broadcasted_iota(jnp.int32, (16, 2 * nrow * 128), 0)
    row_block = wrap(lax.broadcasted_iota(jnp.int32, (16, 2 * nrow * 128), 1) // 128, nrow)
    gap = key_block - row_block
    near = (gap == 0) | (gap == 1) | (gap == -1) | (gap == nkey - 1) | (gap == 1 - nkey) | (key_block >= nkey)
    key_place, row_place = wrap(key_block + nrow * tp_index, nkey), row_block + nrow * tp_index
    left = jnp.where(near, 0.0, jnp.where(key_place < row_place, 1.0, 0.0))
    return left, jnp.where(near, 0.0, 1.0 - left)


def prepare(nrow, nkey, tp_size, ranks, starts, table, mask, ring, vec, sides):
    tp_index = lax.axis_index("tp")
    rows, seq = nrow * 128, nkey * 128
    base = rows * tp_index
    rank_row = jnp.broadcast_to(ranks[...].astype(jnp.float32), (8, seq))
    ring[:, :seq] = rank_row
    ring[:, seq:] = rank_row

    def label(place):
        found = jnp.zeros(place.shape, jnp.int32)
        for k in range(starts.shape[1]):
            start = starts[0, k]
            found = found + jnp.where((place >= start) & (place < start + PIC), k + 1, 0)
        return found

    row_rank, row_label = [], []
    for i in range(nrow):
        row_rank.append(ring[0:1, pl.ds(pl.multiple_of(base + i * 128, 128), 128)])
        row_label.append(label(base + i * 128 + lax.broadcasted_iota(jnp.int32, (1, 128), 1)))

    def one(b, _):
        keys = pl.ds(pl.multiple_of(b * 128, 128), 128)
        rank_k = jnp.broadcast_to(ring[0:1, pl.ds(pl.multiple_of(base + b * 128, 128), 128)], (128, 128)).T
        kpos = b * 128 + lax.broadcasted_iota(jnp.int32, (128, 128), 0)
        label_k = label(wrap(base + kpos, seq))
        for i in range(nrow):
            rpos = i * 128 + lax.broadcasted_iota(jnp.int32, (128, 128), 1)
            same = (label_k == row_label[i]) & (label_k > 0)
            content = (rank_k <= row_rank[i]) | same
            strict = (rank_k < jnp.maximum(row_rank[i], 1.0)) | (same & (kpos != rpos))
            mask[keys, i * 128:(i + 1) * 128] = jnp.where(content, 0.0, NEG)
            mask[keys, rows + i * 128:rows + (i + 1) * 128] = jnp.where(strict, 0.0, NEG)
        return 0
    lax.fori_loop(0, nkey, one, 0)

    heads = table.shape[0]
    lanes = lax.broadcasted_iota(jnp.int32, (heads, 128), 1)
    columns = [jnp.broadcast_to(table[:, n:n + 1] * LOG2E, (heads, 128)) for n in range(NB)]
    for slot in range(12):
        buckets = slot_bucket(slot, lanes, tp_index, tp_size)
        values = columns[0]
        for n in range(1, NB):
            values = jnp.where(buckets == n, columns[n], values)
        for h in range(heads):
            vec[h, slot:slot + 1, :] = values[h:h + 1, :]
    sides[0], sides[1] = far_sides(nrow, nkey, tp_index)


def far_bias(vec, sides, cf, h):
    copies = cf.shape[1] // 128
    left, right = (jnp.concatenate([vec[h, slot:slot + 1, :]] * copies, axis=1) for slot in (10, 11))
    cf[...] = sides[0] * left + sides[1] * right


def prepare_scratch(nrow, nkey, heads):
    F, rows = jnp.float32, 2 * nrow * 128
    return [
        pltpu.VMEM((nkey * 128, rows), F), pltpu.VMEM((8, 2 * nkey * 128), F), pltpu.VMEM((heads, 12, 128), F),
        pltpu.VMEM((2, 16, rows), F), pltpu.VMEM((16, rows), F), pltpu.VMEM((5, 128, 128), F),
    ]


def band_tiles(band, vec, h):
    lane = lax.broadcasted_iota(jnp.int32, (128, 128), 1)
    sub = lax.broadcasted_iota(jnp.int32, (128, 128), 0)
    for k in range(5):
        direct, wrapped = (
            pltpu.roll(jnp.broadcast_to(vec[h, 2 * k + w:2 * k + w + 1, :], (128, 128)), 0, 1, stride=1, stride_axis=0)
            for w in range(2)
        )
        band[k] = jnp.where(lane >= sub, direct, wrapped)

def diagonal_sums(tile):
    lane = lax.broadcasted_iota(jnp.int32, (8, 128), 1)
    sub = lax.broadcasted_iota(jnp.int32, (8, 128), 0)
    direct = wrapped = jnp.zeros((8, 128), jnp.float32)
    for a in range(16):
        rows = tile[8 * a:8 * a + 8, :]
        kept = jnp.where(lane >= sub + 8 * a, rows, 0.0)
        left = rows - kept
        if a:
            kept, left = pltpu.roll(kept, 128 - 8 * a, 1), pltpu.roll(left, 128 - 8 * a, 1)
        direct, wrapped = direct + kept, wrapped + left
    for bit in (1, 2, 4):
        moved = (sub & bit) != 0
        direct = jnp.where(moved, pltpu.roll(direct, 128 - bit, 1), direct)
        wrapped = jnp.where(moved, pltpu.roll(wrapped, 128 - bit, 1), wrapped)
    return jnp.sum(direct, axis=0, keepdims=True), jnp.sum(wrapped, axis=0, keepdims=True)

def head_rows(ref, p, hh, cols):
    z = jnp.zeros((64, cols.stop - cols.start), jnp.bfloat16)
    rows = ref[pl.ds(pl.multiple_of((2 * p + hh) * 64, 64), 64), cols]
    return jnp.concatenate([rows, z] if hh == 0 else [z, rows], axis=0)

def attend_rows(nrow, nkey, kp, vt, qt, ot, lse, t, prepared, exchange):
    mask, _, vec, sides, cf, band = prepared
    ones = jnp.ones((16, 256), jnp.bfloat16)
    nchunk = 2 * nrow * 128 // 256
    def pair(p, _):
        for hh in range(2):
            h = 2 * p + hh
            exchange(h)
            hrows = pl.ds(pl.multiple_of(h * 64, 64), 64)
            band_tiles(band, vec, h)
            far_bias(vec, sides, cf, h)
            for c in range(nchunk):
                cols = slice(c * 256, (c + 1) * 256)
                qh = head_rows(qt, p, hh, cols)
                m8 = jnp.full((8, 256), -jnp.inf, jnp.float32)
                for b in range(nkey):
                    s = nn(kp[p, b * 128:(b + 1) * 128, :], qh)
                    s = s + mask[b * 128:(b + 1) * 128, cols]
                    kinds = [band_kind((2 * c + k) % nrow, b, nrow, nkey) for k in range(2)]
                    if any(k is not None for k in kinds):
                        s = jnp.concatenate([s[:, k * 128:(k + 1) * 128] + (band[kinds[k]] if kinds[k] is not None else 0.0) for k in range(2)], axis=1)
                    t[c, b * 128:(b + 1) * 128, :] = s
                    m8 = jnp.maximum(m8, jnp.max(s.reshape(16, 8, 256), axis=0) + cf[b:b + 1, cols])
                m = jnp.max(m8, axis=0, keepdims=True)
                acc = jnp.zeros((80, 256), jnp.float32)
                for g in range(nkey // 2):
                    ps = []
                    for b in (2 * g, 2 * g + 1):
                        ps.append(jnp.exp2(t[c, b * 128:(b + 1) * 128, :] - (m - cf[b:b + 1, cols])).astype(jnp.bfloat16))
                    lhs = jnp.concatenate([vt[hrows, g * 256:(g + 1) * 256], ones], axis=0)
                    acc = acc + nn(lhs, jnp.concatenate(ps, axis=0))
                l = acc[64:65, :]
                ot[hrows, cols] = (acc[:64, :] / l).astype(jnp.bfloat16)
                lse[h, 0:1, cols] = m + jnp.log2(l)
        return 0
    lax.fori_loop(0, kp.shape[0], pair, 0)

def fwd_kernel(nrow, nkey, tp_size, ranks, starts, table, kp, vt, qt, ot, lse, t, *prepared):
    prepare(nrow, nkey, tp_size, ranks, starts, table, *prepared[:4])
    attend_rows(nrow, nkey, kp, vt, qt, ot, lse, t, prepared, lambda h: None)


def attend_fwd(tp_size, ranks, starts, table, kp, vt, qt):
    pairs, seq, _ = kp.shape
    rows = qt.shape[1]
    nrow, nkey = rows // 256, seq // 128
    V, M = pl.BlockSpec(memory_space=pltpu.MemorySpace.VMEM), pl.BlockSpec(memory_space=pltpu.MemorySpace.SMEM)
    return pl.pallas_call(
        functools.partial(fwd_kernel, nrow, nkey, tp_size),
        out_shape=(jax.ShapeDtypeStruct(qt.shape, jnp.bfloat16), jax.ShapeDtypeStruct((2 * pairs, 1, rows), jnp.float32)),
        in_specs=[V, M, V, V, V, V], out_specs=(V, V),
        scratch_shapes=[pltpu.VMEM((rows // 256, seq, 256), jnp.float32)] + prepare_scratch(nrow, nkey, 2 * pairs),
        compiler_params=pltpu.CompilerParams(vmem_limit_bytes=VLIM),
        name="attend_fwd",
    )(ranks, starts, table, kp, vt, qt)


class Gather:
    def __init__(self, at, shard, g, wa, sems, own_sem):
        self.at, self.shard, self.g, self.wa, self.sems, self.own_sem = at, shard, g, wa, sems, own_sem
        self.blocks = at.order[::-1]

    def send(self, i, src, dst, there):
        return rdma(src, dst, self.sems.at[0, i], self.sems.at[1, i], there)

    def along_z(self, b, upward):
        a = self.at
        here = self.g.at[b, a.y, a.x, a.c]
        return self.send(b + (0 if upward else 4), here, here, a.up if upward else a.down)

    def first(self, b):
        a, wa = self.at, self.wa
        left, right = (self.g.at[b, a.y, a.x, a.c, :, cols] for cols in (slice(0, wa), slice(wa, None)))
        return self.send(8 + b, left, left, a.xn), self.send(12 + b, right, right, a.yn)

    def second(self, b):
        a, wa = self.at, self.wa
        left, right = self.g.at[b, a.y, :, a.c, :, :wa], self.g.at[b, :, a.x, a.c, :, wa:]
        return self.send(16 + b, left, left, a.yn), self.send(20 + b, right, right, a.xn)

    def across(self, b):
        a = self.at
        here = self.g.at[b, :, :, a.c]
        return self.send(24 + b, here, here, a.core)

    def own(self):
        a = self.at
        return pltpu.make_async_copy(self.shard, self.g.at[a.t, a.y, a.x, a.c], self.own_sem)

    def begin(self):
        self.own().start()
        self.own().wait()
        for c in self.first(self.at.t):
            c.start()

    def begin_z(self):
        a = self.at
        @pl.when(a.t < 3)
        def _():
            self.along_z(a.t, True).start()
        @pl.when(a.t > 0)
        def _():
            self.along_z(a.t, False).start()

    def arrive(self, j):
        a, b = self.at, self.blocks[j]
        @pl.when(b < a.t)
        def _():
            self.along_z(b, True).wait_recv()
        @pl.when(b > a.t)
        def _():
            self.along_z(b, False).wait_recv()
        @pl.when((b < a.t) & (a.t < 3))
        def _():
            self.along_z(b, True).start()
        @pl.when((b > a.t) & (a.t > 0))
        def _():
            self.along_z(b, False).start()
        for c in self.first(b):
            c.start()

    def step1(self, j):
        b = self.blocks[j]
        for c in self.first(b):
            c.wait_recv()
        for c in self.second(b):
            c.start()

    def step2(self, j):
        b = self.blocks[j]
        for c in self.second(b):
            c.wait_recv()
        self.across(b).start()

    def step3(self, j):
        self.across(self.blocks[j]).wait_recv()

    def finish(self):
        a = self.at
        for b in range(4):
            @pl.when((b <= a.t) & (a.t < 3))
            def _():
                self.along_z(b, True).wait_send()
            @pl.when((b >= a.t) & (a.t > 0))
            def _():
                self.along_z(b, False).wait_send()
            for c in (*self.first(b), *self.second(b), self.across(b)):
                c.wait_send()


class Chain:
    def __init__(self, at, seq, sems, pieces):
        self.at, self.seq, self.sems, self.pieces = at, seq, sems, pieces
        self.blocks = at.order[::-1]

    def move(self, b, upward, s):
        a = self.at
        i = (b + (0 if upward else 4)) * self.pieces + s
        there = a.t + 1 if upward else a.t - 1
        size = self.seq.shape[1] // self.pieces
        part = slice(s * size, (s + 1) * size)
        return rdma(self.seq.at[(b - a.t + 4) % 4, part], self.seq.at[(b - there + 4) % 4, part], self.sems.at[0, i], self.sems.at[1, i], (a.f, there))

    def begin(self):
        a = self.at
        for s in range(self.pieces):
            @pl.when(a.t < 3)
            def _():
                self.move(a.t, True, s).start()
            @pl.when(a.t > 0)
            def _():
                self.move(a.t, False, s).start()

    def arrive(self, j):
        a, b = self.at, self.blocks[j]
        for s in range(self.pieces):
            @pl.when(b < a.t)
            def _():
                self.move(b, True, s).wait_recv()
            @pl.when(b > a.t)
            def _():
                self.move(b, False, s).wait_recv()
            @pl.when((b < a.t) & (a.t < 3))
            def _():
                self.move(b, True, s).start()
            @pl.when((b > a.t) & (a.t > 0))
            def _():
                self.move(b, False, s).start()

    def finish(self):
        a = self.at
        for b in range(4):
            for s in range(self.pieces):
                @pl.when((b <= a.t) & (a.t < 3))
                def _():
                    self.move(b, True, s).wait_send()
                @pl.when((b >= a.t) & (a.t > 0))
                def _():
                    self.move(b, False, s).wait_send()


def front_kernel(nrow, nkey, content, query, w_query, w_key, w_value, w_out, w_in, w_down, ranks, starts, table,
                 ot, lse, seqt_out, queryt_out, kp_out, vp_out, kt_out, qt_out, w1_out, w2_out,
                 shard1, shard2, seq, seqt, queryt, w1, w2, w1t, kp, vp, kt, vt, qt, t,
                 sems1, sems2, semsc, own_sems, out_sems, *prepared):
    at = Place()
    rows = nrow * 128
    pairs = kp.shape[0]
    narrow = shard1.shape[1] // 4
    width = content.shape[1]
    weights1 = Gather(at, shard1, w1, shard1.shape[1] // 2, sems1, own_sems.at[0])
    weights2 = Gather(at, shard2, w2, shard2.shape[1] // 2, sems2, own_sems.at[1])
    chain = Chain(at, seq, semsc, PIECES)
    shard1[...] = jnp.concatenate([w_out[...].T, w_query[...], w_key[...], w_value[...]], axis=1)
    shard2[:, :w_in.shape[1]] = w_in[...]
    shard2[:, w_in.shape[1]:] = w_down[...]
    seq[0] = content[...]
    at.greet()
    weights1.begin()
    weights1.begin_z()
    weights1.arrive(1)
    weights1.step1(0)
    weights1.arrive(2)
    weights1.step1(1)
    weights1.step2(0)
    weights1.arrive(3)
    chain.begin()
    weights2.begin()
    weights2.begin_z()
    weights1.step1(2)
    weights1.step2(1)
    weights1.step1(3)
    prepare(nrow, nkey, 4, ranks, starts, table, *prepared[:4])
    weights1.step2(2)
    weights1.step2(3)
    for j in range(4):
        weights1.step3(j)

    scale = HEAD ** -0.5 * LOG2E
    for tt in range(4):
        block = w1[tt].reshape(width, 4 * narrow)
        w1t[tt] = block[:, narrow:].T
        for s, x in enumerate((content, query)):
            q = nt(w1t[tt, :narrow, :], x[...])
            qt[tt * narrow:(tt + 1) * narrow, s * rows:(s + 1) * rows] = (q * scale).astype(jnp.bfloat16)

    def project(r):
        x = seq[r]
        cols = pl.ds(pl.multiple_of(r * rows, 128), rows)
        seqt[:, cols] = x.T
        for i, (across, upright) in enumerate(((kp, kt), (vp, vt))):
            for tt in range(4):
                out = nt(w1t[tt, (i + 1) * narrow:(i + 2) * narrow, :], x)
                upright[tt * narrow:(tt + 1) * narrow, cols] = out.astype(jnp.bfloat16)
            for u in range(2):
                halves = [
                    nn(x, w1[2 * u + v].reshape(width, 4 * narrow)[:, (i + 2) * narrow:(i + 3) * narrow]) for v in range(2)
                ]
                joined = jnp.concatenate(halves, axis=1).astype(jnp.bfloat16)
                for p in range(pairs // 2):
                    across[u * (pairs // 2) + p, cols, :] = joined[:, p * 128:(p + 1) * 128]

    queryt[...] = query[...].T
    project(0)
    chain.arrive(1)
    weights2.arrive(1)
    weights2.step1(0)
    project((chain.blocks[1] - at.t + 4) % 4)
    chain.arrive(2)
    weights2.step2(0)
    weights2.step1(1)
    weights2.arrive(2)
    project((chain.blocks[2] - at.t + 4) % 4)
    chain.arrive(3)
    weights2.step2(1)
    weights2.step1(2)
    project((chain.blocks[3] - at.t + 4) % 4)

    outs = [
        pltpu.make_async_copy(src, dst, out_sems.at[i])
        for i, (src, dst) in enumerate(((seqt, seqt_out), (queryt, queryt_out), (kp, kp_out), (vp, vp_out), (kt, kt_out), (qt, qt_out), (w1, w1_out)))
    ]
    for c in outs:
        c.start()

    def second_out(j):
        b = weights2.blocks[j]
        return pltpu.make_async_copy(w2.at[b], w2_out.at[b], out_sems.at[7 + j])

    def exchange(h):
        steps = (
            (weights2.arrive, 3, 2),
            (weights2.step2, 2, 4),
            (weights2.step1, 3, 7),
            (weights2.step2, 3, 11),
        )
        for step, j, place in steps:
            @pl.when(h == place)
            def _():
                step(j)

    attend_rows(nrow, nkey, kp, vt, qt, ot, lse, t, prepared, exchange)
    for j in range(4):
        weights2.step3(j)
        second_out(j).start()
    for c in outs:
        c.wait()
    for j in range(4):
        second_out(j).wait()
    weights1.finish()
    weights2.finish()
    chain.finish()


def front(content, query, w_query, w_key, w_value, w_out, w_in, w_down, ranks, starts, table):
    rows, width = content.shape
    heads, seq_len = table.shape[0], ranks.shape[1]
    pairs, (R, narrow), wide = heads // 2, w_query.shape, w_in.shape[1]
    nrow, nkey = rows // 128, seq_len // 128
    V, A = pl.BlockSpec(memory_space=pltpu.MemorySpace.VMEM), pl.BlockSpec(memory_space=pl.ANY)
    B, F, S, DMA = jnp.bfloat16, jnp.float32, jax.ShapeDtypeStruct, pltpu.SemaphoreType.DMA
    full1, full2 = (4, 2, 2, 2, R, 4 * narrow), (4, 2, 2, 2, R, 2 * wide)
    kept = [((width, seq_len), B), ((width, rows), B), ((pairs, seq_len, 128), B), ((pairs, seq_len, 128), B), ((width, seq_len), B), ((width, 2 * rows), B), (full1, B)]
    outs = [S((width, 2 * rows), B), S((heads, 1, 2 * rows), F)] + [S(*k) for k in kept] + [S(full2, B)]
    scratch = [pltpu.VMEM((R, 4 * narrow), B), pltpu.VMEM((R, 2 * wide), B), pltpu.VMEM((4, rows, width), B), pltpu.VMEM(*kept[0]), pltpu.VMEM(*kept[1]), pltpu.VMEM(full1, B), pltpu.VMEM(full2, B),
               pltpu.VMEM((4, 3 * narrow, width), B), pltpu.VMEM(*kept[2]), pltpu.VMEM(*kept[3]),
               pltpu.VMEM(*kept[4]), pltpu.VMEM(*kept[4]), pltpu.VMEM(*kept[5]),
               pltpu.VMEM((2 * rows // 256, seq_len, 256), F),
               DMA((2, 28)), DMA((2, 28)), DMA((2, 8 * PIECES)), DMA((2,)), DMA((11,))] + prepare_scratch(nrow, nkey, heads)
    return pl.pallas_call(
        functools.partial(front_kernel, nrow, nkey),
        out_shape=tuple(outs), in_specs=[V] * 9 + [pl.BlockSpec(memory_space=pltpu.MemorySpace.SMEM), V], out_specs=tuple([V, V] + [A] * 8), scratch_shapes=scratch,
        compiler_params=pltpu.CompilerParams(vmem_limit_bytes=VLIM, collective_id=3, has_side_effects=True), name="front",
    )(content, query, w_query, w_key, w_value, w_out, w_in, w_down, ranks, starts, table)


def bwd_kernel(nrow, nkey, tp_size, fused, *refs):
    if fused:
        ranks, starts, table, kp, vp, kt, qt, ot, got, lse, g, first, gqt_out, gkt_out, gvt_out, back_table, sum_in, sum_down, sum_out, part, gq, bacc, diag, weights, gqt, gkt, gvt, out_sems, *scratch = refs
        prepared, kept, load_sems, scratch = scratch[:6], scratch[6:12], scratch[12], scratch[13:]
        loads = Loads(list(zip((kp, vp, kt, qt, ot, got), kept)) + [(first.at[b, :, pl.ds(384, 384)], weights.at[b]) for b in range(4)], load_sems)
        kp, vp, kt, qt, ot, got = kept
        at = Place()
        at.greet()
        scatter = Scatter(at, g, *scratch)
        scatter.start()
    else:
        ranks, starts, table, kp, vp, kt, qt, ot, got, lse, gqt, gkt, gvt, back_table, gq, bacc, diag, *prepared = refs
    mask, _, vec, sides, cf, band = prepared
    prepare(nrow, nkey, tp_size, ranks, starts, table, *prepared[:4])
    lane_row = lax.broadcasted_iota(jnp.int32, (1, 128), 1)
    if fused:
        loads.wait(0, 1, 2, 3, 4, 5)

    def exchange(h):
        if not fused:
            return
        steps = (
            (scatter.stage0, 0, 0), (scatter.stage0, 1, 1), (scatter.stage1, 0, 3), (scatter.stage0, 2, 3), (scatter.stage2, 0, 6), (scatter.stage3, 1, 6),
            (scatter.stage1, 1, 6), (scatter.stage0, 3, 6), (scatter.stage1, 2, 8), (scatter.stage2, 1, 9), (scatter.stage3, 2, 9), (scatter.stage1, 3, 11),
        )
        for step, k, place in steps:
            @pl.when(h == place)
            def _():
                step(k)

    rows = 2 * nrow * 128
    nchunk = rows // 256
    full = slice(0, rows)
    block_of = lax.broadcasted_iota(jnp.int32, (16, 256), 0)
    half_of = lax.broadcasted_iota(jnp.int32, (16, 256), 1) // 128
    def pair(p, _):
        for hh in range(2):
            h = 2 * p + hh
            exchange(h)
            hrows = pl.ds(pl.multiple_of(h * 64, 64), 64)
            band_tiles(band, vec, h)
            far_bias(vec, sides, cf, h)
            q_h = qt[hrows, :]
            go_h = got[hrows, :]
            delta = jnp.sum(ot[hrows, :].astype(jnp.float32) * go_h.astype(jnp.float32), axis=0, keepdims=True)
            for k in range(5):
                bacc[k] = jnp.zeros((128, 128), jnp.float32)
            gq[...] = jnp.zeros_like(gq)
            qm = head_rows(qt, p, hh, full)
            gm = head_rows(got, p, hh, full)
            for g in range(nkey // 2):
                pp, gg = [], []
                for c in range(nchunk):
                    cols = slice(c * 256, (c + 1) * 256)
                    pc, gc = [], []
                    for b in (2 * g, 2 * g + 1):
                        keys = slice(b * 128, (b + 1) * 128)
                        s = nn(kp[p, keys, :], qm[:, cols])
                        dp = nn(vp[p, keys, :], gm[:, cols])
                        s = s + mask[keys, cols]
                        kinds = [band_kind((2 * c + k) % nrow, b, nrow, nkey) for k in range(2)]
                        if any(k is not None for k in kinds):
                            s = jnp.concatenate([s[:, k * 128:(k + 1) * 128] + (band[kinds[k]] if kinds[k] is not None else 0.0) for k in range(2)], axis=1)
                        pr = jnp.exp2(s - (lse[h, 0:1, cols] - cf[b:b + 1, cols]))
                        gs = pr * (dp - delta[:, cols])
                        for k in range(2):
                            if kinds[k] is not None:
                                bacc[kinds[k]] += gs[:, k * 128:(k + 1) * 128]
                        pc.append(pr.astype(jnp.bfloat16))
                        gc.append(gs.astype(jnp.bfloat16))
                    pp.append(jnp.concatenate(pc, axis=0))
                    gg.append(jnp.concatenate(gc, axis=0))
                pall = jnp.concatenate(pp, axis=1)
                gall = jnp.concatenate(gg, axis=1)
                keys = slice(g * 256, (g + 1) * 256)
                onehot = (block_of == 2 * g + half_of).astype(jnp.bfloat16)
                gq[...] += nn(jnp.concatenate([kt[hrows, keys], onehot], axis=0), gall)
                gkt[hrows, keys] = (nt(q_h, gall) * LN2).astype(jnp.bfloat16)
                gvt[hrows, keys] = nt(go_h, pall).astype(jnp.bfloat16)
            gqt[hrows, :] = (gq[:64, :] * 0.125).astype(jnp.bfloat16)
            for k in range(5):
                direct, wrapped = diagonal_sums(bacc[k])
                diag[h, 0:1, 256 * k:256 * k + 128] = direct
                diag[h, 0:1, 256 * k + 128:256 * k + 256] = wrapped
            for s in range(2):
                side = jnp.sum(jnp.sum(gq[64:80, :] * sides[s], axis=0, keepdims=True), axis=1, keepdims=True)
                diag[h, 0:1, 1280 + 128 * s:1408 + 128 * s] = jnp.where(lane_row == 0, side, 0.0)
        return 0
    lax.fori_loop(0, kp.shape[0], pair, 0)
    tp_index = lax.axis_index("tp")
    places = lax.broadcasted_iota(jnp.int32, (128, 128), 0)
    numbers = lax.broadcasted_iota(jnp.int32, (128, 128), 1)
    sums = jnp.concatenate([diag[h] for h in range(diag.shape[0])], axis=0)
    total = jnp.zeros((diag.shape[0], 128), jnp.float32)
    for slot in range(12):
        one_hot = jnp.where(slot_bucket(slot, places, tp_index, tp_size) == numbers, 1.0, 0.0)
        total = total + jnp.dot(
            sums[:, slot * 128:(slot + 1) * 128], one_hot, precision=lax.Precision.HIGHEST, preferred_element_type=jnp.float32
        )
    back_table[...] = total
    if fused:
        stores = Loads([(gqt, gqt_out), (gkt, gkt_out), (gvt, gvt_out)], out_sems)
        scatter.stage2(2)
        scatter.stage3(3)
        loads.wait(6, 7, 8, 9)
        span, narrow = part.shape[1], kt.shape[0] // 4
        for d in range(4):
            here = pl.ds(pl.multiple_of(((d - at.t + 4) % 4) * span, 128), span)
            value = jnp.zeros(part.shape[1:], jnp.float32)
            for b in range(4):
                block = slice(b * narrow, (b + 1) * narrow)
                value = value + nt(jnp.concatenate([gkt[block, here], gvt[block, here]], axis=0).T, weights[b])
            part[d] = value.astype(jnp.bfloat16)
        scatter.stage2(3)
        sums = scatter.finish()
        wide = sum_in.shape[1]
        sum_in[...] = sums[:, :wide]
        sum_down[...] = sums[:, wide:2 * wide]
        sum_out[...] = sums[:, 2 * wide:].T
        stores.wait(0, 1, 2)


def attend_bwd(tp_size, ranks, starts, table, kp, vp, kt, qt, ot, got, lse, g=None, first=None):
    pairs, seq, _ = kp.shape
    rows = qt.shape[1]
    heads = 2 * pairs
    nrow, nkey = rows // 256, seq // 128
    V, M = pl.BlockSpec(memory_space=pltpu.MemorySpace.VMEM), pl.BlockSpec(memory_space=pltpu.MemorySpace.SMEM)
    S, F = jax.ShapeDtypeStruct, jnp.float32
    fused = g is not None
    out_specs = [V] * 4
    outs = [S(qt.shape, jnp.bfloat16), S(kt.shape, jnp.bfloat16), S(kt.shape, jnp.bfloat16), S((heads, 128), F)]
    scratch = [pltpu.VMEM((80, rows), F), pltpu.VMEM((5, 128, 128), F), pltpu.VMEM((heads, 1, 1536), F)] + prepare_scratch(nrow, nkey, heads)
    params = dict(vmem_limit_bytes=VLIM)
    args = (ranks, starts, table, kp, vp, kt, qt, ot, got, lse)
    specs = [V, M] + [V] * 8
    if fused:
        narrow = kt.shape[0] // 4
        wide = (g.shape[5] - narrow) // 2
        outs += [S((g.shape[4], wide), F), S((g.shape[4], wide), F), S((narrow, g.shape[4]), F), S((4, rows // 2, kt.shape[0]), jnp.bfloat16)]
        scratch[3:3] = [pltpu.VMEM((4, kt.shape[0], 2 * narrow), jnp.bfloat16)] + [pltpu.VMEM(o.shape, o.dtype) for o in outs[:3]] + [pltpu.SemaphoreType.DMA((3,))]
        scratch += [pltpu.VMEM(a.shape, a.dtype) for a in (kp, vp, kt, qt, ot, got)] + [pltpu.SemaphoreType.DMA((10,))]
        scratch += scatter_scratch(g.shape[0], g.shape[4], g.shape[5])
        params.update(collective_id=2, has_side_effects=True)
        args += (g, first)
        A = pl.BlockSpec(memory_space=pl.ANY)
        specs = specs[:3] + [A] * 6 + [V, A, A]
        out_specs = [A] * 3 + [V] * 5
    return pl.pallas_call(
        functools.partial(bwd_kernel, nrow, nkey, tp_size, fused),
        out_shape=tuple(outs), in_specs=specs, out_specs=tuple(out_specs), scratch_shapes=scratch,
        compiler_params=pltpu.CompilerParams(**params), name="attend_bwd",
    )(*args)


def norm(residual):
    centered = residual - jnp.mean(residual, axis=-1, keepdims=True)
    scale = lax.rsqrt(jnp.mean(centered * centered, axis=-1, keepdims=True) + EPSILON)
    return centered * scale, scale


def norm_step(cotangent, normal, scale, gain):
    inner = cotangent * gain
    mean_inner = jnp.mean(inner, axis=-1, keepdims=True)
    mean_cross = jnp.mean(inner * normal, axis=-1, keepdims=True)
    return scale * (inner - mean_inner - normal * mean_cross)


def middle_kernel(chunk, ot_in, content, query, first, second_in, gain1, shift1, gain2, shift2, ranks, up_content, up_query,
                  content_out, query_out, grads, back_out, got_out, sums,
                  back, got, store_sems, ot, second, x, up, wot, wo_block, onat, n1bt, gft, gat, hidden, slope, gu, out2, stage, sems, out_sems):
    rows = content.shape[0]
    seq, width = ranks.shape[1], content.shape[1]
    narrow, wide = width // 4, second.shape[2] // 2
    loads = Loads(
        [(first.at[t, :, pl.ds(0, 256)], wo_block.at[t]) for t in range(4)] + [(ot_in, ot)]
        + [(second_in.at[t], second.at[t]) for t in range(4)], sems
    )
    base = rows * lax.axis_index("tp")
    x[:rows] = content[...]
    x[rows:] = query[...]
    up[:rows] = up_content[...].astype(jnp.float32)
    for i in range(rows // 128):
        rank = ranks[0:1, pl.ds(pl.multiple_of(base + i * 128, 128), 128)].astype(jnp.float32)
        rank = jnp.broadcast_to(rank, (128, 128)).T
        kept = jnp.where(rank >= seq - seq * 15 // 100, 1.0, 0.0)
        up[rows + i * 128:rows + (i + 1) * 128, :] = up_query[i * 128:(i + 1) * 128, :].astype(jnp.float32) * jnp.concatenate([kept] * (width // 128), axis=1)
    loads.wait(0, 1, 2, 3, 4)
    wot[...] = jnp.concatenate([wo_block[t, :, :narrow] for t in range(4)], axis=1)
    sums[...] = jnp.zeros_like(sums)
    gain1, shift1, gain2, shift2 = (ref[...].reshape(1, width) for ref in (gain1, shift1, gain2, shift2))

    def one(i, _):
        here = pl.ds(pl.multiple_of(i * chunk, chunk), chunk)
        mixed = ot[:, here].T
        onat[here, :] = mixed
        normal1, scale1 = norm(x[here, :].astype(jnp.float32) + nt(mixed, wot[...]))
        normed = normal1 * gain1 + shift1
        low = normed.astype(jnp.bfloat16)
        n1bt[:, here] = low.T
        total = normed
        for t in range(4):
            @pl.when(i == 0)
            def _():
                loads.wait(5 + t)
            lifted = nn(low, second[t, :, :wide])
            phi = 0.5 + 0.5 * lax.erf(lifted * (0.5 ** 0.5))
            act = (lifted * phi).astype(jnp.bfloat16)
            hidden[t, here, :] = act
            slope[t] = phi + lifted * (jnp.exp(-0.5 * lifted * lifted) * 0.3989422804014327)
            total = total + nt(act, second[t, :, wide:])
        normal2, scale2 = norm(total)
        out2[here, :] = (normal2 * gain2 + shift2).astype(jnp.bfloat16)
        cotangent = up[here, :]
        sums[2:3, :] += jnp.sum(cotangent * normal2, axis=0, keepdims=True)
        sums[3:4, :] += jnp.sum(cotangent, axis=0, keepdims=True)
        back2 = norm_step(cotangent, normal2, scale2, gain2)
        gf = back2.astype(jnp.bfloat16)
        gft[:, here] = gf.T
        total = back2
        for t in range(4):
            g = (slope[t] * nn(gf, second[t, :, wide:])).astype(jnp.bfloat16)
            gu[t, here, :] = g
            total = total + nt(g, second[t, :, :wide])
        sums[0:1, :] += jnp.sum(total * normal1, axis=0, keepdims=True)
        sums[1:2, :] += jnp.sum(total, axis=0, keepdims=True)
        back1 = norm_step(total, normal1, scale1, gain1)
        back[here, :] = back1
        ga = back1.astype(jnp.bfloat16)
        gat[:, here] = ga.T
        got[:, here] = nn(ga, wot[...]).astype(jnp.bfloat16).T
        return 0

    lax.fori_loop(0, 2 * rows // chunk, one, 0)
    stores = Loads([(out2.at[:rows], content_out), (out2.at[rows:], query_out), (back, back_out), (got, got_out)], store_sems)
    for t in range(4):
        wo_block[t, :, :narrow] = nn(gat[...], onat[:, t * narrow:(t + 1) * narrow]).astype(jnp.bfloat16)

    def send(t):
        return pltpu.make_async_copy(stage.at[t % 2], grads.at[t], out_sems.at[t % 2])

    for t in range(4):
        if t >= 2:
            send(t - 2).wait()
        stage[t % 2, :, :wide] = nn(n1bt[...], gu[t]).astype(jnp.bfloat16)
        stage[t % 2, :, wide:2 * wide] = nn(gft[...], hidden[t]).astype(jnp.bfloat16)
        stage[t % 2, :, 2 * wide:] = wo_block[t, :, :narrow]
        send(t).start()
    for t in (2, 3):
        send(t).wait()
    stores.wait(0, 1, 2, 3)


def middle(ot, content, query, first, second, norms, ranks, up_content, up_query):
    rows, width = content.shape
    narrow, wide = width // 4, second.shape[2] // 2
    both, chunk = 2 * rows, rows
    V, A = pl.BlockSpec(memory_space=pltpu.MemorySpace.VMEM), pl.BlockSpec(memory_space=pl.ANY)
    B, F, S, DMA = jnp.bfloat16, jnp.float32, jax.ShapeDtypeStruct, pltpu.SemaphoreType.DMA
    return pl.pallas_call(
        functools.partial(middle_kernel, chunk),
        out_shape=(S((rows, width), B), S((rows, width), B), S((4, width, 2 * wide + narrow), B), S((both, width), F), S((width, both), B), S((8, width), F)),
        in_specs=[A, V, V, A, A] + [V] * 7, out_specs=(A, A, A, A, A, V),
        scratch_shapes=[
            pltpu.VMEM((both, width), F), pltpu.VMEM((width, both), B), DMA((4,)), pltpu.VMEM(ot.shape, B), pltpu.VMEM(second.shape, B),
            pltpu.VMEM((both, width), B), pltpu.VMEM((both, width), F), pltpu.VMEM((width, width), B), pltpu.VMEM((4, width, 256), B),
            pltpu.VMEM((both, width), B), pltpu.VMEM((width, both), B), pltpu.VMEM((width, both), B), pltpu.VMEM((width, both), B),
            pltpu.VMEM((4, both, wide), B), pltpu.VMEM((4, chunk, wide), F), pltpu.VMEM((4, both, wide), B), pltpu.VMEM((both, width), B),
            pltpu.VMEM((2, width, 2 * wide + narrow), B), DMA((9,)), DMA((2,)),
        ],
        compiler_params=pltpu.CompilerParams(vmem_limit_bytes=VLIM), name="middle",
    )(ot, content, query, first, second, *norms, ranks, up_content, up_query)


def finish_kernel(count, *refs):
    sources, norms, outs, held, sems = refs[:count], refs[count], refs[count + 1:2 * count + 5], refs[2 * count + 5:-1], refs[-1]
    loads = [pltpu.make_async_copy(src, mid, sems.at[0, i]) for i, (src, mid) in enumerate(zip(sources, held))]
    stores = [pltpu.make_async_copy(mid, dst, sems.at[1, i]) for i, (mid, dst) in enumerate(zip(held, outs))]
    for c in loads:
        c.start()
    for i in range(4):
        outs[count + i][...] = norms[i:i + 1, :].reshape(norms.shape[1])
    for load, store in zip(loads, stores):
        load.wait()
        store.start()
    for c in stores:
        c.wait()


def finish(arrays, norms):
    V, A, S = pl.BlockSpec(memory_space=pltpu.MemorySpace.VMEM), pl.BlockSpec(memory_space=pl.ANY), jax.ShapeDtypeStruct
    count = len(arrays)
    return pl.pallas_call(
        functools.partial(finish_kernel, count),
        out_shape=tuple(S(a.shape, a.dtype) for a in arrays) + tuple(S((norms.shape[1],), norms.dtype) for _ in range(4)),
        in_specs=[A] * count + [V], out_specs=(A,) * count + (V,) * 4, scratch_shapes=[pltpu.VMEM(a.shape, a.dtype) for a in arrays] + [pltpu.SemaphoreType.DMA((2, count))],
        compiler_params=pltpu.CompilerParams(vmem_limit_bytes=VLIM), name="finish",
    )(*arrays, norms)


def dot(spec, a, b):
    return jnp.einsum(spec, a, b, preferred_element_type=jnp.float32)


def norm_stats(residual):
    centered = residual - jnp.mean(residual, axis=-1, keepdims=True)
    scale = lax.rsqrt(jnp.mean(centered * centered, axis=-1, keepdims=True) + EPSILON)
    return centered * scale, scale


def norm_back(cotangent, normal, scale, gain):
    inner = cotangent * gain
    mean_inner = jnp.mean(inner, axis=-1, keepdims=True)
    mean_cross = jnp.mean(inner * normal, axis=-1, keepdims=True)
    back = scale * (inner - mean_inner - normal * mean_cross)
    return back, jnp.sum(cotangent * normal, axis=0), jnp.sum(cotangent, axis=0)


def local(
    tp_size, own_exchange, content, query, w_query, w_key, w_value, w_out, w_in, w_down, gain_first, shift_first,
    gain_second, shift_second, bias_table, ranks, span_starts, upstream_content, upstream_query,
):
    rows, width = content.shape
    seq = ranks.shape[1]
    heads = bias_table.shape[0]
    pairs = heads // 2
    tp_index = lax.axis_index("tp")
    both_axes = ("tp", "fsdp")
    narrow = w_query.shape[1]

    def gather(parts):
        shard = jnp.concatenate(parts, axis=1)
        return lax.all_gather(shard, both_axes, axis=0, tiled=True).reshape(tp_size, width, shard.shape[1])

    wide = w_in.shape[1]
    shift = -rows * tp_index
    both = jnp.concatenate([content, query], axis=0)
    if own_exchange:
        ot, lse, seqt, queryt, kp, vp, kt, qt, first, second = front(
            content, query, w_query, w_key, w_value, w_out, w_in, w_down.T, ranks, span_starts, bias_table
        )
        first, second = first.reshape(tp_size, width, 4 * narrow), second.reshape(tp_size, width, 2 * wide)
    else:
        first, second = gather([w_out.T, w_query, w_key, w_value]), gather([w_in, w_down.T])
    wo, wq, wk, wv = (first[:, :, i * narrow:(i + 1) * narrow] for i in range(4))
    wi, wd = second[:, :, :wide], second[:, :, wide:]
    if not own_exchange:
        seq_rot = jnp.roll(lax.all_gather(content, "tp", axis=0, tiled=True), shift, axis=0)
        qt = (dot("tdc,rd->tcr", wq, both) * (HEAD ** -0.5 * LOG2E)).astype(jnp.bfloat16).reshape(width, 2 * rows)
        kt = dot("tdc,rd->tcr", wk, seq_rot).astype(jnp.bfloat16).reshape(width, seq)
        vt = dot("tdc,rd->tcr", wv, seq_rot).astype(jnp.bfloat16).reshape(width, seq)
        kp = jnp.swapaxes(kt.reshape(pairs, 128, seq), 1, 2)
        vp = jnp.swapaxes(vt.reshape(pairs, 128, seq), 1, 2)
        ot, lse = attend_fwd(tp_size, ranks, span_starts, bias_table, kp, vt, qt)

    if own_exchange:
        norms = [gain_first, shift_first, gain_second, shift_second]
        content_out, query_out, grad_second, back_first, got, norm_stack = middle(
            ot, content, query, first, second, norms, ranks, upstream_content, upstream_query
        )
    else:
        ot_blocks = ot.reshape(tp_size, narrow, 2 * rows)
        residual_first = both.astype(jnp.float32) + dot("tcr,tmc->rm", ot_blocks, wo)
        normal_first, scale_first = norm_stats(residual_first)
        normed_first = normal_first * gain_first + shift_first
        low_first = normed_first.astype(jnp.bfloat16)
        lifted = dot("rd,tdf->trf", low_first, wi)
        phi = 0.5 * (1.0 + lax.erf(lifted * (0.5 ** 0.5)))
        hidden = (lifted * phi).astype(jnp.bfloat16)
        slope = phi + lifted * jnp.exp(-0.5 * lifted * lifted) * 0.3989422804014327
        residual_second = normed_first + dot("trf,tmf->rm", hidden, wd)
        normal_second, scale_second = norm_stats(residual_second)
        normed_second = normal_second * gain_second + shift_second
        rank_rows = lax.dynamic_slice_in_dim(ranks[0], rows * tp_index, rows)
        predicted = (rank_rows >= seq - seq * 15 // 100).astype(jnp.float32)
        upstream = jnp.concatenate(
            [upstream_content.astype(jnp.float32), upstream_query.astype(jnp.float32) * predicted[:, None]], axis=0
        )
        back_second, grad_gain_second, grad_shift_second = norm_back(upstream, normal_second, scale_second, gain_second)
        gf = back_second.astype(jnp.bfloat16)
        gu = (slope * dot("rm,tmf->trf", gf, wd)).astype(jnp.bfloat16)
        grad_down = dot("rm,trf->tmf", gf, hidden)
        grad_in = dot("rd,trf->tdf", low_first, gu)
        back_normed = back_second + dot("trf,tdf->rd", gu, wi)
        back_first, grad_gain_first, grad_shift_first = norm_back(back_normed, normal_first, scale_first, gain_first)
        ga = back_first.astype(jnp.bfloat16)
        grad_out = dot("rm,tcr->tmc", ga, ot_blocks)
        got = dot("rm,tmc->tcr", ga, wo).astype(jnp.bfloat16).reshape(width, 2 * rows)
        content_out, query_out = (normed_second[s * rows:(s + 1) * rows].astype(jnp.bfloat16) for s in range(2))
        norm_stack = jnp.stack([grad_gain_first, grad_shift_first, grad_gain_second, grad_shift_second])

    def scatter(blocks):
        flat = blocks.astype(jnp.bfloat16).reshape(tp_size * width, blocks.shape[2])
        return lax.psum_scatter(flat, both_axes, scatter_dimension=0, tiled=True).astype(jnp.float32)

    if own_exchange:
        grad_second = grad_second.reshape(4, 2, 2, 2, width // 8, grad_second.shape[2])
        gqt, gkt, gvt, grad_table, sum_in, sum_down, sum_out, parts = attend_bwd(
            tp_size, ranks, span_starts, bias_table, kp, vp, kt, qt, ot, got, lse, grad_second, first
        )
        grad_content, grad_query, sum_query, sum_key, sum_value, norms, grad_table = tail(
            parts, gqt, gkt, gvt, seqt, queryt, first, back_first, norm_stack, grad_table
        )
        (grad_content, grad_query, sum_query, sum_key, sum_value, sum_out, sum_in, sum_down, *norms) = finish(
            (grad_content, grad_query, sum_query, sum_key, sum_value, sum_out, sum_in, sum_down), norms
        )
    else:
        sum_down, sum_in, sum_out = scatter(grad_down), scatter(grad_in), scatter(grad_out).T
        gqt, gkt, gvt, grad_table = attend_bwd(tp_size, ranks, span_starts, bias_table, kp, vp, kt, qt, ot, got, lse)
        gq_blocks, gk_blocks, gv_blocks = (g.reshape(tp_size, narrow, g.shape[1]) for g in (gqt, gkt, gvt))
        sum_query = scatter(dot("rd,tcr->tdc", both, gq_blocks))
        sum_key = scatter(dot("rd,tcr->tdc", seq_rot, gk_blocks))
        sum_value = scatter(dot("rd,tcr->tdc", seq_rot, gv_blocks))
        back_seq = dot("tcr,tdc->rd", gk_blocks, wk) + dot("tcr,tdc->rd", gv_blocks, wv)
        back_seq = jnp.roll(back_seq.astype(jnp.bfloat16), -shift, axis=0)
        back_content = lax.psum_scatter(back_seq, "tp", scatter_dimension=0, tiled=True).astype(jnp.float32)
        back_inputs = back_first + dot("tcr,tdc->rd", gq_blocks, wq)
        grad_content, grad_query = back_inputs[:rows] + back_content, back_inputs[rows:]
        norms, grad_table = lax.psum((norm_stack, grad_table), ("fsdp", "tp"))
    return (
        content_out, query_out, grad_content, grad_query, sum_query, sum_key, sum_value, sum_out, sum_in, sum_down.T,
        norms[0], norms[1], norms[2], norms[3], grad_table[:, :NB],
    )


def solution(mesh):
    in_specs = (
        P(("fsdp", "tp"), None),
        P(("fsdp", "tp"), None),
        P("fsdp", "tp"),
        P("fsdp", "tp"),
        P("fsdp", "tp"),
        P("tp", "fsdp"),
        P("fsdp", "tp"),
        P("tp", "fsdp"),
        P(),
        P(),
        P(),
        P(),
        P(),
        P("fsdp", None),
        P("fsdp", None),
        P(("fsdp", "tp"), None),
        P(("fsdp", "tp"), None),
    )
    out_specs = (
        P(("fsdp", "tp"), None),
        P(("fsdp", "tp"), None),
        P(("fsdp", "tp"), None),
        P(("fsdp", "tp"), None),
        P("fsdp", "tp"),
        P("fsdp", "tp"),
        P("fsdp", "tp"),
        P("tp", "fsdp"),
        P("fsdp", "tp"),
        P("tp", "fsdp"),
        P(),
        P(),
        P(),
        P(),
        P(),
    )
    return jax.shard_map(functools.partial(local, mesh.shape["tp"], mesh.shape["tp"] == 4 and mesh.shape["fsdp"] == 8), mesh=mesh, in_specs=in_specs, out_specs=out_specs, check_vma=False)
```
